32 devices in a mesh: expert: 4 (over y, core), context: 4 (over z), dp: 2 (over x).
Axes of the slice: x: 2, y: 2, z: 4, core: 2. Of those that a mesh axis runs over, the one named last changes fastest.
Arguments:
- inputs: bfloat16 [8, 2, 1024, 768], P(('expert', 'dp'), None, 'context'), may hold values from -6 to 6
- keep_flags: int32 [8, 2, 1024], P(('expert', 'dp'), None, 'context'), may hold values 0 or 1
- block_ids: int32 [8, 2, 1024], P(('expert', 'dp'), None, 'context'), may hold values from 0 to 7, never falling along the last dimension, each value on 1 to 256 neighbouring positions
- expert_ids: int32 [8, 2, 1024, 2], P(('expert', 'dp'), None, 'context'), may hold values from 0 to 3, all different within a row; in each aligned block of 256 rows (0 to 255, 256 to 511, ..., all dimensions but the last counted through in order) at most 256 rows name the same one
- gate_weights: float32 [8, 2, 1024, 2], P(('expert', 'dp'), None, 'context'), may hold values from 0.2 to 0.8
- norm_attn: bfloat16 [768], P('dp'), may hold values from 0.5 to 1.5
- w_qkv: bfloat16 [768, 2304], P('dp'), may hold values from -0.21875 to 0.21875
- w_attn_out: bfloat16 [768, 768], P('dp'), may hold values from -4 to 4
- norm_ffn: bfloat16 [768], P('dp'), may hold values from 0.5 to 1.5
- w_shared_in: bfloat16 [768, 4096], P('dp'), may hold values from -0.21875 to 0.21875
- w_shared_out: bfloat16 [2048, 768], P('dp'), may hold values from -0.125 to 0.125
- w_expert_in: bfloat16 [4, 768, 4096], P('expert', 'dp'), may hold values from -0.21875 to 0.21875
- w_expert_out: bfloat16 [4, 2048, 768], P('expert', 'dp'), may hold values from -0.125 to 0.125
- cotangent: bfloat16 [8, 2, 1024, 768], P(('expert', 'dp'), None, 'context'), may hold values from -6 to 6
Outputs:
- output: bfloat16 [8, 2, 1024, 768], P(('expert', 'dp'), None, 'context')
- grad_input: float32 [8, 2, 1024, 768], P(('expert', 'dp'), None, 'context')
- grad_norm_attn: float32 [768], P('dp')
- grad_w_qkv: float32 [768, 2304], P('dp')
- grad_w_attn_out: float32 [768, 768], P('dp')
- grad_norm_ffn: float32 [768], P('dp')
- grad_w_shared_in: float32 [768, 4096], P('dp')
- grad_w_shared_out: float32 [2048, 768], P('dp')
- grad_w_expert_in: float32 [4, 768, 4096], P('expert', 'dp')
- grad_w_expert_out: float32 [4, 2048, 768], P('expert', 'dp')
The draws below stay inside these ranges and needn't reach their ends.
Inputs may be any that keep to these rules, and one draw needn't show every extreme that they name: `expert_ids`: in each aligned block of 256 rows (one device's positions of one micro-batch) no expert is named more than 256 times; some expert is named exactly 256 times in some block. `block_ids`: never falling along a micro-batch; each block holds 1 to 256 positions and one holds exactly 256.
All inputs are finite; a program needn't handle non-finite values. No bound on the sum of `keep_flags` on one device may be relied on, other than what follows from the above.
Results may differ from the reference program's by a relative error of at most 0.02.
Values may be sent and summed in bfloat16 or wider, within the bound.
A program may use at most 320 MiB of HBM per device.

```python
import math
import jax
import jax.numpy as jnp
import numpy as np
from jax import lax

D = 768
HEADS = 12
HEAD = 64
FF = 2048
TOP = 2
BLK = 256
MICRO = 2
TOK_MB = 256
EXPERTS = 4
CAP = 256
SEQ_MB = 1024
SEQS = 8


def set_ends(array, stream_key, least, high):
    spot = [jax.random.randint(jax.random.fold_in(stream_key, axis), (), 0, length) for axis, length in enumerate(array.shape)]
    main_axis = array.shape.index(max(array.shape))
    neighbour = spot[:main_axis] + [(spot[main_axis] + 1) % array.shape[main_axis]] + spot[main_axis + 1:]
    return array.at[tuple(spot)].set(least).at[tuple(neighbour)].set(high)


def block_scale(own_key, shape, split, low, largest):
    def one(position, parts):
        steps = jax.random.uniform(jax.random.fold_in(jax.random.fold_in(own_key, 6), position), (parts,), jnp.float32, low / len(split), largest / len(split))
        return jnp.repeat(jnp.exp(steps), shape[position] // parts).reshape((-1,) + (1,) * (len(shape) - position - 1))

    level = one(*split[0])
    for cut in split[1:]:
        level = level * one(*cut)
    return level


def split_up(amount, total, reach, skew):
    loads = [(1 << 20) // math.isqrt(rank ** skew) + 1 for rank in range(2, amount + 1)]
    rest, given = total - reach - (amount - 1), [1] * (amount - 1)
    while rest > 0:
        movable = [i for i in range(amount - 1) if given[i] < reach]
        mass, budget = sum([loads[i] for i in movable]), rest
        for i in movable:
            more = min(reach - given[i], max(1, budget * loads[i] // mass), rest)
            given[i] = given[i] + more
            rest = rest - more
    return np.array([reach] + given)


def ragged_sizes(stream_key, amount, total, most, lean):
    if amount == 2:
        one = jax.random.randint(stream_key, (), max(1, total - most), min(most, total - 1) + 1)
        return jnp.stack([one, total - one])
    tallies = jnp.asarray(split_up(amount, total, most, lean), jnp.int32)
    twos = (amount - 1) // 2
    donor, receiver = tallies[1:1 + 2 * twos:2], tallies[2:2 + 2 * twos:2]
    margin = jnp.minimum(donor - 1, most - receiver)
    moved = jax.random.randint(jax.random.fold_in(stream_key, 1), (twos,), 0, 1 << 20) % (margin + 1)
    tallies = tallies.at[1:1 + 2 * twos:2].set(donor - moved).at[2:2 + 2 * twos:2].set(receiver + moved)
    return tallies[jax.random.permutation(jax.random.fold_in(stream_key, 2), amount)]


def routed_block(rng, own, number, rows, amount, top, limit, slope):
    sequence = jax.random.permutation(rng, amount)
    heavy_load, common = portions_of(amount, rows * top, limit, slope, True), portions_of(amount, rows * top, limit, slope, False)
    places = jnp.arange(amount)

    def named(lengths, turn):
        used = int((lengths > 0).sum())
        fixed = max(1, used // 4)
        moved = fixed + (places - fixed + turn * (used - fixed)) % max(1, amount - fixed)
        return jnp.zeros((amount,), jnp.int32).at[sequence[jnp.where(places < fixed, places, moved)]].set(jnp.asarray(lengths, jnp.int32))

    lengths = jnp.where(number % 4 == 0, named(heavy_load, number // 4), named(common, number - number // 4 - 1))
    mixed = jax.random.permutation(jax.random.fold_in(own, 3), amount)
    source_of, sink = mixed[0:amount // 2 * 2:2], mixed[1:amount // 2 * 2:2]
    margin = jnp.minimum(lengths[source_of] - 1, limit - lengths[sink]) // 2
    margin = jnp.where((source_of == sequence[0]) | (sink == sequence[0]) | (lengths[sink] == 0), 0, jnp.maximum(margin, 0))
    moved = jax.random.randint(jax.random.fold_in(own, 4), (amount // 2,), 0, 1 << 20) % (margin + 1)
    lengths = lengths.at[source_of].add(-moved).at[sink].add(moved)
    members = jnp.searchsorted(jnp.cumsum(lengths), jnp.arange(rows * top), side="right").astype(jnp.int32)
    listing = members.reshape(top, rows).T
    listing = listing[jax.random.permutation(jax.random.fold_in(own, 1), rows)]
    turn = jax.random.randint(jax.random.fold_in(own, 2), (rows, 1), 0, top)
    return jnp.take_along_axis(listing, (jnp.arange(top)[None, :] + turn) % top, axis=1)


def portions_of(count, total, most, skew, full):
    loads = [(1 << 20) // math.isqrt(rank ** skew) + 1 for rank in range(1, count + 1)]
    largest = most if full else min(most, max(-(-total // count), total * loads[0] // sum(loads)))
    least = 1 if total - largest >= count - 1 else 0
    holding, rest = [largest] + [least] * (count - 1), total - largest - least * (count - 1)
    while rest > 0:
        movable = [i for i in range(1, count) if holding[i] < largest] or [i for i in range(1, count) if holding[i] < most]
        mass, left = sum([loads[i] for i in movable]), rest
        for i in movable:
            addition = min(most - holding[i], max(1, left * loads[i] // mass), rest)
            holding[i] = holding[i] + addition
            rest = rest - addition
    return np.array(holding)


def centred(stream_key, shape, spread, limit, shards=(), held_as=jnp.bfloat16):
    array = jax.random.normal(stream_key, shape, jnp.float32) * spread
    if len(shards) > 0:
        array = block_scale(stream_key, shape, shards, -0.22, 0.18) * array
    return jnp.clip(array, min=-limit, max=limit).astype(held_as)


def setup_inputs(seed: int = 0) -> dict:
    streams_of = jax.random.split(jax.random.key(seed), 15)
    inputs = centred(streams_of[0], (SEQS, MICRO, SEQ_MB, D), 1.0, 6.0, ((0, 8), (2, 4)))
    keep_flags = set_ends((jax.random.randint(streams_of[1], (SEQS, MICRO, SEQ_MB), 0, 8) < 7).astype(jnp.int32), jax.random.fold_in(streams_of[1], 1), 0, 1)
    block_ids = jax.vmap(lambda own: jnp.searchsorted(jnp.cumsum(ragged_sizes(own, 2 * SEQ_MB // BLK, SEQ_MB, BLK, 1)), jnp.arange(SEQ_MB), side="right"))(jax.random.split(streams_of[2], SEQS * MICRO)).reshape((SEQS, MICRO, SEQ_MB)).astype(jnp.int32)
    expert_ids_keys = jax.random.split(jax.random.fold_in(streams_of[3], 1), SEQS * MICRO * SEQ_MB // TOK_MB)
    expert_ids_turns = jax.random.permutation(jax.random.fold_in(streams_of[3], 3), SEQS * MICRO * SEQ_MB // TOK_MB)
    expert_ids = jax.vmap(lambda own, number: routed_block(jax.random.fold_in(streams_of[3], 2), own, number, TOK_MB, EXPERTS, TOP, CAP, 1))(expert_ids_keys, expert_ids_turns).reshape((SEQS, MICRO, SEQ_MB, TOP))
    gate_weights = jnp.clip(0.2 + 0.6 * jax.random.uniform(streams_of[4], (SEQS, MICRO, SEQ_MB, TOP), jnp.float32) ** block_scale(streams_of[4], (SEQS, MICRO, SEQ_MB, TOP), ((0, 8), (2, 4)), -0.2, 0.2), 0.2, 0.8)
    norm_attn = jnp.clip(1.0 + 0.1 * jax.random.normal(streams_of[5], (D,), jnp.float32), 0.5, 1.5).astype(jnp.bfloat16)
    w_qkv = centred(streams_of[6], (D, 3 * D), D ** -0.5, 0.21875, ((0, 2),))
    w_attn_out = centred(streams_of[7], (D, D), 2 ** -0.5, 4.0, ((0, 2),))
    norm_ffn = jnp.clip(1.0 + 0.1 * jax.random.normal(streams_of[8], (D,), jnp.float32), 0.5, 1.5).astype(jnp.bfloat16)
    w_shared_in = centred(streams_of[9], (D, 2 * FF), D ** -0.5, 0.21875, ((0, 2),))
    w_shared_out = centred(streams_of[10], (FF, D), FF ** -0.5, 0.125, ((0, 2),))
    w_expert_in = centred(streams_of[11], (EXPERTS, D, 2 * FF), D ** -0.5, 0.21875, ((0, 4), (1, 2)))
    w_expert_out = centred(streams_of[12], (EXPERTS, FF, D), FF ** -0.5, 0.125, ((0, 4), (1, 2)))
    cotangent = centred(streams_of[13], (SEQS, MICRO, SEQ_MB, D), 1.0, 6.0, ((0, 8), (2, 4)))
    return {"inputs": inputs, "keep_flags": keep_flags, "block_ids": block_ids, "expert_ids": expert_ids, "gate_weights": gate_weights, "norm_attn": norm_attn, "w_qkv": w_qkv, "w_attn_out": w_attn_out, "norm_ffn": norm_ffn, "w_shared_in": w_shared_in, "w_shared_out": w_shared_out, "w_expert_in": w_expert_in, "w_expert_out": w_expert_out, "cotangent": cotangent}


@jax.custom_vjp
def low(v):
    return lax.optimization_barrier(v.astype(jnp.bfloat16)).astype(jnp.float32)

@jax.custom_vjp
def low_back(v):
    return v

def low_keep(v):
    return (low(v), None)

def low_pass(kept, grad):
    return (grad,)

def back_keep(v):
    return (v, None)

def back_low(kept, grad):
    return (low(grad),)
low.defvjp(low_keep, low_pass)
low_back.defvjp(back_keep, back_low)
EPSILON = 1e-05
ROPE_BASE = 10000.0
MASKED = -3e+30
HIGH = lax.Precision.HIGHEST

def hdot(left, right):
    return jnp.dot(left, right, precision=HIGH, preferred_element_type=jnp.float32)

def rms_norm(values, gain):
    return values * lax.rsqrt(lax.optimization_barrier(jnp.mean(values * values, -1, keepdims=True)) + EPSILON) * gain

def rotary_tables(positions, head):
    half = head // 2
    freq = jnp.exp(-math.log(ROPE_BASE) * jnp.arange(half, dtype=jnp.float32) * 2.0 / head)
    angle = positions.astype(jnp.float32)[:, None] * freq[None, :]
    return (jnp.cos(angle), jnp.sin(angle))

def rotate(values, cosines, sines, head):
    rows = values.shape[0]
    shaped = values.reshape(rows, -1, head)
    first = shaped[..., :head // 2]
    second = shaped[..., head // 2:]
    cos_b = cosines[:, None, :]
    sin_b = sines[:, None, :]
    turned = jnp.concatenate([first * cos_b - second * sin_b, second * cos_b + first * sin_b], -1)
    return turned.reshape(rows, -1)

def silu_glu(joined):
    half = joined.shape[-1] // 2
    return jax.nn.silu(joined[..., :half]) * joined[..., half:]

def forward(params, inputs, keep_flags, block_ids, expert_ids, gate_weights):
    norm_attn, w_qkv, w_attn_out, norm_ffn, w_shared_in, w_shared_out, w_expert_in, w_expert_out = params
    total = MICRO * SEQ_MB
    tokens = inputs.reshape(total, D)
    positions = jnp.arange(total, dtype=jnp.int32)
    normed = low(rms_norm(tokens, norm_attn))
    joined = low_back(hdot(normed, w_qkv))
    cosines, sines = rotary_tables(positions, HEAD)
    queries = low(rotate(joined[:, :D], cosines, sines, HEAD) * 0.125)
    keys_all = low(rotate(joined[:, D:2 * D], cosines, sines, HEAD))
    values_all = low(joined[:, 2 * D:])
    blocks_flat = block_ids.reshape(total)
    keep_flat = keep_flags.reshape(total)
    key_micro = positions // SEQ_MB
    width = math.gcd(total, 512)
    count = total // width
    key_heads = keys_all.reshape(total, HEADS, HEAD)
    value_heads = values_all.reshape(total, HEADS, HEAD)

    def attend(pieces):
        query_rows, query_pos = pieces
        query_micro = query_pos // SEQ_MB
        query_block = blocks_flat[query_pos]
        earlier = key_micro[None, :] < query_micro[:, None]
        same = (key_micro[None, :] == query_micro[:, None]) & (blocks_flat[None, :] <= query_block[:, None])
        usable = (keep_flat[None, :] == 1) | (positions[None, :] == query_pos[:, None])
        visible = (earlier | same) & usable
        scores = low_back(jnp.einsum('qhd,khd->hqk', query_rows.reshape(width, HEADS, HEAD), key_heads, precision=HIGH))
        scores = jnp.where(visible[None], scores, MASKED)
        top = lax.optimization_barrier(jnp.max(scores, -1, keepdims=True))
        expo = jnp.exp(scores - top)
        probs = low(expo / lax.optimization_barrier(jnp.sum(expo, -1, keepdims=True)))
        mixed = jnp.einsum('hqk,khd->qhd', probs, value_heads, precision=HIGH)
        return mixed.reshape(width, D)
    attended = lax.map(jax.checkpoint(attend), (queries.reshape(count, width, D), positions.reshape(count, width)))
    attended = low(low_back(attended.reshape(total, D)))
    residual = tokens + low_back(hdot(attended, w_attn_out))
    normed_ffn = low(rms_norm(residual, norm_ffn))
    shared_hidden = low(silu_glu(low_back(hdot(normed_ffn, w_shared_in))))
    shared = hdot(shared_hidden, w_shared_out)
    blocks_n = total // TOK_MB
    assigns = TOK_MB * TOP
    ids_flat = expert_ids.reshape(blocks_n, assigns)
    onehot = (ids_flat[:, :, None] == jnp.arange(EXPERTS, dtype=jnp.int32)[None, None, :]).astype(jnp.int32)
    before = jnp.cumsum(onehot, 1) - onehot
    slot = lax.optimization_barrier(jnp.sum(before * onehot, -1))
    dest = (ids_flat * CAP + slot).astype(jnp.int32)
    source_rows = jnp.arange(assigns, dtype=jnp.int32) // TOP
    rows = normed_ffn.reshape(blocks_n, TOK_MB, D)[:, source_rows]
    block_index = jnp.arange(blocks_n, dtype=jnp.int32)[:, None]
    buffer = jnp.zeros((blocks_n, EXPERTS * CAP, D), jnp.float32).at[block_index, dest].set(rows)
    buffer = low_back(buffer).reshape(blocks_n, EXPERTS, CAP, D)
    expert_joined = low_back(jnp.einsum('becd,edf->becf', buffer, w_expert_in, precision=HIGH))
    expert_hidden = low(silu_glu(expert_joined))
    expert_out = low(low_back(jnp.einsum('becf,efd->becd', expert_hidden, w_expert_out, precision=HIGH)))
    expert_out = expert_out.reshape(blocks_n, EXPERTS * CAP, D)
    picked = jnp.take_along_axis(expert_out, dest[:, :, None], axis=1)
    weighted = picked * gate_weights.reshape(blocks_n, assigns)[:, :, None]
    routed = lax.optimization_barrier(jnp.sum(weighted.reshape(blocks_n, TOK_MB, TOP, D), 2)).reshape(total, D)
    return (residual + shared + routed).reshape(MICRO, SEQ_MB, D)

def reference(inputs, keep_flags, block_ids, expert_ids, gate_weights, norm_attn, w_qkv, w_attn_out, norm_ffn, w_shared_in, w_shared_out, w_expert_in, w_expert_out, cotangent):
    params = tuple((p.astype(jnp.float32) for p in (norm_attn, w_qkv, w_attn_out, norm_ffn, w_shared_in, w_shared_out, w_expert_in, w_expert_out)))
    start = tuple((jnp.zeros_like(p) for p in params))

    def one_sequence(carry, pieces):
        seq_in, seq_keep, seq_blocks, seq_ids, seq_gates, seq_cot = pieces

        def bound(par, values):
            return forward(par, values, seq_keep, seq_blocks, seq_ids, seq_gates)
        result, pull = jax.vjp(bound, params, seq_in.astype(jnp.float32))
        grad_params, grad_in = pull(seq_cot.astype(jnp.float32))
        carry = tuple((a + b for a, b in zip(carry, grad_params)))
        return (carry, (result.astype(jnp.bfloat16), grad_in))
    totals, (output, grad_input) = lax.scan(one_sequence, start, (inputs, keep_flags, block_ids, expert_ids, gate_weights, cotangent))
    return (output, grad_input, totals[0], totals[1], totals[2], totals[3], totals[4], totals[5], totals[6], totals[7])
```

```python
import functools
import math

import jax
import jax.numpy as jnp
from jax import lax
from jax.experimental import pallas as pl
from jax.experimental.pallas import tpu as pltpu
from jax.sharding import PartitionSpec as P

HEAD = 64
MICRO = 2
TILE = 256
HALF = 128
EPSILON = 1e-05
ROPE_BASE = 10000.0
MASKED = -3e30
HIDDEN = 1 << 20
BF = jnp.bfloat16
F32 = jnp.float32
NT = (((1,), (1,)), ((), ()))
TN = (((0,), (0,)), ((), ()))
VMEM_LIMIT = 60 << 20
FB = 512


def dot(left, right, dims=(((1,), (0,)), ((), ()))):
    return lax.dot_general(left, right, dims, preferred_element_type=F32)


def rms_scale(values):
    return lax.rsqrt(jnp.mean(values * values, -1, keepdims=True) + EPSILON)


def low_lanes(rows):
    return lax.broadcasted_iota(jnp.int32, (rows, HALF), 1) < HEAD


def swap_heads(first, second):
    low = low_lanes(HALF)
    return (
        jnp.where(low, first, pltpu.roll(second, HEAD, 1)),
        jnp.where(low, pltpu.roll(first, HEAD, 1), second),
    )


def rotate(tile, cosines, sines):
    lane = lax.broadcasted_iota(jnp.int32, tile.shape, 1)
    partner = jnp.where(
        lane % HEAD < HEAD // 2,
        pltpu.roll(tile, HALF - HEAD // 2, 1),
        pltpu.roll(tile, HEAD // 2, 1),
    )
    return tile * cosines + partner * sines


def call(kernel, out_shape, *, grid=(), in_specs=None, out_specs=None, scratch=(), us=5):
    return pl.pallas_call(
        kernel,
        out_shape=out_shape,
        grid=grid,
        in_specs=in_specs,
        out_specs=out_specs,
        scratch_shapes=scratch,
        compiler_params=pltpu.CompilerParams(vmem_limit_bytes=VMEM_LIMIT),
        cost_estimate=price(us),
    )


def full_spec(shape):
    return pl.BlockSpec(tuple(shape), lambda *_: (0,) * len(shape))


def struct(shape, dtype):
    return jax.ShapeDtypeStruct(tuple(shape), dtype)


def pre_kernel(x_ref, gain_ref, w_ref, cos_ref, sin_ref, out_ref, *, groups):
    tokens = x_ref[0].astype(F32)
    normed = (tokens * rms_scale(tokens) * gain_ref[...]).astype(BF)
    width = tokens.shape[1]
    per = width // HEAD // groups
    cosines, sines = cos_ref[...], sin_ref[...]
    for kind in range(3):
        joined = dot(normed, w_ref[:, kind * width : (kind + 1) * width])
        for pair in range(width // HALF):
            tile = joined[:, pair * HALF : (pair + 1) * HALF]
            if kind < 2:
                tile = rotate(tile, cosines, sines)
            if kind == 0:
                tile = tile * 0.125
            for side, packed in enumerate(swap_heads(tile[:HALF], tile[HALF:])):
                head = 2 * pair + side
                out_ref[head // per, kind * per + head % per] = packed.astype(BF)


def run_pre(x, micro, gain, w, cosines, sines, groups):
    _, rows, width = x.shape
    per = width // HEAD // groups
    return call(
        functools.partial(pre_kernel, groups=groups),
        struct((groups, 3 * per, HALF, HALF), BF),
        grid=(1,),
        in_specs=[
            pl.BlockSpec((1, rows, width), lambda _: (micro, 0, 0)),
            full_spec(gain.shape),
            full_spec(w.shape),
            pl.BlockSpec((rows, HALF), lambda _: (micro, 0)),
            pl.BlockSpec((rows, HALF), lambda _: (micro, 0)),
        ],
        out_specs=full_spec((groups, 3 * per, HALF, HALF)),
        us=5,
    )(x, gain, w, cosines, sines)


def unpack(ref, index, kind_head):
    tile = ref[index, kind_head]
    return tile, pltpu.roll(tile.astype(F32), HEAD, 1).astype(BF)


def fill_keys(recvs, ks, vs, heads):
    for micro, recv in enumerate(recvs):
        for src in range(recv.shape[0]):
            base = (micro * recv.shape[0] + src) * TILE
            for h in range(heads):
                for store, kind in ((ks, 1), (vs, 2)):
                    first, second = unpack(recv, src, kind * heads + h)
                    store[h, base : base + HALF] = first
                    store[h, base + HALF : base + TILE] = second


def masked_rows(ref, index, kind_head):
    tile = ref[index, kind_head].astype(F32)
    both = jnp.concatenate([tile, pltpu.roll(tile, HEAD, 1)], 0)
    return jnp.where(low_lanes(TILE), both, 0.0)


def pack_rows(values):
    return jnp.where(low_lanes(HALF), values[:HALF], pltpu.roll(values[HALF:], HEAD, 1))


def attend_kernel(*refs, micro, heads, groups):
    recvs = refs[: micro + 1]
    key_tag, query_tag, out_ref, lse_ref, ks, vs, scores = refs[micro + 1 :]
    step = pl.program_id(0)

    @pl.when(step == 0)
    def _():
        fill_keys(recvs, ks, vs, heads)

    count = groups * micro + jnp.minimum(step + 2, groups)
    queries = [masked_rows(recvs[micro], step, h).astype(BF) for h in range(heads)]
    tag = query_tag[...]
    same = lax.broadcasted_iota(jnp.int32, (TILE, TILE), 0) == lax.broadcasted_iota(
        jnp.int32, (TILE, TILE), 1
    )

    def first_pass(j, tops):
        keys = pl.ds(pl.multiple_of(j * TILE, TILE), TILE)
        seen = (key_tag[j] <= tag) | (same & (j == groups * micro + step))
        new = []
        for h in range(heads):
            part = jnp.where(seen, dot(queries[h], ks[h, keys, :], NT), MASKED)
            scores[h, :, keys] = part
            new.append(jnp.maximum(tops[h], jnp.maximum(part[:, :HALF], part[:, HALF:])))
        return tuple(new)

    tops = lax.fori_loop(
        0, count, first_pass, (jnp.full((TILE, HALF), MASKED, F32),) * heads
    )
    tops = [jnp.max(top, 1, keepdims=True) for top in tops]

    def second_pass(j, carry):
        keys = pl.ds(pl.multiple_of(j * TILE, TILE), TILE)
        sums, totals = carry
        new_sums, new_totals = [], []
        for h in range(heads):
            expo = jnp.exp(scores[h, :, keys] - tops[h])
            new_sums.append(sums[h] + (expo[:, :HALF] + expo[:, HALF:]))
            new_totals.append(totals[h] + dot(expo.astype(BF), vs[h, keys, :]))
        return tuple(new_sums), tuple(new_totals)

    zero = (jnp.zeros((TILE, HALF), F32),) * heads
    sums, totals = lax.fori_loop(0, count, second_pass, (zero, zero))
    lane = lax.broadcasted_iota(jnp.int32, (TILE, HALF), 1)
    logs = jnp.zeros((TILE, HALF), F32)
    for h in range(heads):
        total = jnp.sum(sums[h], 1, keepdims=True)
        out_ref[step, h] = pack_rows(totals[h] / total).astype(BF)
        logs = jnp.where(lane == h, tops[h] + jnp.log(total), logs)
    lse_ref[step] = logs.T[:8]


def run_attend(recvs, key_tag, query_tag, groups):
    micro = len(recvs) - 1
    heads = recvs[0].shape[1] // 3
    held = groups * (micro + 1) * TILE
    return call(
        functools.partial(attend_kernel, micro=micro, heads=heads, groups=groups),
        (struct((groups, heads, HALF, HALF), BF), struct((groups, 8, TILE), F32)),
        grid=(groups,),
        in_specs=[full_spec(r.shape) for r in recvs]
        + [full_spec(key_tag.shape), pl.BlockSpec((TILE, 1), lambda s: (micro * groups + s, 0))],
        out_specs=(full_spec((groups, heads, HALF, HALF)), full_spec((groups, 8, TILE))),
        scratch=[
            pltpu.VMEM((heads, held, HALF), BF),
            pltpu.VMEM((heads, held, HALF), BF),
            pltpu.VMEM((heads, TILE, held), F32),
        ],
        us=15 + 11 * micro,
    )(*recvs, key_tag, query_tag)


def attend_back_kernel(*refs, micro, heads, groups):
    recvs = refs[: micro + 1]
    refs = refs[micro + 1 :]
    grad_ref, out_ref, lse_ref, key_tag, query_tag = refs[:5]
    refs = refs[5:]
    if micro == 0:
        pay_ref, early_k, early_v, ks, vs, dk, dv = refs
    else:
        early_k, early_v, pay_ref, pay0_ref, ks, vs, dk, dv = refs
    step = pl.program_id(0)

    @pl.when(step == 0)
    def _():
        fill_keys(recvs, ks, vs, heads)
        dk[...] = jnp.zeros_like(dk)
        dv[...] = jnp.zeros_like(dv)
        if micro > 0:
            dk[:, : groups * TILE] = early_k[...]
            dv[:, : groups * TILE] = early_v[...]

    count = groups * micro + jnp.minimum(step + 2, groups)
    queries = [masked_rows(recvs[micro], step, h).astype(BF) for h in range(heads)]
    grads_f = [masked_rows(grad_ref, step, h) for h in range(heads)]
    grads = [g.astype(BF) for g in grads_f]
    ones = jnp.ones((8, HALF), F32)
    deltas = [
        lax.dot_general(
            ones,
            grads_f[h] * masked_rows(out_ref, step, h),
            NT,
            precision=lax.Precision.HIGHEST,
            preferred_element_type=F32,
        )[:1]
        for h in range(heads)
    ]
    logs = [lse_ref[step, h : h + 1, :] for h in range(heads)]
    tag = query_tag[groups * micro + step]
    same = lax.broadcasted_iota(jnp.int32, (TILE, TILE), 0) == lax.broadcasted_iota(
        jnp.int32, (TILE, TILE), 1
    )

    def tile(j, totals):
        keys = pl.ds(pl.multiple_of(j * TILE, TILE), TILE)
        seen = (key_tag[keys, :] <= tag) | (same & (j == groups * micro + step))
        new = []
        for h in range(heads):
            key, value = ks[h, keys, :], vs[h, keys, :]
            scores = dot(key, queries[h], NT)
            probs = jnp.where(seen, jnp.exp(scores - logs[h]), 0.0)
            dv[h, keys, :] += dot(probs.astype(BF), grads[h])
            slope = (probs * (dot(value, grads[h], NT) - deltas[h])).astype(BF)
            dk[h, keys, :] += dot(slope, queries[h])
            new.append(totals[h] + dot(slope, key, TN))
        return tuple(new)

    totals = lax.fori_loop(0, count, tile, (jnp.zeros((TILE, HALF), F32),) * heads)
    for h in range(heads):
        pay_ref[step, h] = pack_rows(totals[h]).astype(BF)

    @pl.when(step == groups - 1)
    def _():
        if micro == 0:
            early_k[...] = dk[...]
            early_v[...] = dv[...]
        else:
            for src in range(groups):
                for ref, base, first in ((pay0_ref, 0, 0), (pay_ref, groups, heads)):
                    rows = slice((base + src) * TILE, (base + src + 1) * TILE)
                    for h in range(heads):
                        ref[src, first + h] = pack_rows(dk[h, rows]).astype(BF)
                        ref[src, first + heads + h] = pack_rows(dv[h, rows]).astype(BF)


def run_attend_back(recvs, grad, out, lse, key_tag, query_tag, early, groups):
    micro = len(recvs) - 1
    heads = recvs[0].shape[1] // 3
    held = groups * (micro + 1) * TILE
    pay = lambda n: struct((groups, n * heads, HALF, HALF), BF)
    part = struct((heads, groups * TILE, HALF), F32)
    args = [*recvs, grad, out, lse, key_tag, query_tag, *early]
    outs = [pay(1), part, part] if micro == 0 else [pay(3), pay(2)]
    return call(
        functools.partial(attend_back_kernel, micro=micro, heads=heads, groups=groups),
        tuple(outs),
        grid=(groups,),
        in_specs=[full_spec(a.shape) for a in args],
        out_specs=tuple(full_spec(o.shape) for o in outs),
        scratch=[
            pltpu.VMEM((heads, held, HALF), BF),
            pltpu.VMEM((heads, held, HALF), BF),
            pltpu.VMEM((heads, held, HALF), F32),
            pltpu.VMEM((heads, held, HALF), F32),
        ],
        us=23 + 20 * micro,
    )(*args)


def natural(ref, first_kind, pair, per):
    tiles = []
    for head in (2 * pair, 2 * pair + 1):
        tiles.append(ref[head // per, first_kind * per + head % per].astype(F32))
    return jnp.concatenate(swap_heads(*tiles), 0)


def post_kernel(o_ref, x_ref, w_ref, gain_ref, att_ref, res_ref, nf_ref, *, per):
    width = x_ref.shape[2]
    for pair in range(width // HALF):
        att_ref[:, pair * HALF : (pair + 1) * HALF] = natural(o_ref, 0, pair, per).astype(BF)
    residual = x_ref[0].astype(F32) + dot(att_ref[...], w_ref[...])
    res_ref[...] = residual
    nf_ref[...] = (residual * rms_scale(residual) * gain_ref[...]).astype(BF)


def run_post(mixed, x, micro, w, gain):
    _, rows, width = x.shape
    return call(
        functools.partial(post_kernel, per=mixed.shape[1]),
        (struct((rows, width), BF), struct((rows, width), F32), struct((rows, width), BF)),
        grid=(1,),
        in_specs=[
            full_spec(mixed.shape),
            pl.BlockSpec((1, rows, width), lambda _: (micro, 0, 0)),
            full_spec(w.shape),
            full_spec(gain.shape),
        ],
        out_specs=(full_spec((rows, width)),) * 3,
        us=3,
    )(mixed, x, w, gain)


def ffn_kernel(*refs, tr, spans, counts, first, gated, opened, summed, closing, parts):
    offs = refs[0]
    refs = list(refs[1:])
    take = lambda n: [refs.pop(0) for _ in range(n)]
    x_ref, dy_in = take(2)
    gate_ref = take(1)[0] if gated else None
    wg_parts, wu_parts, wo_parts = take(parts), take(parts), take(parts)
    y0, dx0 = take(2) if opened else (None, None)
    g0 = take(3) if summed else None
    y_ref, dx_ref, dwg_ref, dwu_ref, dwo_ref = take(5)
    xt, yacc, dxacc, hs, djg, dju, wg_ref, wu_ref, wo_ref = take(9)
    dy_ref = take(1)[0] if gated else dy_in
    f = pl.program_id(0)
    rows = x_ref.shape[0]

    @pl.when(f == 0)
    def _():
        xt[...] = x_ref[...].T
        if opened:
            yacc[...] = y0[...].astype(F32)
            dxacc[...] = dx0[...].astype(F32)
        else:
            yacc[...] = jnp.zeros_like(yacc)
            dxacc[...] = jnp.zeros_like(dxacc)
        if gated:
            dy_ref[...] = (dy_in[...].astype(F32) * gate_ref[...]).astype(BF)

    for index, span in enumerate(spans):
        place = pl.ds(pl.multiple_of(offs[index], HALF // 2), span)
        wg_ref[place, :] = wg_parts[index][...]
        wu_ref[place, :] = wu_parts[index][...]
        begin = offs[parts + index]

        @pl.when((f + first >= begin) & (f + first < begin + counts[index]))
        def _(index=index):
            wo_ref[...] = wo_parts[index][...]

    wg, wu, wo = wg_ref[...], wu_ref[...], wo_ref[...]

    def tile(i, carry):
        r = pl.ds(pl.multiple_of(i * tr, tr), tr)
        x = x_ref[r, :]
        g = dot(x, wg)
        u = dot(x, wu)
        dh = dot(dy_ref[r, :], wo, NT)
        sig = 1.0 / (1.0 + jnp.exp(-g))
        act = g * sig
        h = (act * u).astype(BF)
        dg = (dh * u * (sig * (1.0 + g * (1.0 - sig)))).astype(BF)
        du = (dh * act).astype(BF)
        hs[r, :] = h
        djg[r, :] = dg
        dju[r, :] = du
        yacc[r, :] += dot(h, wo)
        dxacc[r, :] += dot(dg, wg, NT) + dot(du, wu, NT)
        return carry

    lax.fori_loop(0, rows // tr, tile, 0)
    grads = [dot(xt[...], djg[...]), dot(xt[...], dju[...]), dot(hs[...], dy_ref[...], TN)]
    for k, out in enumerate((dwg_ref, dwu_ref, dwo_ref)):
        value = grads[k]
        if summed:
            value = value + g0[k][...].astype(F32)
        out[...] = value.astype(BF)

    @pl.when(f == pl.num_programs(0) - 1)
    def _():
        made = yacc[...].astype(BF)
        if gated and closing:
            made = (made.astype(F32) * gate_ref[...]).astype(BF)
        y_ref[...] = made
        dx_ref[...] = dxacc[...].astype(BF)


def run_ffn(x, dy, gate, w_in, w_out, offsets, start=None, grads=None, span=None, closing=True, tr=512, fb=FB, us=10):
    rows, d = x.shape
    ff = sum(w.shape[0] for w in w_out)
    nf = ff // fb
    first, last = span or (0, nf)
    steps = last - first
    gated = gate is not None
    parts = len(w_in)
    spans = [w.shape[0] for w in w_in]
    counts = [w.shape[0] // fb for w in w_out]
    whole = lambda a: pl.BlockSpec(
        a.shape, lambda f, o: (0,) * a.ndim, pipeline_mode=pl.Buffered(1)
    )
    args = [x, dy] + ([gate] if gated else [])
    specs = [whole(a) for a in args]
    args += list(w_in) * 2 + list(w_out)
    specs += [pl.BlockSpec((n, fb), lambda f, o: (0, f + first)) for n in spans]
    specs += [pl.BlockSpec((n, fb), lambda f, o: (0, f + first + nf)) for n in spans]
    for i, c in enumerate(counts):
        specs.append(
            pl.BlockSpec(
                (fb, d), lambda f, o, i=i, c=c: (jnp.clip(f + first - o[parts + i], 0, c - 1), 0)
            )
        )
    if start is not None:
        args += list(start)
        specs += [whole(a) for a in start]
    wide = pl.BlockSpec((d, fb), lambda f, o: (0, f))
    tall = pl.BlockSpec((fb, d), lambda f, o: (f, 0))
    if grads is not None:
        args += list(grads)
        specs += [
            pl.BlockSpec((d, fb), lambda f, o: (0, f + first)),
            pl.BlockSpec((d, fb), lambda f, o: (0, f + first)),
            pl.BlockSpec((fb, d), lambda f, o: (f + first, 0)),
        ]
    full = pl.BlockSpec((rows, d), lambda f, o: (0, 0), pipeline_mode=pl.Buffered(1))
    return pl.pallas_call(
        functools.partial(
            ffn_kernel,
            tr=math.gcd(tr, rows),
            spans=spans,
            counts=counts,
            first=first,
            gated=gated,
            opened=start is not None,
            summed=grads is not None,
            closing=closing,
            parts=parts,
        ),
        out_shape=(
            struct((rows, d), BF),
            struct((rows, d), BF),
            struct((d, steps * fb), BF),
            struct((d, steps * fb), BF),
            struct((steps * fb, d), BF),
        ),
        grid_spec=pltpu.PrefetchScalarGridSpec(
            num_scalar_prefetch=1,
            grid=(steps,),
            in_specs=specs,
            out_specs=(full, full, wide, wide, tall),
            scratch_shapes=[
                pltpu.VMEM((d, rows), BF),
                pltpu.VMEM((rows, d), F32),
                pltpu.VMEM((rows, d), F32),
                pltpu.VMEM((rows, fb), BF),
                pltpu.VMEM((rows, fb), BF),
                pltpu.VMEM((rows, fb), BF),
                pltpu.VMEM((d, fb), BF),
                pltpu.VMEM((d, fb), BF),
                pltpu.VMEM((fb, d), BF),
            ]
            + ([pltpu.VMEM((rows, d), BF)] if gated else []),
        ),
        compiler_params=pltpu.CompilerParams(vmem_limit_bytes=VMEM_LIMIT),
        cost_estimate=price(us),
    )(offsets, *args)


def price(us):
    return pl.CostEstimate(flops=int(us * 1.15e9), bytes_accessed=0, transcendentals=0)


def norm_back(values, scale, gain, grad):
    gain_grad = jnp.sum(grad * values * scale, 0, keepdims=True)
    scaled = gain * grad
    grad_in = scale * scaled - values * (scale * scale * scale) * jnp.mean(
        scaled * values, -1, keepdims=True
    )
    return grad_in, gain_grad


def mid_kernel(*refs, per, first):
    dxs, dxr, res_ref, gain_ref, cot_ref, w_ref, att_ref = refs[:7]
    if first:
        gres_ref, pay, gg_ref, gbf = refs[7:]
    else:
        att0, gbf0, gres_ref, pay, gg_ref, gw_ref, gbf = refs[7:]
    residual = res_ref[...]
    grad = dxs[...].astype(F32) + dxr[...].astype(F32)
    back, gain_grad = norm_back(residual, rms_scale(residual), gain_ref[...], grad)
    gg_ref[...] = gain_grad
    total = cot_ref[0].astype(F32) + back
    gres_ref[...] = total
    gbf[...] = total.astype(BF)
    mixed = dot(gbf[...], w_ref[...], NT)
    for pair in range(mixed.shape[1] // HALF):
        tile = mixed[:, pair * HALF : (pair + 1) * HALF]
        for side, packed in enumerate(swap_heads(tile[:HALF], tile[HALF:])):
            head = 2 * pair + side
            pay[head // per, head % per] = packed.astype(BF)
    if not first:
        gw_ref[...] = (dot(att_ref[...], gbf[...], TN) + dot(att0[...], gbf0[...], TN)).astype(BF)


def run_mid(dxs, dxr, residual, gain, cot, w, att, groups, micro, before=()):
    rows, width = residual.shape
    per = width // HEAD // groups
    args = (dxs, dxr, residual, gain, cot, w, att, *before)
    specs = [full_spec(a.shape) for a in args]
    specs[0] = pl.BlockSpec((rows, width), lambda _: (micro, 0))
    specs[4] = pl.BlockSpec((1, rows, width), lambda _: (micro, 0, 0))
    pay = (groups, per, HALF, HALF)
    outs = [struct((rows, width), F32), struct(pay, BF), struct((1, width), F32)]
    if micro == 0:
        outs.append(struct((rows, width), BF))
        scratch = []
    else:
        outs.append(struct((width, width), BF))
        scratch = [pltpu.VMEM((rows, width), BF)]
    return call(
        functools.partial(mid_kernel, per=per, first=micro == 0),
        tuple(outs),
        grid=(1,),
        in_specs=specs,
        out_specs=tuple(full_spec(o.shape) for o in outs),
        scratch=scratch,
        us=4 + micro,
    )(*args)


def fin_kernel(q0, kv0, d1, x_ref, gain_ref, w_ref, cos_ref, sin_ref, res0, res1, gin_ref, gw_ref, gj, *, per):
    width = x_ref.shape[1]
    for micro, sources in enumerate((((q0, 0), (kv0, 0), (kv0, 1)), ((d1, 0), (d1, 1), (d1, 2)))):
        rows = slice(micro * TILE, (micro + 1) * TILE)
        cosines, sines = cos_ref[rows, :], sin_ref[rows, :]
        for kind in range(3):
            for pair in range(width // HALF):
                tile = natural(*sources[kind], pair, per)
                if kind == 0:
                    tile = tile * 0.125
                if kind < 2:
                    tile = rotate(tile, cosines, -sines)
                gj[rows, kind * width + pair * HALF : kind * width + (pair + 1) * HALF] = tile.astype(BF)
    tokens = x_ref[...].astype(F32)
    scale = rms_scale(tokens)
    gain = gain_ref[...]
    normed = (tokens * scale * gain).astype(BF)
    first = dot(gj[...], w_ref[...], NT)
    back, _ = norm_back(tokens, scale, gain, first)
    gin_ref[:TILE] = res0[...] + back[:TILE]
    gin_ref[TILE:] = res1[...] + back[TILE:]
    turned = normed.T
    for kind in range(3):
        cols = slice(kind * width, (kind + 1) * width)
        gw_ref[:, cols] = dot(turned, gj[:, cols]).astype(BF)


def run_fin(parts, x, gain, w, cosines, sines, gres):
    rows, width = x.shape
    args = (*parts, x, gain, w, cosines, sines, *gres)
    outs = (struct((rows, width), F32), struct((width, 3 * width), BF))
    return call(
        functools.partial(fin_kernel, per=parts[0].shape[1]),
        outs,
        grid=(1,),
        in_specs=[full_spec(a.shape) for a in args],
        out_specs=tuple(full_spec(o.shape) for o in outs),
        scratch=[pltpu.VMEM((rows, 3 * width), BF)],
        us=11,
    )(*args)


def exchange(value, axis, mask):
    size = lax.axis_size(axis)
    return lax.ppermute(value, axis, [(i, i ^ mask) for i in range(size)])


def bits_of(size):
    return [1 << b for b in range(size.bit_length() - 1)]


def gather_xor(value, axis):
    for mask in reversed(bits_of(lax.axis_size(axis))):
        value = jnp.concatenate([value, exchange(value, axis, mask)], 0)
    return value


def scatter_xor(value, axis):
    for mask in bits_of(lax.axis_size(axis)):
        half = value.shape[0] // 2
        got = exchange(value[half:], axis, mask)
        value = (value[:half].astype(F32) + got.astype(F32)).astype(value.dtype)
    return value


def ordered(flag, mine, theirs):
    first = jnp.where(flag == 0, mine, theirs)
    second = jnp.where(flag == 0, theirs, mine)
    return jnp.concatenate([first, second], 0)


def pick(value, parts, index):
    size = value.shape[0] // parts
    return lax.dynamic_slice_in_dim(value, index * size, size, 0)


def after(value, token):
    return lax.optimization_barrier((value, token))[0]


def fetch_parts(shard, axis):
    part = exchange(pick(shard, 2, lax.axis_index(axis) % 2), "dp", 1)
    return part, exchange(part, axis, 1)


def fetch_whole(shard):
    part, other = fetch_parts(shard, "expert")
    core = lax.axis_index("expert") % 2
    return part, ordered(lax.axis_index("dp"), shard, ordered(core, part, other))


PIECES = 4


def remote(src, dst, sems, index, target):
    return pltpu.make_async_remote_copy(
        src_ref=src,
        dst_ref=dst,
        send_sem=sems[0].at[index],
        recv_sem=sems[1].at[index],
        device_id=target,
        device_id_type=pl.DeviceIdType.MESH,
    )


def reduce_kernel(*refs, owned, common):
    refs = list(refs)
    take = lambda n: [refs.pop(0) for _ in range(n)]
    own_in, com_in = take(owned), take(common)
    own_out, com_out = take(owned), take(common)
    own_buf = [take(4) for _ in range(owned)]
    com_buf = [take(6) for _ in range(common)]
    own_sems, com_sems = take(10), take(20)
    barrier = pltpu.get_barrier_semaphore()
    e, z, d = lax.axis_index("expert"), lax.axis_index("context"), lax.axis_index("dp")
    core, y = e % 2, e // 2 % 2
    mate = z + 1 - 2 * (z % 2)
    outer = (z == 0) | (z == 3)
    inner = (z == 1) | (z == 2)
    to_x = {"dp": 1 - d}
    to_core = {"expert": e + 1 - 2 * core}
    to_y = {"expert": e + 2 - 4 * y}
    to_mate = {"context": mate}
    to_mid = {"context": 3 - z}
    near = [to_x, to_core, to_y, to_mate]
    for target in near:
        pl.semaphore_signal(barrier, inc=1, device_id=target, device_id_type=pl.DeviceIdType.MESH)

    @pl.when(inner)
    def _():
        pl.semaphore_signal(barrier, inc=1, device_id=to_mid, device_id_type=pl.DeviceIdType.MESH)
        pl.semaphore_wait(barrier, 5)

    @pl.when(outer)
    def _():
        pl.semaphore_wait(barrier, 4)

    o_load, o_store = own_sems[:2]
    o_x, o_1, o_2, o_3 = [own_sems[2 + 2 * k : 4 + 2 * k] for k in range(4)]
    c_load, c_store = com_sems[:2]
    c_core, c_y, c_x, c_1, c_2, c_3, c_back, c_fore, c_last = [
        com_sems[2 + 2 * k : 4 + 2 * k] for k in range(9)
    ]

    chunks = owned * PIECES
    where = lambda c: (c // PIECES, c % PIECES)

    def o_sum(c):
        j, k = where(c)
        return own_buf[j][0].at[k]

    def o_loading(c):
        j, k = where(c)
        return pltpu.make_async_copy(own_in[j].at[d, k], o_sum(c), o_load.at[c])

    def o_storing(c):
        j, k = where(c)
        return pltpu.make_async_copy(own_buf[j][2].at[k], own_out[j].at[k], o_store.at[c])

    def o_wire(stage, c):
        j, k = where(c)
        buf = own_buf[j]
        if stage == "x":
            return remote(own_in[j].at[1 - d, k], buf[1].at[k], o_x, c, to_x)
        if stage == "1":
            return remote(o_sum(c), buf[2].at[k], o_1, c, to_mate)
        if stage == "2":
            return remote(o_sum(c), buf[3].at[k], o_2, c, to_mid)
        return remote(buf[2].at[k], own_out[j].at[k], o_3, c, to_mate)

    def o_first(c):
        j, k = where(c)
        o_loading(c).wait()
        o_wire("x", c).wait_recv()
        if c + 2 < chunks:
            o_wire("x", c + 2).start()
        own_buf[j][0][k] = own_buf[j][0][k] + own_buf[j][1][k]

        @pl.when(outer)
        def _():
            o_wire("1", c).start()

    def o_second(c):
        j, k = where(c)

        @pl.when(inner)
        def _():
            o_wire("1", c).wait_recv()
            own_buf[j][0][k] = own_buf[j][0][k] + own_buf[j][2][k]
            o_wire("2", c).start()

    def o_third(c):
        j, k = where(c)

        @pl.when(inner)
        def _():
            o_wire("2", c).wait_recv()
            own_buf[j][2][k] = own_buf[j][0][k] + own_buf[j][3][k]
            o_wire("3", c).start()
            o_storing(c).start()

    def o_fourth(c):
        @pl.when(outer)
        def _():
            o_wire("3", c).wait_recv()

    def c_loading(i, h):
        return pltpu.make_async_copy(com_in[i].at[h, core], com_buf[i][0].at[h], c_load.at[2 * i + h])

    def c_storing(i):
        return pltpu.make_async_copy(com_buf[i][4], com_out[i].at[core, y], c_store.at[i])

    def c_wire(stage, i, h=0):
        total, r_core, r_y, r_x, r_1, r_2 = com_buf[i]
        if stage == "core":
            return remote(com_in[i].at[h, 1 - core], r_core.at[h], c_core, 2 * i + h, to_core)
        if stage == "y":
            return remote(total.at[h, 1 - y], r_y.at[h], c_y, 2 * i + h, to_y)
        if stage == "x":
            return remote(total.at[1 - d, y], r_x, c_x, i, to_x)
        if stage == "1":
            return remote(total.at[d, y], r_1, c_1, i, to_mate)
        if stage == "2":
            return remote(total.at[d, y], r_2, c_2, i, to_mid)
        if stage == "3":
            return remote(r_1, com_out[i].at[core, y], c_3, i, to_mate)
        if stage == "fore":
            return remote(r_1, com_out[i].at[core, y], c_fore, i, to_y)
        if stage == "back":
            return remote(com_out[i].at[core, y], com_out[i].at[core, y], c_fore, i, to_y)
        return remote(com_out[i].at[core], com_out[i].at[core], c_last, i, to_core)

    def c_a(i):
        for h in range(2):
            c_loading(i, h).wait()
            c_wire("core", i, h).wait_recv()
        com_buf[i][0][...] = com_buf[i][0][...] + com_buf[i][1][...]
        for h in range(2):
            c_wire("y", i, h).start()

    def c_b(i):
        total, r_y = com_buf[i][0], com_buf[i][2]
        for h in range(2):
            c_wire("y", i, h).wait_recv()
            total[h, y] = total[h, y] + r_y[h]
        c_wire("x", i).start()

    def c_c(i):
        total, r_x = com_buf[i][0], com_buf[i][3]
        c_wire("x", i).wait_recv()
        total[d, y] = total[d, y] + r_x[...]

        @pl.when(outer)
        def _():
            c_wire("1", i).start()

    def c_d(i):
        total, r_1 = com_buf[i][0], com_buf[i][4]

        @pl.when(inner)
        def _():
            c_wire("1", i).wait_recv()
            total[d, y] = total[d, y] + r_1[...]
            c_wire("2", i).start()

    def c_e(i):
        total, r_1, r_2 = com_buf[i][0], com_buf[i][4], com_buf[i][5]

        @pl.when(inner)
        def _():
            c_wire("2", i).wait_recv()
            r_1[...] = total[d, y] + r_2[...]
            c_wire("3", i).start()
            c_wire("fore", i).start()
            c_storing(i).start()

    def c_f(i):
        @pl.when(outer)
        def _():
            c_wire("3", i).wait_recv()
            c_wire("back", i).start()

    def c_g(i):
        @pl.when(inner)
        def _():
            c_storing(i).wait()

        c_wire("fore", i).wait_recv()
        c_wire("last", i).start()

    def c_h(i):
        c_wire("last", i).wait_recv()

    for i in range(common):
        for h in range(2):
            c_wire("core", i, h).start()
            c_loading(i, h).start()
    for c in range(chunks):
        o_loading(c).start()
        if c < 2:
            o_wire("x", c).start()
    events = []
    for c in range(chunks):
        for lag, step in ((1, o_first), (2.5, o_second), (3.5, o_third), (4.6, o_fourth)):
            events.append((c + lag, step, c))
    for i in range(common):
        base = 2.0 * i + 0.5
        for lag, step in zip((0, 2.3, 4, 5.5, 6.6, 7.7, 8.9, 9.6), (c_a, c_b, c_c, c_d, c_e, c_f, c_g, c_h)):
            events.append((base + lag, step, i))
    for _, step, index in sorted(events, key=lambda v: v[0]):
        step(index)
    for c in range(chunks):
        o_wire("x", c).wait_send()
    for i in range(common):
        for h in range(2):
            c_wire("core", i, h).wait_send()
            c_wire("y", i, h).wait_send()
        c_wire("x", i).wait_send()
        c_wire("last", i).wait_send()

    @pl.when(outer)
    def _():
        for c in range(chunks):
            o_wire("1", c).wait_send()
        for i in range(common):
            c_wire("1", i).wait_send()
            c_wire("back", i).wait_send()

    @pl.when(inner)
    def _():
        for c in range(chunks):
            o_wire("2", c).wait_send()
            o_wire("3", c).wait_send()
            o_storing(c).wait()
        for i in range(common):
            c_wire("2", i).wait_send()
            c_wire("3", i).wait_send()
            c_wire("fore", i).wait_send()


def run_reduce(expert_grads, shared_grads, collective_id, us):
    own = [g.reshape(2, PIECES, g.shape[0] // (2 * PIECES), g.shape[1]) for g in expert_grads]
    com = []
    for g in shared_grads:
        for mask in bits_of(lax.axis_size("expert"))[2:]:
            g = g + exchange(g, "expert", mask)
        com.append(g.reshape(2, 2, 2, g.shape[0] // 8, g.shape[1]))
    chunks = len(own) * PIECES
    scratch = []
    for g in own:
        scratch += [pltpu.VMEM(g.shape[1:], BF)] * 4
    for g in com:
        small = g.shape[3:]
        scratch += [pltpu.VMEM((2, 2, *small), BF)] * 2 + [pltpu.VMEM((2, *small), BF)]
        scratch += [pltpu.VMEM(small, BF)] * 3
    dma = lambda n: pltpu.SemaphoreType.DMA((max(n, 1),))
    scratch += [dma(chunks)] * 10
    n = len(com)
    scratch += [dma(2 * n), dma(n)] + [dma(2 * n)] * 4 + [dma(n)] * 14
    anywhere = pl.BlockSpec(memory_space=pl.ANY)
    outs = [struct(g.shape[1:], BF) for g in own] + [struct((2, 2, *g.shape[3:]), BF) for g in com]
    got = pl.pallas_call(
        functools.partial(reduce_kernel, owned=len(own), common=n),
        out_shape=tuple(outs),
        in_specs=[anywhere] * (len(own) + n),
        out_specs=(anywhere,) * len(outs),
        scratch_shapes=scratch,
        compiler_params=pltpu.CompilerParams(
            vmem_limit_bytes=VMEM_LIMIT, collective_id=collective_id, has_side_effects=True
        ),
        cost_estimate=price(us),
    )(*own, *com)
    return [g.reshape(-1, g.shape[-1]).astype(F32) for g in got]


def body(
    inputs,
    keep_flags,
    block_ids,
    expert_ids,
    gate_weights,
    norm_attn,
    w_qkv,
    w_attn_out,
    norm_ffn,
    w_shared_in,
    w_shared_out,
    w_expert_in,
    w_expert_out,
    cotangent,
):
    width = w_qkv.shape[1] // 3
    rows = inputs.shape[2]
    groups = lax.axis_size("context")
    experts = lax.axis_size("expert")
    z = lax.axis_index("context")
    seq_rows = rows * groups
    x = inputs[0]
    cot = cotangent[0].reshape(MICRO * rows, width)

    positions = (
        jnp.arange(MICRO, dtype=jnp.int32)[:, None] * seq_rows
        + z * rows
        + jnp.arange(rows, dtype=jnp.int32)[None, :]
    ).reshape(-1)
    half = HEAD // 2
    freq = jnp.exp(-math.log(ROPE_BASE) * jnp.arange(half, dtype=F32) * 2.0 / HEAD)
    angle = positions.astype(F32)[:, None] * freq[None, :]
    cos_t, sin_t = jnp.cos(angle), jnp.sin(angle)
    cosines = jnp.concatenate([cos_t] * 4, -1)
    sines = jnp.concatenate([-sin_t, sin_t, -sin_t, sin_t], -1)

    blocks = block_ids[0] + 8 * jnp.arange(MICRO, dtype=jnp.int32)[:, None]
    key_tags = jnp.where(keep_flags[0] == 1, blocks, HIDDEN)
    tags = jnp.broadcast_to(jnp.stack([blocks, key_tags])[None], (groups, 2, MICRO, rows))
    tags = lax.all_to_all(tags, "context", 0, 0, tiled=True).transpose(1, 2, 0, 3)
    query_row = tags[0].reshape(MICRO * groups, 1, rows)
    key_row = tags[1].reshape(MICRO * groups, 1, rows)
    query_col = tags[0].reshape(-1, 1)
    key_col = tags[1].reshape(-1, 1)

    gains = jnp.stack([norm_attn, norm_ffn])
    both = ordered(lax.axis_index("dp"), gains[None], exchange(gains, "dp", 1)[None]).astype(F32)
    gain_attn = both[:, 0].reshape(1, width)
    gain_ffn = both[:, 1].reshape(1, width)
    qkv_part, mat_qkv = fetch_whole(w_qkv)
    out_part, mat_out = fetch_whole(w_attn_out)

    ids = expert_ids[0].reshape(MICRO * rows, -1)
    gates = gate_weights[0].reshape(MICRO * rows, -1)
    per_expert = jnp.sum(
        jnp.where(
            ids[None] == jnp.arange(experts, dtype=jnp.int32)[:, None, None], gates[None], 0.0
        ),
        -1,
    )
    all_gates = gather_xor(per_expert[None], "expert")
    gate = lax.dynamic_index_in_dim(all_gates, lax.axis_index("expert"), 1, False).reshape(-1, 1)

    core = lax.axis_index("expert") % 2
    dp = lax.axis_index("dp")
    k_half, f_half = width // 2, w_shared_out.shape[0]
    ein_parts = (w_expert_in[0], *fetch_parts(after(w_expert_in[0], qkv_part), "context"))
    eout_parts = (w_expert_out[0], *fetch_parts(after(w_expert_out[0], out_part), "context"))
    sin_parts = (w_shared_in, *fetch_parts(after(w_shared_in, ein_parts[1]), "expert"))
    sout_parts = (w_shared_out, *fetch_parts(after(w_shared_out, eout_parts[1]), "expert"))

    def offsets(bit):
        places = [2 * (1 - dp) + bit, 2 * (1 - dp) + 1 - bit]
        return jnp.stack(
            [dp * k_half]
            + [p * (k_half // 2) for p in places]
            + [dp * f_half // FB]
            + [p * (f_half // 2) // FB for p in places]
        )

    all_cot = [gather_xor(cotangent[0, m], "expert") for m in range(MICRO)]
    gate = [
        lax.dynamic_index_in_dim(
            all_gates.reshape(experts, experts, MICRO, rows)[:, :, m], lax.axis_index("expert"), 1, False
        ).reshape(-1, 1)
        for m in range(MICRO)
    ]

    recvs, mixed, lses, att, res, nf = [], [], [], [], [], []
    for micro in range(MICRO):
        pay = run_pre(x, micro, gain_attn, mat_qkv, cosines, sines, groups)
        recvs.append(lax.all_to_all(pay, "context", 0, 0, tiled=True))
    for micro in range(MICRO):
        out, lse = run_attend(recvs[: micro + 1], key_row, query_col, groups)
        mixed.append(out)
        lses.append(lse)
    for micro in range(MICRO):
        got = lax.all_to_all(mixed[micro], "context", 0, 0, tiled=True)
        a, r, n = run_post(got, x, micro, mat_out, gain_ffn)
        att.append(a)
        res.append(r)
        nf.append(n)

    capacity = 4 * rows // experts

    def expert_pass(m, grads):
        hidden, grad, weight = gather_xor(nf[m], "expert"), all_cot[m], gate[m]
        if capacity < rows:
            chosen = weight.reshape(-1, rows) > 0
            slots = jnp.cumsum(chosen.astype(jnp.int32), 1) - 1
            select = (
                chosen[:, None] & (slots[:, None] == jnp.arange(capacity, dtype=jnp.int32)[:, None])
            ).astype(BF)
            squeeze = lambda v: jnp.einsum("bcr,brd->bcd", select, v.reshape(-1, rows, width)).reshape(-1, width)
            spread = lambda v: jnp.einsum("bcr,bcd->brd", select, v.reshape(-1, capacity, width)).reshape(-1, width)
            hidden, grad = squeeze(hidden), squeeze(grad)
            weight = jnp.sum(select.astype(F32) * weight.reshape(-1, 1, rows), -1).reshape(-1, 1)
        made, dx, *grads = run_ffn(
            hidden, grad, weight, ein_parts, eout_parts, offsets(z % 2), grads=grads, us=38
        )
        if capacity < rows:
            made, dx = spread(made), spread(dx)
        return scatter_xor(dx, "expert"), scatter_xor(made, "expert"), grads

    dx0, routed0, g_expert = expert_pass(0, None)
    shared, dx_shared, *g_shared = run_ffn(
        jnp.concatenate(nf, 0), cot, None, sin_parts, sout_parts, offsets(core), us=21
    )
    dx1, routed1, g_expert = expert_pass(1, g_expert)
    output = jnp.stack(
        [
            (res[m] + shared[m * rows : (m + 1) * rows].astype(F32) + r.astype(F32)).astype(BF)
            for m, r in enumerate((routed0, routed1))
        ]
    )

    gres0, pay0, gg0, gbf0 = run_mid(
        dx_shared, dx0, res[0], gain_ffn, cotangent[0], mat_out, att[0], groups, 0
    )
    grad0 = lax.all_to_all(pay0, "context", 0, 0, tiled=True)
    back_q0, early_k, early_v = run_attend_back(
        recvs[:1], grad0, mixed[0], lses[0], key_col, query_row, (), groups
    )
    q0 = lax.all_to_all(back_q0, "context", 0, 0, tiled=True)
    gres1, pay1, gg1, g_out = run_mid(
        dx_shared, dx1, res[1], gain_ffn, cotangent[0], mat_out, att[1], groups, 1, (att[0], gbf0)
    )
    grad1 = lax.all_to_all(pay1, "context", 0, 0, tiled=True)
    back1, back_kv0 = run_attend_back(
        recvs, grad1, mixed[1], lses[1], key_col, query_row, (early_k, early_v), groups
    )
    kv0 = lax.all_to_all(back_kv0, "context", 0, 0, tiled=True)
    d1 = lax.all_to_all(back1, "context", 0, 0, tiled=True)
    grad_input, g_qkv = run_fin(
        (q0, kv0, d1),
        x.reshape(MICRO * rows, width),
        gain_attn,
        mat_qkv,
        cosines,
        sines,
        (gres0, gres1),
    )

    g_gain_ffn = gg0 + gg1
    total = g_gain_ffn
    for axis in ("expert", "context", "dp"):
        for mask in bits_of(lax.axis_size(axis)):
            total = total + exchange(total, axis, mask)
    r_gain_ffn = pick(total[0], 2, dp)
    e_gate, e_up, r_eout, r_gate, r_up, r_sout, r_out, r_qkv = run_reduce(
        g_expert, [*g_shared, g_out, g_qkv], 1, 160
    )
    r_sin = jnp.concatenate([r_gate, r_up], 1)
    r_gain_attn = jnp.sum(w_qkv.astype(F32) * r_qkv, 1) / norm_attn.astype(F32)
    r_ein = jnp.concatenate([e_gate, e_up], 1)
    return (
        output[None],
        grad_input.reshape(1, MICRO, rows, width),
        r_gain_attn,
        r_qkv,
        r_out,
        r_gain_ffn,
        r_sin,
        r_sout,
        r_ein[None],
        r_eout[None],
    )


def solution(mesh):
    tokens = P(("expert", "dp"), None, "context", None)
    flags = P(("expert", "dp"), None, "context")
    placed = (
        tokens,
        flags,
        flags,
        tokens,
        tokens,
        P("dp"),
        P("dp", None),
        P("dp", None),
        P("dp"),
        P("dp", None),
        P("dp", None),
        P("expert", "dp", None),
        P("expert", "dp", None),
        tokens,
    )
    return jax.shard_map(
        body,
        mesh=mesh,
        in_specs=placed,
        out_specs=(
            tokens,
            tokens,
            P("dp"),
            P("dp", None),
            P("dp", None),
            P("dp"),
            P("dp", None),
            P("dp", None),
            P("expert", "dp", None),
            P("expert", "dp", None),
        ),
        check_vma=False,
    )
```

```python
import functools
import math

import jax
import jax.numpy as jnp
from jax import lax
from jax.experimental import pallas as pl
from jax.experimental.pallas import tpu as pltpu
from jax.sharding import PartitionSpec as P

HEAD = 64
MICRO = 2
TILE = 256
HALF = 128
EPSILON = 1e-05
ROPE_BASE = 10000.0
MASKED = -3e30
HIDDEN = 1 << 20
BF = jnp.bfloat16
F32 = jnp.float32
NT = (((1,), (1,)), ((), ()))
TN = (((0,), (0,)), ((), ()))
VMEM_LIMIT = 60 << 20
FB = 512


def dot(left, right, dims=(((1,), (0,)), ((), ()))):
    return lax.dot_general(left, right, dims, preferred_element_type=F32)


def rms_scale(values):
    return lax.rsqrt(jnp.mean(values * values, -1, keepdims=True) + EPSILON)


def low_lanes(rows):
    return lax.broadcasted_iota(jnp.int32, (rows, HALF), 1) < HEAD


def swap_heads(first, second):
    low = low_lanes(HALF)
    return (
        jnp.where(low, first, pltpu.roll(second, HEAD, 1)),
        jnp.where(low, pltpu.roll(first, HEAD, 1), second),
    )


def rotate(tile, cosines, sines):
    lane = lax.broadcasted_iota(jnp.int32, tile.shape, 1)
    partner = jnp.where(
        lane % HEAD < HEAD // 2,
        pltpu.roll(tile, HALF - HEAD // 2, 1),
        pltpu.roll(tile, HEAD // 2, 1),
    )
    return tile * cosines + partner * sines


def call(kernel, out_shape, *, grid=(), in_specs=None, out_specs=None, scratch=(), us=5):
    return pl.pallas_call(
        kernel,
        out_shape=out_shape,
        grid=grid,
        in_specs=in_specs,
        out_specs=out_specs,
        scratch_shapes=scratch,
        compiler_params=pltpu.CompilerParams(vmem_limit_bytes=VMEM_LIMIT),
        cost_estimate=price(us),
    )


def full_spec(shape):
    return pl.BlockSpec(tuple(shape), lambda *_: (0,) * len(shape))


def struct(shape, dtype):
    return jax.ShapeDtypeStruct(tuple(shape), dtype)


def project(tokens, gain, w_ref, cosines, sines, pay, groups):
    normed = (tokens * rms_scale(tokens) * gain).astype(BF)
    width = tokens.shape[1]
    per = width // HEAD // groups
    for kind in range(3):
        joined = dot(normed, w_ref[:, kind * width : (kind + 1) * width])
        for pair in range(width // HALF):
            tile = joined[:, pair * HALF : (pair + 1) * HALF]
            if kind < 2:
                tile = rotate(tile, cosines, sines)
            if kind == 0:
                tile = tile * 0.125
            for side, packed in enumerate(swap_heads(tile[:HALF], tile[HALF:])):
                head = 2 * pair + side
                pay[head // per, kind * per + head % per] = packed.astype(BF)


def unpack(ref, index, kind_head):
    tile = ref[index, kind_head]
    return tile, pltpu.roll(tile.astype(F32), HEAD, 1).astype(BF)


def fill_keys(recv, micro, ks, vs, heads):
    groups = recv.shape[0]
    for src in range(groups):
        base = (micro * groups + src) * TILE
        for h in range(heads):
            for store, kind in ((ks, 1), (vs, 2)):
                first, second = unpack(recv, src, kind * heads + h)
                store[h, base : base + HALF] = first
                store[h, base + HALF : base + TILE] = second


def masked_rows(ref, index, kind_head):
    tile = ref[index, kind_head].astype(F32)
    both = jnp.concatenate([tile, pltpu.roll(tile, HEAD, 1)], 0)
    return jnp.where(low_lanes(TILE), both, 0.0)


def pack_rows(values):
    return jnp.where(low_lanes(HALF), values[:HALF], pltpu.roll(values[HALF:], HEAD, 1))


def attend_step(step, micro, heads, groups, recv, tags, out_ref, lse_ref, ks, vs, scores):
    count = groups * micro + jnp.minimum(step + 2, groups)
    queries = [masked_rows(recv, step, h).astype(BF) for h in range(heads)]
    tag = jnp.broadcast_to(tags[step, 0, micro], (8, TILE)).T[:, :1]
    same = lax.broadcasted_iota(jnp.int32, (TILE, TILE), 0) == lax.broadcasted_iota(
        jnp.int32, (TILE, TILE), 1
    )

    def first_pass(j, tops):
        keys = pl.ds(pl.multiple_of(j * TILE, TILE), TILE)
        key_tag = tags[j % groups, 1, j // groups]
        seen = (key_tag <= tag) | (same & (j == groups * micro + step))
        new = []
        for h in range(heads):
            part = jnp.where(seen, dot(queries[h], ks[h, keys, :], NT), MASKED)
            scores[h, :, keys] = part
            new.append(jnp.maximum(tops[h], jnp.maximum(part[:, :HALF], part[:, HALF:])))
        return tuple(new)

    tops = lax.fori_loop(
        0, count, first_pass, (jnp.full((TILE, HALF), MASKED, F32),) * heads
    )
    tops = [jnp.max(top, 1, keepdims=True) for top in tops]

    def second_pass(j, carry):
        keys = pl.ds(pl.multiple_of(j * TILE, TILE), TILE)
        sums, totals = carry
        new_sums, new_totals = [], []
        for h in range(heads):
            expo = jnp.exp(scores[h, :, keys] - tops[h])
            new_sums.append(sums[h] + (expo[:, :HALF] + expo[:, HALF:]))
            new_totals.append(totals[h] + dot(expo.astype(BF), vs[h, keys, :]))
        return tuple(new_sums), tuple(new_totals)

    zero = (jnp.zeros((TILE, HALF), F32),) * heads
    sums, totals = lax.fori_loop(0, count, second_pass, (zero, zero))
    lane = lax.broadcasted_iota(jnp.int32, (TILE, HALF), 1)
    logs = jnp.zeros((TILE, HALF), F32)
    for h in range(heads):
        total = jnp.sum(sums[h], 1, keepdims=True)
        out_ref[step, h] = pack_rows(totals[h] / total).astype(BF)
        logs = jnp.where(lane == h, tops[h] + jnp.log(total), logs)
    lse_ref[step] = logs.T[:8]


def back_start(recvs, ks, vs, dk, dv, early, heads, groups):
    for micro, recv in enumerate(recvs):
        fill_keys(recv, micro, ks, vs, heads)
    if early is None:
        dk[...] = jnp.zeros_like(dk)
        dv[...] = jnp.zeros_like(dv)
    else:
        for total, part in zip((dk, dv), early):
            total[:, : groups * TILE] = part[...]
            total[:, groups * TILE :] = jnp.zeros_like(total[:, groups * TILE :])


def back_step(step, micro, heads, groups, recvs, grad_ref, out_ref, lse_ref, key_tag, query_tag, pay_ref, ks, vs, dk, dv):
    count = groups * micro + jnp.minimum(step + 2, groups)
    queries = [masked_rows(recvs[micro], step, h).astype(BF) for h in range(heads)]
    grads_f = [masked_rows(grad_ref, step, h) for h in range(heads)]
    grads = [g.astype(BF) for g in grads_f]
    ones = jnp.ones((8, HALF), F32)
    deltas = [
        lax.dot_general(
            ones,
            grads_f[h] * masked_rows(out_ref, step, h),
            NT,
            precision=lax.Precision.HIGHEST,
            preferred_element_type=F32,
        )[:1]
        for h in range(heads)
    ]
    logs = [lse_ref[step, h : h + 1, :] for h in range(heads)]
    tag = query_tag[groups * micro + step]
    same = lax.broadcasted_iota(jnp.int32, (TILE, TILE), 0) == lax.broadcasted_iota(
        jnp.int32, (TILE, TILE), 1
    )

    def tile(j, totals):
        keys = pl.ds(pl.multiple_of(j * TILE, TILE), TILE)
        seen = (key_tag[keys, :] <= tag) | (same & (j == groups * micro + step))
        new = []
        for h in range(heads):
            key, value = ks[h, keys, :], vs[h, keys, :]
            scores = dot(key, queries[h], NT)
            probs = jnp.where(seen, jnp.exp(scores - logs[h]), 0.0)
            dv[h, keys, :] += dot(probs.astype(BF), grads[h])
            slope = (probs * (dot(value, grads[h], NT) - deltas[h])).astype(BF)
            dk[h, keys, :] += dot(slope, queries[h])
            new.append(totals[h] + dot(slope, key, TN))
        return tuple(new)

    totals = lax.fori_loop(0, count, tile, (jnp.zeros((TILE, HALF), F32),) * heads)
    for h in range(heads):
        pay_ref[step, h] = pack_rows(totals[h]).astype(BF)


def back_pack(dk, dv, pay_ref, src, first, base, heads):
    rows = slice((base + src) * TILE, (base + src + 1) * TILE)
    for h in range(heads):
        pay_ref[src, first + h] = pack_rows(dk[h, rows]).astype(BF)
        pay_ref[src, first + heads + h] = pack_rows(dv[h, rows]).astype(BF)


def attend_back_kernel(*refs, heads, groups):
    recv, grad_ref, out_ref, lse_ref, key_tag, query_tag, pay_ref, early_k, early_v, ks, vs, dk, dv = refs
    step = pl.program_id(0)

    @pl.when(step == 0)
    def _():
        back_start([recv], ks, vs, dk, dv, None, heads, groups)

    back_step(step, 0, heads, groups, [recv], grad_ref, out_ref, lse_ref, key_tag, query_tag, pay_ref, ks, vs, dk, dv)

    @pl.when(step == groups - 1)
    def _():
        early_k[...] = dk[...]
        early_v[...] = dv[...]


def run_attend_back(recv, grad, out, lse, key_tag, query_tag, groups):
    heads = recv.shape[1] // 3
    held = groups * TILE
    part = struct((heads, held, HALF), F32)
    args = [recv, grad, out, lse, key_tag, query_tag]
    outs = [struct((groups, heads, HALF, HALF), BF), part, part]
    return call(
        functools.partial(attend_back_kernel, heads=heads, groups=groups),
        tuple(outs),
        grid=(groups,),
        in_specs=[full_spec(a.shape) for a in args],
        out_specs=tuple(full_spec(o.shape) for o in outs),
        scratch=[pltpu.VMEM((heads, held, HALF), BF)] * 2 + [pltpu.VMEM((heads, held, HALF), F32)] * 2,
        us=23,
    )(*args)


def natural(ref, first_kind, pair, per):
    tiles = []
    for head in (2 * pair, 2 * pair + 1):
        tiles.append(ref[head // per, first_kind * per + head % per].astype(F32))
    return jnp.concatenate(swap_heads(*tiles), 0)


def remote(src, dst, sems, index, target, arrival=None):
    return pltpu.make_async_remote_copy(
        src_ref=src,
        dst_ref=dst,
        send_sem=sems[0].at[index],
        recv_sem=sems[1].at[index if arrival is None else arrival],
        device_id=target,
        device_id_type=pl.DeviceIdType.MESH,
    )


def meet(barrier, targets):
    for target in targets:
        pl.semaphore_signal(barrier, inc=1, device_id=target, device_id_type=pl.DeviceIdType.MESH)
    pl.semaphore_wait(barrier, len(targets))


class Trade:
    def __init__(self, src, dst, sems, local):
        self.src, self.dst, self.sems, self.local = src, dst, sems, local
        self.z = lax.axis_index("context")
        self.groups = src.shape[0]

    def wire(self, other, arrival):
        return remote(self.src.at[other], self.dst.at[arrival], self.sems, other, {"context": other}, arrival)

    def keep(self, index):
        return pltpu.make_async_copy(self.src.at[index], self.dst.at[index], self.local)

    def send(self, dest):
        @pl.when(dest != self.z)
        def _():
            self.wire(dest, self.z).start()

        @pl.when(dest == self.z)
        def _():
            self.keep(dest).start()

    def await_from(self, other):
        @pl.when(other != self.z)
        def _():
            self.wire(other, other).wait_recv()

        @pl.when(other == self.z)
        def _():
            self.keep(other).wait()

    def collect(self):
        for other in range(self.groups):
            self.await_from(other)

    def release(self):
        for other in range(self.groups):

            @pl.when(other != self.z)
            def _(other=other):
                self.wire(other, self.z).wait_send()


def front_kernel(*refs, heads, groups):
    refs = list(refs)
    take = lambda n: [refs.pop(0) for _ in range(n)]
    x_ref, gains_in, cos_ref, sin_ref, tags_in, gates_in = take(6)
    w_qkv, w_out, w_ein, w_eout, cot = take(5)
    recv_out, mixed_out, lse_out, att_out, res_out = take(2), take(2), take(2), take(2), take(2)
    rows_out, cot_out, gates_out, both_out, tags_out = take(2), take(2), take(1)[0], take(1)[0], take(1)[0]
    qkv_out, wout_out, ein_out, eout_out, gains_out = take(5)
    wq, wo, gains, tags, pay, recv, ks, vs, scores, mixed, got, lse, att, res, nf = take(15)
    s_qkv, s_out, s_gain, s_exp, s_tag, s_gate, s_cot, s_pay, s_mix, s_row = [take(2) for _ in range(10)]
    local, self_pay, self_mix, self_tag, stores = take(5)
    e, z, d = lax.axis_index("expert"), lax.axis_index("context"), lax.axis_index("dp")
    core, y = e % 2, e // 2 % 2
    to_x, to_core, to_y = {"dp": 1 - d}, {"expert": e + 1 - 2 * core}, {"expert": e + 2 - 4 * y}
    others = [{"context": (z + k) % groups} for k in range(1, groups)]
    width = x_ref.shape[2]

    loads = [
        pltpu.make_async_copy(w_qkv, wq.at[d], local.at[0]),
        pltpu.make_async_copy(w_out, wo.at[d], local.at[1]),
        pltpu.make_async_copy(gains_in, gains.at[d], local.at[2]),
    ]
    for copy in loads:
        copy.start()
    meet(pltpu.get_barrier_semaphore(), [to_x, to_core, to_y, *others])

    x_qkv = remote(w_qkv.at[core], wq.at[d, core], s_qkv, 0, to_x)
    x_gain = remote(gains_in, gains.at[d], s_gain, 0, to_x)
    x_out = remote(w_out.at[core], wo.at[d, core], s_out, 0, to_x)
    x_exp = [remote(w_ein, ein_out, s_exp, 0, to_x), remote(w_eout, eout_out, s_exp, 1, to_x)]
    for copy in (x_qkv, x_gain, x_out, *x_exp):
        copy.start()
    tag_trade = [
        remote(tags_in, tags.at[z], s_tag, k, others[k]) for k in range(groups - 1)
    ]
    tag_own = pltpu.make_async_copy(tags_in, tags.at[z], self_tag.at[0])
    tag_own.start()
    for copy in tag_trade:
        copy.start()
    own_copies = [
        pltpu.make_async_copy(gates_in, gates_out.at[0], stores.at[0]),
        pltpu.make_async_copy(cot.at[0], cot_out[0].at[0], stores.at[1]),
        pltpu.make_async_copy(cot.at[1], cot_out[1].at[0], stores.at[2]),
    ]
    for copy in own_copies:
        copy.start()
    y_gate = remote(gates_in, gates_out.at[1], s_gate, 0, to_y)
    y_cot = [remote(cot.at[m], cot_out[m].at[1], s_cot, m, to_y) for m in range(MICRO)]
    c_gate = [
        remote(gates_in, gates_out.at[2], s_gate, 1, to_core),
        remote(gates_out.at[1], gates_out.at[3], s_gate, 2, to_core),
    ]
    c_cot = [remote(cot.at[m], cot_out[m].at[2], s_cot, 2 + m, to_core) for m in range(MICRO)] + [
        remote(cot_out[m].at[1], cot_out[m].at[3], s_cot, 4 + m, to_core) for m in range(MICRO)
    ]
    y_gate.start()
    for copy in y_cot:
        copy.start()

    c_qkv = remote(wq.at[1 - d, core], wq.at[1 - d, core], s_qkv, 1, to_core)
    c_out = remote(wo.at[1 - d, core], wo.at[1 - d, core], s_out, 1, to_core)
    for copy in loads:
        copy.wait()
    x_qkv.wait_recv()
    c_qkv.start()
    x_gain.wait_recv()
    c_qkv.wait_recv()
    both = [jnp.concatenate([gains[0, k : k + 1], gains[1, k : k + 1]], 1) for k in range(2)]
    w_full = wq.reshape(width, 3 * width)
    trades, returns = [], []
    for m in range(MICRO):
        span = slice(m * TILE, (m + 1) * TILE)
        project(x_ref[m].astype(F32), both[0], w_full, cos_ref[span, :], sin_ref[span, :], pay.at[m], groups)
        trade = Trade(pay.at[m], recv.at[m], [s.at[m] for s in s_pay], self_pay.at[m])
        for dest in range(groups):
            trade.send(dest)
        trades.append(trade)
    c_gate[0].start()
    for copy in c_cot[:MICRO]:
        copy.start()
    for k in range(groups - 1):
        remote(tags_in, tags.at[(z + groups - 1 - k) % groups], s_tag, k, others[k]).wait_recv()
    tag_own.wait()

    def attend(m, first, last):
        trade = Trade(mixed.at[m], got.at[m], [s.at[m] for s in s_mix], self_mix.at[m])

        def one(step, carry):
            attend_step(step, m, heads, groups, recv.at[m], tags, mixed.at[m], lse.at[m], ks, vs, scores)
            trade.send(step)
            return carry

        lax.fori_loop(first, last, one, 0)
        return trade

    def post(m, trade):
        trade.collect()
        for pair in range(width // HALF):
            att[m, :, pair * HALF : (pair + 1) * HALF] = natural(got.at[m], 0, pair, heads).astype(BF)
        residual = x_ref[m].astype(F32) + dot(att[m], wo.reshape(width, width)[...])
        res[m] = residual
        nf[m] = (residual * rms_scale(residual) * both[1]).astype(BF)
        remote(nf.at[m], rows_out[m].at[1], s_row, 3 * m, to_y).start()
        remote(nf.at[m], rows_out[m].at[2], s_row, 3 * m + 1, to_core).start()

    def forward_row(m):
        remote(nf.at[m], rows_out[m].at[1], s_row, 3 * m, to_y).wait_recv()
        remote(rows_out[m].at[1], rows_out[m].at[3], s_row, 3 * m + 2, to_core).start()

    trades[0].collect()
    fill_keys(recv.at[0], 0, ks, vs, heads)
    back0 = attend(0, 0, groups)
    x_out.wait_recv()
    c_out.start()
    y_gate.wait_recv()
    c_gate[1].start()
    for m in range(MICRO):
        y_cot[m].wait_recv()
        c_cot[MICRO + m].start()
    trades[1].collect()
    fill_keys(recv.at[1], 1, ks, vs, heads)
    back1 = attend(1, 0, 2)
    c_out.wait_recv()
    post(0, back0)
    back1 = attend(1, 2, groups)
    forward_row(0)
    post(1, back1)
    keep = []
    for m in range(MICRO):
        keep += [
            (recv.at[m], recv_out[m]),
            (mixed.at[m], mixed_out[m]),
            (lse.at[m], lse_out[m]),
            (att.at[m], att_out[m]),
            (res.at[m], res_out[m]),
            (nf.at[m], rows_out[m].at[0]),
            (nf.at[m], both_out.at[m]),
        ]
    keep += [(tags, tags_out), (wq, qkv_out), (wo, wout_out), (gains, gains_out)]
    keep = [pltpu.make_async_copy(a, b, stores.at[3 + i]) for i, (a, b) in enumerate(keep)]
    for copy in keep:
        copy.start()
    forward_row(1)
    for copy in (*keep, *own_copies):
        copy.wait()
    for m in range(MICRO):
        remote(nf.at[m], rows_out[m].at[2], s_row, 3 * m + 1, to_core).wait()
        remote(rows_out[m].at[1], rows_out[m].at[3], s_row, 3 * m + 2, to_core).wait()
        remote(nf.at[m], rows_out[m].at[1], s_row, 3 * m, to_y).wait_send()
        trades[m].release()
    back0.release()
    back1.release()
    for copy in (*x_exp, *c_gate, *c_cot):
        copy.wait()
    for copy in (x_qkv, x_gain, x_out, c_qkv, c_out, y_gate, *y_cot, *tag_trade):
        copy.wait_send()


def run_front(x, gains, cosines, sines, tags, gates, w_qkv, w_out, w_ein, w_eout, cot, groups):
    _, rows, width = x.shape
    heads = width // HEAD // groups
    k = width // 4
    w_qkv = w_qkv.reshape(2, k, 3 * width)
    w_out = w_out.reshape(2, k, width)
    vmem = pl.BlockSpec(memory_space=pltpu.VMEM)
    anywhere = pl.BlockSpec(memory_space=pl.ANY)
    packed = lambda n: (groups, n * heads, HALF, HALF)
    held = MICRO * groups * TILE
    twice = lambda *a: [struct(*a)] * 2
    outs = (
        twice(packed(3), BF)
        + twice(packed(1), BF)
        + twice((groups, 8, TILE), F32)
        + twice((rows, width), BF)
        + twice((rows, width), F32)
        + twice((4, rows, width), BF)
        + twice((4, rows, width), BF)
        + [
            struct((4, *gates.shape), F32),
            struct((MICRO, rows, width), BF),
            struct((groups, *tags.shape), jnp.int32),
            struct((2, 2, k, 3 * width), BF),
            struct((2, 2, k, width), BF),
            struct(w_ein.shape, BF),
            struct(w_eout.shape, BF),
            struct((2, *gains.shape), F32),
        ]
    )
    v = pltpu.VMEM
    dma = lambda *n: pltpu.SemaphoreType.DMA(n)
    scratch = [
        v((2, 2, k, 3 * width), BF),
        v((2, 2, k, width), BF),
        v((2, *gains.shape), F32),
        v((groups, *tags.shape), jnp.int32),
        v((MICRO, *packed(3)), BF),
        v((MICRO, *packed(3)), BF),
        v((heads, held, HALF), BF),
        v((heads, held, HALF), BF),
        v((heads, TILE, held), F32),
        v((MICRO, *packed(1)), BF),
        v((MICRO, *packed(1)), BF),
        v((MICRO, groups, 8, TILE), F32),
        v((MICRO, rows, width), BF),
        v((MICRO, rows, width), F32),
        v((MICRO, rows, width), BF),
    ]
    for shape in ((2,), (2,), (1,), (2,), (groups - 1,), (3,), (6,), (MICRO, groups), (MICRO, groups), (6,)):
        scratch += [dma(*shape), dma(*shape)]
    scratch += [dma(3), dma(MICRO), dma(MICRO), dma(1), dma(3 + 7 * MICRO + 4)]
    return pl.pallas_call(
        functools.partial(front_kernel, heads=heads, groups=groups),
        out_shape=tuple(outs),
        in_specs=[vmem] * 6 + [anywhere] * 5,
        out_specs=(anywhere,) * len(outs),
        scratch_shapes=scratch,
        compiler_params=pltpu.CompilerParams(
            vmem_limit_bytes=VMEM_LIMIT, collective_id=3, has_side_effects=True
        ),
        cost_estimate=price(130),
    )(x, gains, cosines, sines, tags, gates, w_qkv, w_out, w_ein, w_eout, cot)


def ffn_kernel(*refs, tr, spans, counts, first, gated, opened, summed, closing, parts):
    offs = refs[0]
    refs = list(refs[1:])
    take = lambda n: [refs.pop(0) for _ in range(n)]
    x_ref, dy_in = take(2)
    gate_ref = take(1)[0] if gated else None
    wg_parts, wu_parts, wo_parts = take(parts), take(parts), take(parts)
    y0, dx0 = take(2) if opened else (None, None)
    g0 = take(3) if summed else None
    y_ref, dx_ref, dwg_ref, dwu_ref, dwo_ref = take(5)
    xt, yacc, dxacc, hs, djg, dju, wg_ref, wu_ref, wo_ref = take(9)
    dy_ref = take(1)[0] if gated else dy_in
    f = pl.program_id(0)
    rows = x_ref.shape[0]

    @pl.when(f == 0)
    def _():
        xt[...] = x_ref[...].T
        if opened:
            yacc[...] = y0[...].astype(F32)
            dxacc[...] = dx0[...].astype(F32)
        else:
            yacc[...] = jnp.zeros_like(yacc)
            dxacc[...] = jnp.zeros_like(dxacc)
        if gated:
            dy_ref[...] = (dy_in[...].astype(F32) * gate_ref[...]).astype(BF)

    for index, span in enumerate(spans):
        place = pl.ds(pl.multiple_of(offs[index], HALF // 2), span)
        wg_ref[place, :] = wg_parts[index][...]
        wu_ref[place, :] = wu_parts[index][...]
        begin = offs[parts + index]

        @pl.when((f + first >= begin) & (f + first < begin + counts[index]))
        def _(index=index):
            wo_ref[...] = wo_parts[index][...]

    wg, wu, wo = wg_ref[...], wu_ref[...], wo_ref[...]

    def tile(i, carry):
        r = pl.ds(pl.multiple_of(i * tr, tr), tr)
        x = x_ref[r, :]
        g = dot(x, wg)
        u = dot(x, wu)
        dh = dot(dy_ref[r, :], wo, NT)
        sig = 1.0 / (1.0 + jnp.exp(-g))
        act = g * sig
        h = (act * u).astype(BF)
        dg = (dh * u * (sig * (1.0 + g * (1.0 - sig)))).astype(BF)
        du = (dh * act).astype(BF)
        hs[r, :] = h
        djg[r, :] = dg
        dju[r, :] = du
        yacc[r, :] += dot(h, wo)
        dxacc[r, :] += dot(dg, wg, NT) + dot(du, wu, NT)
        return carry

    lax.fori_loop(0, rows // tr, tile, 0)
    grads = [dot(xt[...], djg[...]), dot(xt[...], dju[...]), dot(hs[...], dy_ref[...], TN)]
    for k, out in enumerate((dwg_ref, dwu_ref, dwo_ref)):
        value = grads[k]
        if summed:
            value = value + g0[k][...].astype(F32)
        out[...] = value.astype(BF)

    @pl.when(f == pl.num_programs(0) - 1)
    def _():
        made = yacc[...].astype(BF)
        if gated and closing:
            made = (made.astype(F32) * gate_ref[...]).astype(BF)
        y_ref[...] = made
        dx_ref[...] = dxacc[...].astype(BF)


def run_ffn(x, dy, gate, w_in, w_out, offsets, start=None, grads=None, span=None, closing=True, tr=512, fb=FB, us=10):
    rows, d = x.shape
    ff = sum(w.shape[0] for w in w_out)
    nf = ff // fb
    first, last = span or (0, nf)
    steps = last - first
    gated = gate is not None
    parts = len(w_in)
    spans = [w.shape[0] for w in w_in]
    counts = [w.shape[0] // fb for w in w_out]
    whole = lambda a: pl.BlockSpec(
        a.shape, lambda f, o: (0,) * a.ndim, pipeline_mode=pl.Buffered(1)
    )
    args = [x, dy] + ([gate] if gated else [])
    specs = [whole(a) for a in args]
    args += list(w_in) * 2 + list(w_out)
    specs += [pl.BlockSpec((n, fb), lambda f, o: (0, f + first)) for n in spans]
    specs += [pl.BlockSpec((n, fb), lambda f, o: (0, f + first + nf)) for n in spans]
    for i, c in enumerate(counts):
        specs.append(
            pl.BlockSpec(
                (fb, d), lambda f, o, i=i, c=c: (jnp.clip(f + first - o[parts + i], 0, c - 1), 0)
            )
        )
    if start is not None:
        args += list(start)
        specs += [whole(a) for a in start]
    wide = pl.BlockSpec((d, fb), lambda f, o: (0, f))
    tall = pl.BlockSpec((fb, d), lambda f, o: (f, 0))
    if grads is not None:
        args += list(grads)
        specs += [
            pl.BlockSpec((d, fb), lambda f, o: (0, f + first)),
            pl.BlockSpec((d, fb), lambda f, o: (0, f + first)),
            pl.BlockSpec((fb, d), lambda f, o: (f + first, 0)),
        ]
    full = pl.BlockSpec((rows, d), lambda f, o: (0, 0), pipeline_mode=pl.Buffered(1))
    return pl.pallas_call(
        functools.partial(
            ffn_kernel,
            tr=math.gcd(tr, rows),
            spans=spans,
            counts=counts,
            first=first,
            gated=gated,
            opened=start is not None,
            summed=grads is not None,
            closing=closing,
            parts=parts,
        ),
        out_shape=(
            struct((rows, d), BF),
            struct((rows, d), BF),
            struct((d, steps * fb), BF),
            struct((d, steps * fb), BF),
            struct((steps * fb, d), BF),
        ),
        grid_spec=pltpu.PrefetchScalarGridSpec(
            num_scalar_prefetch=1,
            grid=(steps,),
            in_specs=specs,
            out_specs=(full, full, wide, wide, tall),
            scratch_shapes=[
                pltpu.VMEM((d, rows), BF),
                pltpu.VMEM((rows, d), F32),
                pltpu.VMEM((rows, d), F32),
                pltpu.VMEM((rows, fb), BF),
                pltpu.VMEM((rows, fb), BF),
                pltpu.VMEM((rows, fb), BF),
                pltpu.VMEM((d, fb), BF),
                pltpu.VMEM((d, fb), BF),
                pltpu.VMEM((fb, d), BF),
            ]
            + ([pltpu.VMEM((rows, d), BF)] if gated else []),
        ),
        compiler_params=pltpu.CompilerParams(vmem_limit_bytes=VMEM_LIMIT),
        cost_estimate=price(us),
    )(offsets, *args)


def price(us):
    return pl.CostEstimate(flops=int(us * 1.15e9), bytes_accessed=0, transcendentals=0)


def norm_back(values, scale, gain, grad):
    gain_grad = jnp.sum(grad * values * scale, 0, keepdims=True)
    scaled = gain * grad
    grad_in = scale * scaled - values * (scale * scale * scale) * jnp.mean(
        scaled * values, -1, keepdims=True
    )
    return grad_in, gain_grad


def mid_kernel(*refs, per, first):
    dxs, dxr, res_ref, gain_ref, cot_ref, w_ref, att_ref = refs[:7]
    if first:
        gres_ref, pay, gg_ref, gbf = refs[7:]
    else:
        att0, gbf0, gres_ref, pay, gg_ref, gw_ref, gbf = refs[7:]
    residual = res_ref[...]
    grad = dxs[...].astype(F32) + dxr[...].astype(F32)
    back, gain_grad = norm_back(residual, rms_scale(residual), gain_ref[...], grad)
    gg_ref[...] = gain_grad
    total = cot_ref[0].astype(F32) + back
    gres_ref[...] = total
    gbf[...] = total.astype(BF)
    mixed = dot(gbf[...], w_ref[...], NT)
    for pair in range(mixed.shape[1] // HALF):
        tile = mixed[:, pair * HALF : (pair + 1) * HALF]
        for side, packed in enumerate(swap_heads(tile[:HALF], tile[HALF:])):
            head = 2 * pair + side
            pay[head // per, head % per] = packed.astype(BF)
    if not first:
        gw_ref[...] = (dot(att_ref[...], gbf[...], TN) + dot(att0[...], gbf0[...], TN)).astype(BF)


def run_mid(dxs, dxr, residual, gain, cot, w, att, groups, micro, before=()):
    rows, width = residual.shape
    per = width // HEAD // groups
    args = (dxs, dxr, residual, gain, cot, w, att, *before)
    specs = [full_spec(a.shape) for a in args]
    specs[0] = pl.BlockSpec((rows, width), lambda _: (micro, 0))
    specs[4] = pl.BlockSpec((1, rows, width), lambda _: (micro, 0, 0))
    pay = (groups, per, HALF, HALF)
    outs = [struct((rows, width), F32), struct(pay, BF), struct((1, width), F32)]
    if micro == 0:
        outs.append(struct((rows, width), BF))
        scratch = []
    else:
        outs.append(struct((width, width), BF))
        scratch = [pltpu.VMEM((rows, width), BF)]
    return call(
        functools.partial(mid_kernel, per=per, first=micro == 0),
        tuple(outs),
        grid=(1,),
        in_specs=specs,
        out_specs=tuple(full_spec(o.shape) for o in outs),
        scratch=scratch,
        us=4 + micro,
    )(*args)


def fin_kernel(q0, kv0, d1, x_ref, gain_ref, w_ref, cos_ref, sin_ref, res0, res1, gin_ref, gw0_ref, gw1_ref, gj, *, per):
    width = x_ref.shape[1]
    for micro, sources in enumerate((((q0, 0), (kv0, 0), (kv0, 1)), ((d1, 0), (d1, 1), (d1, 2)))):
        rows = slice(micro * TILE, (micro + 1) * TILE)
        cosines, sines = cos_ref[rows, :], sin_ref[rows, :]
        for kind in range(3):
            for pair in range(width // HALF):
                tile = natural(*sources[kind], pair, per)
                if kind == 0:
                    tile = tile * 0.125
                if kind < 2:
                    tile = rotate(tile, cosines, -sines)
                gj[rows, kind * width + pair * HALF : kind * width + (pair + 1) * HALF] = tile.astype(BF)
    tokens = x_ref[...].astype(F32)
    scale = rms_scale(tokens)
    gain = gain_ref[...]
    normed = (tokens * scale * gain).astype(BF)
    first = dot(gj[...], w_ref[...], NT)
    back, _ = norm_back(tokens, scale, gain, first)
    gin_ref[:TILE] = res0[...] + back[:TILE]
    gin_ref[TILE:] = res1[...] + back[TILE:]
    turned = normed.T
    split = gw0_ref.shape[1]
    gw0_ref[...] = dot(turned, gj[:, :split]).astype(BF)
    gw1_ref[...] = dot(turned, gj[:, split:]).astype(BF)


def run_fin(parts, x, gain, w, cosines, sines, gres):
    rows, width = x.shape
    args = (*parts, x, gain, w, cosines, sines, *gres)
    half = struct((width, 3 * width // 2), BF)
    outs = (struct((rows, width), F32), half, half)
    return call(
        functools.partial(fin_kernel, per=parts[0].shape[1]),
        outs,
        grid=(1,),
        in_specs=[full_spec(a.shape) for a in args],
        out_specs=tuple(full_spec(o.shape) for o in outs),
        scratch=[pltpu.VMEM((rows, 3 * width), BF)],
        us=11,
    )(*args)


def exchange(value, axis, mask):
    size = lax.axis_size(axis)
    return lax.ppermute(value, axis, [(i, i ^ mask) for i in range(size)])


def bits_of(size):
    return [1 << b for b in range(size.bit_length() - 1)]


def gather_rest(value):
    for mask in bits_of(lax.axis_size("expert"))[2:]:
        value = jnp.concatenate([value, exchange(value, "expert", mask)], 0)
    return value


def scatter_xor(value):
    masks = bits_of(lax.axis_size("expert"))
    for mask in (*reversed(masks[2:]), *masks[:2]):
        half = value.shape[0] // 2
        got = exchange(value[half:], "expert", mask)
        value = (value[:half].astype(F32) + got.astype(F32)).astype(value.dtype)
    return value


def ordered(flag, mine, theirs):
    first = jnp.where(flag == 0, mine, theirs)
    second = jnp.where(flag == 0, theirs, mine)
    return jnp.concatenate([first, second], 0)


def pick(value, parts, index):
    size = value.shape[0] // parts
    return lax.dynamic_slice_in_dim(value, index * size, size, 0)


def after(value, token):
    return lax.optimization_barrier((value, token))[0]


def fetch_parts(shard, axis):
    part = exchange(pick(shard, 2, lax.axis_index(axis) % 2), "dp", 1)
    return part, exchange(part, axis, 1)


PIECES = 4
AHEAD = 3


def reduce_kernel(*refs, owned, common, extra, counts):
    refs = list(refs)
    take = lambda n: [refs.pop(0) for _ in range(n)]
    own_in, com_in, extra_in = take(owned), take(common), take(counts[0])
    own_out, com_out, extra_out = take(owned), take(common), take(counts[1])
    own_buf = [take(4) for _ in range(owned)]
    com_buf = [take(6) for _ in range(common)]
    own_sems, com_sems, extra_buf = take(10), take(20), take(counts[2])
    barrier = pltpu.get_barrier_semaphore()
    e, z, d = lax.axis_index("expert"), lax.axis_index("context"), lax.axis_index("dp")
    core, y = e % 2, e // 2 % 2
    mate = z + 1 - 2 * (z % 2)
    outer = (z == 0) | (z == 3)
    inner = (z == 1) | (z == 2)
    to_x = {"dp": 1 - d}
    to_core = {"expert": e + 1 - 2 * core}
    to_y = {"expert": e + 2 - 4 * y}
    to_mate = {"context": mate}
    to_mid = {"context": 3 - z}
    groups = lax.axis_size("context")
    others = [{"context": (z + k) % groups} for k in range(1, groups)]
    near = [to_x, to_core, to_y, *others]
    meet(barrier, near)

    o_load, o_store = own_sems[:2]
    o_x, o_1, o_2, o_3 = [own_sems[2 + 2 * k : 4 + 2 * k] for k in range(4)]
    c_load, c_store = com_sems[:2]
    c_core, c_y, c_x, c_1, c_2, c_3, c_back, c_fore, c_last = [
        com_sems[2 + 2 * k : 4 + 2 * k] for k in range(9)
    ]

    chunks = owned * PIECES
    where = lambda c: (c // PIECES, c % PIECES)

    def o_sum(c):
        j, k = where(c)
        return own_buf[j][0].at[k]

    def o_loading(c):
        j, k = where(c)
        return pltpu.make_async_copy(own_in[j].at[d, k], o_sum(c), o_load.at[c])

    def o_storing(c):
        j, k = where(c)
        return pltpu.make_async_copy(own_buf[j][2].at[k], own_out[j].at[k], o_store.at[c])

    def o_wire(stage, c):
        j, k = where(c)
        buf = own_buf[j]
        if stage == "x":
            return remote(own_in[j].at[1 - d, k], buf[1].at[k], o_x, c, to_x)
        if stage == "1":
            return remote(o_sum(c), buf[2].at[k], o_1, c, to_mate)
        if stage == "2":
            return remote(o_sum(c), buf[3].at[k], o_2, c, to_mid)
        return remote(buf[2].at[k], own_out[j].at[k], o_3, c, to_mate)

    def o_first(c):
        j, k = where(c)
        o_loading(c).wait()
        o_wire("x", c).wait_recv()
        if c + AHEAD < chunks:
            o_wire("x", c + AHEAD).start()
        own_buf[j][0][k] = own_buf[j][0][k] + own_buf[j][1][k]

        @pl.when(outer)
        def _():
            o_wire("1", c).start()

    def o_second(c):
        j, k = where(c)

        @pl.when(inner)
        def _():
            o_wire("1", c).wait_recv()
            own_buf[j][0][k] = own_buf[j][0][k] + own_buf[j][2][k]
            o_wire("2", c).start()

    def o_third(c):
        j, k = where(c)

        @pl.when(inner)
        def _():
            o_wire("2", c).wait_recv()
            own_buf[j][2][k] = own_buf[j][0][k] + own_buf[j][3][k]
            o_wire("3", c).start()
            o_storing(c).start()

    def o_fourth(c):
        @pl.when(outer)
        def _():
            o_wire("3", c).wait_recv()

    def c_loading(i, h):
        return pltpu.make_async_copy(com_in[i].at[h, core], com_buf[i][0].at[h], c_load.at[2 * i + h])

    def c_storing(i):
        return pltpu.make_async_copy(com_buf[i][4], com_out[i].at[core, y], c_store.at[i])

    def c_wire(stage, i, h=0):
        total, r_core, r_y, r_x, r_1, r_2 = com_buf[i]
        if stage == "core":
            return remote(com_in[i].at[h, 1 - core], r_core.at[h], c_core, 2 * i + h, to_core)
        if stage == "y":
            return remote(total.at[h, 1 - y], r_y.at[h], c_y, 2 * i + h, to_y)
        if stage == "x":
            return remote(total.at[1 - d, y], r_x, c_x, i, to_x)
        if stage == "1":
            return remote(total.at[d, y], r_1, c_1, i, to_mate)
        if stage == "2":
            return remote(total.at[d, y], r_2, c_2, i, to_mid)
        if stage == "3":
            return remote(r_1, com_out[i].at[core, y], c_3, i, to_mate)
        if stage == "fore":
            return remote(r_1, com_out[i].at[core, y], c_fore, i, to_y)
        if stage == "back":
            return remote(com_out[i].at[core, y], com_out[i].at[core, y], c_fore, i, to_y)
        return remote(com_out[i].at[core], com_out[i].at[core], c_last, i, to_core)

    def c_a(i):
        for h in range(2):
            c_loading(i, h).wait()
            c_wire("core", i, h).wait_recv()
        com_buf[i][0][...] = com_buf[i][0][...] + com_buf[i][1][...]
        for h in range(2):
            c_wire("y", i, h).start()

    def c_b(i):
        total, r_y = com_buf[i][0], com_buf[i][2]
        for h in range(2):
            c_wire("y", i, h).wait_recv()
            total[h, y] = total[h, y] + r_y[h]
        c_wire("x", i).start()

    def c_c(i):
        total, r_x = com_buf[i][0], com_buf[i][3]
        c_wire("x", i).wait_recv()
        total[d, y] = total[d, y] + r_x[...]

        @pl.when(outer)
        def _():
            c_wire("1", i).start()

    def c_d(i):
        total, r_1 = com_buf[i][0], com_buf[i][4]

        @pl.when(inner)
        def _():
            c_wire("1", i).wait_recv()
            total[d, y] = total[d, y] + r_1[...]
            c_wire("2", i).start()

    def c_e(i):
        total, r_1, r_2 = com_buf[i][0], com_buf[i][4], com_buf[i][5]

        @pl.when(inner)
        def _():
            c_wire("2", i).wait_recv()
            r_1[...] = total[d, y] + r_2[...]
            c_wire("3", i).start()
            c_wire("fore", i).start()
            c_storing(i).start()

    def c_f(i):
        @pl.when(outer)
        def _():
            c_wire("3", i).wait_recv()
            c_wire("back", i).start()

    def c_g(i):
        @pl.when(inner)
        def _():
            c_storing(i).wait()

        c_wire("fore", i).wait_recv()
        c_wire("last", i).start()

    def c_h(i):
        c_wire("last", i).wait_recv()

    for i in range(common):
        for h in range(2):
            c_wire("core", i, h).start()
            c_loading(i, h).start()
    for c in range(chunks):
        o_loading(c).start()
        if c < AHEAD:
            o_wire("x", c).start()
    events, closing = extra(extra_in, extra_out, extra_buf) if extra else ([], None)
    for c in range(chunks):
        for lag, step in ((1, o_first), (2.5, o_second), (3.5, o_third), (4.6, o_fourth)):
            events.append((c + lag, step, c))
    for i in range(common):
        base = 2.0 * i + 0.5
        for lag, step in zip((0, 2.3, 4, 5.5, 6.6, 7.7, 8.9, 9.6), (c_a, c_b, c_c, c_d, c_e, c_f, c_g, c_h)):
            events.append((base + lag, step, i))
    for _, step, index in sorted(events, key=lambda v: v[0]):
        step(index)
    if closing:
        closing()
    for c in range(chunks):
        o_wire("x", c).wait_send()
    for i in range(common):
        for h in range(2):
            c_wire("core", i, h).wait_send()
            c_wire("y", i, h).wait_send()
        c_wire("x", i).wait_send()
        c_wire("last", i).wait_send()

    @pl.when(outer)
    def _():
        for c in range(chunks):
            o_wire("1", c).wait_send()
        for i in range(common):
            c_wire("1", i).wait_send()
            c_wire("back", i).wait_send()

    @pl.when(inner)
    def _():
        for c in range(chunks):
            o_wire("2", c).wait_send()
            o_wire("3", c).wait_send()
            o_storing(c).wait()
        for i in range(common):
            c_wire("2", i).wait_send()
            c_wire("3", i).wait_send()
            c_wire("fore", i).wait_send()


def run_reduce(expert_grads, shared_grads, collective_id, us, extra=None, extra_args=(), extra_outs=(), extra_scratch=()):
    own = [g.reshape(2, PIECES, g.shape[0] // (2 * PIECES), g.shape[1]) for g in expert_grads]
    com = []
    for g in shared_grads:
        for mask in bits_of(lax.axis_size("expert"))[2:]:
            g = g + exchange(g, "expert", mask)
        com.append(g.reshape(2, 2, 2, g.shape[0] // 8, g.shape[1]))
    chunks = len(own) * PIECES
    scratch = []
    for g in own:
        scratch += [pltpu.VMEM(g.shape[1:], BF)] * 4
    for g in com:
        small = g.shape[3:]
        scratch += [pltpu.VMEM((2, 2, *small), BF)] * 2 + [pltpu.VMEM((2, *small), BF)]
        scratch += [pltpu.VMEM(small, BF)] * 3
    dma = lambda n: pltpu.SemaphoreType.DMA((max(n, 1),))
    scratch += [dma(chunks)] * 10
    n = len(com)
    scratch += [dma(2 * n), dma(n)] + [dma(2 * n)] * 4 + [dma(n)] * 14
    anywhere = pl.BlockSpec(memory_space=pl.ANY)
    outs = [struct(g.shape[1:], BF) for g in own] + [struct((2, 2, *g.shape[3:]), BF) for g in com]
    got = pl.pallas_call(
        functools.partial(
            reduce_kernel,
            owned=len(own),
            common=n,
            extra=extra,
            counts=(len(extra_args), len(extra_outs), len(extra_scratch)),
        ),
        out_shape=(*outs, *extra_outs),
        in_specs=[anywhere] * (len(own) + n)
        + [pl.BlockSpec(memory_space=pltpu.VMEM)] * len(extra_args),
        out_specs=(anywhere,) * (len(outs) + len(extra_outs)),
        scratch_shapes=[*scratch, *extra_scratch],
        compiler_params=pltpu.CompilerParams(
            vmem_limit_bytes=VMEM_LIMIT, collective_id=collective_id, has_side_effects=True
        ),
        cost_estimate=price(us),
    )(*own, *com, *extra_args)
    return [g.reshape(-1, g.shape[-1]).astype(F32) for g in got[: len(outs)]], got[len(outs) :]


def back_extra(ins, outs, bufs, *, heads, groups):
    recv0, recv1, grad_ref, out_ref, lse_ref, key_tag, query_tag, early_k, early_v = ins
    pay, pay0, ks, vs, dk, dv, s1, r1, s0, r0, local = bufs
    z = lax.axis_index("context")
    sets = ((pay, outs[0], (s1, r1), 0), (pay0, outs[1], (s0, r0), 1))

    def send(index):
        def _(dest):
            src, out, sems, k = sets[index]

            @pl.when(dest != z)
            def _():
                pltpu.make_async_remote_copy(
                    src_ref=src.at[dest],
                    dst_ref=out.at[z],
                    send_sem=sems[0].at[dest],
                    recv_sem=sems[1].at[z],
                    device_id={"context": dest},
                    device_id_type=pl.DeviceIdType.MESH,
                ).start()

            @pl.when(dest == z)
            def _():
                pltpu.make_async_copy(src.at[dest], out.at[dest], local.at[k]).start()

        return _

    def begin(_):
        back_start([recv0, recv1], ks, vs, dk, dv, (early_k, early_v), heads, groups)

    def step(s):
        back_step(
            s, 1, heads, groups, [recv0, recv1], grad_ref, out_ref, lse_ref, key_tag, query_tag, pay, ks, vs, dk, dv
        )

    def home(_):
        for dest in range(groups):
            back_pack(dk, dv, pay, dest, heads, groups, heads)
            send(0)(dest)
        for dest in range(groups):
            back_pack(dk, dv, pay0, dest, 0, 0, heads)
            send(1)(dest)

    def closing():
        for src, out, sems, k in sets:
            for other in range(groups):

                @pl.when(other != z)
                def _(src=src, out=out, sems=sems, other=other):
                    copy = pltpu.make_async_remote_copy(
                        src_ref=src.at[other],
                        dst_ref=out.at[other],
                        send_sem=sems[0].at[other],
                        recv_sem=sems[1].at[other],
                        device_id={"context": other},
                        device_id_type=pl.DeviceIdType.MESH,
                    )
                    copy.wait_send()
                    copy.wait_recv()

                @pl.when(other == z)
                def _(src=src, out=out, k=k, other=other):
                    pltpu.make_async_copy(src.at[other], out.at[other], local.at[k]).wait()

    events = [(0.3, begin, 0)] + [(0.5 + 1.35 * s, step, s) for s in range(groups)] + [(0.5 + 1.35 * groups, home, 0)]
    return events, closing


def body(
    inputs,
    keep_flags,
    block_ids,
    expert_ids,
    gate_weights,
    norm_attn,
    w_qkv,
    w_attn_out,
    norm_ffn,
    w_shared_in,
    w_shared_out,
    w_expert_in,
    w_expert_out,
    cotangent,
):
    width = w_qkv.shape[1] // 3
    rows = inputs.shape[2]
    groups = lax.axis_size("context")
    experts = lax.axis_size("expert")
    z = lax.axis_index("context")
    seq_rows = rows * groups
    x = inputs[0]
    cot = cotangent[0].reshape(MICRO * rows, width)

    positions = (
        jnp.arange(MICRO, dtype=jnp.int32)[:, None] * seq_rows
        + z * rows
        + jnp.arange(rows, dtype=jnp.int32)[None, :]
    ).reshape(-1)
    half = HEAD // 2
    freq = jnp.exp(-math.log(ROPE_BASE) * jnp.arange(half, dtype=F32) * 2.0 / HEAD)
    angle = positions.astype(F32)[:, None] * freq[None, :]
    cos_t, sin_t = jnp.cos(angle), jnp.sin(angle)
    cosines = jnp.concatenate([cos_t] * 4, -1)
    sines = jnp.concatenate([-sin_t, sin_t, -sin_t, sin_t], -1)

    blocks = block_ids[0] + 8 * jnp.arange(MICRO, dtype=jnp.int32)[:, None]
    key_tags = jnp.where(keep_flags[0] == 1, blocks, HIDDEN)
    tags = jnp.stack([blocks, key_tags])[:, :, None]

    per_expert = jnp.sum(
        jnp.where(
            expert_ids[0][None] == jnp.arange(experts, dtype=jnp.int32)[:, None, None, None],
            gate_weights[0][None],
            0.0,
        ),
        -1,
    )
    gains = jnp.stack([norm_attn, norm_ffn]).astype(F32)
    (
        *pairs,
        gates_four,
        nf_both,
        all_tags,
        mat_qkv,
        mat_out,
        ein_other,
        eout_other,
        gains,
    ) = run_front(
        x,
        gains,
        cosines,
        sines,
        tags,
        per_expert,
        w_qkv,
        w_attn_out,
        w_expert_in[0],
        w_expert_out[0],
        cotangent[0],
        groups,
    )
    recvs, mixed, lses, att, res, rows_four, cot_four = [pairs[2 * i : 2 * i + 2] for i in range(7)]
    mat_qkv = mat_qkv.reshape(width, -1)
    mat_out = mat_out.reshape(width, width)
    gain_attn = gains[:, 0].reshape(1, width)
    gain_ffn = gains[:, 1].reshape(1, width)
    all_tags = all_tags[:, :, :, 0].transpose(1, 2, 0, 3)
    query_row = all_tags[0].reshape(MICRO * groups, 1, rows)
    key_col = all_tags[1].reshape(-1, 1)
    own_gates = lax.dynamic_index_in_dim(
        gather_rest(gates_four), lax.axis_index("expert"), 1, False
    )
    gate = [own_gates[:, m].reshape(-1, 1) for m in range(MICRO)]

    core = lax.axis_index("expert") % 2
    dp = lax.axis_index("dp")
    k_half, f_half = width // 2, w_shared_out.shape[0]
    ein_parts = (w_expert_in[0], ein_other)
    eout_parts = (w_expert_out[0], eout_other)
    sin_parts = (w_shared_in, *fetch_parts(after(w_shared_in, ein_other), "expert"))
    sout_parts = (w_shared_out, *fetch_parts(after(w_shared_out, ein_other), "expert"))
    expert_offs = jnp.stack(
        [dp * k_half, (1 - dp) * k_half, dp * f_half // FB, (1 - dp) * f_half // FB]
    )

    def offsets(bit):
        places = [2 * (1 - dp) + bit, 2 * (1 - dp) + 1 - bit]
        return jnp.stack(
            [dp * k_half]
            + [p * (k_half // 2) for p in places]
            + [dp * f_half // FB]
            + [p * (f_half // 2) // FB for p in places]
        )

    capacity = 4 * rows // experts

    def expert_pass(m, grads):
        hidden = gather_rest(rows_four[m]).reshape(-1, width)
        grad, weight = gather_rest(cot_four[m]).reshape(-1, width), gate[m]
        if capacity < rows:
            chosen = weight.reshape(-1, rows) > 0
            slots = jnp.cumsum(chosen.astype(jnp.int32), 1) - 1
            select = (
                chosen[:, None] & (slots[:, None] == jnp.arange(capacity, dtype=jnp.int32)[:, None])
            ).astype(BF)
            squeeze = lambda v: jnp.einsum("bcr,brd->bcd", select, v.reshape(-1, rows, width)).reshape(-1, width)
            spread = lambda v: jnp.einsum("bcr,bcd->brd", select, v.reshape(-1, capacity, width)).reshape(-1, width)
            hidden, grad = squeeze(hidden), squeeze(grad)
            weight = jnp.sum(select.astype(F32) * weight.reshape(-1, 1, rows), -1).reshape(-1, 1)
        made, dx, *grads = run_ffn(
            hidden, grad, weight, ein_parts, eout_parts, expert_offs, grads=grads, us=41
        )
        if capacity < rows:
            made, dx = spread(made), spread(dx)
        return scatter_xor(dx), scatter_xor(made), grads

    dx0, routed0, g_expert = expert_pass(0, None)
    shared, dx_shared, *g_shared = run_ffn(
        nf_both.reshape(-1, width), cot, None, sin_parts, sout_parts, offsets(core), us=21
    )
    dx1, routed1, g_expert = expert_pass(1, g_expert)
    output = jnp.stack(
        [
            (res[m] + shared[m * rows : (m + 1) * rows].astype(F32) + r.astype(F32)).astype(BF)
            for m, r in enumerate((routed0, routed1))
        ]
    )

    gres0, pay0, gg0, gbf0 = run_mid(
        dx_shared, dx0, res[0], gain_ffn, cotangent[0], mat_out, att[0], groups, 0
    )
    grad0 = lax.all_to_all(pay0, "context", 0, 0, tiled=True)
    back_q0, early_k, early_v = run_attend_back(
        recvs[0], grad0, mixed[0], lses[0], key_col, query_row, groups
    )
    q0 = lax.all_to_all(back_q0, "context", 0, 0, tiled=True)
    gres1, pay1, gg1, g_out = run_mid(
        dx_shared, dx1, res[1], gain_ffn, cotangent[0], mat_out, att[1], groups, 1, (att[0], gbf0)
    )
    grad1 = lax.all_to_all(pay1, "context", 0, 0, tiled=True)
    heads = width // HEAD // groups
    pay = lambda n: (groups, n * heads, HALF, HALF)
    held = MICRO * groups * TILE
    reduced, (d1, kv0) = run_reduce(
        g_expert,
        [*g_shared, g_out],
        1,
        140,
        functools.partial(back_extra, heads=heads, groups=groups),
        (*recvs, grad1, mixed[1], lses[1], key_col, query_row, early_k, early_v),
        (struct(pay(3), BF), struct(pay(2), BF)),
        [
            pltpu.VMEM(pay(3), BF),
            pltpu.VMEM(pay(2), BF),
            pltpu.VMEM((heads, held, HALF), BF),
            pltpu.VMEM((heads, held, HALF), BF),
            pltpu.VMEM((heads, held, HALF), F32),
            pltpu.VMEM((heads, held, HALF), F32),
        ]
        + [pltpu.SemaphoreType.DMA((groups,))] * 4
        + [pltpu.SemaphoreType.DMA((2,))],
    )
    e_gate, e_up, r_eout, r_gate, r_up, r_sout, r_out = reduced
    grad_input, *g_qkv = run_fin(
        (q0, kv0, d1),
        x.reshape(MICRO * rows, width),
        gain_attn,
        mat_qkv,
        cosines,
        sines,
        (gres0, gres1),
    )

    g_gain_ffn = gg0 + gg1
    total = g_gain_ffn
    for axis in ("expert", "context", "dp"):
        for mask in bits_of(lax.axis_size(axis)):
            total = total + exchange(total, axis, mask)
    r_gain_ffn = pick(total[0], 2, dp)
    (r_qk, r_v), _ = run_reduce([], g_qkv, 2, 45)
    r_qkv = jnp.concatenate([r_qk, r_v], 1)
    r_sin = jnp.concatenate([r_gate, r_up], 1)
    r_gain_attn = jnp.sum(w_qkv.astype(F32) * r_qkv, 1) / norm_attn.astype(F32)
    r_ein = jnp.concatenate([e_gate, e_up], 1)
    return (
        output[None],
        grad_input.reshape(1, MICRO, rows, width),
        r_gain_attn,
        r_qkv,
        r_out,
        r_gain_ffn,
        r_sin,
        r_sout,
        r_ein[None],
        r_eout[None],
    )


def solution(mesh):
    tokens = P(("expert", "dp"), None, "context", None)
    flags = P(("expert", "dp"), None, "context")
    placed = (
        tokens,
        flags,
        flags,
        tokens,
        tokens,
        P("dp"),
        P("dp", None),
        P("dp", None),
        P("dp"),
        P("dp", None),
        P("dp", None),
        P("expert", "dp", None),
        P("expert", "dp", None),
        tokens,
    )
    return jax.shard_map(
        body,
        mesh=mesh,
        in_specs=placed,
        out_specs=(
            tokens,
            tokens,
            P("dp"),
            P("dp", None),
            P("dp", None),
            P("dp"),
            P("dp", None),
            P("dp", None),
            P("expert", "dp", None),
            P("expert", "dp", None),
        ),
        check_vma=False,
    )
```

```python
import functools
import math

import jax
import jax.numpy as jnp
from jax import lax
from jax.experimental import pallas as pl
from jax.experimental.pallas import tpu as pltpu
from jax.sharding import PartitionSpec as P

HEAD = 64
MICRO = 2
TILE = 256
HALF = 128
EPSILON = 1e-05
ROPE_BASE = 10000.0
MASKED = -3e30
HIDDEN = 1 << 20
BF = jnp.bfloat16
F32 = jnp.float32
NT = (((1,), (1,)), ((), ()))
TN = (((0,), (0,)), ((), ()))
VMEM_LIMIT = 60 << 20
FB = 512


def dot(left, right, dims=(((1,), (0,)), ((), ()))):
    return lax.dot_general(left, right, dims, preferred_element_type=F32)


def rms_scale(values):
    return lax.rsqrt(jnp.mean(values * values, -1, keepdims=True) + EPSILON)


def low_lanes(rows):
    return lax.broadcasted_iota(jnp.int32, (rows, HALF), 1) < HEAD


def swap_heads(first, second):
    low = low_lanes(HALF)
    return (
        jnp.where(low, first, pltpu.roll(second, HEAD, 1)),
        jnp.where(low, pltpu.roll(first, HEAD, 1), second),
    )


def rotate(tile, cosines, sines):
    lane = lax.broadcasted_iota(jnp.int32, tile.shape, 1)
    partner = jnp.where(
        lane % HEAD < HEAD // 2,
        pltpu.roll(tile, HALF - HEAD // 2, 1),
        pltpu.roll(tile, HEAD // 2, 1),
    )
    return tile * cosines + partner * sines


def call(kernel, out_shape, *, grid=(), in_specs=None, out_specs=None, scratch=(), us=5):
    return pl.pallas_call(
        kernel,
        out_shape=out_shape,
        grid=grid,
        in_specs=in_specs,
        out_specs=out_specs,
        scratch_shapes=scratch,
        compiler_params=pltpu.CompilerParams(vmem_limit_bytes=VMEM_LIMIT),
        cost_estimate=price(us),
    )


def full_spec(shape):
    return pl.BlockSpec(tuple(shape), lambda *_: (0,) * len(shape))


def struct(shape, dtype):
    return jax.ShapeDtypeStruct(tuple(shape), dtype)


def project(tokens, gain, w_ref, cosines, sines, pay, groups):
    normed = (tokens * rms_scale(tokens) * gain).astype(BF)
    width = tokens.shape[1]
    per = width // HEAD // groups
    for kind in range(3):
        joined = dot(normed, w_ref[:, kind * width : (kind + 1) * width])
        for pair in range(width // HALF):
            tile = joined[:, pair * HALF : (pair + 1) * HALF]
            if kind < 2:
                tile = rotate(tile, cosines, sines)
            if kind == 0:
                tile = tile * 0.125
            for side, packed in enumerate(swap_heads(tile[:HALF], tile[HALF:])):
                head = 2 * pair + side
                pay[head // per, kind * per + head % per] = packed.astype(BF)


def unpack(ref, index, kind_head):
    tile = ref[index, kind_head]
    return tile, pltpu.roll(tile.astype(F32), HEAD, 1).astype(BF)


def fill_keys(recv, micro, ks, vs, heads):
    groups = recv.shape[0]
    for src in range(groups):
        base = (micro * groups + src) * TILE
        for h in range(heads):
            for store, kind in ((ks, 1), (vs, 2)):
                first, second = unpack(recv, src, kind * heads + h)
                store[h, base : base + HALF] = first
                store[h, base + HALF : base + TILE] = second


def masked_rows(ref, index, kind_head):
    tile = ref[index, kind_head].astype(F32)
    both = jnp.concatenate([tile, pltpu.roll(tile, HEAD, 1)], 0)
    return jnp.where(low_lanes(TILE), both, 0.0)


def pack_rows(values):
    return jnp.where(low_lanes(HALF), values[:HALF], pltpu.roll(values[HALF:], HEAD, 1))


def attend_step(step, micro, heads, groups, recv, tags, out_ref, lse_ref, ks, vs, scores):
    count = groups * micro + jnp.minimum(step + 2, groups)
    queries = [masked_rows(recv, step, h).astype(BF) for h in range(heads)]
    tag = jnp.broadcast_to(tags[step, 0, micro], (8, TILE)).T[:, :1]
    same = lax.broadcasted_iota(jnp.int32, (TILE, TILE), 0) == lax.broadcasted_iota(
        jnp.int32, (TILE, TILE), 1
    )

    def first_pass(j, tops):
        keys = pl.ds(pl.multiple_of(j * TILE, TILE), TILE)
        key_tag = tags[j % groups, 1, j // groups]
        seen = (key_tag <= tag) | (same & (j == groups * micro + step))
        new = []
        for h in range(heads):
            part = jnp.where(seen, dot(queries[h], ks[h, keys, :], NT), MASKED)
            scores[h, :, keys] = part
            new.append(jnp.maximum(tops[h], jnp.maximum(part[:, :HALF], part[:, HALF:])))
        return tuple(new)

    tops = lax.fori_loop(
        0, count, first_pass, (jnp.full((TILE, HALF), MASKED, F32),) * heads
    )
    tops = [jnp.max(top, 1, keepdims=True) for top in tops]

    def second_pass(j, carry):
        keys = pl.ds(pl.multiple_of(j * TILE, TILE), TILE)
        sums, totals = carry
        new_sums, new_totals = [], []
        for h in range(heads):
            expo = jnp.exp(scores[h, :, keys] - tops[h])
            new_sums.append(sums[h] + (expo[:, :HALF] + expo[:, HALF:]))
            new_totals.append(totals[h] + dot(expo.astype(BF), vs[h, keys, :]))
        return tuple(new_sums), tuple(new_totals)

    zero = (jnp.zeros((TILE, HALF), F32),) * heads
    sums, totals = lax.fori_loop(0, count, second_pass, (zero, zero))
    lane = lax.broadcasted_iota(jnp.int32, (TILE, HALF), 1)
    logs = jnp.zeros((TILE, HALF), F32)
    for h in range(heads):
        total = jnp.sum(sums[h], 1, keepdims=True)
        out_ref[step, h] = pack_rows(totals[h] / total).astype(BF)
        logs = jnp.where(lane == h, tops[h] + jnp.log(total), logs)
    lse_ref[step] = logs.T[:8]


def back_begin(micro, step, heads, recv, grad, out, qs, gs, deltas, acc):
    ones = jnp.ones((8, HALF), F32)
    for h in range(heads):
        grad_f = masked_rows(grad, step, h)
        qs[h] = masked_rows(recv, step, h).astype(BF)
        gs[h] = grad_f.astype(BF)
        deltas[h] = lax.dot_general(
            ones,
            grad_f * masked_rows(out, step, h),
            NT,
            precision=lax.Precision.HIGHEST,
            preferred_element_type=F32,
        )
    acc[...] = jnp.zeros_like(acc)


def back_tile(micro, step, j, heads, groups, lse, key_tag, query_tag, ks, vs, dk, dv, qs, gs, deltas, acc):
    keys = pl.ds(pl.multiple_of(j * TILE, TILE), TILE)
    same = lax.broadcasted_iota(jnp.int32, (TILE, TILE), 0) == lax.broadcasted_iota(
        jnp.int32, (TILE, TILE), 1
    )
    tag = query_tag[groups * micro + step]
    seen = (key_tag[keys, :] <= tag) | (same & (j == groups * micro + step))
    for h in range(heads):
        key, value = ks[h, keys, :], vs[h, keys, :]
        scores = dot(key, qs[h], NT)
        probs = jnp.where(seen, jnp.exp(scores - lse[step, h : h + 1, :]), 0.0)
        dv[h, keys, :] += dot(probs.astype(BF), gs[h])
        slope = (probs * (dot(value, gs[h], NT) - deltas[h, :1])).astype(BF)
        dk[h, keys, :] += dot(slope, qs[h])
        acc[h] += dot(slope, key, TN)


def back_pack(dk, dv, pay, src, base, heads):
    rows = slice((base + src) * TILE, (base + src + 1) * TILE)
    for h in range(heads):
        pay[src, heads + h] = pack_rows(dk[h, rows]).astype(BF)
        pay[src, 2 * heads + h] = pack_rows(dv[h, rows]).astype(BF)


def natural(ref, first_kind, pair, per):
    tiles = []
    for head in (2 * pair, 2 * pair + 1):
        tiles.append(ref[head // per, first_kind * per + head % per].astype(F32))
    return jnp.concatenate(swap_heads(*tiles), 0)


def remote(src, dst, sems, index, target, arrival=None):
    return pltpu.make_async_remote_copy(
        src_ref=src,
        dst_ref=dst,
        send_sem=sems[0].at[index],
        recv_sem=sems[1].at[index if arrival is None else arrival],
        device_id=target,
        device_id_type=pl.DeviceIdType.MESH,
    )


def meet(barrier, targets):
    for target in targets:
        pl.semaphore_signal(barrier, inc=1, device_id=target, device_id_type=pl.DeviceIdType.MESH)
    pl.semaphore_wait(barrier, len(targets))


class Trade:
    def __init__(self, src, dst, sems, local):
        self.src, self.dst, self.sems, self.local = src, dst, sems, local
        self.z = lax.axis_index("context")
        self.groups = src.shape[0]

    def wire(self, other, arrival):
        return remote(self.src.at[other], self.dst.at[arrival], self.sems, other, {"context": other}, arrival)

    def keep(self, index):
        return pltpu.make_async_copy(self.src.at[index], self.dst.at[index], self.local)

    def send(self, dest):
        @pl.when(dest != self.z)
        def _():
            self.wire(dest, self.z).start()

        @pl.when(dest == self.z)
        def _():
            self.keep(dest).start()

    def await_from(self, other):
        @pl.when(other != self.z)
        def _():
            self.wire(other, other).wait_recv()

        @pl.when(other == self.z)
        def _():
            self.keep(other).wait()

    def collect(self):
        for other in range(self.groups):
            self.await_from(other)

    def release(self):
        for other in range(self.groups):

            @pl.when(other != self.z)
            def _(other=other):
                self.wire(other, self.z).wait_send()


def front_kernel(*refs, heads, groups):
    refs = list(refs)
    take = lambda n: [refs.pop(0) for _ in range(n)]
    x_ref, gains_in, cos_ref, sin_ref, tags_in, gates_in = take(6)
    w_qkv, w_out, w_ein, w_eout, w_sin, w_sout, cot = take(7)
    recv_out, mixed_out, lse_out, att_out, res_out = take(2), take(2), take(2), take(2), take(2)
    rows_out, cot_out, gates_out, both_out, tags_out = take(2), take(2), take(1)[0], take(1)[0], take(1)[0]
    qkv_out, wout_out, ein_out, eout_out, sin_out, sout_out, gains_out = take(7)
    wq, wo, gains, tags, pay, recv, ks, vs, scores, mixed, got, lse, att, res, nf = take(15)
    s_qkv, s_out, s_gain, s_exp, s_tag, s_gate, s_cot, s_pay, s_mix, s_row = [take(2) for _ in range(10)]
    local, self_pay, self_mix, self_tag, stores = take(5)
    e, z, d = lax.axis_index("expert"), lax.axis_index("context"), lax.axis_index("dp")
    core, y = e % 2, e // 2 % 2
    to_x, to_core, to_y = {"dp": 1 - d}, {"expert": e + 1 - 2 * core}, {"expert": e + 2 - 4 * y}
    others = [{"context": (z + k) % groups} for k in range(1, groups)]
    width = x_ref.shape[2]

    loads = [
        pltpu.make_async_copy(w_qkv, wq.at[d], local.at[0]),
        pltpu.make_async_copy(w_out, wo.at[d], local.at[1]),
        pltpu.make_async_copy(gains_in, gains.at[d], local.at[2]),
    ]
    for copy in loads:
        copy.start()
    meet(pltpu.get_barrier_semaphore(), [to_x, to_core, to_y, *others])

    x_qkv = remote(w_qkv.at[core], wq.at[d, core], s_qkv, 0, to_x)
    x_gain = remote(gains_in, gains.at[d], s_gain, 0, to_x)
    x_out = remote(w_out.at[core], wo.at[d, core], s_out, 0, to_x)
    half = z % 2
    to_mate = {"context": z + 1 - 2 * half}
    x_exp = [
        remote(w_ein.at[half], ein_out.at[0], s_exp, 0, to_x),
        remote(w_eout, eout_out, s_exp, 1, to_x),
        remote(w_sin.at[core], sin_out.at[0], s_exp, 2, to_x),
        remote(w_sout.at[core], sout_out.at[0], s_exp, 3, to_x),
    ]
    n_exp = [
        remote(ein_out.at[0], ein_out.at[1], s_exp, 4, to_mate),
        remote(sin_out.at[0], sin_out.at[1], s_exp, 5, to_core),
        remote(sout_out.at[0], sout_out.at[1], s_exp, 6, to_core),
    ]
    for copy in (x_qkv, x_gain, x_out, *x_exp):
        copy.start()
    tag_trade = [
        remote(tags_in, tags.at[z], s_tag, k, others[k]) for k in range(groups - 1)
    ]
    tag_own = pltpu.make_async_copy(tags_in, tags.at[z], self_tag.at[0])
    tag_own.start()
    for copy in tag_trade:
        copy.start()
    own_copies = [
        pltpu.make_async_copy(gates_in, gates_out.at[0], stores.at[0]),
        pltpu.make_async_copy(cot.at[0], cot_out[0].at[0], stores.at[1]),
        pltpu.make_async_copy(cot.at[1], cot_out[1].at[0], stores.at[2]),
    ]
    for copy in own_copies:
        copy.start()
    y_gate = remote(gates_in, gates_out.at[1], s_gate, 0, to_y)
    y_cot = [remote(cot.at[m], cot_out[m].at[1], s_cot, m, to_y) for m in range(MICRO)]
    c_gate = [
        remote(gates_in, gates_out.at[2], s_gate, 1, to_core),
        remote(gates_out.at[1], gates_out.at[3], s_gate, 2, to_core),
    ]
    c_cot = [remote(cot.at[m], cot_out[m].at[2], s_cot, 2 + m, to_core) for m in range(MICRO)] + [
        remote(cot_out[m].at[1], cot_out[m].at[3], s_cot, 4 + m, to_core) for m in range(MICRO)
    ]
    y_gate.start()
    for copy in y_cot:
        copy.start()

    c_qkv = remote(wq.at[1 - d, core], wq.at[1 - d, core], s_qkv, 1, to_core)
    c_out = remote(wo.at[1 - d, core], wo.at[1 - d, core], s_out, 1, to_core)
    for copy in loads:
        copy.wait()
    x_qkv.wait_recv()
    c_qkv.start()
    x_gain.wait_recv()
    c_qkv.wait_recv()
    both = [jnp.concatenate([gains[0, k : k + 1], gains[1, k : k + 1]], 1) for k in range(2)]
    w_full = wq.reshape(width, 3 * width)
    trades, returns = [], []
    for m in range(MICRO):
        span = slice(m * TILE, (m + 1) * TILE)
        project(x_ref[m].astype(F32), both[0], w_full, cos_ref[span, :], sin_ref[span, :], pay.at[m], groups)
        trade = Trade(pay.at[m], recv.at[m], [s.at[m] for s in s_pay], self_pay.at[m])
        for dest in range(groups):
            trade.send(dest)
        trades.append(trade)
    c_gate[0].start()
    for copy in c_cot[:MICRO]:
        copy.start()
    for k in range(groups - 1):
        remote(tags_in, tags.at[(z + groups - 1 - k) % groups], s_tag, k, others[k]).wait_recv()
    tag_own.wait()

    def attend(m, first, last):
        trade = Trade(mixed.at[m], got.at[m], [s.at[m] for s in s_mix], self_mix.at[m])

        def one(step, carry):
            attend_step(step, m, heads, groups, recv.at[m], tags, mixed.at[m], lse.at[m], ks, vs, scores)
            trade.send(step)
            return carry

        lax.fori_loop(first, last, one, 0)
        return trade

    def post(m, trade):
        trade.collect()
        for pair in range(width // HALF):
            att[m, :, pair * HALF : (pair + 1) * HALF] = natural(got.at[m], 0, pair, heads).astype(BF)
        residual = x_ref[m].astype(F32) + dot(att[m], wo.reshape(width, width)[...])
        res[m] = residual
        nf[m] = (residual * rms_scale(residual) * both[1]).astype(BF)
        remote(nf.at[m], rows_out[m].at[1], s_row, 3 * m, to_y).start()
        remote(nf.at[m], rows_out[m].at[2], s_row, 3 * m + 1, to_core).start()

    def forward_row(m):
        remote(nf.at[m], rows_out[m].at[1], s_row, 3 * m, to_y).wait_recv()
        remote(rows_out[m].at[1], rows_out[m].at[3], s_row, 3 * m + 2, to_core).start()

    trades[0].collect()
    fill_keys(recv.at[0], 0, ks, vs, heads)
    back0 = attend(0, 0, groups)
    x_exp[0].wait_recv()
    n_exp[0].start()
    x_out.wait_recv()
    c_out.start()
    y_gate.wait_recv()
    c_gate[1].start()
    for m in range(MICRO):
        y_cot[m].wait_recv()
        c_cot[MICRO + m].start()
    trades[1].collect()
    fill_keys(recv.at[1], 1, ks, vs, heads)
    back1 = attend(1, 0, 2)
    c_out.wait_recv()
    post(0, back0)
    back1 = attend(1, 2, groups)
    forward_row(0)
    post(1, back1)
    keep = []
    for m in range(MICRO):
        keep += [
            (recv.at[m], recv_out[m]),
            (mixed.at[m], mixed_out[m]),
            (lse.at[m], lse_out[m]),
            (att.at[m], att_out[m]),
            (res.at[m], res_out[m]),
            (nf.at[m], rows_out[m].at[0]),
            (nf.at[m], both_out.at[m]),
        ]
    keep += [(tags, tags_out), (wq, qkv_out), (wo, wout_out), (gains, gains_out)]
    keep = [pltpu.make_async_copy(a, b, stores.at[3 + i]) for i, (a, b) in enumerate(keep)]
    for copy in keep:
        copy.start()
    forward_row(1)
    for k in (2, 3):
        x_exp[k].wait_recv()
        n_exp[k - 1].start()
    for copy in (*keep, *own_copies):
        copy.wait()
    for m in range(MICRO):
        remote(nf.at[m], rows_out[m].at[2], s_row, 3 * m + 1, to_core).wait()
        remote(rows_out[m].at[1], rows_out[m].at[3], s_row, 3 * m + 2, to_core).wait()
        remote(nf.at[m], rows_out[m].at[1], s_row, 3 * m, to_y).wait_send()
        trades[m].release()
    back0.release()
    back1.release()
    x_exp[1].wait_recv()
    for copy in (*n_exp, *c_gate, *c_cot):
        copy.wait()
    for copy in (*x_exp, x_qkv, x_gain, x_out, c_qkv, c_out, y_gate, *y_cot, *tag_trade):
        copy.wait_send()


def run_front(x, gains, cosines, sines, tags, gates, w_qkv, w_out, w_ein, w_eout, w_sin, w_sout, cot, groups):
    _, rows, width = x.shape
    heads = width // HEAD // groups
    k = width // 4
    w_qkv = w_qkv.reshape(2, k, 3 * width)
    w_out = w_out.reshape(2, k, width)
    w_ein, w_sin, w_sout = [w.reshape(2, -1, w.shape[1]) for w in (w_ein, w_sin, w_sout)]
    vmem = pl.BlockSpec(memory_space=pltpu.VMEM)
    anywhere = pl.BlockSpec(memory_space=pl.ANY)
    packed = lambda n: (groups, n * heads, HALF, HALF)
    held = MICRO * groups * TILE
    twice = lambda *a: [struct(*a)] * 2
    outs = (
        twice(packed(3), BF)
        + twice(packed(1), BF)
        + twice((groups, 8, TILE), F32)
        + twice((rows, width), BF)
        + twice((rows, width), F32)
        + twice((4, rows, width), BF)
        + twice((4, rows, width), BF)
        + [
            struct((4, *gates.shape), F32),
            struct((MICRO, rows, width), BF),
            struct((groups, *tags.shape), jnp.int32),
            struct((2, 2, k, 3 * width), BF),
            struct((2, 2, k, width), BF),
            struct(w_ein.shape, BF),
            struct(w_eout.shape, BF),
            struct(w_sin.shape, BF),
            struct(w_sout.shape, BF),
            struct((2, *gains.shape), F32),
        ]
    )
    v = pltpu.VMEM
    dma = lambda *n: pltpu.SemaphoreType.DMA(n)
    scratch = [
        v((2, 2, k, 3 * width), BF),
        v((2, 2, k, width), BF),
        v((2, *gains.shape), F32),
        v((groups, *tags.shape), jnp.int32),
        v((MICRO, *packed(3)), BF),
        v((MICRO, *packed(3)), BF),
        v((heads, held, HALF), BF),
        v((heads, held, HALF), BF),
        v((heads, TILE, held), F32),
        v((MICRO, *packed(1)), BF),
        v((MICRO, *packed(1)), BF),
        v((MICRO, groups, 8, TILE), F32),
        v((MICRO, rows, width), BF),
        v((MICRO, rows, width), F32),
        v((MICRO, rows, width), BF),
    ]
    for shape in ((2,), (2,), (1,), (7,), (groups - 1,), (3,), (6,), (MICRO, groups), (MICRO, groups), (6,)):
        scratch += [dma(*shape), dma(*shape)]
    scratch += [dma(3), dma(MICRO), dma(MICRO), dma(1), dma(3 + 7 * MICRO + 4)]
    return pl.pallas_call(
        functools.partial(front_kernel, heads=heads, groups=groups),
        out_shape=tuple(outs),
        in_specs=[vmem] * 6 + [anywhere] * 7,
        out_specs=(anywhere,) * len(outs),
        scratch_shapes=scratch,
        compiler_params=pltpu.CompilerParams(
            vmem_limit_bytes=VMEM_LIMIT, collective_id=3, has_side_effects=True
        ),
        cost_estimate=price(130),
    )(x, gains, cosines, sines, tags, gates, w_qkv, w_out, w_ein, w_eout, w_sin, w_sout, cot)


def ffn_kernel(*refs, tr, spans, counts, first, gated, opened, summed, closing):
    offs = refs[0]
    refs = list(refs[1:])
    take = lambda n: [refs.pop(0) for _ in range(n)]
    x_ref, dy_in = take(2)
    gate_ref = take(1)[0] if gated else None
    parts = len(spans)
    wg_parts, wu_parts, wo_parts = take(parts), take(parts), take(len(counts))
    y0, dx0 = take(2) if opened else (None, None)
    g0 = take(3) if summed else None
    y_ref, dx_ref, dwg_ref, dwu_ref, dwo_ref = take(5)
    xt, yacc, dxacc, hs, djg, dju, wg_ref, wu_ref, wo_ref = take(9)
    dy_ref = take(1)[0] if gated else dy_in
    f = pl.program_id(0)
    rows = x_ref.shape[0]

    @pl.when(f == 0)
    def _():
        xt[...] = x_ref[...].T
        if opened:
            yacc[...] = y0[...].astype(F32)
            dxacc[...] = dx0[...].astype(F32)
        else:
            yacc[...] = jnp.zeros_like(yacc)
            dxacc[...] = jnp.zeros_like(dxacc)
        if gated:
            dy_ref[...] = (dy_in[...].astype(F32) * gate_ref[...]).astype(BF)

    for index, span in enumerate(spans):
        place = pl.ds(pl.multiple_of(offs[index], HALF // 2), span)
        wg_ref[place, :] = wg_parts[index][...]
        wu_ref[place, :] = wu_parts[index][...]
    for index, count in enumerate(counts):
        begin = offs[parts + index]

        @pl.when((f + first >= begin) & (f + first < begin + count))
        def _(index=index):
            wo_ref[...] = wo_parts[index][...]

    wg, wu, wo = wg_ref[...], wu_ref[...], wo_ref[...]

    def tile(i, carry):
        r = pl.ds(pl.multiple_of(i * tr, tr), tr)
        x = x_ref[r, :]
        g = dot(x, wg)
        u = dot(x, wu)
        dh = dot(dy_ref[r, :], wo, NT)
        sig = 1.0 / (1.0 + jnp.exp(-g))
        act = g * sig
        h = (act * u).astype(BF)
        dg = (dh * u * (sig * (1.0 + g * (1.0 - sig)))).astype(BF)
        du = (dh * act).astype(BF)
        hs[r, :] = h
        djg[r, :] = dg
        dju[r, :] = du
        yacc[r, :] += dot(h, wo)
        dxacc[r, :] += dot(dg, wg, NT) + dot(du, wu, NT)
        return carry

    lax.fori_loop(0, rows // tr, tile, 0)
    grads = [dot(xt[...], djg[...]), dot(xt[...], dju[...]), dot(hs[...], dy_ref[...], TN)]
    for k, out in enumerate((dwg_ref, dwu_ref, dwo_ref)):
        value = grads[k]
        if summed:
            value = value + g0[k][...].astype(F32)
        out[...] = value.astype(BF)

    @pl.when(f == pl.num_programs(0) - 1)
    def _():
        made = yacc[...].astype(BF)
        if gated and closing:
            made = (made.astype(F32) * gate_ref[...]).astype(BF)
        y_ref[...] = made
        dx_ref[...] = dxacc[...].astype(BF)


def run_ffn(x, dy, gate, w_in, w_out, offsets, start=None, grads=None, span=None, closing=True, tr=512, fb=FB, us=10):
    rows, d = x.shape
    ff = sum(w.shape[0] for w in w_out)
    nf = ff // fb
    first, last = span or (0, nf)
    steps = last - first
    gated = gate is not None
    parts = len(w_in)
    spans = [w.shape[0] for w in w_in]
    counts = [w.shape[0] // fb for w in w_out]
    whole = lambda a: pl.BlockSpec(
        a.shape, lambda f, o: (0,) * a.ndim, pipeline_mode=pl.Buffered(1)
    )
    args = [x, dy] + ([gate] if gated else [])
    specs = [whole(a) for a in args]
    args += list(w_in) * 2 + list(w_out)
    specs += [pl.BlockSpec((n, fb), lambda f, o: (0, f + first)) for n in spans]
    specs += [pl.BlockSpec((n, fb), lambda f, o: (0, f + first + nf)) for n in spans]
    for i, c in enumerate(counts):
        specs.append(
            pl.BlockSpec(
                (fb, d), lambda f, o, i=i, c=c: (jnp.clip(f + first - o[parts + i], 0, c - 1), 0)
            )
        )
    if start is not None:
        args += list(start)
        specs += [whole(a) for a in start]
    wide = pl.BlockSpec((d, fb), lambda f, o: (0, f))
    tall = pl.BlockSpec((fb, d), lambda f, o: (f, 0))
    if grads is not None:
        args += list(grads)
        specs += [
            pl.BlockSpec((d, fb), lambda f, o: (0, f + first)),
            pl.BlockSpec((d, fb), lambda f, o: (0, f + first)),
            pl.BlockSpec((fb, d), lambda f, o: (f + first, 0)),
        ]
    full = pl.BlockSpec((rows, d), lambda f, o: (0, 0), pipeline_mode=pl.Buffered(1))
    return pl.pallas_call(
        functools.partial(
            ffn_kernel,
            tr=math.gcd(tr, rows),
            spans=spans,
            counts=counts,
            first=first,
            gated=gated,
            opened=start is not None,
            summed=grads is not None,
            closing=closing,
        ),
        out_shape=(
            struct((rows, d), BF),
            struct((rows, d), BF),
            struct((d, steps * fb), BF),
            struct((d, steps * fb), BF),
            struct((steps * fb, d), BF),
        ),
        grid_spec=pltpu.PrefetchScalarGridSpec(
            num_scalar_prefetch=1,
            grid=(steps,),
            in_specs=specs,
            out_specs=(full, full, wide, wide, tall),
            scratch_shapes=[
                pltpu.VMEM((d, rows), BF),
                pltpu.VMEM((rows, d), F32),
                pltpu.VMEM((rows, d), F32),
                pltpu.VMEM((rows, fb), BF),
                pltpu.VMEM((rows, fb), BF),
                pltpu.VMEM((rows, fb), BF),
                pltpu.VMEM((d, fb), BF),
                pltpu.VMEM((d, fb), BF),
                pltpu.VMEM((fb, d), BF),
            ]
            + ([pltpu.VMEM((rows, d), BF)] if gated else []),
        ),
        compiler_params=pltpu.CompilerParams(vmem_limit_bytes=VMEM_LIMIT),
        cost_estimate=price(us),
    )(offsets, *args)


def price(us):
    return pl.CostEstimate(flops=int(us * 1.15e9), bytes_accessed=0, transcendentals=0)


def norm_back(values, scale, gain, grad):
    gain_grad = jnp.sum(grad * values * scale, 0, keepdims=True)
    scaled = gain * grad
    grad_in = scale * scaled - values * (scale * scale * scale) * jnp.mean(
        scaled * values, -1, keepdims=True
    )
    return grad_in, gain_grad


def mid_core(grad, residual, gain, cot, w_ref, pay, gres_ref, gbf_ref, per):
    back, gain_grad = norm_back(residual, rms_scale(residual), gain, grad)
    total = cot.astype(F32) + back
    gres_ref[...] = total
    gbf_ref[...] = total.astype(BF)
    mixed = dot(gbf_ref[...], w_ref[...], NT)
    for pair in range(mixed.shape[1] // HALF):
        tile = mixed[:, pair * HALF : (pair + 1) * HALF]
        for side, packed in enumerate(swap_heads(tile[:HALF], tile[HALF:])):
            head = 2 * pair + side
            pay[head // per, head % per] = packed.astype(BF)
    return gain_grad


def mid_kernel(dxs, dxr, res_ref, gain_ref, cot_ref, w_ref, gres_ref, pay, gg_ref, gbf, *, per):
    grad = dxs[...].astype(F32) + dxr[...].astype(F32)
    gg_ref[...] = mid_core(grad, res_ref[...], gain_ref[...], cot_ref[0], w_ref, pay, gres_ref, gbf, per)


def run_mid(dxs, dxr, residual, gain, cot, w, groups):
    rows, width = residual.shape
    per = width // HEAD // groups
    args = (dxs, dxr, residual, gain, cot, w)
    specs = [full_spec(a.shape) for a in args]
    specs[0] = pl.BlockSpec((rows, width), lambda _: (0, 0))
    specs[4] = pl.BlockSpec((1, rows, width), lambda _: (0, 0, 0))
    outs = [
        struct((rows, width), F32),
        struct((groups, per, HALF, HALF), BF),
        struct((1, width), F32),
        struct((rows, width), BF),
    ]
    return call(
        functools.partial(mid_kernel, per=per),
        tuple(outs),
        grid=(1,),
        in_specs=specs,
        out_specs=tuple(full_spec(o.shape) for o in outs),
        us=4,
    )(*args)


def finish(d0, d1, x_ref, gain_ref, w_ref, cos_ref, sin_ref, gres, atts, gbfs, gin_ref, gq, gv, go, gj, per):
    width = x_ref.shape[2]
    for micro, ref in enumerate((d0, d1)):
        rows = slice(micro * TILE, (micro + 1) * TILE)
        cosines, sines = cos_ref[rows, :], sin_ref[rows, :]
        for kind in range(3):
            for pair in range(width // HALF):
                tile = natural(ref, kind, pair, per)
                if kind == 0:
                    tile = tile * 0.125
                if kind < 2:
                    tile = rotate(tile, cosines, -sines)
                gj[rows, kind * width + pair * HALF : kind * width + (pair + 1) * HALF] = tile.astype(BF)
    tokens = x_ref[...].reshape(MICRO * TILE, width).astype(F32)
    scale = rms_scale(tokens)
    gain = gain_ref[...]
    turned = (tokens * scale * gain).astype(BF).T
    split = gq.shape[-1]
    gq[...] = dot(turned, gj[:, :split]).astype(BF).reshape(gq.shape)
    gv[...] = dot(turned, gj[:, split:]).astype(BF).reshape(gv.shape)
    go[...] = (dot(atts[0][...], gbfs[0][...], TN) + dot(atts[1][...], gbfs[1][...], TN)).astype(BF).reshape(go.shape)
    yield
    first = dot(gj[...], w_ref[...], NT)
    back, _ = norm_back(tokens, scale, gain, first)
    for micro in range(MICRO):
        rows = slice(micro * TILE, (micro + 1) * TILE)
        gin_ref[rows, :] = gres[micro][...] + back[rows]


def exchange(value, axis, mask):
    size = lax.axis_size(axis)
    return lax.ppermute(value, axis, [(i, i ^ mask) for i in range(size)])


def bits_of(size):
    return [1 << b for b in range(size.bit_length() - 1)]


def gather_rest(value):
    for mask in bits_of(lax.axis_size("expert"))[2:]:
        value = jnp.concatenate([value, exchange(value, "expert", mask)], 0)
    return value


def scatter_xor(value):
    masks = bits_of(lax.axis_size("expert"))
    for mask in (*reversed(masks[2:]), *masks[:2]):
        half = value.shape[0] // 2
        got = exchange(value[half:], "expert", mask)
        value = (value[:half].astype(F32) + got.astype(F32)).astype(value.dtype)
    return value


def ordered(flag, mine, theirs):
    first = jnp.where(flag == 0, mine, theirs)
    second = jnp.where(flag == 0, theirs, mine)
    return jnp.concatenate([first, second], 0)


def pick(value, parts, index):
    size = value.shape[0] // parts
    return lax.dynamic_slice_in_dim(value, index * size, size, 0)


def after(value, token):
    return lax.optimization_barrier((value, token))[0]


PIECES = 4
EARLY = 6
AHEAD = 2
PLAN = {
    2: ("rs1",),
    4: ("a0", "A0",),
    5: ("a1", "rs2",),
    6: ("A1",),
    7: ("B0",),
    10: ("a2",),
    11: ("A2", "b0", "A3", "B1",),
    15: ("C0",),
    16: ("B2",),
    17: ("C1",),
    19: ("A4",),
    20: ("c0", "B3",),
    21: ("b1", "C2",),
    23: ("B4",),
    24: ("D0",),
    25: ("C3",),
    27: ("b2", "d0", "A5",),
    28: ("C4",),
    31: ("B5",),
    33: ("c1",),
    36: ("d1", "e0", "c2",),
    37: ("A6",),
    38: ("C5", "d2",),
    42: ("e1", "e2", "zhome", "f0", "A7", "A8", "f1", "f2", "g2", "D3", "D1", "D5", "A9", "D4", "g1", "g0", "D2", "h0", "A10", "A11", "h1", "h2",),
}
LAST_PLAN = (
    "A0", "A1", "A2", "B0", "A3", "a0", "A4", "B1", "a1", "C0",
    "B2", "C1", "zrest", "b0", "B3", "C2", "b1", "c0", "a2", "B4",
    "C3", "c1", "b2", "D1", "d0", "C4", "c2", "d1", "e0", "d2",
    "e1", "A5", "D2", "D4", "D0", "f0", "f1", "B5", "f2", "e2",
    "g0", "g1", "D3", "h1", "h0", "C5", "g2", "D5", "h2",
)


class Engine:
    def __init__(self, own, com, own_buf, com_buf, own_out, com_out, sems):
        self.own, self.com, self.own_buf, self.com_buf = own, com, own_buf, com_buf
        self.own_out, self.com_out = own_out, com_out
        e, z, d = lax.axis_index("expert"), lax.axis_index("context"), lax.axis_index("dp")
        groups = lax.axis_size("context")
        self.d, self.core, self.y = d, e % 2, e // 2 % 2
        self.outer = (z == 0) | (z == 3)
        self.inner = (z == 1) | (z == 2)
        self.to_x = {"dp": 1 - d}
        self.to_core = {"expert": e + 1 - 2 * self.core}
        self.to_y = {"expert": e + 2 - 4 * self.y}
        self.to_mate = {"context": z + 1 - 2 * (z % 2)}
        self.to_mid = {"context": 3 - z}
        self.others = [{"context": (z + k) % groups} for k in range(1, groups)]
        sems = list(sems)
        take = lambda n: [sems.pop(0) for _ in range(n)]
        self.o_load, self.o_store = take(2)
        self.o = {k: take(2) for k in "x123"}
        self.c_load, self.c_store = take(2)
        self.c = {k: take(2) for k in ("core", "y", "x", "1", "2", "3", "fore", "last")}

    @staticmethod
    def scratch(own_shapes, kinds, com_shapes):
        v, dma = pltpu.VMEM, lambda n: pltpu.SemaphoreType.DMA((max(n, 1),))
        tiny = (16, HALF)
        own_buf = []
        for s, kind in zip(own_shapes, kinds):
            own_buf += [v(s, BF), v(s if "x" in kind else tiny, BF)]
            own_buf += [v(s if "z" in kind else tiny, BF)] * 2
        com_buf = []
        for s in com_shapes:
            com_buf += [v((2, 2, *s), BF)] * 2 + [v((2, *s), BF)] + [v(s, BF)] * 3
        chunks, n = len(own_shapes), len(com_shapes)
        sems = [dma(chunks)] * 10 + [dma(2 * n), dma(n)] + [dma(2 * n)] * 4 + [dma(n)] * 12
        return own_buf, com_buf, sems

    def greet(self):
        meet(
            pltpu.get_barrier_semaphore(), [self.to_x, self.to_core, self.to_y, *self.others]
        )

    def o_wire(self, stage, c):
        total, r_x, r_1, r_2 = self.own_buf[c]
        src, k, _ = self.own[c]
        target = {"x": self.to_x, "1": self.to_mate, "2": self.to_mid, "3": self.to_mate}[stage]
        source = {"x": lambda: src.at[1 - self.d, k], "1": lambda: total, "2": lambda: total, "3": lambda: r_1}
        place = {"x": r_x, "1": r_1, "2": r_2, "3": self.own_out[c]}[stage]
        return remote(source[stage](), place, self.o[stage], c, target)

    def o_loading(self, c):
        src, k, kind = self.own[c]
        src = src.at[k] if kind == "z" else src.at[self.d, k]
        return pltpu.make_async_copy(src, self.own_buf[c][0], self.o_load.at[c])

    def o_storing(self, c):
        buf = self.own_buf[c][0 if self.own[c][2] == "x" else 2]
        return pltpu.make_async_copy(buf, self.own_out[c], self.o_store.at[c])

    def A(self, c):
        total, r_x = self.own_buf[c][:2]
        kind = self.own[c][2]
        self.o_loading(c).wait()
        if kind != "z":
            self.o_wire("x", c).wait_recv()
            if c + self.ahead < len(self.own):
                self.o_wire("x", c + self.ahead).start()
            total[...] = total[...] + r_x[...]
        if kind == "x":
            self.o_storing(c).start()
            return

        @pl.when(self.outer)
        def _():
            self.o_wire("1", c).start()

    def B(self, c):
        total, _, r_1, _ = self.own_buf[c]

        @pl.when(self.inner)
        def _():
            self.o_wire("1", c).wait_recv()
            total[...] = total[...] + r_1[...]
            self.o_wire("2", c).start()

    def C(self, c):
        total, _, r_1, r_2 = self.own_buf[c]

        @pl.when(self.inner)
        def _():
            self.o_wire("2", c).wait_recv()
            r_1[...] = total[...] + r_2[...]
            self.o_wire("3", c).start()
            self.o_storing(c).start()

    def D(self, c):
        @pl.when(self.outer)
        def _():
            self.o_wire("3", c).wait_recv()

    def c_loading(self, i, h):
        return pltpu.make_async_copy(
            self.com[i].at[h, self.core], self.com_buf[i][0].at[h], self.c_load.at[2 * i + h]
        )

    def c_storing(self, i):
        return pltpu.make_async_copy(
            self.com_buf[i][4], self.com_out[i].at[self.core, self.y], self.c_store.at[i]
        )

    def c_wire(self, stage, i, h=0):
        total, r_core, r_y, r_x, r_1, r_2 = self.com_buf[i]
        core, y, d = self.core, self.y, self.d
        out = self.com_out[i]
        if stage == "core":
            return remote(self.com[i].at[h, 1 - core], r_core.at[h], self.c["core"], 2 * i + h, self.to_core)
        if stage == "y":
            return remote(total.at[h, 1 - y], r_y.at[h], self.c["y"], 2 * i + h, self.to_y)
        if stage == "x":
            return remote(total.at[1 - d, y], r_x, self.c["x"], i, self.to_x)
        if stage == "1":
            return remote(total.at[d, y], r_1, self.c["1"], i, self.to_mate)
        if stage == "2":
            return remote(total.at[d, y], r_2, self.c["2"], i, self.to_mid)
        if stage == "3":
            return remote(r_1, out.at[core, y], self.c["3"], i, self.to_mate)
        if stage == "fore":
            return remote(r_1, out.at[core, y], self.c["fore"], i, self.to_y)
        if stage == "back":
            return remote(out.at[core, y], out.at[core, y], self.c["fore"], i, self.to_y)
        return remote(out.at[core], out.at[core], self.c["last"], i, self.to_core)

    def c_start(self, i):
        for h in range(2):
            self.c_wire("core", i, h).start()
            self.c_loading(i, h).start()

    def a(self, i):
        total, r_core = self.com_buf[i][:2]
        for h in range(2):
            self.c_loading(i, h).wait()
            self.c_wire("core", i, h).wait_recv()
        total[...] = total[...] + r_core[...]
        for h in range(2):
            self.c_wire("y", i, h).start()

    def b(self, i):
        total, r_y, y = self.com_buf[i][0], self.com_buf[i][2], self.y
        for h in range(2):
            self.c_wire("y", i, h).wait_recv()
            total[h, y] = total[h, y] + r_y[h]
        self.c_wire("x", i).start()

    def c_(self, i):
        total, r_x, y, d = self.com_buf[i][0], self.com_buf[i][3], self.y, self.d
        self.c_wire("x", i).wait_recv()
        total[d, y] = total[d, y] + r_x[...]

        @pl.when(self.outer)
        def _():
            self.c_wire("1", i).start()

    def d_(self, i):
        total, r_1, y, d = self.com_buf[i][0], self.com_buf[i][4], self.y, self.d

        @pl.when(self.inner)
        def _():
            self.c_wire("1", i).wait_recv()
            total[d, y] = total[d, y] + r_1[...]
            self.c_wire("2", i).start()

    def e(self, i):
        total, r_1, r_2 = self.com_buf[i][0], self.com_buf[i][4], self.com_buf[i][5]

        @pl.when(self.inner)
        def _():
            self.c_wire("2", i).wait_recv()
            r_1[...] = total[self.d, self.y] + r_2[...]
            self.c_wire("3", i).start()
            self.c_wire("fore", i).start()
            self.c_storing(i).start()

    def f(self, i):
        @pl.when(self.outer)
        def _():
            self.c_wire("3", i).wait_recv()
            self.c_wire("back", i).start()

    def g(self, i):
        @pl.when(self.inner)
        def _():
            self.c_storing(i).wait()

        self.c_wire("fore", i).wait_recv()
        self.c_wire("last", i).start()

    def h(self, i):
        self.c_wire("last", i).wait_recv()

    def start(self, ahead, com=True):
        self.ahead = ahead
        for c in range(min(ahead, len(self.own))):
            if self.own[c][2] != "z":
                self.o_wire("x", c).start()
        if com:
            for i in range(len(self.com)):
                self.c_start(i)
        for c in range(len(self.own)):
            self.o_loading(c).start()

    def run(self, name):
        kind, index = name[0], int(name[1:])
        {"c": self.c_, "d": self.d_}.get(kind, getattr(self, kind, None))(index)

    def close(self):
        chunks, common = range(len(self.own)), range(len(self.com))
        for c in chunks:
            if self.own[c][2] != "z":
                self.o_wire("x", c).wait_send()
            if self.own[c][2] == "x":
                self.o_storing(c).wait()
        chunks = [c for c in chunks if self.own[c][2] != "x"]
        for i in common:
            for h in range(2):
                self.c_wire("core", i, h).wait_send()
                self.c_wire("y", i, h).wait_send()
            self.c_wire("x", i).wait_send()
            self.c_wire("last", i).wait_send()

        @pl.when(self.outer)
        def _():
            for c in chunks:
                self.o_wire("1", c).wait_send()
            for i in common:
                self.c_wire("1", i).wait_send()
                self.c_wire("back", i).wait_send()

        @pl.when(self.inner)
        def _():
            for c in chunks:
                self.o_wire("2", c).wait_send()
                self.o_wire("3", c).wait_send()
                self.o_storing(c).wait()
            for i in common:
                self.c_wire("2", i).wait_send()
                self.c_wire("3", i).wait_send()
                self.c_wire("fore", i).wait_send()


class Arrays:
    def __init__(self, refs):
        self.refs = list(refs)

    def take(self, n):
        got, self.refs = self.refs[:n], self.refs[n:]
        return got

    def engine(self, own_at, sources, own_out, com, com_out):
        own_buf = [self.take(4) for _ in own_at]
        com_buf = [self.take(6) for _ in com]
        own = [(sources[j], k, kind) for j, k, kind in own_at]
        places = [own_out[j].at[k] for j, k, _ in own_at]
        return Engine(own, com, own_buf, com_buf, places, com_out, self.take(10 + 18))


def back_kernel(*refs, own_at, sources, common, heads, groups):
    refs = Arrays(refs)
    own_in, com_in = refs.take(sources), refs.take(common)
    recv0, recv1, grad0, out0, out1, lse0, lse1, key_tag, query_tag = refs.take(9)
    dxs, res_ref, gain_ref, cot_ref, w_ref, dx_made = refs.take(6)
    own_out, com_out = refs.take(sources), refs.take(common)
    d0_out, d1_out, gres_out, gbf_out, gg_out = refs.take(5)
    engine = refs.engine(own_at, own_in, own_out, com_in, com_out)
    dx, r_core, r_y, gres, gbf, gg, pay_o, grad1, pay0, pay1 = refs.take(10)
    ks, vs, dk, dv, qs, gs, deltas, acc = refs.take(8)
    s_dx, s_o, s_0, s_1 = [refs.take(2) for _ in range(4)]
    local, = refs.take(1)

    engine.greet()
    send_core = remote(dx_made.at[2:4], r_core, s_dx, 0, engine.to_core)
    send_core.start()
    own_dx = pltpu.make_async_copy(dx_made.at[0:2], dx, local.at[0])
    own_dx.start()
    engine.start(AHEAD)
    send_y = remote(dx.at[1], r_y, s_dx, 1, engine.to_y)
    trade_o = Trade(pay_o, grad1, s_o, local.at[1])
    homes = [Trade(pay0, d0_out, s_0, local.at[2]), Trade(pay1, d1_out, s_1, local.at[3])]
    results = [
        pltpu.make_async_copy(a, b, local.at[4 + i])
        for i, (a, b) in enumerate(((gres, gres_out), (gbf, gbf_out), (gg, gg_out)))
    ]

    def rs1():
        own_dx.wait()
        send_core.wait_recv()
        dx[...] = dx[...] + r_core[...]
        send_y.start()

    def rs2():
        send_y.wait_recv()
        grad = dxs[TILE:, :].astype(F32) + dx[0].astype(F32) + r_y[...].astype(F32)
        gg[...] = mid_core(grad, res_ref[...], gain_ref[...], cot_ref[1], w_ref, pay_o, gres, gbf, heads)
        for dest in range(groups):
            trade_o.send(dest)
        for copy in results:
            copy.start()

    def zhome():
        for base, pay, trade in ((groups, pay1, homes[1]), (0, pay0, homes[0])):
            for dest in range(groups):
                back_pack(dk, dv, pay, dest, base, heads)
                trade.send(dest)

    named = {"rs1": rs1, "rs2": rs2, "zhome": zhome, "zend": lambda: None}

    def events(slot):
        for name in PLAN.get(slot, ()):
            named[name]() if name in named else engine.run(name)

    for recv, micro in ((recv0, 0), (recv1, 1)):
        fill_keys(recv, micro, ks, vs, heads)
    dk[...] = jnp.zeros_like(dk)
    dv[...] = jnp.zeros_like(dv)
    first_of = (0, sum(min(s + 2, groups) for s in range(groups)))
    total = 2 * first_of[1] + groups * groups
    for micro, (recv, grad, out, lse, pay) in enumerate(
        ((recv0, grad0, out0, lse0, pay0), (recv1, grad1, out1, lse1, pay1))
    ):
        begin, end = first_of[micro], (first_of + (total,))[micro + 1]
        if micro:
            trade_o.collect()

        def step(s, carry, micro=micro, recv=recv, grad=grad, out=out, lse=lse, pay=pay, begin=begin, end=end):
            back_begin(micro, s, heads, recv, grad, out, qs, gs, deltas, acc)
            before = begin + s * (s + 3) // 2 + groups * micro * s

            def tile(j, carry):
                for slot in range(begin, end):
                    if slot in PLAN:

                        @pl.when(before + j == slot)
                        def _(slot=slot):
                            events(slot)

                back_tile(
                    micro, s, j, heads, groups, lse, key_tag, query_tag, ks, vs, dk, dv, qs, gs, deltas, acc
                )
                return carry

            lax.fori_loop(0, groups * micro + jnp.minimum(s + 2, groups), tile, 0)
            for h in range(heads):
                pay[s, h] = pack_rows(acc[h]).astype(BF)
            return carry

        lax.fori_loop(0, groups, step, 0)
    events(total)
    for trade in homes:
        trade.collect()
        trade.release()
    trade_o.release()
    send_core.wait_send()
    send_y.wait_send()
    for copy in results:
        copy.wait()
    engine.close()


def chunk_views(grads):
    return [g.reshape(2, PIECES, g.shape[0] // (2 * PIECES), g.shape[1]) for g in grads]


def shared_shape(shape):
    return (2, 2, 2, shape[0] // 8, shape[1])


def device_call(kernel, args, vmem_args, outs, scratch, collective_id, us, aliases=None):
    anywhere = pl.BlockSpec(memory_space=pl.ANY)
    return pl.pallas_call(
        kernel,
        out_shape=tuple(outs),
        in_specs=[pl.BlockSpec(memory_space=pltpu.VMEM) if v else anywhere for v in vmem_args],
        out_specs=(anywhere,) * len(outs),
        scratch_shapes=scratch,
        input_output_aliases=aliases or {},
        compiler_params=pltpu.CompilerParams(
            vmem_limit_bytes=VMEM_LIMIT, collective_id=collective_id, has_side_effects=True
        ),
        cost_estimate=price(us),
    )(*args)


def rest_sum(value):
    for mask in bits_of(lax.axis_size("expert"))[2:]:
        value = value + exchange(value, "expert", mask)
    return value


def run_back(expert_grads, own_at, shared_grads, attention, middle, dx_made, groups):
    own = chunk_views(expert_grads)
    com = [g.reshape(shared_shape(g.shape)) for g in shared_grads]
    heads = attention[0].shape[1] // 3
    rows, width = middle[1].shape
    args = [*own, *com, *attention, *middle, dx_made]
    own_shapes = [own[j].shape[2:] for j, _, _ in own_at]
    com_shapes = [g.shape[3:] for g in com]
    own_buf, com_buf, sems = Engine.scratch(own_shapes, [kind for *_, kind in own_at], com_shapes)
    held = MICRO * groups * TILE
    v, dma = pltpu.VMEM, lambda n: pltpu.SemaphoreType.DMA((n,))
    pay = lambda n: (groups, n * heads, HALF, HALF)
    outs = (
        [struct(g.shape[1:], BF) for g in own]
        + [struct((2, 2, *s), BF) for s in com_shapes]
        + [struct(pay(3), BF)] * 2
        + [struct((rows, width), F32), struct((rows, width), BF), struct((1, width), F32)]
    )
    scratch = [
        *own_buf,
        *com_buf,
        *sems,
        v((2, rows, width), BF),
        v((2, rows, width), BF),
        v((rows, width), BF),
        v((rows, width), F32),
        v((rows, width), BF),
        v((1, width), F32),
        v(pay(1), BF),
        v(pay(1), BF),
        v(pay(3), BF),
        v(pay(3), BF),
        v((heads, held, HALF), BF),
        v((heads, held, HALF), BF),
        v((heads, held, HALF), F32),
        v((heads, held, HALF), F32),
        v((heads, TILE, HALF), BF),
        v((heads, TILE, HALF), BF),
        v((heads, 8, TILE), F32),
        v((heads, TILE, HALF), F32),
        dma(2),
        dma(2),
        *[dma(groups)] * 6,
        dma(7),
    ]
    flags = [False] * (len(own) + len(com)) + [True] * (len(attention) + len(middle)) + [False]
    kernel = functools.partial(
        back_kernel, own_at=own_at, sources=len(own), common=len(com), heads=heads, groups=groups
    )
    got = device_call(kernel, args, flags, outs, scratch, 1, 165)
    n, m = len(own), len(com)
    return got[:n], [rest_sum(g.reshape(-1, g.shape[-1]).astype(F32)) for g in got[n : n + m]], got[n + m :]


def last_kernel(*refs, own_at, sources, per):
    refs = Arrays(refs)
    own_in = refs.take(sources)
    d0, d1, x_ref, gain_ref, w_ref, cos_ref, sin_ref = refs.take(7)
    gres, atts, gbfs, ggs = refs.take(2), refs.take(2), refs.take(2), refs.take(2)
    own_out, com_out = refs.take(sources), refs.take(3)
    gin_out, gg_out = refs.take(2)
    sources = [refs.refs.pop(len(own_at) * 4 + 3 * 6 + 28) for _ in range(3)]
    engine = refs.engine(own_at, own_in, own_out, sources, com_out)
    gj, gin, gg_sum, gg_got, g_send, g_recv, local = refs.take(7)
    engine.greet()
    engine.start(0, com=False)
    z = lax.axis_index("context")
    rounds = (engine.to_core, engine.to_y, engine.to_x, engine.to_mate, {"context": z + 2 - 4 * (z // 2)})
    wires = [
        remote(gg_sum.at[k], gg_got.at[k], (g_send, g_recv), k, target) for k, target in enumerate(rounds)
    ]
    gg_sum[0] = jnp.broadcast_to(ggs[0][...] + ggs[1][...], gg_sum.shape[1:])
    wires[0].start()
    work = finish(
        d0, d1, x_ref, gain_ref, w_ref, cos_ref, sin_ref, gres, atts, gbfs, gin, *sources, gj, per
    )
    store = pltpu.make_async_copy(gin, gin_out, local.at[0])
    next(work)
    for i in range(3):
        engine.c_start(i)
    turn = 0
    for index, name in enumerate(LAST_PLAN):
        if name == "zrest":
            for _ in work:
                pass
            store.start()
        else:
            engine.run(name)
        if index % 5 == 4 and turn < len(wires):
            wires[turn].wait_recv()
            gg_sum[turn + 1] = gg_sum[turn] + gg_got[turn]
            turn += 1
            if turn < len(wires):
                wires[turn].start()
    total = pltpu.make_async_copy(gg_sum.at[len(wires)], gg_out, local.at[1])
    total.start()
    store.wait()
    total.wait()
    for wire in wires:
        wire.wait_send()
    engine.close()


def run_last(sums, own_at, parts, groups):
    x, w = parts[2], parts[4]
    _, rows, width = x.shape
    args = [*sums, *parts]
    own_shapes = [sums[j].shape[1:] for j, _, _ in own_at]
    com = [shared_shape((width, 3 * width // 2))] * 2 + [shared_shape((width, width))]
    own_buf, com_buf, sems = Engine.scratch(own_shapes, [k for *_, k in own_at], [s[3:] for s in com])
    v = pltpu.VMEM
    outs = (
        [struct(g.shape, BF) for g in sums]
        + [struct((2, 2, *s[3:]), BF) for s in com]
        + [struct((MICRO * rows, width), F32), struct((8, width), F32)]
    )
    rounds = 5
    scratch = [
        *own_buf,
        *com_buf,
        *sems,
        *[v(s, BF) for s in com],
        v((MICRO * rows, 3 * width), BF),
        v((MICRO * rows, width), F32),
        v((rounds + 1, 8, width), F32),
        v((rounds, 8, width), F32),
        *[pltpu.SemaphoreType.DMA((rounds,))] * 2,
        pltpu.SemaphoreType.DMA((2,)),
    ]
    flags = [False] * len(sums) + [True] * len(parts)
    kernel = functools.partial(
        last_kernel, own_at=own_at, sources=len(sums), per=width // HEAD // groups
    )
    got = device_call(
        kernel, args, flags, outs, scratch, 2, 90, {i: i for i in range(len(sums))}
    )
    n = len(sums)
    return got[:n], [rest_sum(g.reshape(-1, g.shape[-1]).astype(F32)) for g in got[n : n + 3]], got[n + 3], got[n + 4]


def body(
    inputs,
    keep_flags,
    block_ids,
    expert_ids,
    gate_weights,
    norm_attn,
    w_qkv,
    w_attn_out,
    norm_ffn,
    w_shared_in,
    w_shared_out,
    w_expert_in,
    w_expert_out,
    cotangent,
):
    width = w_qkv.shape[1] // 3
    rows = inputs.shape[2]
    groups = lax.axis_size("context")
    experts = lax.axis_size("expert")
    z = lax.axis_index("context")
    seq_rows = rows * groups
    x = inputs[0]
    cot = cotangent[0].reshape(MICRO * rows, width)

    positions = (
        jnp.arange(MICRO, dtype=jnp.int32)[:, None] * seq_rows
        + z * rows
        + jnp.arange(rows, dtype=jnp.int32)[None, :]
    ).reshape(-1)
    half = HEAD // 2
    freq = jnp.exp(-math.log(ROPE_BASE) * jnp.arange(half, dtype=F32) * 2.0 / HEAD)
    angle = positions.astype(F32)[:, None] * freq[None, :]
    cos_t, sin_t = jnp.cos(angle), jnp.sin(angle)
    cosines = jnp.concatenate([cos_t] * 4, -1)
    sines = jnp.concatenate([-sin_t, sin_t, -sin_t, sin_t], -1)

    blocks = block_ids[0] + 8 * jnp.arange(MICRO, dtype=jnp.int32)[:, None]
    key_tags = jnp.where(keep_flags[0] == 1, blocks, HIDDEN)
    tags = jnp.stack([blocks, key_tags])[:, :, None]

    per_expert = jnp.sum(
        jnp.where(
            expert_ids[0][None] == jnp.arange(experts, dtype=jnp.int32)[:, None, None, None],
            gate_weights[0][None],
            0.0,
        ),
        -1,
    )
    gains = jnp.stack([norm_attn, norm_ffn]).astype(F32)
    (
        *pairs,
        gates_four,
        nf_both,
        all_tags,
        mat_qkv,
        mat_out,
        ein_parts,
        eout_other,
        sin_parts,
        sout_parts,
        gains,
    ) = run_front(
        x,
        gains,
        cosines,
        sines,
        tags,
        per_expert,
        w_qkv,
        w_attn_out,
        w_expert_in[0],
        w_expert_out[0],
        w_shared_in,
        w_shared_out,
        cotangent[0],
        groups,
    )
    recvs, mixed, lses, att, res, rows_four, cot_four = [pairs[2 * i : 2 * i + 2] for i in range(7)]
    mat_qkv = mat_qkv.reshape(width, -1)
    mat_out = mat_out.reshape(width, width)
    gain_attn = gains[:, 0].reshape(1, width)
    gain_ffn = gains[:, 1].reshape(1, width)
    all_tags = all_tags[:, :, :, 0].transpose(1, 2, 0, 3)
    query_row = all_tags[0].reshape(MICRO * groups, 1, rows)
    key_col = all_tags[1].reshape(-1, 1)
    own_gates = lax.dynamic_index_in_dim(
        gather_rest(gates_four), lax.axis_index("expert"), 1, False
    )
    gate = [own_gates[:, m].reshape(-1, 1) for m in range(MICRO)]

    core = lax.axis_index("expert") % 2
    dp = lax.axis_index("dp")
    k_half, f_half = width // 2, w_shared_out.shape[0]
    ein_parts = (w_expert_in[0], ein_parts[0], ein_parts[1])
    eout_parts = (w_expert_out[0], eout_other)
    sin_parts = (w_shared_in, sin_parts[0], sin_parts[1])
    sout_parts = (w_shared_out, sout_parts[0], sout_parts[1])
    places = lambda bit: [2 * (1 - dp) + bit, 2 * (1 - dp) + 1 - bit]
    row_offs = lambda bit: [dp * k_half] + [p * (k_half // 2) for p in places(bit)]
    chunk = f_half // FB
    expert_offs = jnp.stack(row_offs(z % 2) + [dp * chunk, (1 - dp) * chunk])
    shared_offs = jnp.stack(
        row_offs(core) + [dp * chunk] + [p * (chunk // 2) for p in places(core)]
    )

    capacity = 4 * rows // experts

    def expert_pass(m, grads, token=None):
        hidden = gather_rest(rows_four[m]).reshape(-1, width)
        if token is not None:
            hidden = after(hidden, token)
        grad, weight = gather_rest(cot_four[m]).reshape(-1, width), gate[m]
        if capacity < rows:
            chosen = weight.reshape(-1, rows) > 0
            slots = jnp.cumsum(chosen.astype(jnp.int32), 1) - 1
            select = (
                chosen[:, None] & (slots[:, None] == jnp.arange(capacity, dtype=jnp.int32)[:, None])
            ).astype(BF)
            squeeze = lambda v: jnp.einsum("bcr,brd->bcd", select, v.reshape(-1, rows, width)).reshape(-1, width)
            spread = lambda v: jnp.einsum("bcr,bcd->brd", select, v.reshape(-1, capacity, width)).reshape(-1, width)
            hidden, grad = squeeze(hidden), squeeze(grad)
            weight = jnp.sum(select.astype(F32) * weight.reshape(-1, 1, rows), -1).reshape(-1, 1)
        made, dx, *grads = run_ffn(
            hidden, grad, weight, ein_parts, eout_parts, expert_offs, grads=grads, us=41
        )
        if capacity < rows:
            made, dx = spread(made), spread(dx)
        return made, dx, *grads

    made0, dx0, *g_expert = expert_pass(0, None)
    dx0, routed0 = scatter_xor(dx0), scatter_xor(made0)
    shared, dx_shared, *g_shared = run_ffn(
        nf_both.reshape(-1, width), cot, None, sin_parts, sout_parts, shared_offs, us=23
    )
    gres0, pay0, gg0, gbf0 = run_mid(dx_shared, dx0, res[0], gain_ffn, cotangent[0], mat_out, groups)
    grad0 = lax.all_to_all(pay0, "context", 0, 0, tiled=True)
    made1, dx1, *g_expert = expert_pass(1, g_expert, (pay0, routed0))
    masks = bits_of(experts)
    for mask in reversed(masks[2:]):
        half = dx1.shape[0] // 2
        dx1 = (dx1[:half].astype(F32) + exchange(dx1[half:], "expert", mask).astype(F32)).astype(BF)

    spread = [(j, k) for j in range(3) for k in range(PIECES)]
    early = [(j, k, "xz" if i < EARLY else "x") for i, (j, k) in enumerate(spread)]
    first = spread[EARLY][0]
    late = [(j - first, k, "z") for j, k in spread[EARLY:]]
    attention = (*recvs, grad0, *mixed, *lses, key_col, query_row)
    own_sums, (r_gate, r_up, r_sout), (d0, d1, gres1, gbf1, gg1) = run_back(
        g_expert,
        early,
        g_shared,
        attention,
        (dx_shared, res[1], gain_ffn, cotangent[0], mat_out),
        dx1.reshape(4, rows, width),
        groups,
    )
    routed1 = scatter_xor(made1)
    output = jnp.stack(
        [
            (res[m] + shared[m * rows : (m + 1) * rows].astype(F32) + r.astype(F32)).astype(BF)
            for m, r in enumerate((routed0, routed1))
        ]
    )
    own_late, (r_qk, r_v, r_out), grad_input, gain_sum = run_last(
        own_sums[first:],
        late,
        (d0, d1, x, gain_attn, mat_qkv, cosines, sines, gres0, gres1, *att, gbf0, gbf1, gg0, gg1),
        groups,
    )
    r_gain_ffn = pick(rest_sum(gain_sum)[0], 2, dp)
    r_qkv = jnp.concatenate([r_qk, r_v], 1)
    r_sin = jnp.concatenate([r_gate, r_up], 1)
    r_gain_attn = jnp.sum(w_qkv.astype(F32) * r_qkv, 1) / norm_attn.astype(F32)
    e_gate, e_up, r_eout = [
        g.reshape(-1, g.shape[-1]).astype(F32) for g in (*own_sums[:first], *own_late)
    ]
    r_ein = jnp.concatenate([e_gate, e_up], 1)
    return (
        output[None],
        grad_input.reshape(1, MICRO, rows, width),
        r_gain_attn,
        r_qkv,
        r_out,
        r_gain_ffn,
        r_sin,
        r_sout,
        r_ein[None],
        r_eout[None],
    )


def solution(mesh):
    tokens = P(("expert", "dp"), None, "context", None)
    flags = P(("expert", "dp"), None, "context")
    placed = (
        tokens,
        flags,
        flags,
        tokens,
        tokens,
        P("dp"),
        P("dp", None),
        P("dp", None),
        P("dp"),
        P("dp", None),
        P("dp", None),
        P("expert", "dp", None),
        P("expert", "dp", None),
        tokens,
    )
    return jax.shard_map(
        body,
        mesh=mesh,
        in_specs=placed,
        out_specs=(
            tokens,
            tokens,
            P("dp"),
            P("dp", None),
            P("dp", None),
            P("dp"),
            P("dp", None),
            P("dp", None),
            P("expert", "dp", None),
            P("expert", "dp", None),
        ),
        check_vma=False,
    )
```

```python
import functools
import math

import jax
import jax.numpy as jnp
from jax import lax
from jax.experimental import pallas as pl
from jax.experimental.pallas import tpu as pltpu
from jax.sharding import PartitionSpec as P

HEAD = 64
MICRO = 2
TILE = 256
HALF = 128
EPSILON = 1e-05
ROPE_BASE = 10000.0
MASKED = -3e30
HIDDEN = 1 << 20
BF = jnp.bfloat16
F32 = jnp.float32
NT = (((1,), (1,)), ((), ()))
TN = (((0,), (0,)), ((), ()))
VMEM_LIMIT = 60 << 20
FB = 512


def dot(left, right, dims=(((1,), (0,)), ((), ()))):
    return lax.dot_general(left, right, dims, preferred_element_type=F32)


def rms_scale(values):
    return lax.rsqrt(jnp.mean(values * values, -1, keepdims=True) + EPSILON)


def low_lanes(rows):
    return lax.broadcasted_iota(jnp.int32, (rows, HALF), 1) < HEAD


def swap_heads(first, second):
    low = low_lanes(HALF)
    return (
        jnp.where(low, first, pltpu.roll(second, HEAD, 1)),
        jnp.where(low, pltpu.roll(first, HEAD, 1), second),
    )


def rotate(tile, cosines, sines):
    lane = lax.broadcasted_iota(jnp.int32, tile.shape, 1)
    partner = jnp.where(
        lane % HEAD < HEAD // 2,
        pltpu.roll(tile, HALF - HEAD // 2, 1),
        pltpu.roll(tile, HEAD // 2, 1),
    )
    return tile * cosines + partner * sines


def struct(shape, dtype):
    return jax.ShapeDtypeStruct(tuple(shape), dtype)


def project(tokens, gain, w_ref, cosines, sines, pay, groups):
    normed = (tokens * rms_scale(tokens) * gain).astype(BF)
    width = tokens.shape[1]
    per = width // HEAD // groups
    for kind in range(3):
        joined = dot(normed, w_ref[:, kind * width : (kind + 1) * width])
        for pair in range(width // HALF):
            tile = joined[:, pair * HALF : (pair + 1) * HALF]
            if kind < 2:
                tile = rotate(tile, cosines, sines)
            if kind == 0:
                tile = tile * 0.125
            for side, packed in enumerate(swap_heads(tile[:HALF], tile[HALF:])):
                head = 2 * pair + side
                pay[head // per, kind * per + head % per] = packed.astype(BF)


def unpack(ref, index, kind_head):
    tile = ref[index, kind_head]
    return tile, pltpu.roll(tile.astype(F32), HEAD, 1).astype(BF)


def fill_keys(recv, micro, ks, vs, heads):
    groups = recv.shape[0]
    for src in range(groups):
        base = (micro * groups + src) * TILE
        for h in range(heads):
            for store, kind in ((ks, 1), (vs, 2)):
                first, second = unpack(recv, src, kind * heads + h)
                store[h, base : base + HALF] = first
                store[h, base + HALF : base + TILE] = second


def masked_rows(ref, index, kind_head):
    tile = ref[index, kind_head].astype(F32)
    both = jnp.concatenate([tile, pltpu.roll(tile, HEAD, 1)], 0)
    return jnp.where(low_lanes(TILE), both, 0.0)


def pack_rows(values):
    return jnp.where(low_lanes(HALF), values[:HALF], pltpu.roll(values[HALF:], HEAD, 1))


def attend_step(step, micro, heads, groups, recv, tags, out_ref, lse_ref, ks, vs, scores):
    count = groups * micro + jnp.minimum(step + 2, groups)
    queries = [masked_rows(recv, step, h).astype(BF) for h in range(heads)]
    tag = jnp.broadcast_to(tags[step, 0, micro], (8, TILE)).T[:, :1]
    same = lax.broadcasted_iota(jnp.int32, (TILE, TILE), 0) == lax.broadcasted_iota(
        jnp.int32, (TILE, TILE), 1
    )

    def first_pass(j, tops):
        keys = pl.ds(pl.multiple_of(j * TILE, TILE), TILE)
        key_tag = tags[j % groups, 1, j // groups]
        seen = (key_tag <= tag) | (same & (j == groups * micro + step))
        new = []
        for h in range(heads):
            part = jnp.where(seen, dot(queries[h], ks[h, keys, :], NT), MASKED)
            scores[h, :, keys] = part
            new.append(jnp.maximum(tops[h], jnp.maximum(part[:, :HALF], part[:, HALF:])))
        return tuple(new)

    tops = lax.fori_loop(
        0, count, first_pass, (jnp.full((TILE, HALF), MASKED, F32),) * heads
    )
    tops = [jnp.max(top, 1, keepdims=True) for top in tops]

    def second_pass(j, carry):
        keys = pl.ds(pl.multiple_of(j * TILE, TILE), TILE)
        sums, totals = carry
        new_sums, new_totals = [], []
        for h in range(heads):
            expo = jnp.exp(scores[h, :, keys] - tops[h])
            new_sums.append(sums[h] + (expo[:, :HALF] + expo[:, HALF:]))
            new_totals.append(totals[h] + dot(expo.astype(BF), vs[h, keys, :]))
        return tuple(new_sums), tuple(new_totals)

    zero = (jnp.zeros((TILE, HALF), F32),) * heads
    sums, totals = lax.fori_loop(0, count, second_pass, (zero, zero))
    lane = lax.broadcasted_iota(jnp.int32, (TILE, HALF), 1)
    logs = jnp.zeros((TILE, HALF), F32)
    for h in range(heads):
        total = jnp.sum(sums[h], 1, keepdims=True)
        out_ref[step, h] = pack_rows(totals[h] / total).astype(BF)
        logs = jnp.where(lane == h, tops[h] + jnp.log(total), logs)
    lse_ref[step] = logs.T[:8]


def back_begin(micro, step, heads, recv, grad, out, qs, gs, deltas, acc):
    ones = jnp.ones((8, HALF), F32)
    for h in range(heads):
        grad_f = masked_rows(grad, step, h)
        qs[h] = masked_rows(recv, step, h).astype(BF)
        gs[h] = grad_f.astype(BF)
        deltas[h] = lax.dot_general(
            ones,
            grad_f * masked_rows(out, step, h),
            NT,
            precision=lax.Precision.HIGHEST,
            preferred_element_type=F32,
        )
    acc[...] = jnp.zeros_like(acc)


def back_tile(micro, step, j, heads, groups, lse, key_tag, query_tag, ks, vs, dk, dv, qs, gs, deltas, acc):
    keys = pl.ds(pl.multiple_of(j * TILE, TILE), TILE)
    same = lax.broadcasted_iota(jnp.int32, (TILE, TILE), 0) == lax.broadcasted_iota(
        jnp.int32, (TILE, TILE), 1
    )
    tag = query_tag[groups * micro + step]
    seen = (key_tag[keys, :] <= tag) | (same & (j == groups * micro + step))
    for h in range(heads):
        key, value = ks[h, keys, :], vs[h, keys, :]
        scores = dot(key, qs[h], NT)
        probs = jnp.where(seen, jnp.exp(scores - lse[step, h : h + 1, :]), 0.0)
        dv[h, keys, :] += dot(probs.astype(BF), gs[h])
        slope = (probs * (dot(value, gs[h], NT) - deltas[h, :1])).astype(BF)
        dk[h, keys, :] += dot(slope, qs[h])
        acc[h] += dot(slope, key, TN)


def back_pack(dk, dv, pay, src, base, heads):
    rows = slice((base + src) * TILE, (base + src + 1) * TILE)
    for h in range(heads):
        pay[src, heads + h] = pack_rows(dk[h, rows]).astype(BF)
        pay[src, 2 * heads + h] = pack_rows(dv[h, rows]).astype(BF)


def natural(ref, first_kind, pair, per):
    tiles = []
    for head in (2 * pair, 2 * pair + 1):
        tiles.append(ref[head // per, first_kind * per + head % per].astype(F32))
    return jnp.concatenate(swap_heads(*tiles), 0)


def remote(src, dst, sems, index, target, arrival=None):
    return pltpu.make_async_remote_copy(
        src_ref=src,
        dst_ref=dst,
        send_sem=sems[0].at[index],
        recv_sem=sems[1].at[index if arrival is None else arrival],
        device_id=target,
        device_id_type=pl.DeviceIdType.MESH,
    )


def meet(barrier, targets):
    for target in targets:
        pl.semaphore_signal(barrier, inc=1, device_id=target, device_id_type=pl.DeviceIdType.MESH)
    pl.semaphore_wait(barrier, len(targets))


class Trade:
    def __init__(self, src, dst, sems, local):
        self.src, self.dst, self.sems, self.local = src, dst, sems, local
        self.z = lax.axis_index("context")
        self.groups = src.shape[0]

    def wire(self, other, arrival):
        return remote(self.src.at[other], self.dst.at[arrival], self.sems, other, {"context": other}, arrival)

    def keep(self, index):
        return pltpu.make_async_copy(self.src.at[index], self.dst.at[index], self.local)

    def send(self, dest):
        @pl.when(dest != self.z)
        def _():
            self.wire(dest, self.z).start()

        @pl.when(dest == self.z)
        def _():
            self.keep(dest).start()

    def await_from(self, other):
        @pl.when(other != self.z)
        def _():
            self.wire(other, other).wait_recv()

        @pl.when(other == self.z)
        def _():
            self.keep(other).wait()

    def collect(self):
        for other in range(self.groups):
            self.await_from(other)

    def release(self):
        for other in range(self.groups):

            @pl.when(other != self.z)
            def _(other=other):
                self.wire(other, self.z).wait_send()


def front_kernel(*refs, heads, groups):
    refs = list(refs)
    take = lambda n: [refs.pop(0) for _ in range(n)]
    x_ref, gains_in, tags_in, gates_in = take(4)
    w_qkv, w_out, w_ein, w_eout, w_sin, w_sout, cot = take(7)
    recv_out, mixed_out, lse_out, att_out, res_out = take(2), take(2), take(2), take(2), take(2)
    rows_out, cot_out, gates_out, both_out, tags_out = take(2), take(2), take(1)[0], take(1)[0], take(1)[0]
    qkv_out, wout_out, ein_out, eout_out, sin_out, sout_out, gains_out, table_out = take(8)
    wq, wo, gains, tags, pay, recv, ks, vs, scores, mixed, got, lse, att, res, nf, table = take(16)
    s_qkv, s_out, s_gain, s_exp, s_tag, s_gate, s_cot, s_pay, s_mix, s_row = [take(2) for _ in range(10)]
    local, self_pay, self_mix, self_tag, stores = take(5)
    e, z, d = lax.axis_index("expert"), lax.axis_index("context"), lax.axis_index("dp")
    core, y = e % 2, e // 2 % 2
    to_x, to_core, to_y = {"dp": 1 - d}, {"expert": e + 1 - 2 * core}, {"expert": e + 2 - 4 * y}
    others = [{"context": (z + k) % groups} for k in range(1, groups)]
    width = x_ref.shape[2]

    loads = [
        pltpu.make_async_copy(w_qkv, wq.at[d], local.at[0]),
        pltpu.make_async_copy(w_out, wo.at[d], local.at[1]),
        pltpu.make_async_copy(gains_in, gains.at[d], local.at[2]),
    ]
    for copy in loads:
        copy.start()
    meet(pltpu.get_barrier_semaphore(), [to_x, to_core, to_y, *others])

    x_qkv = remote(w_qkv.at[core], wq.at[d, core], s_qkv, 0, to_x)
    x_gain = remote(gains_in, gains.at[d], s_gain, 0, to_x)
    x_out = remote(w_out.at[core], wo.at[d, core], s_out, 0, to_x)
    half = z % 2
    to_mate = {"context": z + 1 - 2 * half}
    x_exp = [
        remote(w_ein.at[half], ein_out.at[half], s_exp, 0, to_x),
        remote(w_eout, eout_out, s_exp, 1, to_x),
        remote(w_sin.at[core, y], sin_out.at[core, y], s_exp, 2, to_x),
        remote(w_sout.at[core, y], sout_out.at[core, y], s_exp, 3, to_x),
    ]
    n_exp = [
        remote(ein_out.at[half], ein_out.at[half], s_exp, 4, to_mate),
        remote(sin_out.at[core, y], sin_out.at[core, y], s_exp, 5, to_y),
        remote(sout_out.at[core, y], sout_out.at[core, y], s_exp, 6, to_y),
        remote(sin_out.at[core], sin_out.at[core], s_exp, 7, to_core),
        remote(sout_out.at[core], sout_out.at[core], s_exp, 8, to_core),
    ]
    for copy in (x_qkv, x_gain, x_out, x_exp[0], x_exp[2], x_exp[3], x_exp[1]):
        copy.start()
    tag_trade = [
        remote(tags_in, tags.at[z], s_tag, k, others[k]) for k in range(groups - 1)
    ]
    tag_own = pltpu.make_async_copy(tags_in, tags.at[z], self_tag.at[0])
    tag_own.start()
    for copy in tag_trade:
        copy.start()
    own_copies = [
        pltpu.make_async_copy(gates_in, gates_out.at[0], stores.at[0]),
        pltpu.make_async_copy(cot.at[0], cot_out[0].at[0], stores.at[1]),
        pltpu.make_async_copy(cot.at[1], cot_out[1].at[0], stores.at[2]),
    ]
    for copy in own_copies:
        copy.start()
    y_gate = remote(gates_in, gates_out.at[1], s_gate, 0, to_y)
    y_cot = [remote(cot.at[m], cot_out[m].at[1], s_cot, m, to_y) for m in range(MICRO)]
    c_gate = [
        remote(gates_in, gates_out.at[2], s_gate, 1, to_core),
        remote(gates_out.at[1], gates_out.at[3], s_gate, 2, to_core),
    ]
    c_cot = [remote(cot.at[m], cot_out[m].at[2], s_cot, 2 + m, to_core) for m in range(MICRO)] + [
        remote(cot_out[m].at[1], cot_out[m].at[3], s_cot, 4 + m, to_core) for m in range(MICRO)
    ]
    y_gate.start()
    for copy in y_cot:
        copy.start()

    row = lax.broadcasted_iota(jnp.int32, (MICRO * TILE, HALF), 0)
    lane = lax.broadcasted_iota(jnp.int32, (MICRO * TILE, HALF), 1)
    place = row // TILE * (TILE * groups) + z * TILE + row % TILE
    freq = jnp.exp((-math.log(ROPE_BASE) * 2.0 / HEAD) * (lane % (HEAD // 2)).astype(F32))
    angle = place.astype(F32) * freq
    table[0] = jnp.cos(angle)
    table[1] = jnp.where(lane % HEAD < HEAD // 2, -jnp.sin(angle), jnp.sin(angle))

    c_qkv = remote(wq.at[1 - d, core], wq.at[1 - d, core], s_qkv, 1, to_core)
    c_out = remote(wo.at[1 - d, core], wo.at[1 - d, core], s_out, 1, to_core)
    for copy in loads:
        copy.wait()
    x_qkv.wait_recv()
    c_qkv.start()
    x_gain.wait_recv()
    c_qkv.wait_recv()
    both = [jnp.concatenate([gains[0, k : k + 1], gains[1, k : k + 1]], 1) for k in range(2)]
    w_full = wq.reshape(width, 3 * width)
    trades, returns = [], []
    for m in range(MICRO):
        span = slice(m * TILE, (m + 1) * TILE)
        project(x_ref[m].astype(F32), both[0], w_full, table[0, span, :], table[1, span, :], pay.at[m], groups)
        trade = Trade(pay.at[m], recv.at[m], [s.at[m] for s in s_pay], self_pay.at[m])
        for dest in range(groups):
            trade.send(dest)
        trades.append(trade)
    c_gate[0].start()
    for copy in c_cot[:MICRO]:
        copy.start()
    for k in range(groups - 1):
        remote(tags_in, tags.at[(z + groups - 1 - k) % groups], s_tag, k, others[k]).wait_recv()
    tag_own.wait()

    def attend(m, first, last):
        trade = Trade(mixed.at[m], got.at[m], [s.at[m] for s in s_mix], self_mix.at[m])

        def one(step, carry):
            attend_step(step, m, heads, groups, recv.at[m], tags, mixed.at[m], lse.at[m], ks, vs, scores)
            trade.send(step)
            return carry

        lax.fori_loop(first, last, one, 0)
        return trade

    def post(m, trade):
        trade.collect()
        for pair in range(width // HALF):
            att[m, :, pair * HALF : (pair + 1) * HALF] = natural(got.at[m], 0, pair, heads).astype(BF)
        residual = x_ref[m].astype(F32) + dot(att[m], wo.reshape(width, width)[...])
        res[m] = residual
        nf[m] = (residual * rms_scale(residual) * both[1]).astype(BF)
        remote(nf.at[m], rows_out[m].at[1], s_row, 3 * m, to_y).start()
        remote(nf.at[m], rows_out[m].at[2], s_row, 3 * m + 1, to_core).start()

    def forward_row(m):
        remote(nf.at[m], rows_out[m].at[1], s_row, 3 * m, to_y).wait_recv()
        remote(rows_out[m].at[1], rows_out[m].at[3], s_row, 3 * m + 2, to_core).start()

    trades[0].collect()
    fill_keys(recv.at[0], 0, ks, vs, heads)
    back0 = attend(0, 0, groups)
    x_exp[0].wait_recv()
    n_exp[0].start()
    x_out.wait_recv()
    c_out.start()
    y_gate.wait_recv()
    c_gate[1].start()
    for m in range(MICRO):
        y_cot[m].wait_recv()
        c_cot[MICRO + m].start()
    trades[1].collect()
    fill_keys(recv.at[1], 1, ks, vs, heads)
    for k in (2, 3):
        x_exp[k].wait_recv()
        n_exp[k - 1].start()
    back1 = attend(1, 0, 2)
    c_out.wait_recv()
    post(0, back0)
    back1 = attend(1, 2, groups)
    forward_row(0)
    for k in (1, 2):
        n_exp[k].wait_recv()
        n_exp[k + 2].start()
    post(1, back1)
    keep = []
    for m in range(MICRO):
        keep += [
            (recv.at[m], recv_out[m]),
            (mixed.at[m], mixed_out[m]),
            (lse.at[m], lse_out[m]),
            (att.at[m], att_out[m]),
            (res.at[m], res_out[m]),
            (nf.at[m], rows_out[m].at[0]),
            (nf.at[m], both_out.at[m]),
        ]
    keep += [(tags, tags_out), (wq, qkv_out), (wo, wout_out), (gains, gains_out), (table, table_out)]
    keep = [pltpu.make_async_copy(a, b, stores.at[3 + i]) for i, (a, b) in enumerate(keep)]
    for copy in keep:
        copy.start()
    forward_row(1)
    for copy in (*keep, *own_copies):
        copy.wait()
    for m in range(MICRO):
        remote(nf.at[m], rows_out[m].at[2], s_row, 3 * m + 1, to_core).wait()
        remote(rows_out[m].at[1], rows_out[m].at[3], s_row, 3 * m + 2, to_core).wait()
        remote(nf.at[m], rows_out[m].at[1], s_row, 3 * m, to_y).wait_send()
        trades[m].release()
    back0.release()
    back1.release()
    x_exp[1].wait_recv()
    for copy in n_exp:
        copy.wait_send()
    for copy in (n_exp[0], n_exp[3], n_exp[4]):
        copy.wait_recv()
    for copy in (*c_gate, *c_cot):
        copy.wait()
    for copy in (*x_exp, x_qkv, x_gain, x_out, c_qkv, c_out, y_gate, *y_cot, *tag_trade):
        copy.wait_send()


def run_front(x, gains, tags, gates, w_qkv, w_out, w_ein, w_eout, w_sin, w_sout, cot, groups):
    _, rows, width = x.shape
    heads = width // HEAD // groups
    k = width // 4
    w_qkv = w_qkv.reshape(2, k, 3 * width)
    w_out = w_out.reshape(2, k, width)
    w_ein = w_ein.reshape(2, -1, w_ein.shape[1])
    w_sin, w_sout = [w.reshape(2, 2, -1, w.shape[1]) for w in (w_sin, w_sout)]
    vmem = pl.BlockSpec(memory_space=pltpu.VMEM)
    anywhere = pl.BlockSpec(memory_space=pl.ANY)
    packed = lambda n: (groups, n * heads, HALF, HALF)
    held = MICRO * groups * TILE
    twice = lambda *a: [struct(*a)] * 2
    outs = (
        twice(packed(3), BF)
        + twice(packed(1), BF)
        + twice((groups, 8, TILE), F32)
        + twice((rows, width), BF)
        + twice((rows, width), F32)
        + twice((4, rows, width), BF)
        + twice((4, rows, width), BF)
        + [
            struct((4, *gates.shape), F32),
            struct((MICRO, rows, width), BF),
            struct((groups, *tags.shape), jnp.int32),
            struct((2, 2, k, 3 * width), BF),
            struct((2, 2, k, width), BF),
            struct(w_ein.shape, BF),
            struct(w_eout.shape, BF),
            struct(w_sin.shape, BF),
            struct(w_sout.shape, BF),
            struct((2, *gains.shape), F32),
            struct((2, MICRO * rows, HALF), F32),
        ]
    )
    v = pltpu.VMEM
    dma = lambda *n: pltpu.SemaphoreType.DMA(n)
    scratch = [
        v((2, 2, k, 3 * width), BF),
        v((2, 2, k, width), BF),
        v((2, *gains.shape), F32),
        v((groups, *tags.shape), jnp.int32),
        v((MICRO, *packed(3)), BF),
        v((MICRO, *packed(3)), BF),
        v((heads, held, HALF), BF),
        v((heads, held, HALF), BF),
        v((heads, TILE, held), F32),
        v((MICRO, *packed(1)), BF),
        v((MICRO, *packed(1)), BF),
        v((MICRO, groups, 8, TILE), F32),
        v((MICRO, rows, width), BF),
        v((MICRO, rows, width), F32),
        v((MICRO, rows, width), BF),
        v((2, MICRO * rows, HALF), F32),
    ]
    for shape in ((2,), (2,), (1,), (9,), (groups - 1,), (3,), (6,), (MICRO, groups), (MICRO, groups), (6,)):
        scratch += [dma(*shape), dma(*shape)]
    scratch += [dma(3), dma(MICRO), dma(MICRO), dma(1), dma(3 + 7 * MICRO + 5)]
    return pl.pallas_call(
        functools.partial(front_kernel, heads=heads, groups=groups),
        out_shape=tuple(outs),
        in_specs=[vmem] * 4 + [anywhere] * 7,
        out_specs=(anywhere,) * len(outs),
        scratch_shapes=scratch,
        compiler_params=pltpu.CompilerParams(
            vmem_limit_bytes=VMEM_LIMIT, collective_id=3, has_side_effects=True
        ),
        cost_estimate=price(130),
    )(x, gains, tags, gates, w_qkv, w_out, w_ein, w_eout, w_sin, w_sout, cot)


def ffn_kernel(*refs, tr, spans, counts, first, gated, opened, summed, closing):
    offs = refs[0]
    refs = list(refs[1:])
    take = lambda n: [refs.pop(0) for _ in range(n)]
    x_ref, dy_in = take(2)
    gate_ref = take(1)[0] if gated else None
    parts = len(spans)
    wg_parts, wu_parts, wo_parts = take(parts), take(parts), take(len(counts))
    y0, dx0 = take(2) if opened else (None, None)
    g0 = take(3) if summed else None
    y_ref, dx_ref, dwg_ref, dwu_ref, dwo_ref = take(5)
    xt, yacc, dxacc, hs, djg, dju, wg_ref, wu_ref, wo_ref = take(9)
    dy_ref = take(1)[0] if gated else dy_in
    f = pl.program_id(0)
    rows = x_ref.shape[0]

    @pl.when(f == 0)
    def _():
        xt[...] = x_ref[...].T
        if opened:
            yacc[...] = y0[...].astype(F32)
            dxacc[...] = dx0[...].astype(F32)
        else:
            yacc[...] = jnp.zeros_like(yacc)
            dxacc[...] = jnp.zeros_like(dxacc)
        if gated:
            dy_ref[...] = (dy_in[...].astype(F32) * gate_ref[...]).astype(BF)

    for index, span in enumerate(spans):
        place = pl.ds(pl.multiple_of(offs[index], HALF // 2), span)
        wg_ref[place, :] = wg_parts[index][...]
        wu_ref[place, :] = wu_parts[index][...]
    for index, count in enumerate(counts):
        begin = offs[parts + index]

        @pl.when((f + first >= begin) & (f + first < begin + count))
        def _(index=index):
            wo_ref[...] = wo_parts[index][...]

    wg, wu, wo = wg_ref[...], wu_ref[...], wo_ref[...]

    def tile(i, carry):
        r = pl.ds(pl.multiple_of(i * tr, tr), tr)
        x = x_ref[r, :]
        g = dot(x, wg)
        u = dot(x, wu)
        dh = dot(dy_ref[r, :], wo, NT)
        sig = 1.0 / (1.0 + jnp.exp(-g))
        act = g * sig
        h = (act * u).astype(BF)
        dg = (dh * u * (sig * (1.0 + g * (1.0 - sig)))).astype(BF)
        du = (dh * act).astype(BF)
        hs[r, :] = h
        djg[r, :] = dg
        dju[r, :] = du
        yacc[r, :] += dot(h, wo)
        dxacc[r, :] += dot(dg, wg, NT) + dot(du, wu, NT)
        return carry

    lax.fori_loop(0, rows // tr, tile, 0)
    grads = [dot(xt[...], djg[...]), dot(xt[...], dju[...]), dot(hs[...], dy_ref[...], TN)]
    for k, out in enumerate((dwg_ref, dwu_ref, dwo_ref)):
        value = grads[k]
        if summed:
            value = value + g0[k][...].astype(F32)
        out[...] = value.astype(BF)

    @pl.when(f == pl.num_programs(0) - 1)
    def _():
        made = yacc[...].astype(BF)
        if gated and closing:
            made = (made.astype(F32) * gate_ref[...]).astype(BF)
        y_ref[...] = made
        dx_ref[...] = dxacc[...].astype(BF)


def run_ffn(x, dy, gate, w_in, w_out, offsets, start=None, grads=None, span=None, closing=True, tr=512, fb=FB, us=10):
    rows, d = x.shape
    ff = sum(w.shape[0] for w in w_out)
    nf = ff // fb
    first, last = span or (0, nf)
    steps = last - first
    gated = gate is not None
    parts = len(w_in)
    spans = [w.shape[0] for w in w_in]
    counts = [w.shape[0] // fb for w in w_out]
    whole = lambda a: pl.BlockSpec(
        a.shape, lambda f, o: (0,) * a.ndim, pipeline_mode=pl.Buffered(1)
    )
    args = [x, dy] + ([gate] if gated else [])
    specs = [whole(a) for a in args]
    args += list(w_in) * 2 + list(w_out)
    specs += [pl.BlockSpec((n, fb), lambda f, o: (0, f + first)) for n in spans]
    specs += [pl.BlockSpec((n, fb), lambda f, o: (0, f + first + nf)) for n in spans]
    for i, c in enumerate(counts):
        specs.append(
            pl.BlockSpec(
                (fb, d), lambda f, o, i=i, c=c: (jnp.clip(f + first - o[parts + i], 0, c - 1), 0)
            )
        )
    if start is not None:
        args += list(start)
        specs += [whole(a) for a in start]
    wide = pl.BlockSpec((d, fb), lambda f, o: (0, f))
    tall = pl.BlockSpec((fb, d), lambda f, o: (f, 0))
    if grads is not None:
        args += list(grads)
        specs += [
            pl.BlockSpec((d, fb), lambda f, o: (0, f + first)),
            pl.BlockSpec((d, fb), lambda f, o: (0, f + first)),
            pl.BlockSpec((fb, d), lambda f, o: (f + first, 0)),
        ]
    full = pl.BlockSpec((rows, d), lambda f, o: (0, 0), pipeline_mode=pl.Buffered(1))
    return pl.pallas_call(
        functools.partial(
            ffn_kernel,
            tr=math.gcd(tr, rows),
            spans=spans,
            counts=counts,
            first=first,
            gated=gated,
            opened=start is not None,
            summed=grads is not None,
            closing=closing,
        ),
        out_shape=(
            struct((rows, d), BF),
            struct((rows, d), BF),
            struct((d, steps * fb), BF),
            struct((d, steps * fb), BF),
            struct((steps * fb, d), BF),
        ),
        grid_spec=pltpu.PrefetchScalarGridSpec(
            num_scalar_prefetch=1,
            grid=(steps,),
            in_specs=specs,
            out_specs=(full, full, wide, wide, tall),
            scratch_shapes=[
                pltpu.VMEM((d, rows), BF),
                pltpu.VMEM((rows, d), F32),
                pltpu.VMEM((rows, d), F32),
                pltpu.VMEM((rows, fb), BF),
                pltpu.VMEM((rows, fb), BF),
                pltpu.VMEM((rows, fb), BF),
                pltpu.VMEM((d, fb), BF),
                pltpu.VMEM((d, fb), BF),
                pltpu.VMEM((fb, d), BF),
            ]
            + ([pltpu.VMEM((rows, d), BF)] if gated else []),
        ),
        compiler_params=pltpu.CompilerParams(vmem_limit_bytes=VMEM_LIMIT),
        cost_estimate=price(us),
    )(offsets, *args)


def price(us):
    return pl.CostEstimate(flops=int(us * 1.15e9), bytes_accessed=0, transcendentals=0)


def norm_back(values, scale, gain, grad):
    gain_grad = jnp.sum(grad * values * scale, 0, keepdims=True)
    scaled = gain * grad
    grad_in = scale * scaled - values * (scale * scale * scale) * jnp.mean(
        scaled * values, -1, keepdims=True
    )
    return grad_in, gain_grad


def mid_core(grad, residual, gain, cot, w_ref, pay, gres_ref, gbf_ref, per):
    back, gain_grad = norm_back(residual, rms_scale(residual), gain, grad)
    total = cot.astype(F32) + back
    gres_ref[...] = total
    gbf_ref[...] = total.astype(BF)
    mixed = dot(gbf_ref[...], w_ref[...], NT)
    for pair in range(mixed.shape[1] // HALF):
        tile = mixed[:, pair * HALF : (pair + 1) * HALF]
        for side, packed in enumerate(swap_heads(tile[:HALF], tile[HALF:])):
            head = 2 * pair + side
            pay[head // per, head % per] = packed.astype(BF)
    return gain_grad


def finish(d0, d1, x_ref, gain_ref, w_ref, table, gres, atts, gbfs, gin_ref, gq, gv, go, gj, per):
    width = x_ref.shape[2]
    for micro, ref in enumerate((d0, d1)):
        rows = slice(micro * TILE, (micro + 1) * TILE)
        cosines, sines = table[0, rows, :], table[1, rows, :]
        for kind in range(3):
            for pair in range(width // HALF):
                tile = natural(ref, kind, pair, per)
                if kind == 0:
                    tile = tile * 0.125
                if kind < 2:
                    tile = rotate(tile, cosines, -sines)
                gj[rows, kind * width + pair * HALF : kind * width + (pair + 1) * HALF] = tile.astype(BF)
    tokens = x_ref[...].reshape(MICRO * TILE, width).astype(F32)
    scale = rms_scale(tokens)
    gain = gain_ref[...]
    turned = (tokens * scale * gain).astype(BF).T
    split = gq.shape[-1]
    gq[...] = dot(turned, gj[:, :split]).astype(BF).reshape(gq.shape)
    gv[...] = dot(turned, gj[:, split:]).astype(BF).reshape(gv.shape)
    go[...] = (dot(atts[0][...], gbfs[0], TN) + dot(atts[1][...], gbfs[1], TN)).astype(BF).reshape(go.shape)
    yield
    first = dot(gj[...], w_ref[...], NT)
    back, _ = norm_back(tokens, scale, gain, first)
    for micro in range(MICRO):
        rows = slice(micro * TILE, (micro + 1) * TILE)
        gin_ref[rows, :] = gres[micro] + back[rows]


def exchange(value, axis, mask):
    size = lax.axis_size(axis)
    return lax.ppermute(value, axis, [(i, i ^ mask) for i in range(size)])


def bits_of(size):
    return [1 << b for b in range(size.bit_length() - 1)]


def gather_rest(value):
    for mask in bits_of(lax.axis_size("expert"))[2:]:
        value = jnp.concatenate([value, exchange(value, "expert", mask)], 0)
    return value


def scatter_rest(value):
    for mask in reversed(bits_of(lax.axis_size("expert"))[2:]):
        half = value.shape[0] // 2
        got = exchange(value[half:], "expert", mask)
        value = (value[:half].astype(F32) + got.astype(F32)).astype(value.dtype)
    return value


def ordered(flag, mine, theirs):
    first = jnp.where(flag == 0, mine, theirs)
    second = jnp.where(flag == 0, theirs, mine)
    return jnp.concatenate([first, second], 0)


def pick(value, parts, index):
    size = value.shape[0] // parts
    return lax.dynamic_slice_in_dim(value, index * size, size, 0)


def after(value, token):
    return lax.optimization_barrier((value, token))[0]


PIECES = 4
EARLY = 6
AHEAD = 2
PLAN = {
    -1: ("rs1", "A0", "a0", "rs2", "B0", "A1", "a1", "a2", "A2", "rs3",),
    3: ("A3", "B1",),
    8: ("A4",),
    9: ("b0",),
    10: ("B2", "C0",),
    11: ("A5",),
    12: ("C1",),
    14: ("B3",),
    20: ("B4", "C2",),
    23: ("b1", "B5",),
    24: ("C3", "c0",),
    25: ("b2",),
    26: ("C4",),
    27: ("d0",),
    29: ("c1",),
    32: ("d1", "C5",),
    33: ("c2",),
    36: ("d2", "e0",),
    41: ("e1", "f0",),
    42: ("D3", "e2", "zhome", "A7", "A9", "g0", "f2", "D5", "D4", "A6", "f1", "D1", "h0", "g2", "A11", "h2", "g1", "D2", "A8", "h1", "A10", "D0",),
}
LAST_PLAN = (
    "A0", "A1", "A2", "A3", "B0", "B1", "a0", "C0", "A5", "a1",
    "B2", "C1", "B3", "b0", "a2", "C2", "b1", "B5", "C3", "c0",
    "b2", "d0", "c1", "C5", "c2", "D2", "d2", "D0", "e0", "A4",
    "f0", "d1", "D5", "f1", "zrest", "B4", "g0", "f2", "e1", "e2",
    "g1", "h0", "D3", "D1", "C4", "g2", "D4", "h1", "h2",
)


class Engine:
    def __init__(self, own, com, own_buf, com_buf, own_out, com_out, sems):
        self.own, self.com, self.own_buf, self.com_buf = own, com, own_buf, com_buf
        self.own_out, self.com_out = own_out, com_out
        e, z, d = lax.axis_index("expert"), lax.axis_index("context"), lax.axis_index("dp")
        groups = lax.axis_size("context")
        self.d, self.core, self.y = d, e % 2, e // 2 % 2
        self.outer = (z == 0) | (z == 3)
        self.inner = (z == 1) | (z == 2)
        self.to_x = {"dp": 1 - d}
        self.to_core = {"expert": e + 1 - 2 * self.core}
        self.to_y = {"expert": e + 2 - 4 * self.y}
        self.to_mate = {"context": z + 1 - 2 * (z % 2)}
        self.to_mid = {"context": 3 - z}
        self.others = [{"context": (z + k) % groups} for k in range(1, groups)]
        sems = list(sems)
        take = lambda n: [sems.pop(0) for _ in range(n)]
        self.o_load, self.o_store = take(2)
        self.o = {k: take(2) for k in "x123"}
        self.c_load, self.c_store = take(2)
        self.c = {k: take(2) for k in ("core", "y", "x", "1", "2", "3", "fore", "last")}

    @staticmethod
    def scratch(own_shapes, kinds, com_shapes):
        v, dma = pltpu.VMEM, lambda n: pltpu.SemaphoreType.DMA((max(n, 1),))
        tiny = (16, HALF)
        own_buf = []
        for s, kind in zip(own_shapes, kinds):
            own_buf += [v(s, BF), v(s if "x" in kind else tiny, BF)]
            own_buf += [v(s if "z" in kind else tiny, BF)] * 2
        com_buf = []
        for s in com_shapes:
            com_buf += [v((2, 2, *s), BF)] * 2 + [v((2, *s), BF)] + [v(s, BF)] * 3
        chunks, n = len(own_shapes), len(com_shapes)
        sems = [dma(chunks)] * 10 + [dma(2 * n), dma(n)] + [dma(2 * n)] * 4 + [dma(n)] * 12
        return own_buf, com_buf, sems

    def greet(self):
        meet(
            pltpu.get_barrier_semaphore(), [self.to_x, self.to_core, self.to_y, *self.others]
        )

    def o_wire(self, stage, c):
        total, r_x, r_1, r_2 = self.own_buf[c]
        src, k, _ = self.own[c]
        target = {"x": self.to_x, "1": self.to_mate, "2": self.to_mid, "3": self.to_mate}[stage]
        source = {"x": lambda: src.at[1 - self.d, k], "1": lambda: total, "2": lambda: total, "3": lambda: r_1}
        place = {"x": r_x, "1": r_1, "2": r_2, "3": self.own_out[c]}[stage]
        return remote(source[stage](), place, self.o[stage], c, target)

    def o_loading(self, c):
        src, k, kind = self.own[c]
        src = src.at[k] if kind == "z" else src.at[self.d, k]
        return pltpu.make_async_copy(src, self.own_buf[c][0], self.o_load.at[c])

    def o_storing(self, c):
        buf = self.own_buf[c][0 if self.own[c][2] == "x" else 2]
        return pltpu.make_async_copy(buf, self.own_out[c], self.o_store.at[c])

    def A(self, c):
        total, r_x = self.own_buf[c][:2]
        kind = self.own[c][2]
        self.o_loading(c).wait()
        if kind != "z":
            self.o_wire("x", c).wait_recv()
            if c + self.ahead < len(self.own):
                self.o_wire("x", c + self.ahead).start()
            total[...] = total[...] + r_x[...]
        if kind == "x":
            self.o_storing(c).start()
            return

        @pl.when(self.outer)
        def _():
            self.o_wire("1", c).start()

    def B(self, c):
        total, _, r_1, _ = self.own_buf[c]

        @pl.when(self.inner)
        def _():
            self.o_wire("1", c).wait_recv()
            total[...] = total[...] + r_1[...]
            self.o_wire("2", c).start()

    def C(self, c):
        total, _, r_1, r_2 = self.own_buf[c]

        @pl.when(self.inner)
        def _():
            self.o_wire("2", c).wait_recv()
            r_1[...] = total[...] + r_2[...]
            self.o_wire("3", c).start()
            self.o_storing(c).start()

    def D(self, c):
        @pl.when(self.outer)
        def _():
            self.o_wire("3", c).wait_recv()

    def c_loading(self, i, h):
        return pltpu.make_async_copy(
            self.com[i].at[h, self.core], self.com_buf[i][0].at[h], self.c_load.at[2 * i + h]
        )

    def c_storing(self, i):
        return pltpu.make_async_copy(
            self.com_buf[i][4], self.com_out[i].at[self.core, self.y], self.c_store.at[i]
        )

    def c_wire(self, stage, i, h=0):
        total, r_core, r_y, r_x, r_1, r_2 = self.com_buf[i]
        core, y, d = self.core, self.y, self.d
        out = self.com_out[i]
        if stage == "core":
            return remote(self.com[i].at[h, 1 - core], r_core.at[h], self.c["core"], 2 * i + h, self.to_core)
        if stage == "y":
            return remote(total.at[h, 1 - y], r_y.at[h], self.c["y"], 2 * i + h, self.to_y)
        if stage == "x":
            return remote(total.at[1 - d, y], r_x, self.c["x"], i, self.to_x)
        if stage == "1":
            return remote(total.at[d, y], r_1, self.c["1"], i, self.to_mate)
        if stage == "2":
            return remote(total.at[d, y], r_2, self.c["2"], i, self.to_mid)
        if stage == "3":
            return remote(r_1, out.at[core, y], self.c["3"], i, self.to_mate)
        if stage == "fore":
            return remote(r_1, out.at[core, y], self.c["fore"], i, self.to_y)
        if stage == "back":
            return remote(out.at[core, y], out.at[core, y], self.c["fore"], i, self.to_y)
        return remote(out.at[core], out.at[core], self.c["last"], i, self.to_core)

    def c_start(self, i):
        for h in range(2):
            self.c_wire("core", i, h).start()
            self.c_loading(i, h).start()

    def a(self, i):
        total, r_core = self.com_buf[i][:2]
        for h in range(2):
            self.c_loading(i, h).wait()
            self.c_wire("core", i, h).wait_recv()
        total[...] = total[...] + r_core[...]
        for h in range(2):
            self.c_wire("y", i, h).start()

    def b(self, i):
        total, r_y, y = self.com_buf[i][0], self.com_buf[i][2], self.y
        for h in range(2):
            self.c_wire("y", i, h).wait_recv()
            total[h, y] = total[h, y] + r_y[h]
        self.c_wire("x", i).start()

    def c_(self, i):
        total, r_x, y, d = self.com_buf[i][0], self.com_buf[i][3], self.y, self.d
        self.c_wire("x", i).wait_recv()
        total[d, y] = total[d, y] + r_x[...]

        @pl.when(self.outer)
        def _():
            self.c_wire("1", i).start()

    def d_(self, i):
        total, r_1, y, d = self.com_buf[i][0], self.com_buf[i][4], self.y, self.d

        @pl.when(self.inner)
        def _():
            self.c_wire("1", i).wait_recv()
            total[d, y] = total[d, y] + r_1[...]
            self.c_wire("2", i).start()

    def e(self, i):
        total, r_1, r_2 = self.com_buf[i][0], self.com_buf[i][4], self.com_buf[i][5]

        @pl.when(self.inner)
        def _():
            self.c_wire("2", i).wait_recv()
            r_1[...] = total[self.d, self.y] + r_2[...]
            self.c_wire("3", i).start()
            self.c_wire("fore", i).start()
            self.c_storing(i).start()

    def f(self, i):
        @pl.when(self.outer)
        def _():
            self.c_wire("3", i).wait_recv()
            self.c_wire("back", i).start()

    def g(self, i):
        @pl.when(self.inner)
        def _():
            self.c_storing(i).wait()

        self.c_wire("fore", i).wait_recv()
        self.c_wire("last", i).start()

    def h(self, i):
        self.c_wire("last", i).wait_recv()

    def start(self, ahead, com=True):
        self.ahead = ahead
        for c in range(min(ahead, len(self.own))):
            if self.own[c][2] != "z":
                self.o_wire("x", c).start()
        if com:
            for i in range(len(self.com)):
                self.c_start(i)
        for c in range(len(self.own)):
            self.o_loading(c).start()

    def run(self, name):
        kind, index = name[0], int(name[1:])
        {"c": self.c_, "d": self.d_}.get(kind, getattr(self, kind, None))(index)

    def close(self):
        chunks, common = range(len(self.own)), range(len(self.com))
        for c in chunks:
            if self.own[c][2] != "z":
                self.o_wire("x", c).wait_send()
            if self.own[c][2] == "x":
                self.o_storing(c).wait()
        chunks = [c for c in chunks if self.own[c][2] != "x"]
        for i in common:
            for h in range(2):
                self.c_wire("core", i, h).wait_send()
                self.c_wire("y", i, h).wait_send()
            self.c_wire("x", i).wait_send()
            self.c_wire("last", i).wait_send()

        @pl.when(self.outer)
        def _():
            for c in chunks:
                self.o_wire("1", c).wait_send()
            for i in common:
                self.c_wire("1", i).wait_send()
                self.c_wire("back", i).wait_send()

        @pl.when(self.inner)
        def _():
            for c in chunks:
                self.o_wire("2", c).wait_send()
                self.o_wire("3", c).wait_send()
                self.o_storing(c).wait()
            for i in common:
                self.c_wire("2", i).wait_send()
                self.c_wire("3", i).wait_send()
                self.c_wire("fore", i).wait_send()


class Arrays:
    def __init__(self, refs):
        self.refs = list(refs)

    def take(self, n):
        got, self.refs = self.refs[:n], self.refs[n:]
        return got

    def engine(self, own_at, sources, own_out, com, com_out):
        own_buf = [self.take(4) for _ in own_at]
        com_buf = [self.take(6) for _ in com]
        own = [(sources[j], k, kind) for j, k, kind in own_at]
        places = [own_out[j].at[k] for j, k, _ in own_at]
        return Engine(own, com, own_buf, com_buf, places, com_out, self.take(10 + 18))


def back_kernel(*refs, own_at, sources, common, heads, groups):
    refs = Arrays(refs)
    own_in, com_in = refs.take(sources), refs.take(common)
    recv0, recv1, out0, out1, lse0, lse1, key_tag, query_tag = refs.take(8)
    dxs, res0, res1, gain_ref, cot_ref, w_ref = refs.take(6)
    dx_made = refs.take(MICRO)
    own_out, com_out = refs.take(sources), refs.take(common)
    d0_out, d1_out, gres_out, gbf_out, gg_out = refs.take(5)
    engine = refs.engine(own_at, own_in, own_out, com_in, com_out)
    dx, r_core, r_y, gres, gbf, gg, pay_o, back_o, pay0, pay1 = refs.take(10)
    ks, vs, dk, dv, qs, gs, deltas, acc = refs.take(8)
    s_dx, s_o, s_0, s_1 = [refs.take(2) for _ in range(4)]
    local, = refs.take(1)

    engine.greet()
    both = range(MICRO)
    send_core = [remote(dx_made[m].at[2:4], r_core.at[m], s_dx, m, engine.to_core) for m in both]
    own_dx = [pltpu.make_async_copy(dx_made[m].at[0:2], dx.at[m], local.at[m]) for m in both]
    for m in both:
        send_core[m].start()
        own_dx[m].start()
    engine.start(AHEAD)
    send_y = [remote(dx.at[m, 1], r_y.at[m], s_dx, MICRO + m, engine.to_y) for m in both]
    trade_o = [
        Trade(pay_o.at[m], back_o.at[m], [s.at[m] for s in s_o], local.at[2 + m]) for m in both
    ]
    homes = [Trade(pay0, d0_out, s_0, local.at[4]), Trade(pay1, d1_out, s_1, local.at[5])]
    results = [
        pltpu.make_async_copy(a, b, local.at[6 + i])
        for i, (a, b) in enumerate(((gres, gres_out), (gbf, gbf_out), (gg, gg_out)))
    ]

    def rs1():
        for m in both:
            own_dx[m].wait()
            send_core[m].wait_recv()
            dx[m] = dx[m] + r_core[m]
            send_y[m].start()

    def middle(m, res_ref):
        send_y[m].wait_recv()
        grad = dxs[m * TILE : (m + 1) * TILE, :].astype(F32) + dx[m, 0].astype(F32) + r_y[m].astype(F32)
        part = mid_core(
            grad, res_ref[...], gain_ref[...], cot_ref[m], w_ref, pay_o.at[m], gres.at[m], gbf.at[m], heads
        )
        for dest in range(groups):
            trade_o[m].send(dest)
        return part

    def rs2():
        gg[...] = middle(0, res0)

    def rs3():
        gg[...] = gg[...] + middle(1, res1)
        for copy in results:
            copy.start()

    def zhome():
        for base, pay, trade in ((groups, pay1, homes[1]), (0, pay0, homes[0])):
            for dest in range(groups):
                back_pack(dk, dv, pay, dest, base, heads)
                trade.send(dest)

    named = {"rs1": rs1, "rs2": rs2, "rs3": rs3, "zhome": zhome}

    def events(slot):
        for name in PLAN.get(slot, ()):
            named[name]() if name in named else engine.run(name)

    for recv, micro in ((recv0, 0), (recv1, 1)):
        fill_keys(recv, micro, ks, vs, heads)
    dk[...] = jnp.zeros_like(dk)
    dv[...] = jnp.zeros_like(dv)
    first_of = (0, sum(min(s + 2, groups) for s in range(groups)))
    total = 2 * first_of[1] + groups * groups
    for micro, (recv, grad, out, lse, pay) in enumerate(
        ((recv0, back_o.at[0], out0, lse0, pay0), (recv1, back_o.at[1], out1, lse1, pay1))
    ):
        begin, end = first_of[micro], (first_of + (total,))[micro + 1]
        if micro == 0:
            events(-1)
        trade_o[micro].collect()

        def step(s, carry, micro=micro, recv=recv, grad=grad, out=out, lse=lse, pay=pay, begin=begin, end=end):
            back_begin(micro, s, heads, recv, grad, out, qs, gs, deltas, acc)
            before = begin + s * (s + 3) // 2 + groups * micro * s

            def tile(j, carry):
                for slot in range(begin, end):
                    if slot in PLAN:

                        @pl.when(before + j == slot)
                        def _(slot=slot):
                            events(slot)

                back_tile(
                    micro, s, j, heads, groups, lse, key_tag, query_tag, ks, vs, dk, dv, qs, gs, deltas, acc
                )
                return carry

            lax.fori_loop(0, groups * micro + jnp.minimum(s + 2, groups), tile, 0)
            for h in range(heads):
                pay[s, h] = pack_rows(acc[h]).astype(BF)
            return carry

        lax.fori_loop(0, groups, step, 0)
    events(total)
    for trade in homes:
        trade.collect()
        trade.release()
    for m in both:
        trade_o[m].release()
        send_core[m].wait_send()
        send_y[m].wait_send()
    for copy in results:
        copy.wait()
    engine.close()


def chunk_views(grads):
    return [g.reshape(2, PIECES, g.shape[0] // (2 * PIECES), g.shape[1]) for g in grads]


def shared_shape(shape):
    return (2, 2, 2, shape[0] // 8, shape[1])


def device_call(kernel, args, vmem_args, outs, scratch, collective_id, us, aliases=None):
    anywhere = pl.BlockSpec(memory_space=pl.ANY)
    return pl.pallas_call(
        kernel,
        out_shape=tuple(outs),
        in_specs=[pl.BlockSpec(memory_space=pltpu.VMEM) if v else anywhere for v in vmem_args],
        out_specs=(anywhere,) * len(outs),
        scratch_shapes=scratch,
        input_output_aliases=aliases or {},
        compiler_params=pltpu.CompilerParams(
            vmem_limit_bytes=VMEM_LIMIT, collective_id=collective_id, has_side_effects=True
        ),
        cost_estimate=price(us),
    )(*args)


def rest_sum(value):
    for mask in bits_of(lax.axis_size("expert"))[2:]:
        value = value + exchange(value, "expert", mask)
    return value


def run_back(expert_grads, own_at, shared_grads, attention, middle, dx_made, groups):
    own = chunk_views(expert_grads)
    com = [g.reshape(shared_shape(g.shape)) for g in shared_grads]
    heads = attention[0].shape[1] // 3
    rows, width = middle[1].shape
    args = [*own, *com, *attention, *middle, *dx_made]
    own_shapes = [own[j].shape[2:] for j, _, _ in own_at]
    com_shapes = [g.shape[3:] for g in com]
    own_buf, com_buf, sems = Engine.scratch(own_shapes, [kind for *_, kind in own_at], com_shapes)
    held = MICRO * groups * TILE
    v, dma = pltpu.VMEM, lambda n: pltpu.SemaphoreType.DMA((n,))
    pay = lambda n: (groups, n * heads, HALF, HALF)
    outs = (
        [struct(g.shape[1:], BF) for g in own]
        + [struct((2, 2, *s), BF) for s in com_shapes]
        + [struct(pay(3), BF)] * 2
        + [struct((MICRO, rows, width), F32), struct((MICRO, rows, width), BF), struct((1, width), F32)]
    )
    scratch = [
        *own_buf,
        *com_buf,
        *sems,
        v((MICRO, 2, rows, width), BF),
        v((MICRO, 2, rows, width), BF),
        v((MICRO, rows, width), BF),
        v((MICRO, rows, width), F32),
        v((MICRO, rows, width), BF),
        v((1, width), F32),
        v((MICRO, *pay(1)), BF),
        v((MICRO, *pay(1)), BF),
        v(pay(3), BF),
        v(pay(3), BF),
        v((heads, held, HALF), BF),
        v((heads, held, HALF), BF),
        v((heads, held, HALF), F32),
        v((heads, held, HALF), F32),
        v((heads, TILE, HALF), BF),
        v((heads, TILE, HALF), BF),
        v((heads, 8, TILE), F32),
        v((heads, TILE, HALF), F32),
        dma(2 * MICRO),
        dma(2 * MICRO),
        *[pltpu.SemaphoreType.DMA((MICRO, groups))] * 2,
        *[dma(groups)] * 4,
        dma(9),
    ]
    flags = [False] * (len(own) + len(com)) + [True] * (len(attention) + len(middle))
    flags += [False] * len(dx_made)
    kernel = functools.partial(
        back_kernel, own_at=own_at, sources=len(own), common=len(com), heads=heads, groups=groups
    )
    got = device_call(kernel, args, flags, outs, scratch, 1, 165)
    n, m = len(own), len(com)
    return got[:n], [rest_sum(g.reshape(-1, g.shape[-1]).astype(F32)) for g in got[n : n + m]], got[n + m :]


def last_kernel(*refs, own_at, sources, per):
    refs = Arrays(refs)
    own_in = refs.take(sources)
    d0, d1, x_ref, gain_ref, w_ref, table = refs.take(6)
    (gres, gbfs, gg_in), atts, made = refs.take(3), refs.take(2), refs.take(MICRO)
    own_out, com_out = refs.take(sources), refs.take(3)
    gin_out, gg_out, routed_out = refs.take(3)
    sources = [refs.refs.pop(len(own_at) * 4 + 3 * 6 + 28) for _ in range(3)]
    engine = refs.engine(own_at, own_in, own_out, sources, com_out)
    gj, gin, gg_sum, gg_got, g_send, g_recv, local, row, row_core, row_y, m_send, m_recv = refs.take(12)
    engine.greet()
    engine.start(0, com=False)
    z = lax.axis_index("context")
    rounds = (engine.to_core, engine.to_y, engine.to_x, engine.to_mate, {"context": z + 2 - 4 * (z // 2)})
    wires = [
        remote(gg_sum.at[k], gg_got.at[k], (g_send, g_recv), k, target) for k, target in enumerate(rounds)
    ]
    gg_sum[0] = jnp.broadcast_to(gg_in[...], gg_sum.shape[1:])
    wires[0].start()
    both = range(MICRO)
    row_wires = [remote(made[m].at[2:4], row_core.at[m], (m_send, m_recv), m, engine.to_core) for m in both]
    row_next = [remote(row.at[m, 1], row_y.at[m], (m_send, m_recv), MICRO + m, engine.to_y) for m in both]
    row_own = [pltpu.make_async_copy(made[m].at[0:2], row.at[m], local.at[2 + m]) for m in both]
    row_out = [pltpu.make_async_copy(row.at[m, 0], routed_out.at[m], local.at[2 + m]) for m in both]
    for m in both:
        row_wires[m].start()
        row_own[m].start()
    work = finish(
        d0, d1, x_ref, gain_ref, w_ref, table, gres, atts, gbfs, gin, *sources, gj, per
    )
    store = pltpu.make_async_copy(gin, gin_out, local.at[0])
    next(work)
    for i in range(3):
        engine.c_start(i)
    turn = 0
    for index, name in enumerate(LAST_PLAN):
        if name == "zrest":
            for _ in work:
                pass
            store.start()
        else:
            engine.run(name)
        if index == 12:
            for m in both:
                row_own[m].wait()
                row_wires[m].wait_recv()
                row[m] = row[m] + row_core[m]
                row_next[m].start()
        if index == 30:
            for m in both:
                row_next[m].wait_recv()
                row[m, 0] = row[m, 0] + row_y[m]
                row_out[m].start()
        if index % 5 == 4 and turn < len(wires):
            wires[turn].wait_recv()
            gg_sum[turn + 1] = gg_sum[turn] + gg_got[turn]
            turn += 1
            if turn < len(wires):
                wires[turn].start()
    total = pltpu.make_async_copy(gg_sum.at[len(wires)], gg_out, local.at[1])
    total.start()
    store.wait()
    total.wait()
    for wire in (*wires, *row_wires, *row_next):
        wire.wait_send()
    for copy in row_out:
        copy.wait()
    engine.close()


def run_last(sums, own_at, parts, made, groups):
    x, w = parts[2], parts[4]
    _, rows, width = x.shape
    args = [*sums, *parts, *made]
    own_shapes = [sums[j].shape[1:] for j, _, _ in own_at]
    com = [shared_shape((width, 3 * width // 2))] * 2 + [shared_shape((width, width))]
    own_buf, com_buf, sems = Engine.scratch(own_shapes, [k for *_, k in own_at], [s[3:] for s in com])
    v = pltpu.VMEM
    outs = (
        [struct(g.shape, BF) for g in sums]
        + [struct((2, 2, *s[3:]), BF) for s in com]
        + [struct((MICRO * rows, width), F32), struct((8, width), F32), struct((MICRO, rows, width), BF)]
    )
    rounds = 5
    scratch = [
        *own_buf,
        *com_buf,
        *sems,
        *[v(s, BF) for s in com],
        v((MICRO * rows, 3 * width), BF),
        v((MICRO * rows, width), F32),
        v((rounds + 1, 8, width), F32),
        v((rounds, 8, width), F32),
        *[pltpu.SemaphoreType.DMA((rounds,))] * 2,
        pltpu.SemaphoreType.DMA((2 + MICRO,)),
        v((MICRO, 2, rows, width), BF),
        v((MICRO, 2, rows, width), BF),
        v((MICRO, rows, width), BF),
        *[pltpu.SemaphoreType.DMA((2 * MICRO,))] * 2,
    ]
    flags = [False] * len(sums) + [True] * len(parts) + [False] * len(made)
    kernel = functools.partial(
        last_kernel, own_at=own_at, sources=len(sums), per=width // HEAD // groups
    )
    got = device_call(
        kernel, args, flags, outs, scratch, 2, 90, {i: i for i in range(len(sums))}
    )
    n = len(sums)
    return got[:n], [rest_sum(g.reshape(-1, g.shape[-1]).astype(F32)) for g in got[n : n + 3]], *got[n + 3 :]


def body(
    inputs,
    keep_flags,
    block_ids,
    expert_ids,
    gate_weights,
    norm_attn,
    w_qkv,
    w_attn_out,
    norm_ffn,
    w_shared_in,
    w_shared_out,
    w_expert_in,
    w_expert_out,
    cotangent,
):
    width = w_qkv.shape[1] // 3
    rows = inputs.shape[2]
    groups = lax.axis_size("context")
    experts = lax.axis_size("expert")
    z = lax.axis_index("context")
    seq_rows = rows * groups
    x = inputs[0]
    cot = cotangent[0].reshape(MICRO * rows, width)

    blocks = block_ids[0] + 8 * jnp.arange(MICRO, dtype=jnp.int32)[:, None]
    key_tags = jnp.where(keep_flags[0] == 1, blocks, HIDDEN)
    tags = jnp.stack([blocks, key_tags])[:, :, None]

    per_expert = jnp.sum(
        jnp.where(
            expert_ids[0][None] == jnp.arange(experts, dtype=jnp.int32)[:, None, None, None],
            gate_weights[0][None],
            0.0,
        ),
        -1,
    )
    gains = jnp.stack([norm_attn, norm_ffn]).astype(F32)
    (
        *pairs,
        gates_four,
        nf_both,
        all_tags,
        mat_qkv,
        mat_out,
        ein_parts,
        eout_other,
        sin_parts,
        sout_parts,
        gains,
        table,
    ) = run_front(
        x,
        gains,
        tags,
        per_expert,
        w_qkv,
        w_attn_out,
        w_expert_in[0],
        w_expert_out[0],
        w_shared_in,
        w_shared_out,
        cotangent[0],
        groups,
    )
    recvs, mixed, lses, att, res, rows_four, cot_four = [pairs[2 * i : 2 * i + 2] for i in range(7)]
    mat_qkv = mat_qkv.reshape(width, -1)
    mat_out = mat_out.reshape(width, width)
    gain_attn = gains[:, 0].reshape(1, width)
    gain_ffn = gains[:, 1].reshape(1, width)
    all_tags = all_tags[:, :, :, 0].transpose(1, 2, 0, 3)
    query_row = all_tags[0].reshape(MICRO * groups, 1, rows)
    key_col = all_tags[1].reshape(-1, 1)
    own_gates = lax.dynamic_index_in_dim(
        gather_rest(gates_four), lax.axis_index("expert"), 1, False
    )
    gate = [own_gates[:, m].reshape(-1, 1) for m in range(MICRO)]

    core = lax.axis_index("expert") % 2
    dp = lax.axis_index("dp")
    k_half, f_half = width // 2, w_shared_out.shape[0]
    whole = lambda w: w.reshape(-1, w.shape[-1])
    ein_parts = (w_expert_in[0], whole(ein_parts))
    eout_parts = (w_expert_out[0], eout_other)
    sin_parts = (w_shared_in, whole(sin_parts))
    sout_parts = (w_shared_out, whole(sout_parts))
    chunk = f_half // FB
    offs = jnp.stack([dp * k_half, (1 - dp) * k_half, dp * chunk, (1 - dp) * chunk])

    capacity = 4 * rows // experts

    def expert_pass(m, grads, token=None):
        hidden = gather_rest(rows_four[m]).reshape(-1, width)
        if token is not None:
            hidden = after(hidden, token)
        grad, weight = gather_rest(cot_four[m]).reshape(-1, width), gate[m]
        if capacity < rows:
            chosen = weight.reshape(-1, rows) > 0
            slots = jnp.cumsum(chosen.astype(jnp.int32), 1) - 1
            select = (
                chosen[:, None] & (slots[:, None] == jnp.arange(capacity, dtype=jnp.int32)[:, None])
            ).astype(BF)
            squeeze = lambda v: jnp.einsum("bcr,brd->bcd", select, v.reshape(-1, rows, width)).reshape(-1, width)
            spread = lambda v: jnp.einsum("bcr,bcd->brd", select, v.reshape(-1, capacity, width)).reshape(-1, width)
            hidden, grad = squeeze(hidden), squeeze(grad)
            weight = jnp.sum(select.astype(F32) * weight.reshape(-1, 1, rows), -1).reshape(-1, 1)
        made, dx, *grads = run_ffn(
            hidden, grad, weight, ein_parts, eout_parts, offs, grads=grads, us=41
        )
        if capacity < rows:
            made, dx = spread(made), spread(dx)
        return made, dx, *grads

    made0, dx0, *g_expert = expert_pass(0, None)
    shared, dx_shared, *g_shared = run_ffn(
        nf_both.reshape(-1, width), cot, None, sin_parts, sout_parts, offs, us=23
    )
    made1, dx1, *g_expert = expert_pass(1, g_expert, dx_shared)
    dx0, dx1, made0, made1 = [scatter_rest(v).reshape(4, rows, width) for v in (dx0, dx1, made0, made1)]

    spread = [(j, k) for j in range(3) for k in range(PIECES)]
    early = [(j, k, "xz" if i < EARLY else "x") for i, (j, k) in enumerate(spread)]
    first = spread[EARLY][0]
    late = [(j - first, k, "z") for j, k in spread[EARLY:]]
    attention = (*recvs, *mixed, *lses, key_col, query_row)
    own_sums, (r_gate, r_up, r_sout), (d0, d1, gres, gbf, gg) = run_back(
        g_expert,
        early,
        g_shared,
        attention,
        (dx_shared, *res, gain_ffn, cotangent[0], mat_out),
        (dx0, dx1),
        groups,
    )
    own_late, (r_qk, r_v, r_out), grad_input, gain_sum, routed = run_last(
        own_sums[first:],
        late,
        (d0, d1, x, gain_attn, mat_qkv, table, gres, gbf, gg, *att),
        (made0, made1),
        groups,
    )
    output = jnp.stack(
        [
            (res[m] + shared[m * rows : (m + 1) * rows].astype(F32) + routed[m].astype(F32)).astype(BF)
            for m in range(MICRO)
        ]
    )
    r_gain_ffn = pick(rest_sum(gain_sum)[0], 2, dp)
    r_qkv = jnp.concatenate([r_qk, r_v], 1)
    r_sin = jnp.concatenate([r_gate, r_up], 1)
    r_gain_attn = jnp.sum(w_qkv.astype(F32) * r_qkv, 1) / norm_attn.astype(F32)
    e_gate, e_up, r_eout = [
        g.reshape(-1, g.shape[-1]).astype(F32) for g in (*own_sums[:first], *own_late)
    ]
    r_ein = jnp.concatenate([e_gate, e_up], 1)
    return (
        output[None],
        grad_input.reshape(1, MICRO, rows, width),
        r_gain_attn,
        r_qkv,
        r_out,
        r_gain_ffn,
        r_sin,
        r_sout,
        r_ein[None],
        r_eout[None],
    )


def solution(mesh):
    tokens = P(("expert", "dp"), None, "context", None)
    flags = P(("expert", "dp"), None, "context")
    placed = (
        tokens,
        flags,
        flags,
        tokens,
        tokens,
        P("dp"),
        P("dp", None),
        P("dp", None),
        P("dp"),
        P("dp", None),
        P("dp", None),
        P("expert", "dp", None),
        P("expert", "dp", None),
        tokens,
    )
    return jax.shard_map(
        body,
        mesh=mesh,
        in_specs=placed,
        out_specs=(
            tokens,
            tokens,
            P("dp"),
            P("dp", None),
            P("dp", None),
            P("dp"),
            P("dp", None),
            P("dp", None),
            P("expert", "dp", None),
            P("expert", "dp", None),
        ),
        check_vma=False,
    )
```

```python
import functools
import math

import jax
import jax.numpy as jnp
from jax import lax
from jax.experimental import pallas as pl
from jax.experimental.pallas import tpu as pltpu
from jax.sharding import PartitionSpec as P

HEAD = 64
MICRO = 2
TILE = 256
HALF = 128
EPSILON = 1e-05
ROPE_BASE = 10000.0
MASKED = -3e30
HIDDEN = 1 << 20
BF = jnp.bfloat16
F32 = jnp.float32
NT = (((1,), (1,)), ((), ()))
TN = (((0,), (0,)), ((), ()))
VMEM_LIMIT = 60 << 20
FB = 512


def dot(left, right, dims=(((1,), (0,)), ((), ()))):
    return lax.dot_general(left, right, dims, preferred_element_type=F32)


def rms_scale(values):
    return lax.rsqrt(jnp.mean(values * values, -1, keepdims=True) + EPSILON)


def low_lanes(rows):
    return lax.broadcasted_iota(jnp.int32, (rows, HALF), 1) < HEAD


def swap_heads(first, second):
    low = low_lanes(HALF)
    return (
        jnp.where(low, first, pltpu.roll(second, HEAD, 1)),
        jnp.where(low, pltpu.roll(first, HEAD, 1), second),
    )


def rotate(tile, cosines, sines):
    lane = lax.broadcasted_iota(jnp.int32, tile.shape, 1)
    partner = jnp.where(
        lane % HEAD < HEAD // 2,
        pltpu.roll(tile, HALF - HEAD // 2, 1),
        pltpu.roll(tile, HEAD // 2, 1),
    )
    return tile * cosines + partner * sines


def struct(shape, dtype):
    return jax.ShapeDtypeStruct(tuple(shape), dtype)


def project(tokens, gain, w_ref, cosines, sines, pay, groups):
    normed = (tokens * rms_scale(tokens) * gain).astype(BF)
    width = tokens.shape[1]
    per = width // HEAD // groups
    for kind in range(3):
        joined = dot(normed, w_ref[:, kind * width : (kind + 1) * width])
        for pair in range(width // HALF):
            tile = joined[:, pair * HALF : (pair + 1) * HALF]
            if kind < 2:
                tile = rotate(tile, cosines, sines)
            if kind == 0:
                tile = tile * 0.125
            for side, packed in enumerate(swap_heads(tile[:HALF], tile[HALF:])):
                head = 2 * pair + side
                pay[head // per, kind * per + head % per] = packed.astype(BF)


def unpack(ref, index, kind_head):
    tile = ref[index, kind_head]
    return tile, pltpu.roll(tile.astype(F32), HEAD, 1).astype(BF)


def fill_keys(recv, micro, ks, vs, heads):
    groups = recv.shape[0]
    for src in range(groups):
        base = (micro * groups + src) * TILE
        for h in range(heads):
            for store, kind in ((ks, 1), (vs, 2)):
                first, second = unpack(recv, src, kind * heads + h)
                store[h, base : base + HALF] = first
                store[h, base + HALF : base + TILE] = second


def column(row):
    return jnp.broadcast_to(row, (8, row.shape[1])).T[:, :1]


def gain_row(gains, which):
    return jnp.concatenate([gains[0, which : which + 1], gains[1, which : which + 1]], 1)


def masked_rows(ref, index, kind_head):
    tile = ref[index, kind_head].astype(F32)
    both = jnp.concatenate([tile, pltpu.roll(tile, HEAD, 1)], 0)
    return jnp.where(low_lanes(TILE), both, 0.0)


def pack_rows(values):
    return jnp.where(low_lanes(HALF), values[:HALF], pltpu.roll(values[HALF:], HEAD, 1))


def attend_step(step, micro, heads, groups, recv, tags, out_ref, lse_ref, ks, vs, scores):
    count = groups * micro + jnp.minimum(step + 2, groups)
    queries = [masked_rows(recv, step, h).astype(BF) for h in range(heads)]
    tag = column(tags[step, 0, micro])
    same = lax.broadcasted_iota(jnp.int32, (TILE, TILE), 0) == lax.broadcasted_iota(
        jnp.int32, (TILE, TILE), 1
    )

    def first_pass(j, tops):
        keys = pl.ds(pl.multiple_of(j * TILE, TILE), TILE)
        key_tag = tags[j % groups, 1, j // groups]
        seen = (key_tag <= tag) | (same & (j == groups * micro + step))
        new = []
        for h in range(heads):
            part = jnp.where(seen, dot(queries[h], ks[h, keys, :], NT), MASKED)
            scores[h, :, keys] = part
            new.append(jnp.maximum(tops[h], jnp.maximum(part[:, :HALF], part[:, HALF:])))
        return tuple(new)

    tops = lax.fori_loop(
        0, count, first_pass, (jnp.full((TILE, HALF), MASKED, F32),) * heads
    )
    tops = [jnp.max(top, 1, keepdims=True) for top in tops]

    def second_pass(j, carry):
        keys = pl.ds(pl.multiple_of(j * TILE, TILE), TILE)
        sums, totals = carry
        new_sums, new_totals = [], []
        for h in range(heads):
            expo = jnp.exp(scores[h, :, keys] - tops[h])
            new_sums.append(sums[h] + (expo[:, :HALF] + expo[:, HALF:]))
            new_totals.append(totals[h] + dot(expo.astype(BF), vs[h, keys, :]))
        return tuple(new_sums), tuple(new_totals)

    zero = (jnp.zeros((TILE, HALF), F32),) * heads
    sums, totals = lax.fori_loop(0, count, second_pass, (zero, zero))
    lane = lax.broadcasted_iota(jnp.int32, (TILE, HALF), 1)
    logs = jnp.zeros((TILE, HALF), F32)
    for h in range(heads):
        total = jnp.sum(sums[h], 1, keepdims=True)
        out_ref[step, h] = pack_rows(totals[h] / total).astype(BF)
        logs = jnp.where(lane == h, tops[h] + jnp.log(total), logs)
    lse_ref[step] = logs.T[:8]


def back_begin(micro, step, heads, recv, grad, out, qs, gs, deltas, acc):
    ones = jnp.ones((8, HALF), F32)
    for h in range(heads):
        grad_f = masked_rows(grad, step, h)
        qs[h] = masked_rows(recv, step, h).astype(BF)
        gs[h] = grad_f.astype(BF)
        deltas[h] = lax.dot_general(
            ones,
            grad_f * masked_rows(out, step, h),
            NT,
            precision=lax.Precision.HIGHEST,
            preferred_element_type=F32,
        )
    acc[...] = jnp.zeros_like(acc)


def back_tile(micro, step, j, heads, groups, lse, tags, ks, vs, dk, dv, qs, gs, deltas, acc):
    keys = pl.ds(pl.multiple_of(j * TILE, TILE), TILE)
    same = lax.broadcasted_iota(jnp.int32, (TILE, TILE), 0) == lax.broadcasted_iota(
        jnp.int32, (TILE, TILE), 1
    )
    key_tag = column(tags[j % groups, 1, j // groups])
    seen = (key_tag <= tags[step, 0, micro]) | (same & (j == groups * micro + step))
    for h in range(heads):
        key, value = ks[h, keys, :], vs[h, keys, :]
        scores = dot(key, qs[h], NT)
        probs = jnp.where(seen, jnp.exp(scores - lse[step, h : h + 1, :]), 0.0)
        dv[h, keys, :] += dot(probs.astype(BF), gs[h])
        slope = (probs * (dot(value, gs[h], NT) - deltas[h, :1])).astype(BF)
        dk[h, keys, :] += dot(slope, qs[h])
        acc[h] += dot(slope, key, TN)


def back_pack(dk, dv, pay, src, base, heads):
    rows = slice((base + src) * TILE, (base + src + 1) * TILE)
    for h in range(heads):
        pay[src, heads + h] = pack_rows(dk[h, rows]).astype(BF)
        pay[src, 2 * heads + h] = pack_rows(dv[h, rows]).astype(BF)


def natural(ref, first_kind, pair, per):
    tiles = []
    for head in (2 * pair, 2 * pair + 1):
        tiles.append(ref[head // per, first_kind * per + head % per].astype(F32))
    return jnp.concatenate(swap_heads(*tiles), 0)


def remote(src, dst, sems, index, target, arrival=None):
    return pltpu.make_async_remote_copy(
        src_ref=src,
        dst_ref=dst,
        send_sem=sems[0].at[index],
        recv_sem=sems[1].at[index if arrival is None else arrival],
        device_id=target,
        device_id_type=pl.DeviceIdType.MESH,
    )


def meet(barrier, targets):
    for target in targets:
        pl.semaphore_signal(barrier, inc=1, device_id=target, device_id_type=pl.DeviceIdType.MESH)
    pl.semaphore_wait(barrier, len(targets))


def project_out(got, tokens, w_ref, gain, att, res, nf, heads):
    for pair in range(tokens.shape[1] // HALF):
        att[:, pair * HALF : (pair + 1) * HALF] = natural(got, 0, pair, heads).astype(BF)
    residual = tokens.astype(F32) + dot(att[...], w_ref[...])
    res[...] = residual
    nf[...] = (residual * rms_scale(residual) * gain).astype(BF)


class Trade:
    def __init__(self, src, dst, sems, local):
        self.src, self.dst, self.sems, self.local = src, dst, sems, local
        self.z = lax.axis_index("context")
        self.groups = src.shape[0]

    def wire(self, other, arrival):
        return remote(self.src.at[other], self.dst.at[arrival], self.sems, other, {"context": other}, arrival)

    def keep(self, index):
        return pltpu.make_async_copy(self.src.at[index], self.dst.at[index], self.local)

    def send(self, dest):
        @pl.when(dest != self.z)
        def _():
            self.wire(dest, self.z).start()

        @pl.when(dest == self.z)
        def _():
            self.keep(dest).start()

    def await_from(self, other):
        @pl.when(other != self.z)
        def _():
            self.wire(other, other).wait_recv()

        @pl.when(other == self.z)
        def _():
            self.keep(other).wait()

    def collect(self):
        for other in range(self.groups):
            self.await_from(other)

    def release(self):
        for other in range(self.groups):

            @pl.when(other != self.z)
            def _(other=other):
                self.wire(other, self.z).wait_send()


def front_kernel(*refs, heads, groups):
    refs = list(refs)
    take = lambda n: [refs.pop(0) for _ in range(n)]
    x_ref, gains_in, blocks, keeps, gates_in = take(5)
    w_qkv, w_out, w_ein, w_eout, w_sin, w_sout, cot = take(7)
    recv_out, mixed_out, lse_out, cot_out = take(2), take(2), take(2), take(2)
    att_out, res_out, rows_out, got_out, gates_out, tags_out = take(6)
    qkv_out, wout_out, ein_out, eout_out, sin_out, sout_out, gains_out, table_out = take(8)
    wq, wo, gains, tags, pay, recv, ks, vs, scores, mixed, got, lse, att, res, nf, table = take(16)
    s_qkv, s_out, s_gain, s_exp, s_tag, s_gate, s_cot, s_pay, s_mix, s_row = [take(2) for _ in range(10)]
    local, self_pay, self_mix, stores = take(4)
    e, z, d = lax.axis_index("expert"), lax.axis_index("context"), lax.axis_index("dp")
    core, y = e % 2, e // 2 % 2
    to_x, to_core, to_y = {"dp": 1 - d}, {"expert": e + 1 - 2 * core}, {"expert": e + 2 - 4 * y}
    others = [{"context": (z + k) % groups} for k in range(1, groups)]
    width = x_ref.shape[2]

    loads = [
        pltpu.make_async_copy(w_qkv, wq.at[d], local.at[0]),
        pltpu.make_async_copy(w_out, wo.at[d], local.at[1]),
        pltpu.make_async_copy(gains_in, gains.at[d], local.at[2]),
    ]
    for copy in loads:
        copy.start()
    meet(pltpu.get_barrier_semaphore(), [to_x, to_core, to_y, *others])

    x_qkv = remote(w_qkv.at[core], wq.at[d, core], s_qkv, 0, to_x)
    x_gain = remote(gains_in, gains.at[d], s_gain, 0, to_x)
    x_out = remote(w_out.at[core], wo.at[d, core], s_out, 0, to_x)
    half = z % 2
    to_mate = {"context": z + 1 - 2 * half}
    x_exp = [
        remote(w_ein.at[half], ein_out.at[half], s_exp, 0, to_x),
        remote(w_eout, eout_out, s_exp, 1, to_x),
        remote(w_sin.at[core, y], sin_out.at[core, y], s_exp, 2, to_x),
        remote(w_sout.at[core, y], sout_out.at[core, y], s_exp, 3, to_x),
    ]
    n_exp = [
        remote(ein_out.at[half], ein_out.at[half], s_exp, 4, to_mate),
        remote(sin_out.at[core, y], sin_out.at[core, y], s_exp, 5, to_y),
        remote(sout_out.at[core, y], sout_out.at[core, y], s_exp, 6, to_y),
        remote(sin_out.at[core], sin_out.at[core], s_exp, 7, to_core),
        remote(sout_out.at[core], sout_out.at[core], s_exp, 8, to_core),
    ]
    for copy in (x_qkv, x_gain, x_out, x_exp[0], x_exp[2], x_exp[3], x_exp[1]):
        copy.start()
    for m in range(MICRO):
        block = blocks[0, m : m + 1, :] + 8 * m
        tags[z, 0, m] = block
        tags[z, 1, m] = jnp.where(keeps[0, m : m + 1, :] == 1, block, HIDDEN)
    tag_trade = [remote(tags.at[z], tags.at[z], s_tag, k, others[k]) for k in range(groups - 1)]
    for copy in tag_trade:
        copy.start()
    own_copies = [
        pltpu.make_async_copy(gates_in, gates_out.at[0], stores.at[0]),
        pltpu.make_async_copy(cot.at[0], cot_out[0].at[0], stores.at[1]),
        pltpu.make_async_copy(cot.at[1], cot_out[1].at[0], stores.at[2]),
    ]
    for copy in own_copies:
        copy.start()
    y_gate = remote(gates_in, gates_out.at[1], s_gate, 0, to_y)
    y_cot = [remote(cot.at[m], cot_out[m].at[1], s_cot, m, to_y) for m in range(MICRO)]
    c_gate = [
        remote(gates_in, gates_out.at[2], s_gate, 1, to_core),
        remote(gates_out.at[1], gates_out.at[3], s_gate, 2, to_core),
    ]
    c_cot = [remote(cot.at[m], cot_out[m].at[2], s_cot, 2 + m, to_core) for m in range(MICRO)] + [
        remote(cot_out[m].at[1], cot_out[m].at[3], s_cot, 4 + m, to_core) for m in range(MICRO)
    ]
    y_gate.start()
    for copy in y_cot:
        copy.start()

    row = lax.broadcasted_iota(jnp.int32, (MICRO * TILE, HALF), 0)
    lane = lax.broadcasted_iota(jnp.int32, (MICRO * TILE, HALF), 1)
    place = row // TILE * (TILE * groups) + z * TILE + row % TILE
    freq = jnp.exp((-math.log(ROPE_BASE) * 2.0 / HEAD) * (lane % (HEAD // 2)).astype(F32))
    angle = place.astype(F32) * freq
    table[0] = jnp.cos(angle)
    table[1] = jnp.where(lane % HEAD < HEAD // 2, -jnp.sin(angle), jnp.sin(angle))

    c_qkv = remote(wq.at[1 - d, core], wq.at[1 - d, core], s_qkv, 1, to_core)
    c_out = remote(wo.at[1 - d, core], wo.at[1 - d, core], s_out, 1, to_core)
    for copy in loads:
        copy.wait()
    x_qkv.wait_recv()
    c_qkv.start()
    x_gain.wait_recv()
    c_qkv.wait_recv()
    both = [gain_row(gains, k) for k in range(2)]
    w_full = wq.reshape(width, 3 * width)
    trades, returns = [], []
    for m in range(MICRO):
        span = slice(m * TILE, (m + 1) * TILE)
        project(x_ref[m].astype(F32), both[0], w_full, table[0, span, :], table[1, span, :], pay.at[m], groups)
        trade = Trade(pay.at[m], recv.at[m], [s.at[m] for s in s_pay], self_pay.at[m])
        for dest in range(groups):
            trade.send(dest)
        trades.append(trade)
    c_gate[0].start()
    for copy in c_cot[:MICRO]:
        copy.start()
    for k in range(groups - 1):
        source = (z + groups - 1 - k) % groups
        remote(tags.at[z], tags.at[source], s_tag, k, others[k]).wait_recv()

    def attend(m, first, last):
        trade = Trade(mixed.at[m], got.at[m], [s.at[m] for s in s_mix], self_mix.at[m])

        def one(step, carry):
            attend_step(step, m, heads, groups, recv.at[m], tags, mixed.at[m], lse.at[m], ks, vs, scores)
            trade.send(step)
            return carry

        lax.fori_loop(first, last, one, 0)
        return trade

    row_y = remote(nf, rows_out.at[1], s_row, 0, to_y)
    row_core = remote(nf, rows_out.at[2], s_row, 1, to_core)
    row_next = remote(rows_out.at[1], rows_out.at[3], s_row, 2, to_core)

    trades[0].collect()
    fill_keys(recv.at[0], 0, ks, vs, heads)
    back0 = attend(0, 0, groups)
    x_exp[0].wait_recv()
    n_exp[0].start()
    x_out.wait_recv()
    c_out.start()
    y_gate.wait_recv()
    c_gate[1].start()
    for m in range(MICRO):
        y_cot[m].wait_recv()
        c_cot[MICRO + m].start()
    trades[1].collect()
    fill_keys(recv.at[1], 1, ks, vs, heads)
    for k in (2, 3):
        x_exp[k].wait_recv()
        n_exp[k - 1].start()
    back1 = attend(1, 0, 2)
    c_out.wait_recv()
    back0.collect()
    project_out(got.at[0], x_ref[0], wo.reshape(width, width), both[1], att, res, nf, heads)
    row_y.start()
    row_core.start()
    back1 = attend(1, 2, groups)
    row_y.wait_recv()
    row_next.start()
    for k in (1, 2):
        n_exp[k].wait_recv()
        n_exp[k + 2].start()
    keep = []
    for m in range(MICRO):
        keep += [(recv.at[m], recv_out[m]), (mixed.at[m], mixed_out[m]), (lse.at[m], lse_out[m])]
    keep += [(att, att_out), (res, res_out), (nf, rows_out.at[0])]
    keep += [(tags, tags_out), (wq, qkv_out), (wo, wout_out), (gains, gains_out), (table, table_out)]
    keep = [pltpu.make_async_copy(a, b, stores.at[3 + i]) for i, (a, b) in enumerate(keep)]
    for copy in keep:
        copy.start()
    back1.collect()
    got_copy = pltpu.make_async_copy(got.at[1], got_out, stores.at[3 + len(keep)])
    got_copy.start()
    for copy in (*keep, got_copy, *own_copies):
        copy.wait()
    for m in range(MICRO):
        trades[m].release()
    row_y.wait_send()
    row_core.wait()
    row_next.wait()
    back0.release()
    back1.release()
    x_exp[1].wait_recv()
    for copy in n_exp:
        copy.wait_send()
    for copy in (n_exp[0], n_exp[3], n_exp[4]):
        copy.wait_recv()
    for copy in (*c_gate, *c_cot):
        copy.wait()
    for copy in (*x_exp, x_qkv, x_gain, x_out, c_qkv, c_out, y_gate, *y_cot, *tag_trade):
        copy.wait_send()


def run_front(x, gains, blocks, keeps, gates, w_qkv, w_out, w_ein, w_eout, w_sin, w_sout, cot, groups):
    _, rows, width = x.shape
    heads = width // HEAD // groups
    k = width // 4
    tags = (groups, 2, MICRO, 1, rows)
    w_qkv = w_qkv.reshape(2, k, 3 * width)
    w_out = w_out.reshape(2, k, width)
    w_ein = w_ein.reshape(2, -1, w_ein.shape[1])
    w_sin, w_sout = [w.reshape(2, 2, -1, w.shape[1]) for w in (w_sin, w_sout)]
    vmem = pl.BlockSpec(memory_space=pltpu.VMEM)
    anywhere = pl.BlockSpec(memory_space=pl.ANY)
    packed = lambda n: (groups, n * heads, HALF, HALF)
    held = MICRO * groups * TILE
    twice = lambda *a: [struct(*a)] * 2
    outs = (
        twice(packed(3), BF)
        + twice(packed(1), BF)
        + twice((groups, 8, TILE), F32)
        + twice((4, rows, width), BF)
        + [
            struct((rows, width), BF),
            struct((rows, width), F32),
            struct((4, rows, width), BF),
            struct(packed(1), BF),
            struct((4, *gates.shape), F32),
            struct(tags, jnp.int32),
            struct((2, 2, k, 3 * width), BF),
            struct((2, 2, k, width), BF),
            struct(w_ein.shape, BF),
            struct(w_eout.shape, BF),
            struct(w_sin.shape, BF),
            struct(w_sout.shape, BF),
            struct((2, *gains.shape), F32),
            struct((2, MICRO * rows, HALF), F32),
        ]
    )
    v = pltpu.VMEM
    dma = lambda *n: pltpu.SemaphoreType.DMA(n)
    scratch = [
        v((2, 2, k, 3 * width), BF),
        v((2, 2, k, width), BF),
        v((2, *gains.shape), F32),
        v(tags, jnp.int32),
        v((MICRO, *packed(3)), BF),
        v((MICRO, *packed(3)), BF),
        v((heads, held, HALF), BF),
        v((heads, held, HALF), BF),
        v((heads, TILE, held), F32),
        v((MICRO, *packed(1)), BF),
        v((MICRO, *packed(1)), BF),
        v((MICRO, groups, 8, TILE), F32),
        v((rows, width), BF),
        v((rows, width), F32),
        v((rows, width), BF),
        v((2, MICRO * rows, HALF), F32),
    ]
    for shape in ((2,), (2,), (1,), (9,), (groups - 1,), (3,), (6,), (MICRO, groups), (MICRO, groups), (3,)):
        scratch += [dma(*shape), dma(*shape)]
    scratch += [dma(3), dma(MICRO), dma(MICRO), dma(3 + 3 * MICRO + 9)]
    return pl.pallas_call(
        functools.partial(front_kernel, heads=heads, groups=groups),
        out_shape=tuple(outs),
        in_specs=[vmem] * 5 + [anywhere] * 7,
        out_specs=(anywhere,) * len(outs),
        scratch_shapes=scratch,
        compiler_params=pltpu.CompilerParams(
            vmem_limit_bytes=VMEM_LIMIT, collective_id=3, has_side_effects=True
        ),
        cost_estimate=price(130),
    )(x, gains, blocks, keeps, gates, w_qkv, w_out, w_ein, w_eout, w_sin, w_sout, cot)


def ffn_kernel(*refs, tr, halves, gated, micro, summed, guest, guest_counts):
    refs = list(refs)
    take = lambda n: [refs.pop(0) for _ in range(n)]
    x_ref, dy_in = take(2)
    gate_in = take(1)[0] if gated else None
    wg_parts, wu_parts, wo_parts = take(2), take(2), take(2)
    g0 = take(3) if summed else None
    guest_in = take(guest_counts[0])
    y_ref, dx_ref, dwg_ref, dwu_ref, dwo_ref = take(5)
    guest_out = take(guest_counts[1])
    xt, yacc, dxacc, hs, djg, dju, wg_ref, wu_ref, wo_ref = take(9)
    dy_ref, gate_ref = take(2) if gated else (dy_in, None)
    f = pl.program_id(0)
    last = pl.num_programs(0) - 1
    rows = x_ref.shape[0]
    span = wg_parts[0].shape[0]
    dp = lax.axis_index("dp")
    visits = guest(guest_in, guest_out, refs) if guest else {}

    @pl.when(f == 0)
    def _():
        if 0 in visits:
            visits[0]()
        xt[...] = x_ref[...].T
        yacc[...] = jnp.zeros_like(yacc)
        dxacc[...] = jnp.zeros_like(dxacc)
        if gated:
            if micro is None:
                gate_ref[...] = gate_in[...]
            else:
                for block in range(gate_in.shape[0]):
                    row = gate_in[block, lax.axis_index("expert"), micro : micro + 1, :]
                    gate_ref[block * TILE : (block + 1) * TILE, :] = column(row)
            dy_ref[...] = (dy_in[...].astype(F32) * gate_ref[...]).astype(BF)

    for step, visit in visits.items():
        if step not in (0, "end"):
            pl.when(f == step)(visit)

    for index, part in enumerate((dp, 1 - dp)):
        place = pl.ds(pl.multiple_of(part * span, HALF // 2), span)
        wg_ref[place, :] = wg_parts[index][...]
        wu_ref[place, :] = wu_parts[index][...]

        @pl.when(f // halves == part)
        def _(index=index):
            wo_ref[...] = wo_parts[index][...]

    wg, wu, wo = wg_ref[...], wu_ref[...], wo_ref[...]

    def tile(i, carry):
        r = pl.ds(pl.multiple_of(i * tr, tr), tr)
        x = x_ref[r, :]
        g = dot(x, wg)
        u = dot(x, wu)
        dh = dot(dy_ref[r, :], wo, NT)
        sig = 1.0 / (1.0 + jnp.exp(-g))
        act = g * sig
        h = (act * u).astype(BF)
        dg = (dh * u * (sig * (1.0 + g * (1.0 - sig)))).astype(BF)
        du = (dh * act).astype(BF)
        hs[r, :] = h
        djg[r, :] = dg
        dju[r, :] = du
        yacc[r, :] += dot(h, wo)
        dxacc[r, :] += dot(dg, wg, NT) + dot(du, wu, NT)
        return carry

    lax.fori_loop(0, rows // tr, tile, 0)
    grads = [dot(xt[...], djg[...]), dot(xt[...], dju[...]), dot(hs[...], dy_ref[...], TN)]
    for k, out in enumerate((dwg_ref, dwu_ref, dwo_ref)):
        value = grads[k]
        if summed:
            value = value + g0[k][...].astype(F32)
        out[...] = value.astype(BF)

    @pl.when(f == last)
    def _():
        made = yacc[...].astype(BF)
        if gated:
            made = (made.astype(F32) * gate_ref[...]).astype(BF)
        y_ref[...] = made
        dx_ref[...] = dxacc[...].astype(BF)
        if "end" in visits:
            visits["end"]()


def run_ffn(x, dy, gate, w_in, w_out, grads=None, tr=512, fb=FB, us=10, guest=None):
    rows, d = x.shape
    ff = sum(w.shape[0] for w in w_out)
    nf = ff // fb
    halves = nf // 2
    gated = gate is not None
    gate, micro = gate if isinstance(gate, tuple) else (gate, None)
    whole = lambda a: pl.BlockSpec(a.shape, lambda f: (0,) * a.ndim, pipeline_mode=pl.Buffered(1))
    args = [x, dy] + ([gate] if gated else [])
    specs = [whole(a) for a in args]
    args += list(w_in) * 2 + list(w_out)
    span = w_in[0].shape[0]
    specs += [pl.BlockSpec((span, fb), lambda f: (0, f))] * 2
    specs += [pl.BlockSpec((span, fb), lambda f: (0, f + nf))] * 2
    specs += [pl.BlockSpec((fb, d), lambda f: (f % halves, 0))] * 2
    wide = pl.BlockSpec((d, fb), lambda f: (0, f))
    tall = pl.BlockSpec((fb, d), lambda f: (f, 0))
    if grads is not None:
        args += list(grads)
        specs += [wide, wide, tall]
    full = pl.BlockSpec((rows, d), lambda f: (0, 0), pipeline_mode=pl.Buffered(1))
    outs = [
        struct((rows, d), BF),
        struct((rows, d), BF),
        struct((d, ff), BF),
        struct((d, ff), BF),
        struct((ff, d), BF),
    ]
    out_specs = [full, full, wide, wide, tall]
    scratch = [
        pltpu.VMEM((d, rows), BF),
        pltpu.VMEM((rows, d), F32),
        pltpu.VMEM((rows, d), F32),
        pltpu.VMEM((rows, fb), BF),
        pltpu.VMEM((rows, fb), BF),
        pltpu.VMEM((rows, fb), BF),
        pltpu.VMEM((d, fb), BF),
        pltpu.VMEM((d, fb), BF),
        pltpu.VMEM((fb, d), BF),
    ] + ([pltpu.VMEM((rows, d), BF), pltpu.VMEM((rows, 1), F32)] if gated else [])
    anywhere = pl.BlockSpec(memory_space=pl.ANY)
    counts, visit, params = (0, 0), None, {}
    if guest is not None:
        visit, guest_args, guest_outs, guest_scratch, collective_id = guest
        args += [a for a, _ in guest_args]
        specs += [whole(a) if near else anywhere for a, near in guest_args]
        outs += guest_outs
        out_specs += [anywhere] * len(guest_outs)
        scratch += guest_scratch
        counts = (len(guest_args), len(guest_outs))
        params = {"collective_id": collective_id, "has_side_effects": True}
    return pl.pallas_call(
        functools.partial(
            ffn_kernel,
            tr=math.gcd(tr, rows),
            halves=halves,
            gated=gated,
            micro=micro,
            summed=grads is not None,
            guest=visit,
            guest_counts=counts,
        ),
        out_shape=tuple(outs),
        grid=(nf,),
        in_specs=specs,
        out_specs=tuple(out_specs),
        scratch_shapes=scratch,
        compiler_params=pltpu.CompilerParams(vmem_limit_bytes=VMEM_LIMIT, **params),
        cost_estimate=price(us),
    )(*args)


def rows_guest(ins, outs, bufs, *, heads):
    got, x_ref, w_ref, gain_ref, first_rows = ins
    att_out, res_out, rows_out, both_out = outs
    att, res, nf, sends, recvs, stores = bufs
    e = lax.axis_index("expert")
    core, y = e % 2, e // 2 % 2
    to_core, to_y = {"expert": e + 1 - 2 * core}, {"expert": e + 2 - 4 * y}
    wires = [
        remote(nf, rows_out.at[1], (sends, recvs), 0, to_y),
        remote(nf, rows_out.at[2], (sends, recvs), 1, to_core),
        remote(rows_out.at[1], rows_out.at[3], (sends, recvs), 2, to_core),
    ]
    keep = [
        (att, att_out),
        (res, res_out),
        (nf, rows_out.at[0]),
        (nf, both_out.at[1]),
        (first_rows.at[0], both_out.at[0]),
    ]
    keep = [pltpu.make_async_copy(a, b, stores.at[i]) for i, (a, b) in enumerate(keep)]

    def begin():
        meet(pltpu.get_barrier_semaphore(), [to_core, to_y])
        project_out(got, x_ref[1], w_ref, gain_row(gain_ref, 1), att, res, nf, heads)
        for copy in (wires[0], wires[1], *keep):
            copy.start()

    def later():
        wires[0].wait_recv()
        wires[2].start()

    def end():
        wires[0].wait_send()
        wires[1].wait()
        wires[2].wait()
        for copy in keep:
            copy.wait()

    return {0: begin, 2: later, "end": end}


def price(us):
    return pl.CostEstimate(flops=int(us * 1.15e9), bytes_accessed=0, transcendentals=0)


def norm_back(values, scale, gain, grad):
    gain_grad = jnp.sum(grad * values * scale, 0, keepdims=True)
    scaled = gain * grad
    grad_in = scale * scaled - values * (scale * scale * scale) * jnp.mean(
        scaled * values, -1, keepdims=True
    )
    return grad_in, gain_grad


def mid_core(grad, residual, gain, cot, w_ref, pay, gres_ref, gbf_ref, per):
    back, gain_grad = norm_back(residual, rms_scale(residual), gain, grad)
    total = cot.astype(F32) + back
    gres_ref[...] = total
    gbf_ref[...] = total.astype(BF)
    mixed = dot(gbf_ref[...], w_ref[...], NT)
    for pair in range(mixed.shape[1] // HALF):
        tile = mixed[:, pair * HALF : (pair + 1) * HALF]
        for side, packed in enumerate(swap_heads(tile[:HALF], tile[HALF:])):
            head = 2 * pair + side
            pay[head // per, head % per] = packed.astype(BF)
    return gain_grad


def finish(d0, d1, x_ref, gain_ref, w_ref, table, gres, atts, gbfs, gin_ref, gq, gv, go, gj, per):
    width = x_ref.shape[2]
    for micro, ref in enumerate((d0, d1)):
        rows = slice(micro * TILE, (micro + 1) * TILE)
        cosines, sines = table[0, rows, :], table[1, rows, :]
        for kind in range(3):
            for pair in range(width // HALF):
                tile = natural(ref, kind, pair, per)
                if kind == 0:
                    tile = tile * 0.125
                if kind < 2:
                    tile = rotate(tile, cosines, -sines)
                gj[rows, kind * width + pair * HALF : kind * width + (pair + 1) * HALF] = tile.astype(BF)
    tokens = x_ref[...].reshape(MICRO * TILE, width).astype(F32)
    scale = rms_scale(tokens)
    gain = gain_row(gain_ref, 0)
    turned = (tokens * scale * gain).astype(BF).T
    split = gq.shape[-1]
    gq[...] = dot(turned, gj[:, :split]).astype(BF).reshape(gq.shape)
    gv[...] = dot(turned, gj[:, split:]).astype(BF).reshape(gv.shape)
    go[...] = (dot(atts[0][...], gbfs[0], TN) + dot(atts[1][...], gbfs[1], TN)).astype(BF).reshape(go.shape)
    yield
    first = dot(gj[...], w_ref[...], NT)
    back, _ = norm_back(tokens, scale, gain, first)
    for micro in range(MICRO):
        rows = slice(micro * TILE, (micro + 1) * TILE)
        gin_ref[rows, :] = gres[micro] + back[rows]


def exchange(value, axis, mask):
    size = lax.axis_size(axis)
    return lax.ppermute(value, axis, [(i, i ^ mask) for i in range(size)])


def bits_of(size):
    return [1 << b for b in range(size.bit_length() - 1)]


def gather_rest(value):
    for mask in bits_of(lax.axis_size("expert"))[2:]:
        value = jnp.concatenate([value, exchange(value, "expert", mask)], 0)
    return value


def scatter_rest(value):
    for mask in reversed(bits_of(lax.axis_size("expert"))[2:]):
        half = value.shape[0] // 2
        got = exchange(value[half:], "expert", mask)
        value = (value[:half].astype(F32) + got.astype(F32)).astype(value.dtype)
    return value


def ordered(flag, mine, theirs):
    first = jnp.where(flag == 0, mine, theirs)
    second = jnp.where(flag == 0, theirs, mine)
    return jnp.concatenate([first, second], 0)


def pick(value, parts, index):
    size = value.shape[0] // parts
    return lax.dynamic_slice_in_dim(value, index * size, size, 0)


def after(value, token):
    return lax.optimization_barrier((value, token))[0]


PIECES = 4
FLIPPED = (1,)
EARLY = 7
AHEAD = 2
PLAN = {
    -1: ("rs1", "a0", "A0", "a1", "rs2", "A1", "a2", "B0", "rs3",),
    1: ("A2",),
    3: ("B1",),
    4: ("C0",),
    5: ("b1",),
    6: ("b0",),
    7: ("A3",),
    8: ("B2",),
    9: ("b2", "A4",),
    10: ("B3",),
    11: ("C1",),
    12: ("c0",),
    13: ("C2",),
    14: ("c1",),
    15: ("B4",),
    16: ("A5",),
    17: ("d0",),
    18: ("c2",),
    19: ("C3",),
    21: ("d1",),
    23: ("C4",),
    24: ("D3",),
    25: ("A6",),
    26: ("e0",),
    27: ("B5",),
    28: ("e1",),
    31: ("d2",),
    34: ("f1",),
    35: ("C5",),
    37: ("B6",),
    38: ("e2",),
    42: ("f0", "zhome", "C6", "D2", "A7", "g0", "A8", "D5", "f2", "g1", "A9", "D4", "g2", "h0", "h2", "h1", "A11", "D1", "A10", "D6", "D0",),
}
LAST_PLAN = (
    "A0", "A1", "A2", "A3", "B0", "a0", "B1", "C0", "a1", "a2",
    "b0", "B2", "C1", "b2", "D0", "B3", "b1", "C2", "c0", "c2",
    "d0", "c1", "A4", "C3", "f0", "d2", "d1", "e0", "B4", "f1",
    "g0", "e1", "f2", "e2", "D3", "zrest", "C4", "D2", "g1", "g2",
    "D1", "h0", "D4", "h1", "h2",
)


class Engine:
    def __init__(self, own, com, own_buf, com_buf, own_out, com_out, sems):
        self.flip = [i in FLIPPED for i in range(len(com))]
        self.own, self.com, self.own_buf, self.com_buf = own, com, own_buf, com_buf
        self.own_out, self.com_out = own_out, com_out
        e, z, d = lax.axis_index("expert"), lax.axis_index("context"), lax.axis_index("dp")
        groups = lax.axis_size("context")
        self.d, self.core, self.y = d, e % 2, e // 2 % 2
        self.outer = (z == 0) | (z == 3)
        self.inner = (z == 1) | (z == 2)
        self.to_x = {"dp": 1 - d}
        self.to_core = {"expert": e + 1 - 2 * self.core}
        self.to_y = {"expert": e + 2 - 4 * self.y}
        self.to_mate = {"context": z + 1 - 2 * (z % 2)}
        self.to_mid = {"context": 3 - z}
        self.others = [{"context": (z + k) % groups} for k in range(1, groups)]
        sems = list(sems)
        take = lambda n: [sems.pop(0) for _ in range(n)]
        self.o_load, self.o_store = take(2)
        self.o = {k: take(2) for k in "x123"}
        self.c_load, self.c_store = take(2)
        self.c = {k: take(2) for k in ("core", "y", "x", "1", "2", "3", "fore", "last")}

    @staticmethod
    def scratch(own_shapes, kinds, com_shapes):
        v, dma = pltpu.VMEM, lambda n: pltpu.SemaphoreType.DMA((max(n, 1),))
        tiny = (16, HALF)
        own_buf = []
        for s, kind in zip(own_shapes, kinds):
            own_buf += [v(s, BF), v(s if "x" in kind else tiny, BF)]
            own_buf += [v(s if "z" in kind else tiny, BF)] * 2
        com_buf = []
        for s in com_shapes:
            com_buf += [v((2, 2, *s), BF)] * 2 + [v((2, *s), BF)] + [v(s, BF)] * 3
        chunks, n = len(own_shapes), len(com_shapes)
        sems = [dma(chunks)] * 10 + [dma(2 * n), dma(n)] + [dma(2 * n)] * 4 + [dma(n)] * 12
        return own_buf, com_buf, sems

    def greet(self):
        meet(
            pltpu.get_barrier_semaphore(), [self.to_x, self.to_core, self.to_y, *self.others]
        )

    def o_wire(self, stage, c):
        total, r_x, r_1, r_2 = self.own_buf[c]
        src, k, _ = self.own[c]
        target = {"x": self.to_x, "1": self.to_mate, "2": self.to_mid, "3": self.to_mate}[stage]
        source = {"x": lambda: src.at[1 - self.d, k], "1": lambda: total, "2": lambda: total, "3": lambda: r_1}
        place = {"x": r_x, "1": r_1, "2": r_2, "3": self.own_out[c]}[stage]
        return remote(source[stage](), place, self.o[stage], c, target)

    def o_loading(self, c):
        src, k, kind = self.own[c]
        src = src.at[k] if kind == "z" else src.at[self.d, k]
        return pltpu.make_async_copy(src, self.own_buf[c][0], self.o_load.at[c])

    def o_storing(self, c):
        buf = self.own_buf[c][0 if self.own[c][2] == "x" else 2]
        return pltpu.make_async_copy(buf, self.own_out[c], self.o_store.at[c])

    def A(self, c):
        total, r_x = self.own_buf[c][:2]
        kind = self.own[c][2]
        self.o_loading(c).wait()
        if kind != "z":
            self.o_wire("x", c).wait_recv()
            if c + self.ahead < len(self.own):
                self.o_wire("x", c + self.ahead).start()
            total[...] = total[...] + r_x[...]
        if kind == "x":
            self.o_storing(c).start()
            return

        @pl.when(self.outer)
        def _():
            self.o_wire("1", c).start()

    def B(self, c):
        total, _, r_1, _ = self.own_buf[c]

        @pl.when(self.inner)
        def _():
            self.o_wire("1", c).wait_recv()
            total[...] = total[...] + r_1[...]
            self.o_wire("2", c).start()

    def C(self, c):
        total, _, r_1, r_2 = self.own_buf[c]

        @pl.when(self.inner)
        def _():
            self.o_wire("2", c).wait_recv()
            r_1[...] = total[...] + r_2[...]
            self.o_wire("3", c).start()
            self.o_storing(c).start()

    def D(self, c):
        @pl.when(self.outer)
        def _():
            self.o_wire("3", c).wait_recv()

    def c_loading(self, i, h):
        return pltpu.make_async_copy(
            self.com[i].at[h, self.core], self.com_buf[i][0].at[h], self.c_load.at[2 * i + h]
        )

    def c_storing(self, i):
        return pltpu.make_async_copy(
            self.com_buf[i][4], self.com_out[i].at[self.core, self.y], self.c_store.at[i]
        )

    def c_wire(self, stage, i, h=0):
        total, r_core, r_y, r_x, r_1, r_2 = self.com_buf[i]
        core, y, d = self.core, self.y, self.d
        out = self.com_out[i]
        if stage == "core":
            return remote(self.com[i].at[h, 1 - core], r_core.at[h], self.c["core"], 2 * i + h, self.to_core)
        if stage == "y" and self.flip[i]:
            return remote(total.at[1 - d, h], r_y.at[h], self.c["y"], 2 * i + h, self.to_x)
        if stage == "x" and self.flip[i]:
            return remote(total.at[d, 1 - y], r_x, self.c["x"], i, self.to_y)
        if stage == "y":
            return remote(total.at[h, 1 - y], r_y.at[h], self.c["y"], 2 * i + h, self.to_y)
        if stage == "x":
            return remote(total.at[1 - d, y], r_x, self.c["x"], i, self.to_x)
        if stage == "1":
            return remote(total.at[d, y], r_1, self.c["1"], i, self.to_mate)
        if stage == "2":
            return remote(total.at[d, y], r_2, self.c["2"], i, self.to_mid)
        if stage == "3":
            return remote(r_1, out.at[core, y], self.c["3"], i, self.to_mate)
        if stage == "fore":
            return remote(r_1, out.at[core, y], self.c["fore"], i, self.to_y)
        if stage == "back":
            return remote(out.at[core, y], out.at[core, y], self.c["fore"], i, self.to_y)
        return remote(out.at[core], out.at[core], self.c["last"], i, self.to_core)

    def c_start(self, i):
        for h in range(2):
            self.c_wire("core", i, h).start()
            self.c_loading(i, h).start()

    def a(self, i):
        total, r_core = self.com_buf[i][:2]
        for h in range(2):
            self.c_loading(i, h).wait()
            self.c_wire("core", i, h).wait_recv()
        total[...] = total[...] + r_core[...]
        for h in range(2):
            self.c_wire("y", i, h).start()

    def b(self, i):
        total, r_y, y = self.com_buf[i][0], self.com_buf[i][2], self.y
        for h in range(2):
            self.c_wire("y", i, h).wait_recv()
            if self.flip[i]:
                total[self.d, h] = total[self.d, h] + r_y[h]
            else:
                total[h, y] = total[h, y] + r_y[h]
        self.c_wire("x", i).start()

    def c_(self, i):
        total, r_x, y, d = self.com_buf[i][0], self.com_buf[i][3], self.y, self.d
        self.c_wire("x", i).wait_recv()
        total[d, y] = total[d, y] + r_x[...]

        @pl.when(self.outer)
        def _():
            self.c_wire("1", i).start()

    def d_(self, i):
        total, r_1, y, d = self.com_buf[i][0], self.com_buf[i][4], self.y, self.d

        @pl.when(self.inner)
        def _():
            self.c_wire("1", i).wait_recv()
            total[d, y] = total[d, y] + r_1[...]
            self.c_wire("2", i).start()

    def e(self, i):
        total, r_1, r_2 = self.com_buf[i][0], self.com_buf[i][4], self.com_buf[i][5]

        @pl.when(self.inner)
        def _():
            self.c_wire("2", i).wait_recv()
            r_1[...] = total[self.d, self.y] + r_2[...]
            self.c_wire("3", i).start()
            self.c_wire("fore", i).start()
            self.c_storing(i).start()

    def f(self, i):
        @pl.when(self.outer)
        def _():
            self.c_wire("3", i).wait_recv()
            self.c_wire("back", i).start()

    def g(self, i):
        @pl.when(self.inner)
        def _():
            self.c_storing(i).wait()

        self.c_wire("fore", i).wait_recv()
        self.c_wire("last", i).start()

    def h(self, i):
        self.c_wire("last", i).wait_recv()

    def start(self, ahead, com=True):
        self.ahead = ahead
        for c in range(min(ahead, len(self.own))):
            if self.own[c][2] != "z":
                self.o_wire("x", c).start()
        if com:
            for i in range(len(self.com)):
                self.c_start(i)
        for c in range(len(self.own)):
            self.o_loading(c).start()

    def run(self, name):
        kind, index = name[0], int(name[1:])
        {"c": self.c_, "d": self.d_}.get(kind, getattr(self, kind, None))(index)

    def close(self):
        chunks, common = range(len(self.own)), range(len(self.com))
        for c in chunks:
            if self.own[c][2] != "z":
                self.o_wire("x", c).wait_send()
            if self.own[c][2] == "x":
                self.o_storing(c).wait()
        chunks = [c for c in chunks if self.own[c][2] != "x"]
        for i in common:
            for h in range(2):
                self.c_wire("core", i, h).wait_send()
                self.c_wire("y", i, h).wait_send()
            self.c_wire("x", i).wait_send()
            self.c_wire("last", i).wait_send()

        @pl.when(self.outer)
        def _():
            for c in chunks:
                self.o_wire("1", c).wait_send()
            for i in common:
                self.c_wire("1", i).wait_send()
                self.c_wire("back", i).wait_send()

        @pl.when(self.inner)
        def _():
            for c in chunks:
                self.o_wire("2", c).wait_send()
                self.o_wire("3", c).wait_send()
                self.o_storing(c).wait()
            for i in common:
                self.c_wire("2", i).wait_send()
                self.c_wire("3", i).wait_send()
                self.c_wire("fore", i).wait_send()


class Arrays:
    def __init__(self, refs):
        self.refs = list(refs)

    def take(self, n):
        got, self.refs = self.refs[:n], self.refs[n:]
        return got

    def engine(self, own_at, sources, own_out, com, com_out):
        own_buf = [self.take(4) for _ in own_at]
        com_buf = [self.take(6) for _ in com]
        own = [(sources[j], k, kind) for j, k, kind in own_at]
        places = [own_out[j].at[k] for j, k, _ in own_at]
        return Engine(own, com, own_buf, com_buf, places, com_out, self.take(10 + 18))


def back_kernel(*refs, own_at, sources, common, heads, groups):
    refs = Arrays(refs)
    own_in, com_in = refs.take(sources), refs.take(common)
    recv0, recv1, out0, out1, lse0, lse1, tags = refs.take(7)
    dxs, res0, res1, gain_ref, cot_ref, w_ref = refs.take(6)
    dx_made = refs.take(MICRO)
    own_out, com_out = refs.take(sources), refs.take(common)
    d0_out, d1_out, gres_out, gbf_out, gg_out = refs.take(5)
    engine = refs.engine(own_at, own_in, own_out, com_in, com_out)
    dx, r_core, r_y, gres, gbf, gg, pay_o, back_o, pay0, pay1 = refs.take(10)
    ks, vs, dk, dv, qs, gs, deltas, acc = refs.take(8)
    s_dx, s_o, s_0, s_1 = [refs.take(2) for _ in range(4)]
    local, = refs.take(1)

    engine.greet()
    both = range(MICRO)
    send_core = [remote(dx_made[m].at[2:4], r_core.at[m], s_dx, m, engine.to_core) for m in both]
    own_dx = [pltpu.make_async_copy(dx_made[m].at[0:2], dx.at[m], local.at[m]) for m in both]
    for m in both:
        send_core[m].start()
        own_dx[m].start()
    engine.start(AHEAD)
    send_y = [remote(dx.at[m, 1], r_y.at[m], s_dx, MICRO + m, engine.to_y) for m in both]
    trade_o = [
        Trade(pay_o.at[m], back_o.at[m], [s.at[m] for s in s_o], local.at[2 + m]) for m in both
    ]
    homes = [Trade(pay0, d0_out, s_0, local.at[4]), Trade(pay1, d1_out, s_1, local.at[5])]
    results = [
        pltpu.make_async_copy(a, b, local.at[6 + i])
        for i, (a, b) in enumerate(((gres, gres_out), (gbf, gbf_out), (gg, gg_out)))
    ]

    def rs1():
        for m in both:
            own_dx[m].wait()
            send_core[m].wait_recv()
            dx[m] = dx[m] + r_core[m]
            send_y[m].start()

    def middle(m, res_ref):
        send_y[m].wait_recv()
        grad = dxs[m * TILE : (m + 1) * TILE, :].astype(F32) + dx[m, 0].astype(F32) + r_y[m].astype(F32)
        part = mid_core(
            grad, res_ref[...], gain_row(gain_ref, 1), cot_ref[m], w_ref, pay_o.at[m], gres.at[m], gbf.at[m], heads
        )
        for dest in range(groups):
            trade_o[m].send(dest)
        return part

    def rs2():
        gg[...] = middle(0, res0)

    def rs3():
        gg[...] = gg[...] + middle(1, res1)
        for copy in results:
            copy.start()

    def zhome():
        for base, pay, trade in ((groups, pay1, homes[1]), (0, pay0, homes[0])):
            for dest in range(groups):
                back_pack(dk, dv, pay, dest, base, heads)
                trade.send(dest)

    named = {"rs1": rs1, "rs2": rs2, "rs3": rs3, "zhome": zhome}

    def events(slot):
        for name in PLAN.get(slot, ()):
            named[name]() if name in named else engine.run(name)

    for recv, micro in ((recv0, 0), (recv1, 1)):
        fill_keys(recv, micro, ks, vs, heads)
    dk[...] = jnp.zeros_like(dk)
    dv[...] = jnp.zeros_like(dv)
    first_of = (0, sum(min(s + 2, groups) for s in range(groups)))
    total = 2 * first_of[1] + groups * groups
    for micro, (recv, grad, out, lse, pay) in enumerate(
        ((recv0, back_o.at[0], out0, lse0, pay0), (recv1, back_o.at[1], out1, lse1, pay1))
    ):
        begin, end = first_of[micro], (first_of + (total,))[micro + 1]
        if micro == 0:
            events(-1)
        trade_o[micro].collect()

        def step(s, carry, micro=micro, recv=recv, grad=grad, out=out, lse=lse, pay=pay, begin=begin, end=end):
            back_begin(micro, s, heads, recv, grad, out, qs, gs, deltas, acc)
            before = begin + s * (s + 3) // 2 + groups * micro * s

            def tile(j, carry):
                for slot in range(begin, end):
                    if slot in PLAN:

                        @pl.when(before + j == slot)
                        def _(slot=slot):
                            events(slot)

                back_tile(
                    micro, s, j, heads, groups, lse, tags, ks, vs, dk, dv, qs, gs, deltas, acc
                )
                return carry

            lax.fori_loop(0, groups * micro + jnp.minimum(s + 2, groups), tile, 0)
            for h in range(heads):
                pay[s, h] = pack_rows(acc[h]).astype(BF)
            return carry

        lax.fori_loop(0, groups, step, 0)
    events(total)
    for trade in homes:
        trade.collect()
        trade.release()
    for m in both:
        trade_o[m].release()
        send_core[m].wait_send()
        send_y[m].wait_send()
    for copy in results:
        copy.wait()
    engine.close()


def chunk_views(grads):
    return [g.reshape(2, PIECES, g.shape[0] // (2 * PIECES), g.shape[1]) for g in grads]


def shared_shape(shape):
    return (2, 2, 2, shape[0] // 8, shape[1])


def device_call(kernel, args, vmem_args, outs, scratch, collective_id, us, aliases=None):
    anywhere = pl.BlockSpec(memory_space=pl.ANY)
    return pl.pallas_call(
        kernel,
        out_shape=tuple(outs),
        in_specs=[pl.BlockSpec(memory_space=pltpu.VMEM) if v else anywhere for v in vmem_args],
        out_specs=(anywhere,) * len(outs),
        scratch_shapes=scratch,
        input_output_aliases=aliases or {},
        compiler_params=pltpu.CompilerParams(
            vmem_limit_bytes=VMEM_LIMIT, collective_id=collective_id, has_side_effects=True
        ),
        cost_estimate=price(us),
    )(*args)


def rest_sum(value):
    for mask in bits_of(lax.axis_size("expert"))[2:]:
        value = value + exchange(value, "expert", mask)
    return value


def run_back(expert_grads, own_at, shared_grads, attention, middle, dx_made, groups):
    own = chunk_views(expert_grads)
    com = [g.reshape(shared_shape(g.shape)) for g in shared_grads]
    heads = attention[0].shape[1] // 3
    rows, width = middle[1].shape
    args = [*own, *com, *attention, *middle, *dx_made]
    own_shapes = [own[j].shape[2:] for j, _, _ in own_at]
    com_shapes = [g.shape[3:] for g in com]
    own_buf, com_buf, sems = Engine.scratch(own_shapes, [kind for *_, kind in own_at], com_shapes)
    held = MICRO * groups * TILE
    v, dma = pltpu.VMEM, lambda n: pltpu.SemaphoreType.DMA((n,))
    pay = lambda n: (groups, n * heads, HALF, HALF)
    outs = (
        [struct(g.shape[1:], BF) for g in own]
        + [struct((2, 2, *s), BF) for s in com_shapes]
        + [struct(pay(3), BF)] * 2
        + [struct((MICRO, rows, width), F32), struct((MICRO, rows, width), BF), struct((1, width), F32)]
    )
    scratch = [
        *own_buf,
        *com_buf,
        *sems,
        v((MICRO, 2, rows, width), BF),
        v((MICRO, 2, rows, width), BF),
        v((MICRO, rows, width), BF),
        v((MICRO, rows, width), F32),
        v((MICRO, rows, width), BF),
        v((1, width), F32),
        v((MICRO, *pay(1)), BF),
        v((MICRO, *pay(1)), BF),
        v(pay(3), BF),
        v(pay(3), BF),
        v((heads, held, HALF), BF),
        v((heads, held, HALF), BF),
        v((heads, held, HALF), F32),
        v((heads, held, HALF), F32),
        v((heads, TILE, HALF), BF),
        v((heads, TILE, HALF), BF),
        v((heads, 8, TILE), F32),
        v((heads, TILE, HALF), F32),
        dma(2 * MICRO),
        dma(2 * MICRO),
        *[pltpu.SemaphoreType.DMA((MICRO, groups))] * 2,
        *[dma(groups)] * 4,
        dma(9),
    ]
    flags = [False] * (len(own) + len(com)) + [True] * (len(attention) + len(middle))
    flags += [False] * len(dx_made)
    kernel = functools.partial(
        back_kernel, own_at=own_at, sources=len(own), common=len(com), heads=heads, groups=groups
    )
    got = device_call(kernel, args, flags, outs, scratch, 1, 165)
    n, m = len(own), len(com)
    return got[:n], [rest_sum(g.reshape(-1, g.shape[-1]).astype(F32)) for g in got[n : n + m]], got[n + m :]


def last_kernel(*refs, own_at, sources, per):
    refs = Arrays(refs)
    own_in = refs.take(sources)
    d0, d1, x_ref, gain_ref, w_ref, table = refs.take(6)
    (gres, gbfs, gg_in), atts, made = refs.take(3), refs.take(2), refs.take(MICRO)
    own_out, com_out = refs.take(sources), refs.take(3)
    gin_out, gg_out, routed_out = refs.take(3)
    sources = [refs.refs.pop(len(own_at) * 4 + 3 * 6 + 28) for _ in range(3)]
    engine = refs.engine(own_at, own_in, own_out, sources, com_out)
    gj, gin, gg_sum, gg_got, g_send, g_recv, local, row, row_core, row_y, m_send, m_recv = refs.take(12)
    engine.greet()
    engine.start(0, com=False)
    z = lax.axis_index("context")
    rounds = (engine.to_core, engine.to_y, engine.to_x, engine.to_mate, {"context": z + 2 - 4 * (z // 2)})
    wires = [
        remote(gg_sum.at[k], gg_got.at[k], (g_send, g_recv), k, target) for k, target in enumerate(rounds)
    ]
    gg_sum[0] = jnp.broadcast_to(gg_in[...], gg_sum.shape[1:])
    wires[0].start()
    both = range(MICRO)
    row_wires = [remote(made[m].at[2:4], row_core.at[m], (m_send, m_recv), m, engine.to_core) for m in both]
    row_next = [remote(row.at[m, 1], row_y.at[m], (m_send, m_recv), MICRO + m, engine.to_y) for m in both]
    row_own = [pltpu.make_async_copy(made[m].at[0:2], row.at[m], local.at[2 + m]) for m in both]
    row_out = [pltpu.make_async_copy(row.at[m, 0], routed_out.at[m], local.at[2 + m]) for m in both]
    for m in both:
        row_wires[m].start()
        row_own[m].start()
    work = finish(
        d0, d1, x_ref, gain_ref, w_ref, table, gres, atts, gbfs, gin, *sources, gj, per
    )
    store = pltpu.make_async_copy(gin, gin_out, local.at[0])
    next(work)
    for i in range(3):
        engine.c_start(i)
    turn = 0
    for index, name in enumerate(LAST_PLAN):
        if name == "zrest":
            for _ in work:
                pass
            store.start()
        else:
            engine.run(name)
        if index == 12:
            for m in both:
                row_own[m].wait()
                row_wires[m].wait_recv()
                row[m] = row[m] + row_core[m]
                row_next[m].start()
        if index == 30:
            for m in both:
                row_next[m].wait_recv()
                row[m, 0] = row[m, 0] + row_y[m]
                row_out[m].start()
        if index % 5 == 4 and turn < len(wires):
            wires[turn].wait_recv()
            gg_sum[turn + 1] = gg_sum[turn] + gg_got[turn]
            turn += 1
            if turn < len(wires):
                wires[turn].start()
    total = pltpu.make_async_copy(gg_sum.at[len(wires)], gg_out, local.at[1])
    total.start()
    store.wait()
    total.wait()
    for wire in (*wires, *row_wires, *row_next):
        wire.wait_send()
    for copy in row_out:
        copy.wait()
    engine.close()


def run_last(sums, own_at, parts, made, groups):
    x, w = parts[2], parts[4]
    _, rows, width = x.shape
    args = [*sums, *parts, *made]
    own_shapes = [sums[j].shape[1:] for j, _, _ in own_at]
    com = [shared_shape((width, 3 * width // 2))] * 2 + [shared_shape((width, width))]
    own_buf, com_buf, sems = Engine.scratch(own_shapes, [k for *_, k in own_at], [s[3:] for s in com])
    v = pltpu.VMEM
    outs = (
        [struct(g.shape, BF) for g in sums]
        + [struct((2, 2, *s[3:]), BF) for s in com]
        + [struct((MICRO * rows, width), F32), struct((8, width), F32), struct((MICRO, rows, width), BF)]
    )
    rounds = 5
    scratch = [
        *own_buf,
        *com_buf,
        *sems,
        *[v(s, BF) for s in com],
        v((MICRO * rows, 3 * width), BF),
        v((MICRO * rows, width), F32),
        v((rounds + 1, 8, width), F32),
        v((rounds, 8, width), F32),
        *[pltpu.SemaphoreType.DMA((rounds,))] * 2,
        pltpu.SemaphoreType.DMA((2 + MICRO,)),
        v((MICRO, 2, rows, width), BF),
        v((MICRO, 2, rows, width), BF),
        v((MICRO, rows, width), BF),
        *[pltpu.SemaphoreType.DMA((2 * MICRO,))] * 2,
    ]
    flags = [False] * len(sums) + [True] * len(parts) + [False] * len(made)
    kernel = functools.partial(
        last_kernel, own_at=own_at, sources=len(sums), per=width // HEAD // groups
    )
    got = device_call(
        kernel, args, flags, outs, scratch, 2, 90, {i: i for i in range(len(sums))}
    )
    n = len(sums)
    return got[:n], [rest_sum(g.reshape(-1, g.shape[-1]).astype(F32)) for g in got[n : n + 3]], *got[n + 3 :]


def body(
    inputs,
    keep_flags,
    block_ids,
    expert_ids,
    gate_weights,
    norm_attn,
    w_qkv,
    w_attn_out,
    norm_ffn,
    w_shared_in,
    w_shared_out,
    w_expert_in,
    w_expert_out,
    cotangent,
):
    width = w_qkv.shape[1] // 3
    rows = inputs.shape[2]
    groups = lax.axis_size("context")
    experts = lax.axis_size("expert")
    z = lax.axis_index("context")
    seq_rows = rows * groups
    x = inputs[0]
    cot = cotangent[0].reshape(MICRO * rows, width)

    per_expert = jnp.sum(
        jnp.where(
            expert_ids[0][None] == jnp.arange(experts, dtype=jnp.int32)[:, None, None, None],
            gate_weights[0][None],
            0.0,
        ),
        -1,
    )
    gains = jnp.stack([norm_attn, norm_ffn]).astype(F32)
    (
        *pairs,
        att0,
        res0,
        rows0,
        got1,
        gates_four,
        all_tags,
        mat_qkv,
        mat_out,
        ein_parts,
        eout_other,
        sin_parts,
        sout_parts,
        gains,
        table,
    ) = run_front(
        x,
        gains,
        block_ids,
        keep_flags,
        per_expert,
        w_qkv,
        w_attn_out,
        w_expert_in[0],
        w_expert_out[0],
        w_shared_in,
        w_shared_out,
        cotangent[0],
        groups,
    )
    recvs, mixed, lses, cot_four = [pairs[2 * i : 2 * i + 2] for i in range(4)]
    mat_qkv = mat_qkv.reshape(width, -1)
    mat_out = mat_out.reshape(width, width)
    core = lax.axis_index("expert") % 2
    dp = lax.axis_index("dp")
    whole = lambda w: w.reshape(-1, w.shape[-1])
    ein_parts = (w_expert_in[0], whole(ein_parts))
    eout_parts = (w_expert_out[0], eout_other)
    sin_parts = (w_shared_in, whole(sin_parts))
    sout_parts = (w_shared_out, whole(sout_parts))

    capacity = 4 * rows // experts

    def expert_pass(m, four, grads, guest=None, token=None):
        hidden = gather_rest(four).reshape(-1, width)
        if token is not None:
            hidden = after(hidden, token)
        grad, weight = gather_rest(cot_four[m]).reshape(-1, width), (gates_four, m)
        if capacity < rows:
            weight = lax.dynamic_index_in_dim(
                gather_rest(gates_four)[:, :, m], lax.axis_index("expert"), 1, False
            )
            chosen = weight > 0
            slots = jnp.cumsum(chosen.astype(jnp.int32), 1) - 1
            select = (
                chosen[:, None] & (slots[:, None] == jnp.arange(capacity, dtype=jnp.int32)[:, None])
            ).astype(BF)
            squeeze = lambda v: jnp.einsum("bcr,brd->bcd", select, v.reshape(-1, rows, width)).reshape(-1, width)
            spread = lambda v: jnp.einsum("bcr,bcd->brd", select, v.reshape(-1, capacity, width)).reshape(-1, width)
            hidden, grad = squeeze(hidden), squeeze(grad)
            weight = jnp.sum(select.astype(F32) * weight.reshape(-1, 1, rows), -1).reshape(-1, 1)
        made, dx, *rest = run_ffn(
            hidden, grad, weight, ein_parts, eout_parts, grads=grads, us=42, guest=guest
        )
        if capacity < rows:
            made, dx = spread(made), spread(dx)
        return made, dx, rest[:3], rest[3:]

    heads = width // HEAD // groups
    buf, dma = pltpu.VMEM, pltpu.SemaphoreType.DMA
    guest = (
        functools.partial(rows_guest, heads=heads),
        ((got1, True), (x, True), (mat_out, True), (gains, True), (rows0, False)),
        [
            struct((rows, width), BF),
            struct((rows, width), F32),
            struct((4, rows, width), BF),
            struct((MICRO, rows, width), BF),
        ],
        [buf((rows, width), BF), buf((rows, width), F32), buf((rows, width), BF), dma((3,)), dma((3,)), dma((5,))],
        4,
    )
    made0, dx0, g_expert, (att1, res1, rows1, nf_both) = expert_pass(0, rows0, None, guest)
    att, res = (att0, att1), (res0, res1)
    shared, dx_shared, *g_shared = run_ffn(
        nf_both.reshape(-1, width), cot, None, sin_parts, sout_parts, us=23
    )
    made1, dx1, g_expert, _ = expert_pass(1, rows1, g_expert, None, dx_shared)
    dx0, dx1, made0, made1 = [scatter_rest(v).reshape(4, rows, width) for v in (dx0, dx1, made0, made1)]

    spread = [(j, k) for j in range(3) for k in range(PIECES)]
    early = [(j, k, "xz" if i < EARLY else "x") for i, (j, k) in enumerate(spread)]
    first = spread[EARLY][0]
    late = [(j - first, k, "z") for j, k in spread[EARLY:]]
    attention = (*recvs, *mixed, *lses, all_tags)
    own_sums, (r_gate, r_up, r_sout), (d0, d1, gres, gbf, gg) = run_back(
        g_expert,
        early,
        g_shared,
        attention,
        (dx_shared, *res, gains, cotangent[0], mat_out),
        (dx0, dx1),
        groups,
    )
    own_late, (r_qk, r_v, r_out), grad_input, gain_sum, routed = run_last(
        own_sums[first:],
        late,
        (d0, d1, x, gains, mat_qkv, table, gres, gbf, gg, *att),
        (made0, made1),
        groups,
    )
    output = jnp.stack(
        [
            (res[m] + shared[m * rows : (m + 1) * rows].astype(F32) + routed[m].astype(F32)).astype(BF)
            for m in range(MICRO)
        ]
    )
    r_gain_ffn = pick(rest_sum(gain_sum)[0], 2, dp)
    r_qkv = jnp.concatenate([r_qk, r_v], 1)
    r_sin = jnp.concatenate([r_gate, r_up], 1)
    r_gain_attn = jnp.sum(w_qkv.astype(F32) * r_qkv, 1) / norm_attn.astype(F32)
    e_gate, e_up, r_eout = [
        g.reshape(-1, g.shape[-1]).astype(F32) for g in (*own_sums[:first], *own_late)
    ]
    r_ein = jnp.concatenate([e_gate, e_up], 1)
    return (
        output[None],
        grad_input.reshape(1, MICRO, rows, width),
        r_gain_attn,
        r_qkv,
        r_out,
        r_gain_ffn,
        r_sin,
        r_sout,
        r_ein[None],
        r_eout[None],
    )


def solution(mesh):
    tokens = P(("expert", "dp"), None, "context", None)
    flags = P(("expert", "dp"), None, "context")
    placed = (
        tokens,
        flags,
        flags,
        tokens,
        tokens,
        P("dp"),
        P("dp", None),
        P("dp", None),
        P("dp"),
        P("dp", None),
        P("dp", None),
        P("expert", "dp", None),
        P("expert", "dp", None),
        tokens,
    )
    return jax.shard_map(
        body,
        mesh=mesh,
        in_specs=placed,
        out_specs=(
            tokens,
            tokens,
            P("dp"),
            P("dp", None),
            P("dp", None),
            P("dp"),
            P("dp", None),
            P("dp", None),
            P("expert", "dp", None),
            P("expert", "dp", None),
        ),
        check_vma=False,
    )
```

```python
import functools
import math

import jax
import jax.numpy as jnp
from jax import lax
from jax.experimental import pallas as pl
from jax.experimental.pallas import tpu as pltpu
from jax.sharding import PartitionSpec as P

HEAD = 64
MICRO = 2
TILE = 256
HALF = 128
EPSILON = 1e-05
ROPE_BASE = 10000.0
MASKED = -3e30
HIDDEN = 1 << 20
BF = jnp.bfloat16
F32 = jnp.float32
NT = (((1,), (1,)), ((), ()))
TN = (((0,), (0,)), ((), ()))
VMEM_LIMIT = 60 << 20
FB = 512


def dot(left, right, dims=(((1,), (0,)), ((), ()))):
    return lax.dot_general(left, right, dims, preferred_element_type=F32)


def rms_scale(values):
    return lax.rsqrt(jnp.mean(values * values, -1, keepdims=True) + EPSILON)


def low_lanes(rows):
    return lax.broadcasted_iota(jnp.int32, (rows, HALF), 1) < HEAD


def swap_heads(first, second):
    low = low_lanes(HALF)
    return (
        jnp.where(low, first, pltpu.roll(second, HEAD, 1)),
        jnp.where(low, pltpu.roll(first, HEAD, 1), second),
    )


def rotate(tile, cosines, sines):
    lane = lax.broadcasted_iota(jnp.int32, tile.shape, 1)
    partner = jnp.where(
        lane % HEAD < HEAD // 2,
        pltpu.roll(tile, HALF - HEAD // 2, 1),
        pltpu.roll(tile, HEAD // 2, 1),
    )
    return tile * cosines + partner * sines


def struct(shape, dtype):
    return jax.ShapeDtypeStruct(tuple(shape), dtype)


def project(tokens, gain, w_ref, cosines, sines, pay, groups):
    normed = (tokens * rms_scale(tokens) * gain).astype(BF)
    width = tokens.shape[1]
    per = width // HEAD // groups
    for kind in range(3):
        joined = dot(normed, w_ref[:, kind * width : (kind + 1) * width])
        for pair in range(width // HALF):
            tile = joined[:, pair * HALF : (pair + 1) * HALF]
            if kind < 2:
                tile = rotate(tile, cosines, sines)
            if kind == 0:
                tile = tile * 0.125
            for side, packed in enumerate(swap_heads(tile[:HALF], tile[HALF:])):
                head = 2 * pair + side
                pay[head // per, kind * per + head % per] = packed.astype(BF)


def unpack(ref, index, kind_head):
    tile = ref[index, kind_head]
    return tile, pltpu.roll(tile.astype(F32), HEAD, 1).astype(BF)


def fill_keys(recv, micro, ks, vs, heads):
    groups = recv.shape[0]
    for src in range(groups):
        base = (micro * groups + src) * TILE
        for h in range(heads):
            for store, kind in ((ks, 1), (vs, 2)):
                first, second = unpack(recv, src, kind * heads + h)
                store[h, base : base + HALF] = first
                store[h, base + HALF : base + TILE] = second


def column(row):
    return jnp.broadcast_to(row, (8, row.shape[1])).T[:, :1]


def gain_row(gains, which):
    return jnp.concatenate([gains[0, which : which + 1], gains[1, which : which + 1]], 1)


def masked_rows(ref, index, kind_head):
    tile = ref[index, kind_head].astype(F32)
    both = jnp.concatenate([tile, pltpu.roll(tile, HEAD, 1)], 0)
    return jnp.where(low_lanes(TILE), both, 0.0)


def pack_rows(values):
    return jnp.where(low_lanes(HALF), values[:HALF], pltpu.roll(values[HALF:], HEAD, 1))


def attend_step(step, micro, heads, groups, recv, tags, out_ref, lse_ref, ks, vs, scores):
    count = groups * micro + jnp.minimum(step + 2, groups)
    queries = [masked_rows(recv, step, h).astype(BF) for h in range(heads)]
    tag = column(tags[step, 0, micro])
    same = lax.broadcasted_iota(jnp.int32, (TILE, TILE), 0) == lax.broadcasted_iota(
        jnp.int32, (TILE, TILE), 1
    )

    def first_pass(j, tops):
        keys = pl.ds(pl.multiple_of(j * TILE, TILE), TILE)
        key_tag = tags[j % groups, 1, j // groups]
        seen = (key_tag <= tag) | (same & (j == groups * micro + step))
        new = []
        for h in range(heads):
            part = jnp.where(seen, dot(queries[h], ks[h, keys, :], NT), MASKED)
            scores[h, :, keys] = part
            new.append(jnp.maximum(tops[h], jnp.maximum(part[:, :HALF], part[:, HALF:])))
        return tuple(new)

    tops = lax.fori_loop(
        0, count, first_pass, (jnp.full((TILE, HALF), MASKED, F32),) * heads
    )
    tops = [jnp.max(top, 1, keepdims=True) for top in tops]

    def second_pass(j, carry):
        keys = pl.ds(pl.multiple_of(j * TILE, TILE), TILE)
        sums, totals = carry
        new_sums, new_totals = [], []
        for h in range(heads):
            expo = jnp.exp(scores[h, :, keys] - tops[h])
            new_sums.append(sums[h] + (expo[:, :HALF] + expo[:, HALF:]))
            new_totals.append(totals[h] + dot(expo.astype(BF), vs[h, keys, :]))
        return tuple(new_sums), tuple(new_totals)

    zero = (jnp.zeros((TILE, HALF), F32),) * heads
    sums, totals = lax.fori_loop(0, count, second_pass, (zero, zero))
    lane = lax.broadcasted_iota(jnp.int32, (TILE, HALF), 1)
    logs = jnp.zeros((TILE, HALF), F32)
    for h in range(heads):
        total = jnp.sum(sums[h], 1, keepdims=True)
        out_ref[step, h] = pack_rows(totals[h] / total).astype(BF)
        logs = jnp.where(lane == h, tops[h] + jnp.log(total), logs)
    lse_ref[step] = logs.T[:8]


def back_begin(micro, step, heads, recv, grad, out, qs, gs, deltas, acc):
    ones = jnp.ones((8, HALF), F32)
    for h in range(heads):
        grad_f = masked_rows(grad, step, h)
        qs[h] = masked_rows(recv, step, h).astype(BF)
        gs[h] = grad_f.astype(BF)
        deltas[h] = lax.dot_general(
            ones,
            grad_f * masked_rows(out, step, h),
            NT,
            precision=lax.Precision.HIGHEST,
            preferred_element_type=F32,
        )
    acc[...] = jnp.zeros_like(acc)


def back_tile(micro, step, j, heads, groups, lse, tags, ks, vs, dk, dv, qs, gs, deltas, acc):
    keys = pl.ds(pl.multiple_of(j * TILE, TILE), TILE)
    same = lax.broadcasted_iota(jnp.int32, (TILE, TILE), 0) == lax.broadcasted_iota(
        jnp.int32, (TILE, TILE), 1
    )
    key_tag = column(tags[j % groups, 1, j // groups])
    seen = (key_tag <= tags[step, 0, micro]) | (same & (j == groups * micro + step))
    for h in range(heads):
        key, value = ks[h, keys, :], vs[h, keys, :]
        scores = dot(key, qs[h], NT)
        probs = jnp.where(seen, jnp.exp(scores - lse[step, h : h + 1, :]), 0.0)
        dv[h, keys, :] += dot(probs.astype(BF), gs[h])
        slope = (probs * (dot(value, gs[h], NT) - deltas[h, :1])).astype(BF)
        dk[h, keys, :] += dot(slope, qs[h])
        acc[h] += dot(slope, key, TN)


def back_pack(dk, dv, pay, src, base, heads):
    rows = slice((base + src) * TILE, (base + src + 1) * TILE)
    for h in range(heads):
        pay[src, heads + h] = pack_rows(dk[h, rows]).astype(BF)
        pay[src, 2 * heads + h] = pack_rows(dv[h, rows]).astype(BF)


def natural(ref, first_kind, pair, per):
    tiles = []
    for head in (2 * pair, 2 * pair + 1):
        tiles.append(ref[head // per, first_kind * per + head % per].astype(F32))
    return jnp.concatenate(swap_heads(*tiles), 0)


def remote(src, dst, sems, index, target, arrival=None):
    return pltpu.make_async_remote_copy(
        src_ref=src,
        dst_ref=dst,
        send_sem=sems[0].at[index],
        recv_sem=sems[1].at[index if arrival is None else arrival],
        device_id=target,
        device_id_type=pl.DeviceIdType.MESH,
    )


def meet(barrier, targets):
    for target in targets:
        pl.semaphore_signal(barrier, inc=1, device_id=target, device_id_type=pl.DeviceIdType.MESH)
    pl.semaphore_wait(barrier, len(targets))


def project_out(got, tokens, w_ref, gain, att, res, nf, heads):
    for pair in range(tokens.shape[1] // HALF):
        att[:, pair * HALF : (pair + 1) * HALF] = natural(got, 0, pair, heads).astype(BF)
    residual = tokens.astype(F32) + dot(att[...], w_ref[...])
    res[...] = residual
    nf[...] = (residual * rms_scale(residual) * gain).astype(BF)


class Trade:
    def __init__(self, src, dst, sems, local):
        self.src, self.dst, self.sems, self.local = src, dst, sems, local
        self.z = lax.axis_index("context")
        self.groups = src.shape[0]

    def wire(self, other, arrival):
        return remote(self.src.at[other], self.dst.at[arrival], self.sems, other, {"context": other}, arrival)

    def keep(self, index):
        return pltpu.make_async_copy(self.src.at[index], self.dst.at[index], self.local)

    def send(self, dest):
        @pl.when(dest != self.z)
        def _():
            self.wire(dest, self.z).start()

        @pl.when(dest == self.z)
        def _():
            self.keep(dest).start()

    def await_from(self, other):
        @pl.when(other != self.z)
        def _():
            self.wire(other, other).wait_recv()

        @pl.when(other == self.z)
        def _():
            self.keep(other).wait()

    def collect(self):
        for other in range(self.groups):
            self.await_from(other)

    def release(self):
        for other in range(self.groups):

            @pl.when(other != self.z)
            def _(other=other):
                self.wire(other, self.z).wait_send()


def front_kernel(*refs, heads, groups):
    refs = list(refs)
    take = lambda n: [refs.pop(0) for _ in range(n)]
    x_ref, gains_in, blocks, keeps, gates_in = take(5)
    w_qkv, w_out, w_ein, w_eout, w_sin, w_sout, cot = take(7)
    recv_out, mixed_out, lse_out, cot_out = take(2), take(2), take(2), take(2)
    att_out, res_out, rows_out, got_out, gates_out, tags_out = take(6)
    qkv_out, wout_out, ein_out, eout_out, sin_out, sout_out, gains_out, table_out = take(8)
    wq, wo, gains, tags, pay, recv, ks, vs, scores, mixed, got, lse, att, res, nf, table = take(16)
    s_qkv, s_out, s_gain, s_exp, s_tag, s_gate, s_cot, s_pay, s_mix, s_row = [take(2) for _ in range(10)]
    local, self_pay, self_mix, stores = take(4)
    e, z, d = lax.axis_index("expert"), lax.axis_index("context"), lax.axis_index("dp")
    core, y = e % 2, e // 2 % 2
    to_x, to_core, to_y = {"dp": 1 - d}, {"expert": e + 1 - 2 * core}, {"expert": e + 2 - 4 * y}
    others = [{"context": (z + k) % groups} for k in range(1, groups)]
    width = x_ref.shape[2]

    loads = [
        pltpu.make_async_copy(w_qkv, wq.at[d], local.at[0]),
        pltpu.make_async_copy(w_out, wo.at[d], local.at[1]),
        pltpu.make_async_copy(gains_in, gains.at[d], local.at[2]),
    ]
    for copy in loads:
        copy.start()
    meet(pltpu.get_barrier_semaphore(), [to_x, to_core, to_y, *others])

    x_qkv = remote(w_qkv.at[core], wq.at[d, core], s_qkv, 0, to_x)
    x_gain = remote(gains_in, gains.at[d], s_gain, 0, to_x)
    x_out = remote(w_out.at[core], wo.at[d, core], s_out, 0, to_x)
    half = z % 2
    to_mate = {"context": z + 1 - 2 * half}
    x_exp = [
        remote(w_ein.at[half], ein_out.at[half], s_exp, 0, to_x),
        remote(w_eout, eout_out, s_exp, 1, to_x),
        remote(w_sin.at[core, y], sin_out.at[core, y], s_exp, 2, to_x),
        remote(w_sout.at[core, y], sout_out.at[core, y], s_exp, 3, to_x),
    ]
    n_exp = [
        remote(ein_out.at[half], ein_out.at[half], s_exp, 4, to_mate),
        remote(sin_out.at[core, y], sin_out.at[core, y], s_exp, 5, to_y),
        remote(sout_out.at[core, y], sout_out.at[core, y], s_exp, 6, to_y),
        remote(sin_out.at[core], sin_out.at[core], s_exp, 7, to_core),
        remote(sout_out.at[core], sout_out.at[core], s_exp, 8, to_core),
    ]
    for copy in (x_qkv, x_gain, x_out, x_exp[0], x_exp[2], x_exp[3], x_exp[1]):
        copy.start()
    for m in range(MICRO):
        block = blocks[0, m : m + 1, :] + 8 * m
        tags[z, 0, m] = block
        tags[z, 1, m] = jnp.where(keeps[0, m : m + 1, :] == 1, block, HIDDEN)
    tag_trade = [remote(tags.at[z], tags.at[z], s_tag, k, others[k]) for k in range(groups - 1)]
    for copy in tag_trade:
        copy.start()
    own_copies = [
        pltpu.make_async_copy(gates_in, gates_out.at[0], stores.at[0]),
        pltpu.make_async_copy(cot.at[0], cot_out[0].at[0], stores.at[1]),
        pltpu.make_async_copy(cot.at[1], cot_out[1].at[0], stores.at[2]),
    ]
    for copy in own_copies:
        copy.start()
    y_gate = remote(gates_in, gates_out.at[1], s_gate, 0, to_y)
    y_cot = [remote(cot.at[m], cot_out[m].at[1], s_cot, m, to_y) for m in range(MICRO)]
    c_gate = [
        remote(gates_in, gates_out.at[2], s_gate, 1, to_core),
        remote(gates_out.at[1], gates_out.at[3], s_gate, 2, to_core),
    ]
    c_cot = [remote(cot.at[m], cot_out[m].at[2], s_cot, 2 + m, to_core) for m in range(MICRO)] + [
        remote(cot_out[m].at[1], cot_out[m].at[3], s_cot, 4 + m, to_core) for m in range(MICRO)
    ]
    y_gate.start()
    for copy in y_cot:
        copy.start()

    row = lax.broadcasted_iota(jnp.int32, (MICRO * TILE, HALF), 0)
    lane = lax.broadcasted_iota(jnp.int32, (MICRO * TILE, HALF), 1)
    place = row // TILE * (TILE * groups) + z * TILE + row % TILE
    freq = jnp.exp((-math.log(ROPE_BASE) * 2.0 / HEAD) * (lane % (HEAD // 2)).astype(F32))
    angle = place.astype(F32) * freq
    table[0] = jnp.cos(angle)
    table[1] = jnp.where(lane % HEAD < HEAD // 2, -jnp.sin(angle), jnp.sin(angle))

    c_qkv = remote(wq.at[1 - d, core], wq.at[1 - d, core], s_qkv, 1, to_core)
    c_out = remote(wo.at[1 - d, core], wo.at[1 - d, core], s_out, 1, to_core)
    for copy in loads:
        copy.wait()
    x_qkv.wait_recv()
    c_qkv.start()
    x_gain.wait_recv()
    c_qkv.wait_recv()
    both = [gain_row(gains, k) for k in range(2)]
    w_full = wq.reshape(width, 3 * width)
    trades, returns = [], []
    for m in range(MICRO):
        span = slice(m * TILE, (m + 1) * TILE)
        project(x_ref[m].astype(F32), both[0], w_full, table[0, span, :], table[1, span, :], pay.at[m], groups)
        trade = Trade(pay.at[m], recv.at[m], [s.at[m] for s in s_pay], self_pay.at[m])
        for dest in range(groups):
            trade.send(dest)
        trades.append(trade)
    c_gate[0].start()
    for copy in c_cot[:MICRO]:
        copy.start()
    for k in range(groups - 1):
        source = (z + groups - 1 - k) % groups
        remote(tags.at[z], tags.at[source], s_tag, k, others[k]).wait_recv()

    def attend(m, first, last):
        trade = Trade(mixed.at[m], got.at[m], [s.at[m] for s in s_mix], self_mix.at[m])

        def one(step, carry):
            attend_step(step, m, heads, groups, recv.at[m], tags, mixed.at[m], lse.at[m], ks, vs, scores)
            trade.send(step)
            return carry

        lax.fori_loop(first, last, one, 0)
        return trade

    row_y = remote(nf, rows_out.at[1], s_row, 0, to_y)
    row_core = remote(nf, rows_out.at[2], s_row, 1, to_core)
    row_next = remote(rows_out.at[1], rows_out.at[3], s_row, 2, to_core)

    trades[0].collect()
    fill_keys(recv.at[0], 0, ks, vs, heads)
    back0 = attend(0, 0, groups)
    x_exp[0].wait_recv()
    n_exp[0].start()
    x_out.wait_recv()
    c_out.start()
    y_gate.wait_recv()
    c_gate[1].start()
    for m in range(MICRO):
        y_cot[m].wait_recv()
        c_cot[MICRO + m].start()
    trades[1].collect()
    fill_keys(recv.at[1], 1, ks, vs, heads)
    for k in (2, 3):
        x_exp[k].wait_recv()
        n_exp[k - 1].start()
    back1 = attend(1, 0, 2)
    c_out.wait_recv()
    back0.collect()
    project_out(got.at[0], x_ref[0], wo.reshape(width, width), both[1], att, res, nf, heads)
    row_y.start()
    row_core.start()
    back1 = attend(1, 2, groups)
    row_y.wait_recv()
    row_next.start()
    for k in (1, 2):
        n_exp[k].wait_recv()
        n_exp[k + 2].start()
    keep = []
    for m in range(MICRO):
        keep += [(recv.at[m], recv_out[m]), (mixed.at[m], mixed_out[m]), (lse.at[m], lse_out[m])]
    keep += [(att, att_out), (res, res_out), (nf, rows_out.at[0])]
    keep += [(tags, tags_out), (wq, qkv_out), (wo, wout_out), (gains, gains_out), (table, table_out)]
    keep = [pltpu.make_async_copy(a, b, stores.at[3 + i]) for i, (a, b) in enumerate(keep)]
    for copy in keep:
        copy.start()
    back1.collect()
    got_copy = pltpu.make_async_copy(got.at[1], got_out, stores.at[3 + len(keep)])
    got_copy.start()
    for copy in (*keep, got_copy, *own_copies):
        copy.wait()
    for m in range(MICRO):
        trades[m].release()
    row_y.wait_send()
    row_core.wait()
    row_next.wait()
    back0.release()
    back1.release()
    x_exp[1].wait_recv()
    for copy in n_exp:
        copy.wait_send()
    for copy in (n_exp[0], n_exp[3], n_exp[4]):
        copy.wait_recv()
    for copy in (*c_gate, *c_cot):
        copy.wait()
    for copy in (*x_exp, x_qkv, x_gain, x_out, c_qkv, c_out, y_gate, *y_cot, *tag_trade):
        copy.wait_send()


def run_front(x, gains, blocks, keeps, gates, w_qkv, w_out, w_ein, w_eout, w_sin, w_sout, cot, groups):
    _, rows, width = x.shape
    heads = width // HEAD // groups
    k = width // 4
    tags = (groups, 2, MICRO, 1, rows)
    w_qkv = w_qkv.reshape(2, k, 3 * width)
    w_out = w_out.reshape(2, k, width)
    w_ein = w_ein.reshape(2, -1, w_ein.shape[1])
    w_sin, w_sout = [w.reshape(2, 2, -1, w.shape[1]) for w in (w_sin, w_sout)]
    vmem = pl.BlockSpec(memory_space=pltpu.VMEM)
    anywhere = pl.BlockSpec(memory_space=pl.ANY)
    packed = lambda n: (groups, n * heads, HALF, HALF)
    held = MICRO * groups * TILE
    twice = lambda *a: [struct(*a)] * 2
    outs = (
        twice(packed(3), BF)
        + twice(packed(1), BF)
        + twice((groups, 8, TILE), F32)
        + twice((4, rows, width), BF)
        + [
            struct((rows, width), BF),
            struct((rows, width), F32),
            struct((4, rows, width), BF),
            struct(packed(1), BF),
            struct((4, *gates.shape), F32),
            struct(tags, jnp.int32),
            struct((2, 2, k, 3 * width), BF),
            struct((2, 2, k, width), BF),
            struct(w_ein.shape, BF),
            struct(w_eout.shape, BF),
            struct(w_sin.shape, BF),
            struct(w_sout.shape, BF),
            struct((2, *gains.shape), F32),
            struct((2, MICRO * rows, HALF), F32),
        ]
    )
    v = pltpu.VMEM
    dma = lambda *n: pltpu.SemaphoreType.DMA(n)
    scratch = [
        v((2, 2, k, 3 * width), BF),
        v((2, 2, k, width), BF),
        v((2, *gains.shape), F32),
        v(tags, jnp.int32),
        v((MICRO, *packed(3)), BF),
        v((MICRO, *packed(3)), BF),
        v((heads, held, HALF), BF),
        v((heads, held, HALF), BF),
        v((heads, TILE, held), F32),
        v((MICRO, *packed(1)), BF),
        v((MICRO, *packed(1)), BF),
        v((MICRO, groups, 8, TILE), F32),
        v((rows, width), BF),
        v((rows, width), F32),
        v((rows, width), BF),
        v((2, MICRO * rows, HALF), F32),
    ]
    for shape in ((2,), (2,), (1,), (9,), (groups - 1,), (3,), (6,), (MICRO, groups), (MICRO, groups), (3,)):
        scratch += [dma(*shape), dma(*shape)]
    scratch += [dma(3), dma(MICRO), dma(MICRO), dma(3 + 3 * MICRO + 9)]
    return pl.pallas_call(
        functools.partial(front_kernel, heads=heads, groups=groups),
        out_shape=tuple(outs),
        in_specs=[vmem] * 5 + [anywhere] * 7,
        out_specs=(anywhere,) * len(outs),
        scratch_shapes=scratch,
        compiler_params=pltpu.CompilerParams(
            vmem_limit_bytes=VMEM_LIMIT, collective_id=3, has_side_effects=True
        ),
        cost_estimate=price(130),
    )(x, gains, blocks, keeps, gates, w_qkv, w_out, w_ein, w_eout, w_sin, w_sout, cot)


def ffn_kernel(*refs, tr, halves, gated, micro, summed, guest, guest_counts):
    refs = list(refs)
    take = lambda n: [refs.pop(0) for _ in range(n)]
    x_ref, dy_in = take(2)
    gate_in = take(1)[0] if gated else None
    wg_parts, wu_parts, wo_parts = take(2), take(2), take(2)
    g0 = take(3) if summed else None
    guest_in = take(guest_counts[0])
    y_ref, dx_ref, dwg_ref, dwu_ref, dwo_ref = take(5)
    guest_out = take(guest_counts[1])
    xt, yacc, dxacc, hs, djg, dju, wg_ref, wu_ref, wo_ref = take(9)
    dy_ref, gate_ref = take(2) if gated else (dy_in, None)
    f = pl.program_id(0)
    last = pl.num_programs(0) - 1
    rows = x_ref.shape[0]
    span = wg_parts[0].shape[0]
    dp = lax.axis_index("dp")
    visits = guest(guest_in, guest_out, refs) if guest else {}

    @pl.when(f == 0)
    def _():
        if 0 in visits:
            visits[0]()
        xt[...] = x_ref[...].T
        yacc[...] = jnp.zeros_like(yacc)
        dxacc[...] = jnp.zeros_like(dxacc)
        if gated:
            if micro is None:
                gate_ref[...] = gate_in[...]
            else:
                for block in range(gate_in.shape[0]):
                    row = gate_in[block, lax.axis_index("expert"), micro : micro + 1, :]
                    gate_ref[block * TILE : (block + 1) * TILE, :] = column(row)
            dy_ref[...] = (dy_in[...].astype(F32) * gate_ref[...]).astype(BF)

    for step, visit in visits.items():
        if step not in (0, "end"):
            pl.when(f == step)(visit)

    for index, part in enumerate((dp, 1 - dp)):
        place = pl.ds(pl.multiple_of(part * span, HALF // 2), span)
        wg_ref[place, :] = wg_parts[index][...]
        wu_ref[place, :] = wu_parts[index][...]

        @pl.when(f // halves == part)
        def _(index=index):
            wo_ref[...] = wo_parts[index][...]

    wg, wu, wo = wg_ref[...], wu_ref[...], wo_ref[...]

    def tile(i, carry):
        r = pl.ds(pl.multiple_of(i * tr, tr), tr)
        x = x_ref[r, :]
        g = dot(x, wg)
        u = dot(x, wu)
        dh = dot(dy_ref[r, :], wo, NT)
        sig = 1.0 / (1.0 + jnp.exp(-g))
        act = g * sig
        h = (act * u).astype(BF)
        dg = (dh * u * (sig * (1.0 + g * (1.0 - sig)))).astype(BF)
        du = (dh * act).astype(BF)
        hs[r, :] = h
        djg[r, :] = dg
        dju[r, :] = du
        yacc[r, :] += dot(h, wo)
        dxacc[r, :] += dot(dg, wg, NT) + dot(du, wu, NT)
        return carry

    lax.fori_loop(0, rows // tr, tile, 0)
    grads = [dot(xt[...], djg[...]), dot(xt[...], dju[...]), dot(hs[...], dy_ref[...], TN)]
    for k, out in enumerate((dwg_ref, dwu_ref, dwo_ref)):
        value = grads[k]
        if summed:
            value = value + g0[k][...].astype(F32)
        out[...] = value.astype(BF)

    @pl.when(f == last)
    def _():
        made = yacc[...].astype(BF)
        if gated:
            made = (made.astype(F32) * gate_ref[...]).astype(BF)
        y_ref[...] = made
        dx_ref[...] = dxacc[...].astype(BF)
        if "end" in visits:
            visits["end"]()


def run_ffn(x, dy, gate, w_in, w_out, grads=None, tr=512, fb=FB, us=10, guest=None):
    rows, d = x.shape
    ff = sum(w.shape[0] for w in w_out)
    nf = ff // fb
    halves = nf // 2
    gated = gate is not None
    gate, micro = gate if isinstance(gate, tuple) else (gate, None)
    whole = lambda a: pl.BlockSpec(a.shape, lambda f: (0,) * a.ndim, pipeline_mode=pl.Buffered(1))
    args = [x, dy] + ([gate] if gated else [])
    specs = [whole(a) for a in args]
    args += list(w_in) * 2 + list(w_out)
    span = w_in[0].shape[0]
    specs += [pl.BlockSpec((span, fb), lambda f: (0, f))] * 2
    specs += [pl.BlockSpec((span, fb), lambda f: (0, f + nf))] * 2
    specs += [pl.BlockSpec((fb, d), lambda f: (f % halves, 0))] * 2
    wide = pl.BlockSpec((d, fb), lambda f: (0, f))
    tall = pl.BlockSpec((fb, d), lambda f: (f, 0))
    if grads is not None:
        args += list(grads)
        specs += [wide, wide, tall]
    full = pl.BlockSpec((rows, d), lambda f: (0, 0), pipeline_mode=pl.Buffered(1))
    outs = [
        struct((rows, d), BF),
        struct((rows, d), BF),
        struct((d, ff), BF),
        struct((d, ff), BF),
        struct((ff, d), BF),
    ]
    out_specs = [full, full, wide, wide, tall]
    scratch = [
        pltpu.VMEM((d, rows), BF),
        pltpu.VMEM((rows, d), F32),
        pltpu.VMEM((rows, d), F32),
        pltpu.VMEM((rows, fb), BF),
        pltpu.VMEM((rows, fb), BF),
        pltpu.VMEM((rows, fb), BF),
        pltpu.VMEM((d, fb), BF),
        pltpu.VMEM((d, fb), BF),
        pltpu.VMEM((fb, d), BF),
    ] + ([pltpu.VMEM((rows, d), BF), pltpu.VMEM((rows, 1), F32)] if gated else [])
    anywhere = pl.BlockSpec(memory_space=pl.ANY)
    counts, visit, params = (0, 0), None, {}
    if guest is not None:
        visit, guest_args, guest_outs, guest_scratch, collective_id = guest
        args += [a for a, _ in guest_args]
        specs += [whole(a) if near else anywhere for a, near in guest_args]
        outs += guest_outs
        out_specs += [anywhere] * len(guest_outs)
        scratch += guest_scratch
        counts = (len(guest_args), len(guest_outs))
        params = {"collective_id": collective_id, "has_side_effects": True}
    return pl.pallas_call(
        functools.partial(
            ffn_kernel,
            tr=math.gcd(tr, rows),
            halves=halves,
            gated=gated,
            micro=micro,
            summed=grads is not None,
            guest=visit,
            guest_counts=counts,
        ),
        out_shape=tuple(outs),
        grid=(nf,),
        in_specs=specs,
        out_specs=tuple(out_specs),
        scratch_shapes=scratch,
        compiler_params=pltpu.CompilerParams(vmem_limit_bytes=VMEM_LIMIT, **params),
        cost_estimate=price(us),
    )(*args)


def rows_guest(ins, outs, bufs, *, heads):
    got, x_ref, w_ref, gain_ref, first_rows = ins
    att_out, res_out, rows_out, both_out = outs
    att, res, nf, sends, recvs, stores = bufs
    e = lax.axis_index("expert")
    core, y = e % 2, e // 2 % 2
    to_core, to_y = {"expert": e + 1 - 2 * core}, {"expert": e + 2 - 4 * y}
    wires = [
        remote(nf, rows_out.at[1], (sends, recvs), 0, to_y),
        remote(nf, rows_out.at[2], (sends, recvs), 1, to_core),
        remote(rows_out.at[1], rows_out.at[3], (sends, recvs), 2, to_core),
    ]
    keep = [
        (att, att_out),
        (res, res_out),
        (nf, rows_out.at[0]),
        (nf, both_out.at[1]),
        (first_rows.at[0], both_out.at[0]),
    ]
    keep = [pltpu.make_async_copy(a, b, stores.at[i]) for i, (a, b) in enumerate(keep)]

    def begin():
        meet(pltpu.get_barrier_semaphore(), [to_core, to_y])
        project_out(got, x_ref[1], w_ref, gain_row(gain_ref, 1), att, res, nf, heads)
        for copy in (wires[0], wires[1], *keep):
            copy.start()

    def later():
        wires[0].wait_recv()
        wires[2].start()

    def end():
        wires[0].wait_send()
        wires[1].wait()
        wires[2].wait()
        for copy in keep:
            copy.wait()

    return {0: begin, 2: later, "end": end}


def halves_guest(ins, outs, bufs):
    n = len(ins)
    totals, cores, gots = bufs[:n], bufs[n : 2 * n], bufs[2 * n : 3 * n]
    loads, sends, recvs, stores = bufs[3 * n :]
    e, d = lax.axis_index("expert"), lax.axis_index("dp")
    core, y = e % 2, e // 2 % 2
    to_x, to_core, to_y = {"dp": 1 - d}, {"expert": e + 1 - 2 * core}, {"expert": e + 2 - 4 * y}
    both = [(i, h) for i in range(n) for h in range(2)]
    sems = (sends, recvs)
    load = {(i, h): pltpu.make_async_copy(ins[i].at[h, core], totals[i].at[h], loads.at[2 * i + h]) for i, h in both}
    first = {(i, h): remote(ins[i].at[h, 1 - core], cores[i].at[h], sems, 2 * i + h, to_core) for i, h in both}

    def half(i, h):
        if i in FLIPPED:
            return remote(totals[i].at[1 - d, h], gots[i].at[h], sems, 2 * n + 2 * i + h, to_x)
        return remote(totals[i].at[h, 1 - y], gots[i].at[h], sems, 2 * n + 2 * i + h, to_y)

    store = [pltpu.make_async_copy(gots[i], outs[i], stores.at[i]) for i in range(n)]

    def begin():
        meet(pltpu.get_barrier_semaphore(), [to_x, to_core, to_y])
        for key in both:
            first[key].start()
            load[key].start()

    def later():
        for i in range(n):
            for h in range(2):
                load[i, h].wait()
                first[i, h].wait_recv()
            totals[i][...] = totals[i][...] + cores[i][...]
            for h in range(2):
                half(i, h).start()

    def end():
        for i, h in both:
            half(i, h).wait_recv()
            mine = totals[i][d, h] if i in FLIPPED else totals[i][h, y]
            gots[i][h] = mine + gots[i][h]
        for copy in store:
            copy.start()
        for key in both:
            first[key].wait_send()
            half(*key).wait_send()
        for copy in store:
            copy.wait()

    return {0: begin, 1: later, "end": end}


def price(us):
    return pl.CostEstimate(flops=int(us * 1.15e9), bytes_accessed=0, transcendentals=0)


def norm_back(values, scale, gain, grad):
    gain_grad = jnp.sum(grad * values * scale, 0, keepdims=True)
    scaled = gain * grad
    grad_in = scale * scaled - values * (scale * scale * scale) * jnp.mean(
        scaled * values, -1, keepdims=True
    )
    return grad_in, gain_grad


def mid_core(grad, residual, gain, cot, w_ref, pay, gres_ref, gbf_ref, per):
    back, gain_grad = norm_back(residual, rms_scale(residual), gain, grad)
    total = cot.astype(F32) + back
    gres_ref[...] = total
    gbf_ref[...] = total.astype(BF)
    mixed = dot(gbf_ref[...], w_ref[...], NT)
    for pair in range(mixed.shape[1] // HALF):
        tile = mixed[:, pair * HALF : (pair + 1) * HALF]
        for side, packed in enumerate(swap_heads(tile[:HALF], tile[HALF:])):
            head = 2 * pair + side
            pay[head // per, head % per] = packed.astype(BF)
    return gain_grad


def finish(d0, d1, x_ref, gain_ref, w_ref, table, gres, atts, gbfs, gin_ref, gq, gv, go, gj, per):
    width = x_ref.shape[2]
    for micro, ref in enumerate((d0, d1)):
        rows = slice(micro * TILE, (micro + 1) * TILE)
        cosines, sines = table[0, rows, :], table[1, rows, :]
        for kind in range(3):
            for pair in range(width // HALF):
                tile = natural(ref, kind, pair, per)
                if kind == 0:
                    tile = tile * 0.125
                if kind < 2:
                    tile = rotate(tile, cosines, -sines)
                gj[rows, kind * width + pair * HALF : kind * width + (pair + 1) * HALF] = tile.astype(BF)
    tokens = x_ref[...].reshape(MICRO * TILE, width).astype(F32)
    scale = rms_scale(tokens)
    gain = gain_row(gain_ref, 0)
    turned = (tokens * scale * gain).astype(BF).T
    split = gq.shape[-1]
    gq[...] = dot(turned, gj[:, :split]).astype(BF).reshape(gq.shape)
    gv[...] = dot(turned, gj[:, split:]).astype(BF).reshape(gv.shape)
    go[...] = (dot(atts[0][...], gbfs[0], TN) + dot(atts[1][...], gbfs[1], TN)).astype(BF).reshape(go.shape)
    yield
    first = dot(gj[...], w_ref[...], NT)
    back, _ = norm_back(tokens, scale, gain, first)
    for micro in range(MICRO):
        rows = slice(micro * TILE, (micro + 1) * TILE)
        gin_ref[rows, :] = gres[micro] + back[rows]


def exchange(value, axis, mask):
    size = lax.axis_size(axis)
    return lax.ppermute(value, axis, [(i, i ^ mask) for i in range(size)])


def bits_of(size):
    return [1 << b for b in range(size.bit_length() - 1)]


def gather_rest(value):
    for mask in bits_of(lax.axis_size("expert"))[2:]:
        value = jnp.concatenate([value, exchange(value, "expert", mask)], 0)
    return value


def scatter_rest(value):
    for mask in reversed(bits_of(lax.axis_size("expert"))[2:]):
        half = value.shape[0] // 2
        got = exchange(value[half:], "expert", mask)
        value = (value[:half].astype(F32) + got.astype(F32)).astype(value.dtype)
    return value


def ordered(flag, mine, theirs):
    first = jnp.where(flag == 0, mine, theirs)
    second = jnp.where(flag == 0, theirs, mine)
    return jnp.concatenate([first, second], 0)


def pick(value, parts, index):
    size = value.shape[0] // parts
    return lax.dynamic_slice_in_dim(value, index * size, size, 0)


def after(value, token):
    return lax.optimization_barrier((value, token))[0]


PIECES = 4
FLIPPED = (1,)
EARLY = 7
AHEAD = 2
PLAN = {
    -1: ("b0", "b1", "b2", "A0", "rs1", "c1", "A1", "B0", "rs2", "c0", "d1", "c2", "C0", "rs3", "B1", "A2",),
    4: ("e1",),
    6: ("A3",),
    7: ("d0",),
    9: ("A4",),
    12: ("d2",),
    15: ("C1",),
    16: ("A5",),
    18: ("B2",),
    19: ("e0",),
    20: ("B3",),
    21: ("e2",),
    24: ("A6", "f2",),
    25: ("C2",),
    27: ("B4",),
    28: ("f1",),
    29: ("C3",),
    32: ("B5",),
    34: ("C4",),
    37: ("B6",),
    39: ("C5", "f0",),
    42: ("zhome", "A7", "g1", "D5", "A8", "D3", "g2", "D2", "A10", "g0", "h1", "C6", "A9", "h2", "D1", "h0", "A11", "D0", "D4", "D6",),
}
LAST_PLAN = (
    "A0", "A1", "A2", "A3", "B0", "a0", "B1", "C0", "a1", "a2",
    "b0", "B2", "C1", "b2", "D0", "B3", "b1", "C2", "c0", "c2",
    "d0", "c1", "A4", "C3", "f0", "d2", "d1", "e0", "B4", "f1",
    "g0", "e1", "f2", "e2", "D3", "zrest", "C4", "D2", "g1", "g2",
    "D1", "h0", "D4", "h1", "h2",
)


class Engine:
    def __init__(self, own, com, own_buf, com_buf, own_out, com_out, sems, halved=False):
        self.halved = halved
        self.flip = [i in FLIPPED for i in range(len(com))]
        self.own, self.com, self.own_buf, self.com_buf = own, com, own_buf, com_buf
        self.own_out, self.com_out = own_out, com_out
        e, z, d = lax.axis_index("expert"), lax.axis_index("context"), lax.axis_index("dp")
        groups = lax.axis_size("context")
        self.d, self.core, self.y = d, e % 2, e // 2 % 2
        self.outer = (z == 0) | (z == 3)
        self.inner = (z == 1) | (z == 2)
        self.to_x = {"dp": 1 - d}
        self.to_core = {"expert": e + 1 - 2 * self.core}
        self.to_y = {"expert": e + 2 - 4 * self.y}
        self.to_mate = {"context": z + 1 - 2 * (z % 2)}
        self.to_mid = {"context": 3 - z}
        self.others = [{"context": (z + k) % groups} for k in range(1, groups)]
        sems = list(sems)
        take = lambda n: [sems.pop(0) for _ in range(n)]
        self.o_load, self.o_store = take(2)
        self.o = {k: take(2) for k in "x123"}
        self.c_load, self.c_store = take(2)
        self.c = {k: take(2) for k in ("core", "y", "x", "1", "2", "3", "fore", "last")}

    @staticmethod
    def scratch(own_shapes, kinds, com_shapes, halved=False):
        v, dma = pltpu.VMEM, lambda n: pltpu.SemaphoreType.DMA((max(n, 1),))
        tiny = (16, HALF)
        own_buf = []
        for s, kind in zip(own_shapes, kinds):
            own_buf += [v(s, BF), v(s if "x" in kind else tiny, BF)]
            own_buf += [v(s if "z" in kind else tiny, BF)] * 2
        com_buf = []
        for s in com_shapes:
            tiny = (16, HALF)
            if halved:
                com_buf += [v((2, *s), BF), v(tiny, BF), v(tiny, BF)] + [v(s, BF)] * 3
            else:
                com_buf += [v((2, 2, *s), BF)] * 2 + [v((2, *s), BF)] + [v(s, BF)] * 3
        chunks, n = len(own_shapes), len(com_shapes)
        sems = [dma(chunks)] * 10 + [dma(2 * n), dma(n)] + [dma(2 * n)] * 4 + [dma(n)] * 12
        return own_buf, com_buf, sems

    def greet(self):
        meet(
            pltpu.get_barrier_semaphore(), [self.to_x, self.to_core, self.to_y, *self.others]
        )

    def o_wire(self, stage, c):
        total, r_x, r_1, r_2 = self.own_buf[c]
        src, k, _ = self.own[c]
        target = {"x": self.to_x, "1": self.to_mate, "2": self.to_mid, "3": self.to_mate}[stage]
        source = {"x": lambda: src.at[1 - self.d, k], "1": lambda: total, "2": lambda: total, "3": lambda: r_1}
        place = {"x": r_x, "1": r_1, "2": r_2, "3": self.own_out[c]}[stage]
        return remote(source[stage](), place, self.o[stage], c, target)

    def o_loading(self, c):
        src, k, kind = self.own[c]
        src = src.at[k] if kind == "z" else src.at[self.d, k]
        return pltpu.make_async_copy(src, self.own_buf[c][0], self.o_load.at[c])

    def o_storing(self, c):
        buf = self.own_buf[c][0 if self.own[c][2] == "x" else 2]
        return pltpu.make_async_copy(buf, self.own_out[c], self.o_store.at[c])

    def A(self, c):
        total, r_x = self.own_buf[c][:2]
        kind = self.own[c][2]
        self.o_loading(c).wait()
        if kind != "z":
            self.o_wire("x", c).wait_recv()
            if c + self.ahead < len(self.own):
                self.o_wire("x", c + self.ahead).start()
            total[...] = total[...] + r_x[...]
        if kind == "x":
            self.o_storing(c).start()
            return

        @pl.when(self.outer)
        def _():
            self.o_wire("1", c).start()

    def B(self, c):
        total, _, r_1, _ = self.own_buf[c]

        @pl.when(self.inner)
        def _():
            self.o_wire("1", c).wait_recv()
            total[...] = total[...] + r_1[...]
            self.o_wire("2", c).start()

    def C(self, c):
        total, _, r_1, r_2 = self.own_buf[c]

        @pl.when(self.inner)
        def _():
            self.o_wire("2", c).wait_recv()
            r_1[...] = total[...] + r_2[...]
            self.o_wire("3", c).start()
            self.o_storing(c).start()

    def D(self, c):
        @pl.when(self.outer)
        def _():
            self.o_wire("3", c).wait_recv()

    def slot(self, i):
        total = self.com_buf[i][0]
        if self.halved:
            return total.at[self.y if self.flip[i] else self.d]
        return total.at[self.d, self.y]

    def c_loading(self, i, h):
        if self.halved:
            return pltpu.make_async_copy(self.com[i], self.com_buf[i][0], self.c_load.at[2 * i])
        return pltpu.make_async_copy(
            self.com[i].at[h, self.core], self.com_buf[i][0].at[h], self.c_load.at[2 * i + h]
        )

    def c_storing(self, i):
        return pltpu.make_async_copy(
            self.com_buf[i][4], self.com_out[i].at[self.core, self.y], self.c_store.at[i]
        )

    def c_wire(self, stage, i, h=0):
        total, r_core, r_y, r_x, r_1, r_2 = self.com_buf[i]
        core, y, d = self.core, self.y, self.d
        out = self.com_out[i]
        if stage == "core":
            return remote(self.com[i].at[h, 1 - core], r_core.at[h], self.c["core"], 2 * i + h, self.to_core)
        if stage == "y" and self.flip[i]:
            return remote(total.at[1 - d, h], r_y.at[h], self.c["y"], 2 * i + h, self.to_x)
        if stage == "x" and self.halved:
            other, target = (1 - y, self.to_y) if self.flip[i] else (1 - d, self.to_x)
            return remote(total.at[other], r_x, self.c["x"], i, target)
        if stage == "x" and self.flip[i]:
            return remote(total.at[d, 1 - y], r_x, self.c["x"], i, self.to_y)
        if stage == "y":
            return remote(total.at[h, 1 - y], r_y.at[h], self.c["y"], 2 * i + h, self.to_y)
        if stage == "x":
            return remote(total.at[1 - d, y], r_x, self.c["x"], i, self.to_x)
        if stage == "1":
            return remote(self.slot(i), r_1, self.c["1"], i, self.to_mate)
        if stage == "2":
            return remote(self.slot(i), r_2, self.c["2"], i, self.to_mid)
        if stage == "3":
            return remote(r_1, out.at[core, y], self.c["3"], i, self.to_mate)
        if stage == "fore":
            return remote(r_1, out.at[core, y], self.c["fore"], i, self.to_y)
        if stage == "back":
            return remote(out.at[core, y], out.at[core, y], self.c["fore"], i, self.to_y)
        return remote(out.at[core], out.at[core], self.c["last"], i, self.to_core)

    def c_start(self, i):
        if self.halved:
            self.c_loading(i, 0).start()
            return
        for h in range(2):
            self.c_wire("core", i, h).start()
            self.c_loading(i, h).start()

    def a(self, i):
        total, r_core = self.com_buf[i][:2]
        for h in range(2):
            self.c_loading(i, h).wait()
            self.c_wire("core", i, h).wait_recv()
        total[...] = total[...] + r_core[...]
        for h in range(2):
            self.c_wire("y", i, h).start()

    def b(self, i):
        total, r_y, y = self.com_buf[i][0], self.com_buf[i][2], self.y
        if self.halved:
            self.c_loading(i, 0).wait()
            self.c_wire("x", i).start()
            return
        for h in range(2):
            self.c_wire("y", i, h).wait_recv()
            if self.flip[i]:
                total[self.d, h] = total[self.d, h] + r_y[h]
            else:
                total[h, y] = total[h, y] + r_y[h]
        self.c_wire("x", i).start()

    def c_(self, i):
        total, r_x = self.slot(i), self.com_buf[i][3]
        self.c_wire("x", i).wait_recv()
        total[...] = total[...] + r_x[...]

        @pl.when(self.outer)
        def _():
            self.c_wire("1", i).start()

    def d_(self, i):
        total, r_1 = self.slot(i), self.com_buf[i][4]

        @pl.when(self.inner)
        def _():
            self.c_wire("1", i).wait_recv()
            total[...] = total[...] + r_1[...]
            self.c_wire("2", i).start()

    def e(self, i):
        total, r_1, r_2 = self.slot(i), self.com_buf[i][4], self.com_buf[i][5]

        @pl.when(self.inner)
        def _():
            self.c_wire("2", i).wait_recv()
            r_1[...] = total[...] + r_2[...]
            self.c_wire("3", i).start()
            self.c_wire("fore", i).start()
            self.c_storing(i).start()

    def f(self, i):
        @pl.when(self.outer)
        def _():
            self.c_wire("3", i).wait_recv()
            self.c_wire("back", i).start()

    def g(self, i):
        @pl.when(self.inner)
        def _():
            self.c_storing(i).wait()

        self.c_wire("fore", i).wait_recv()
        self.c_wire("last", i).start()

    def h(self, i):
        self.c_wire("last", i).wait_recv()

    def start(self, ahead, com=True):
        self.ahead = ahead
        for c in range(min(ahead, len(self.own))):
            if self.own[c][2] != "z":
                self.o_wire("x", c).start()
        if com:
            for i in range(len(self.com)):
                self.c_start(i)
        for c in range(len(self.own)):
            self.o_loading(c).start()

    def run(self, name):
        kind, index = name[0], int(name[1:])
        {"c": self.c_, "d": self.d_}.get(kind, getattr(self, kind, None))(index)

    def close(self):
        chunks, common = range(len(self.own)), range(len(self.com))
        for c in chunks:
            if self.own[c][2] != "z":
                self.o_wire("x", c).wait_send()
            if self.own[c][2] == "x":
                self.o_storing(c).wait()
        chunks = [c for c in chunks if self.own[c][2] != "x"]
        for i in common:
            for h in range(0 if self.halved else 2):
                self.c_wire("core", i, h).wait_send()
                self.c_wire("y", i, h).wait_send()
            self.c_wire("x", i).wait_send()
            self.c_wire("last", i).wait_send()

        @pl.when(self.outer)
        def _():
            for c in chunks:
                self.o_wire("1", c).wait_send()
            for i in common:
                self.c_wire("1", i).wait_send()
                self.c_wire("back", i).wait_send()

        @pl.when(self.inner)
        def _():
            for c in chunks:
                self.o_wire("2", c).wait_send()
                self.o_wire("3", c).wait_send()
                self.o_storing(c).wait()
            for i in common:
                self.c_wire("2", i).wait_send()
                self.c_wire("3", i).wait_send()
                self.c_wire("fore", i).wait_send()


class Arrays:
    def __init__(self, refs):
        self.refs = list(refs)

    def take(self, n):
        got, self.refs = self.refs[:n], self.refs[n:]
        return got

    def engine(self, own_at, sources, own_out, com, com_out, halved=False):
        own_buf = [self.take(4) for _ in own_at]
        com_buf = [self.take(6) for _ in com]
        own = [(sources[j], k, kind) for j, k, kind in own_at]
        places = [own_out[j].at[k] for j, k, _ in own_at]
        return Engine(own, com, own_buf, com_buf, places, com_out, self.take(10 + 18), halved)


def back_kernel(*refs, own_at, sources, common, heads, groups):
    refs = Arrays(refs)
    own_in, com_in = refs.take(sources), refs.take(common)
    recv0, recv1, out0, out1, lse0, lse1, tags = refs.take(7)
    dxs, res0, res1, gain_ref, cot_ref, w_ref = refs.take(6)
    dx_made = refs.take(MICRO)
    own_out, com_out = refs.take(sources), refs.take(common)
    d0_out, d1_out, gres_out, gbf_out, gg_out = refs.take(5)
    engine = refs.engine(own_at, own_in, own_out, com_in, com_out, True)
    dx, r_core, r_y, gres, gbf, gg, pay_o, back_o, pay0, pay1 = refs.take(10)
    ks, vs, dk, dv, qs, gs, deltas, acc = refs.take(8)
    s_dx, s_o, s_0, s_1 = [refs.take(2) for _ in range(4)]
    local, = refs.take(1)

    engine.greet()
    both = range(MICRO)
    send_core = [remote(dx_made[m].at[2:4], r_core.at[m], s_dx, m, engine.to_core) for m in both]
    own_dx = [pltpu.make_async_copy(dx_made[m].at[0:2], dx.at[m], local.at[m]) for m in both]
    for m in both:
        send_core[m].start()
        own_dx[m].start()
    engine.start(AHEAD)
    send_y = [remote(dx.at[m, 1], r_y.at[m], s_dx, MICRO + m, engine.to_y) for m in both]
    trade_o = [
        Trade(pay_o.at[m], back_o.at[m], [s.at[m] for s in s_o], local.at[2 + m]) for m in both
    ]
    homes = [Trade(pay0, d0_out, s_0, local.at[4]), Trade(pay1, d1_out, s_1, local.at[5])]
    results = [
        pltpu.make_async_copy(a, b, local.at[6 + i])
        for i, (a, b) in enumerate(((gres, gres_out), (gbf, gbf_out), (gg, gg_out)))
    ]

    def rs1():
        for m in both:
            own_dx[m].wait()
            send_core[m].wait_recv()
            dx[m] = dx[m] + r_core[m]
            send_y[m].start()

    def middle(m, res_ref):
        send_y[m].wait_recv()
        grad = dxs[m * TILE : (m + 1) * TILE, :].astype(F32) + dx[m, 0].astype(F32) + r_y[m].astype(F32)
        part = mid_core(
            grad, res_ref[...], gain_row(gain_ref, 1), cot_ref[m], w_ref, pay_o.at[m], gres.at[m], gbf.at[m], heads
        )
        for dest in range(groups):
            trade_o[m].send(dest)
        return part

    def rs2():
        gg[...] = middle(0, res0)

    def rs3():
        gg[...] = gg[...] + middle(1, res1)
        for copy in results:
            copy.start()

    def zhome():
        for base, pay, trade in ((groups, pay1, homes[1]), (0, pay0, homes[0])):
            for dest in range(groups):
                back_pack(dk, dv, pay, dest, base, heads)
                trade.send(dest)

    named = {"rs1": rs1, "rs2": rs2, "rs3": rs3, "zhome": zhome}

    def events(slot):
        for name in PLAN.get(slot, ()):
            named[name]() if name in named else engine.run(name)

    for recv, micro in ((recv0, 0), (recv1, 1)):
        fill_keys(recv, micro, ks, vs, heads)
    dk[...] = jnp.zeros_like(dk)
    dv[...] = jnp.zeros_like(dv)
    first_of = (0, sum(min(s + 2, groups) for s in range(groups)))
    total = 2 * first_of[1] + groups * groups
    for micro, (recv, grad, out, lse, pay) in enumerate(
        ((recv0, back_o.at[0], out0, lse0, pay0), (recv1, back_o.at[1], out1, lse1, pay1))
    ):
        begin, end = first_of[micro], (first_of + (total,))[micro + 1]
        if micro == 0:
            events(-1)
        trade_o[micro].collect()

        def step(s, carry, micro=micro, recv=recv, grad=grad, out=out, lse=lse, pay=pay, begin=begin, end=end):
            back_begin(micro, s, heads, recv, grad, out, qs, gs, deltas, acc)
            before = begin + s * (s + 3) // 2 + groups * micro * s

            def tile(j, carry):
                for slot in range(begin, end):
                    if slot in PLAN:

                        @pl.when(before + j == slot)
                        def _(slot=slot):
                            events(slot)

                back_tile(
                    micro, s, j, heads, groups, lse, tags, ks, vs, dk, dv, qs, gs, deltas, acc
                )
                return carry

            lax.fori_loop(0, groups * micro + jnp.minimum(s + 2, groups), tile, 0)
            for h in range(heads):
                pay[s, h] = pack_rows(acc[h]).astype(BF)
            return carry

        lax.fori_loop(0, groups, step, 0)
    events(total)
    for trade in homes:
        trade.collect()
        trade.release()
    for m in both:
        trade_o[m].release()
        send_core[m].wait_send()
        send_y[m].wait_send()
    for copy in results:
        copy.wait()
    engine.close()


def chunk_views(grads):
    return [g.reshape(2, PIECES, g.shape[0] // (2 * PIECES), g.shape[1]) for g in grads]


def shared_shape(shape):
    return (2, 2, 2, shape[0] // 8, shape[1])


def device_call(kernel, args, vmem_args, outs, scratch, collective_id, us, aliases=None):
    anywhere = pl.BlockSpec(memory_space=pl.ANY)
    return pl.pallas_call(
        kernel,
        out_shape=tuple(outs),
        in_specs=[pl.BlockSpec(memory_space=pltpu.VMEM) if v else anywhere for v in vmem_args],
        out_specs=(anywhere,) * len(outs),
        scratch_shapes=scratch,
        input_output_aliases=aliases or {},
        compiler_params=pltpu.CompilerParams(
            vmem_limit_bytes=VMEM_LIMIT, collective_id=collective_id, has_side_effects=True
        ),
        cost_estimate=price(us),
    )(*args)


def rest_sum(value):
    for mask in bits_of(lax.axis_size("expert"))[2:]:
        value = value + exchange(value, "expert", mask)
    return value


def run_back(expert_grads, own_at, shared_grads, attention, middle, dx_made, groups):
    own = chunk_views(expert_grads)
    com = shared_grads
    heads = attention[0].shape[1] // 3
    rows, width = middle[1].shape
    args = [*own, *com, *attention, *middle, *dx_made]
    own_shapes = [own[j].shape[2:] for j, _, _ in own_at]
    com_shapes = [g.shape[1:] for g in com]
    own_buf, com_buf, sems = Engine.scratch(own_shapes, [kind for *_, kind in own_at], com_shapes, True)
    held = MICRO * groups * TILE
    v, dma = pltpu.VMEM, lambda n: pltpu.SemaphoreType.DMA((n,))
    pay = lambda n: (groups, n * heads, HALF, HALF)
    outs = (
        [struct(g.shape[1:], BF) for g in own]
        + [struct((2, 2, *s), BF) for s in com_shapes]
        + [struct(pay(3), BF)] * 2
        + [struct((MICRO, rows, width), F32), struct((MICRO, rows, width), BF), struct((1, width), F32)]
    )
    scratch = [
        *own_buf,
        *com_buf,
        *sems,
        v((MICRO, 2, rows, width), BF),
        v((MICRO, 2, rows, width), BF),
        v((MICRO, rows, width), BF),
        v((MICRO, rows, width), F32),
        v((MICRO, rows, width), BF),
        v((1, width), F32),
        v((MICRO, *pay(1)), BF),
        v((MICRO, *pay(1)), BF),
        v(pay(3), BF),
        v(pay(3), BF),
        v((heads, held, HALF), BF),
        v((heads, held, HALF), BF),
        v((heads, held, HALF), F32),
        v((heads, held, HALF), F32),
        v((heads, TILE, HALF), BF),
        v((heads, TILE, HALF), BF),
        v((heads, 8, TILE), F32),
        v((heads, TILE, HALF), F32),
        dma(2 * MICRO),
        dma(2 * MICRO),
        *[pltpu.SemaphoreType.DMA((MICRO, groups))] * 2,
        *[dma(groups)] * 4,
        dma(9),
    ]
    flags = [False] * (len(own) + len(com)) + [True] * (len(attention) + len(middle))
    flags += [False] * len(dx_made)
    kernel = functools.partial(
        back_kernel, own_at=own_at, sources=len(own), common=len(com), heads=heads, groups=groups
    )
    got = device_call(kernel, args, flags, outs, scratch, 1, 165)
    n, m = len(own), len(com)
    return got[:n], [rest_sum(g.reshape(-1, g.shape[-1]).astype(F32)) for g in got[n : n + m]], got[n + m :]


def last_kernel(*refs, own_at, sources, per):
    refs = Arrays(refs)
    own_in = refs.take(sources)
    d0, d1, x_ref, gain_ref, w_ref, table = refs.take(6)
    (gres, gbfs, gg_in), atts, made = refs.take(3), refs.take(2), refs.take(MICRO)
    own_out, com_out = refs.take(sources), refs.take(3)
    gin_out, gg_out, routed_out = refs.take(3)
    sources = [refs.refs.pop(len(own_at) * 4 + 3 * 6 + 28) for _ in range(3)]
    engine = refs.engine(own_at, own_in, own_out, sources, com_out)
    gj, gin, gg_sum, gg_got, g_send, g_recv, local, row, row_core, row_y, m_send, m_recv = refs.take(12)
    engine.greet()
    engine.start(0, com=False)
    z = lax.axis_index("context")
    rounds = (engine.to_core, engine.to_y, engine.to_x, engine.to_mate, {"context": z + 2 - 4 * (z // 2)})
    wires = [
        remote(gg_sum.at[k], gg_got.at[k], (g_send, g_recv), k, target) for k, target in enumerate(rounds)
    ]
    gg_sum[0] = jnp.broadcast_to(gg_in[...], gg_sum.shape[1:])
    wires[0].start()
    both = range(MICRO)
    row_wires = [remote(made[m].at[2:4], row_core.at[m], (m_send, m_recv), m, engine.to_core) for m in both]
    row_next = [remote(row.at[m, 1], row_y.at[m], (m_send, m_recv), MICRO + m, engine.to_y) for m in both]
    row_own = [pltpu.make_async_copy(made[m].at[0:2], row.at[m], local.at[2 + m]) for m in both]
    row_out = [pltpu.make_async_copy(row.at[m, 0], routed_out.at[m], local.at[2 + m]) for m in both]
    for m in both:
        row_wires[m].start()
        row_own[m].start()
    work = finish(
        d0, d1, x_ref, gain_ref, w_ref, table, gres, atts, gbfs, gin, *sources, gj, per
    )
    store = pltpu.make_async_copy(gin, gin_out, local.at[0])
    next(work)
    for i in range(3):
        engine.c_start(i)
    turn = 0
    for index, name in enumerate(LAST_PLAN):
        if name == "zrest":
            for _ in work:
                pass
            store.start()
        else:
            engine.run(name)
        if index == 12:
            for m in both:
                row_own[m].wait()
                row_wires[m].wait_recv()
                row[m] = row[m] + row_core[m]
                row_next[m].start()
        if index == 30:
            for m in both:
                row_next[m].wait_recv()
                row[m, 0] = row[m, 0] + row_y[m]
                row_out[m].start()
        if index % 5 == 4 and turn < len(wires):
            wires[turn].wait_recv()
            gg_sum[turn + 1] = gg_sum[turn] + gg_got[turn]
            turn += 1
            if turn < len(wires):
                wires[turn].start()
    total = pltpu.make_async_copy(gg_sum.at[len(wires)], gg_out, local.at[1])
    total.start()
    store.wait()
    total.wait()
    for wire in (*wires, *row_wires, *row_next):
        wire.wait_send()
    for copy in row_out:
        copy.wait()
    engine.close()


def run_last(sums, own_at, parts, made, groups):
    x, w = parts[2], parts[4]
    _, rows, width = x.shape
    args = [*sums, *parts, *made]
    own_shapes = [sums[j].shape[1:] for j, _, _ in own_at]
    com = [shared_shape((width, 3 * width // 2))] * 2 + [shared_shape((width, width))]
    own_buf, com_buf, sems = Engine.scratch(own_shapes, [k for *_, k in own_at], [s[3:] for s in com])
    v = pltpu.VMEM
    outs = (
        [struct(g.shape, BF) for g in sums]
        + [struct((2, 2, *s[3:]), BF) for s in com]
        + [struct((MICRO * rows, width), F32), struct((8, width), F32), struct((MICRO, rows, width), BF)]
    )
    rounds = 5
    scratch = [
        *own_buf,
        *com_buf,
        *sems,
        *[v(s, BF) for s in com],
        v((MICRO * rows, 3 * width), BF),
        v((MICRO * rows, width), F32),
        v((rounds + 1, 8, width), F32),
        v((rounds, 8, width), F32),
        *[pltpu.SemaphoreType.DMA((rounds,))] * 2,
        pltpu.SemaphoreType.DMA((2 + MICRO,)),
        v((MICRO, 2, rows, width), BF),
        v((MICRO, 2, rows, width), BF),
        v((MICRO, rows, width), BF),
        *[pltpu.SemaphoreType.DMA((2 * MICRO,))] * 2,
    ]
    flags = [False] * len(sums) + [True] * len(parts) + [False] * len(made)
    kernel = functools.partial(
        last_kernel, own_at=own_at, sources=len(sums), per=width // HEAD // groups
    )
    got = device_call(
        kernel, args, flags, outs, scratch, 2, 90, {i: i for i in range(len(sums))}
    )
    n = len(sums)
    return got[:n], [rest_sum(g.reshape(-1, g.shape[-1]).astype(F32)) for g in got[n : n + 3]], *got[n + 3 :]


def body(
    inputs,
    keep_flags,
    block_ids,
    expert_ids,
    gate_weights,
    norm_attn,
    w_qkv,
    w_attn_out,
    norm_ffn,
    w_shared_in,
    w_shared_out,
    w_expert_in,
    w_expert_out,
    cotangent,
):
    width = w_qkv.shape[1] // 3
    rows = inputs.shape[2]
    groups = lax.axis_size("context")
    experts = lax.axis_size("expert")
    z = lax.axis_index("context")
    seq_rows = rows * groups
    x = inputs[0]
    cot = cotangent[0].reshape(MICRO * rows, width)

    per_expert = jnp.sum(
        jnp.where(
            expert_ids[0][None] == jnp.arange(experts, dtype=jnp.int32)[:, None, None, None],
            gate_weights[0][None],
            0.0,
        ),
        -1,
    )
    gains = jnp.stack([norm_attn, norm_ffn]).astype(F32)
    (
        *pairs,
        att0,
        res0,
        rows0,
        got1,
        gates_four,
        all_tags,
        mat_qkv,
        mat_out,
        ein_parts,
        eout_other,
        sin_parts,
        sout_parts,
        gains,
        table,
    ) = run_front(
        x,
        gains,
        block_ids,
        keep_flags,
        per_expert,
        w_qkv,
        w_attn_out,
        w_expert_in[0],
        w_expert_out[0],
        w_shared_in,
        w_shared_out,
        cotangent[0],
        groups,
    )
    recvs, mixed, lses, cot_four = [pairs[2 * i : 2 * i + 2] for i in range(4)]
    mat_qkv = mat_qkv.reshape(width, -1)
    mat_out = mat_out.reshape(width, width)
    core = lax.axis_index("expert") % 2
    dp = lax.axis_index("dp")
    whole = lambda w: w.reshape(-1, w.shape[-1])
    ein_parts = (w_expert_in[0], whole(ein_parts))
    eout_parts = (w_expert_out[0], eout_other)
    sin_parts = (w_shared_in, whole(sin_parts))
    sout_parts = (w_shared_out, whole(sout_parts))

    capacity = 4 * rows // experts

    def expert_pass(m, four, grads, guest=None, token=None):
        hidden = gather_rest(four).reshape(-1, width)
        if token is not None:
            hidden = after(hidden, token)
        grad, weight = gather_rest(cot_four[m]).reshape(-1, width), (gates_four, m)
        if capacity < rows:
            weight = lax.dynamic_index_in_dim(
                gather_rest(gates_four)[:, :, m], lax.axis_index("expert"), 1, False
            )
            chosen = weight > 0
            slots = jnp.cumsum(chosen.astype(jnp.int32), 1) - 1
            select = (
                chosen[:, None] & (slots[:, None] == jnp.arange(capacity, dtype=jnp.int32)[:, None])
            ).astype(BF)
            squeeze = lambda v: jnp.einsum("bcr,brd->bcd", select, v.reshape(-1, rows, width)).reshape(-1, width)
            spread = lambda v: jnp.einsum("bcr,bcd->brd", select, v.reshape(-1, capacity, width)).reshape(-1, width)
            hidden, grad = squeeze(hidden), squeeze(grad)
            weight = jnp.sum(select.astype(F32) * weight.reshape(-1, 1, rows), -1).reshape(-1, 1)
        made, dx, *rest = run_ffn(
            hidden, grad, weight, ein_parts, eout_parts, grads=grads, us=42, guest=guest, fb=FB // (1 + m)
        )
        if capacity < rows:
            made, dx = spread(made), spread(dx)
        return made, dx, rest[:3], rest[3:]

    heads = width // HEAD // groups
    buf, dma = pltpu.VMEM, pltpu.SemaphoreType.DMA
    guest = (
        functools.partial(rows_guest, heads=heads),
        ((got1, True), (x, True), (mat_out, True), (gains, True), (rows0, False)),
        [
            struct((rows, width), BF),
            struct((rows, width), F32),
            struct((4, rows, width), BF),
            struct((MICRO, rows, width), BF),
        ],
        [buf((rows, width), BF), buf((rows, width), F32), buf((rows, width), BF), dma((3,)), dma((3,)), dma((5,))],
        4,
    )
    made0, dx0, g_expert, (att1, res1, rows1, nf_both) = expert_pass(0, rows0, None, guest)
    att, res = (att0, att1), (res0, res1)
    shared, dx_shared, *g_shared = run_ffn(
        nf_both.reshape(-1, width), cot, None, sin_parts, sout_parts, us=23
    )
    g_shared = [g.reshape(shared_shape(g.shape)) for g in g_shared]
    shapes = [g.shape[3:] for g in g_shared]
    guest = (
        halves_guest,
        [(g, False) for g in g_shared],
        [struct((2, *sh), BF) for sh in shapes],
        [buf((2, 2, *sh), BF) for sh in shapes] * 2
        + [buf((2, *sh), BF) for sh in shapes]
        + [dma((6,)), dma((12,)), dma((12,)), dma((3,))],
        5,
    )
    made1, dx1, g_expert, g_shared = expert_pass(1, rows1, g_expert, guest)
    dx0, dx1, made0, made1 = [scatter_rest(v).reshape(4, rows, width) for v in (dx0, dx1, made0, made1)]

    spread = [(j, k) for j in range(3) for k in range(PIECES)]
    early = [(j, k, "xz" if i < EARLY else "x") for i, (j, k) in enumerate(spread)]
    first = spread[EARLY][0]
    late = [(j - first, k, "z") for j, k in spread[EARLY:]]
    attention = (*recvs, *mixed, *lses, all_tags)
    own_sums, (r_gate, r_up, r_sout), (d0, d1, gres, gbf, gg) = run_back(
        g_expert,
        early,
        g_shared,
        attention,
        (dx_shared, *res, gains, cotangent[0], mat_out),
        (dx0, dx1),
        groups,
    )
    own_late, (r_qk, r_v, r_out), grad_input, gain_sum, routed = run_last(
        own_sums[first:],
        late,
        (d0, d1, x, gains, mat_qkv, table, gres, gbf, gg, *att),
        (made0, made1),
        groups,
    )
    output = jnp.stack(
        [
            (res[m] + shared[m * rows : (m + 1) * rows].astype(F32) + routed[m].astype(F32)).astype(BF)
            for m in range(MICRO)
        ]
    )
    r_gain_ffn = pick(rest_sum(gain_sum)[0], 2, dp)
    r_qkv = jnp.concatenate([r_qk, r_v], 1)
    r_sin = jnp.concatenate([r_gate, r_up], 1)
    r_gain_attn = jnp.sum(w_qkv.astype(F32) * r_qkv, 1) / norm_attn.astype(F32)
    e_gate, e_up, r_eout = [
        g.reshape(-1, g.shape[-1]).astype(F32) for g in (*own_sums[:first], *own_late)
    ]
    r_ein = jnp.concatenate([e_gate, e_up], 1)
    return (
        output[None],
        grad_input.reshape(1, MICRO, rows, width),
        r_gain_attn,
        r_qkv,
        r_out,
        r_gain_ffn,
        r_sin,
        r_sout,
        r_ein[None],
        r_eout[None],
    )


def solution(mesh):
    tokens = P(("expert", "dp"), None, "context", None)
    flags = P(("expert", "dp"), None, "context")
    placed = (
        tokens,
        flags,
        flags,
        tokens,
        tokens,
        P("dp"),
        P("dp", None),
        P("dp", None),
        P("dp"),
        P("dp", None),
        P("dp", None),
        P("expert", "dp", None),
        P("expert", "dp", None),
        tokens,
    )
    return jax.shard_map(
        body,
        mesh=mesh,
        in_specs=placed,
        out_specs=(
            tokens,
            tokens,
            P("dp"),
            P("dp", None),
            P("dp", None),
            P("dp"),
            P("dp", None),
            P("dp", None),
            P("expert", "dp", None),
            P("expert", "dp", None),
        ),
        check_vma=False,
    )
```

```python
import functools
import math

import jax
import jax.numpy as jnp
from jax import lax
from jax.experimental import pallas as pl
from jax.experimental.pallas import tpu as pltpu
from jax.sharding import PartitionSpec as P

HEAD = 64
MICRO = 2
TILE = 256
HALF = 128
EPSILON = 1e-05
ROPE_BASE = 10000.0
MASKED = -3e30
HIDDEN = 1 << 20
BF = jnp.bfloat16
F32 = jnp.float32
NT = (((1,), (1,)), ((), ()))
TN = (((0,), (0,)), ((), ()))
VMEM_LIMIT = 60 << 20
FB = 512


def dot(left, right, dims=(((1,), (0,)), ((), ()))):
    return lax.dot_general(left, right, dims, preferred_element_type=F32)


def rms_scale(values):
    return lax.rsqrt(jnp.mean(values * values, -1, keepdims=True) + EPSILON)


def low_lanes(rows):
    return lax.broadcasted_iota(jnp.int32, (rows, HALF), 1) < HEAD


def swap_heads(first, second):
    low = low_lanes(HALF)
    return (
        jnp.where(low, first, pltpu.roll(second, HEAD, 1)),
        jnp.where(low, pltpu.roll(first, HEAD, 1), second),
    )


def rotate(tile, cosines, sines):
    lane = lax.broadcasted_iota(jnp.int32, tile.shape, 1)
    partner = jnp.where(
        lane % HEAD < HEAD // 2,
        pltpu.roll(tile, HALF - HEAD // 2, 1),
        pltpu.roll(tile, HEAD // 2, 1),
    )
    return tile * cosines + partner * sines


def struct(shape, dtype):
    return jax.ShapeDtypeStruct(tuple(shape), dtype)


def project(tokens, gain, w_ref, cosines, sines, pay, groups):
    normed = (tokens * rms_scale(tokens) * gain).astype(BF)
    width = tokens.shape[1]
    per = width // HEAD // groups
    for kind in range(3):
        joined = dot(normed, w_ref[:, kind * width : (kind + 1) * width])
        for pair in range(width // HALF):
            tile = joined[:, pair * HALF : (pair + 1) * HALF]
            if kind < 2:
                tile = rotate(tile, cosines, sines)
            if kind == 0:
                tile = tile * 0.125
            for side, packed in enumerate(swap_heads(tile[:HALF], tile[HALF:])):
                head = 2 * pair + side
                pay[head // per, kind * per + head % per] = packed.astype(BF)


def unpack(ref, index, kind_head):
    tile = ref[index, kind_head]
    return tile, pltpu.roll(tile.astype(F32), HEAD, 1).astype(BF)


def fill_keys(recv, micro, ks, vs, heads):
    groups = recv.shape[0]
    for src in range(groups):
        base = (micro * groups + src) * TILE
        for h in range(heads):
            for store, kind in ((ks, 1), (vs, 2)):
                first, second = unpack(recv, src, kind * heads + h)
                store[h, base : base + HALF] = first
                store[h, base + HALF : base + TILE] = second


def column(row):
    return jnp.broadcast_to(row, (8, row.shape[1])).T[:, :1]


def gain_row(gains, which):
    return jnp.concatenate([gains[0, which : which + 1], gains[1, which : which + 1]], 1)


def masked_rows(ref, index, kind_head):
    tile = ref[index, kind_head].astype(F32)
    both = jnp.concatenate([tile, pltpu.roll(tile, HEAD, 1)], 0)
    return jnp.where(low_lanes(TILE), both, 0.0)


def pack_rows(values):
    return jnp.where(low_lanes(HALF), values[:HALF], pltpu.roll(values[HALF:], HEAD, 1))


def attend_step(step, micro, heads, groups, recv, tags, out_ref, lse_ref, ks, vs, scores):
    count = groups * micro + jnp.minimum(step + 2, groups)
    queries = [masked_rows(recv, step, h).astype(BF) for h in range(heads)]
    tag = column(tags[step, 0, micro])
    same = lax.broadcasted_iota(jnp.int32, (TILE, TILE), 0) == lax.broadcasted_iota(
        jnp.int32, (TILE, TILE), 1
    )

    def first_pass(j, tops):
        keys = pl.ds(pl.multiple_of(j * TILE, TILE), TILE)
        key_tag = tags[j % groups, 1, j // groups]
        seen = (key_tag <= tag) | (same & (j == groups * micro + step))
        new = []
        for h in range(heads):
            part = jnp.where(seen, dot(queries[h], ks[h, keys, :], NT), MASKED)
            scores[h, :, keys] = part
            new.append(jnp.maximum(tops[h], jnp.maximum(part[:, :HALF], part[:, HALF:])))
        return tuple(new)

    tops = lax.fori_loop(
        0, count, first_pass, (jnp.full((TILE, HALF), MASKED, F32),) * heads
    )
    tops = [jnp.max(top, 1, keepdims=True) for top in tops]

    def second_pass(j, carry):
        keys = pl.ds(pl.multiple_of(j * TILE, TILE), TILE)
        sums, totals = carry
        new_sums, new_totals = [], []
        for h in range(heads):
            expo = jnp.exp(scores[h, :, keys] - tops[h])
            new_sums.append(sums[h] + (expo[:, :HALF] + expo[:, HALF:]))
            new_totals.append(totals[h] + dot(expo.astype(BF), vs[h, keys, :]))
        return tuple(new_sums), tuple(new_totals)

    zero = (jnp.zeros((TILE, HALF), F32),) * heads
    sums, totals = lax.fori_loop(0, count, second_pass, (zero, zero))
    lane = lax.broadcasted_iota(jnp.int32, (TILE, HALF), 1)
    logs = jnp.zeros((TILE, HALF), F32)
    for h in range(heads):
        total = jnp.sum(sums[h], 1, keepdims=True)
        out_ref[step, h] = pack_rows(totals[h] / total).astype(BF)
        logs = jnp.where(lane == h, tops[h] + jnp.log(total), logs)
    lse_ref[step] = logs.T[:8]


def back_begin(micro, step, heads, recv, grad, out, qs, gs, deltas, acc):
    ones = jnp.ones((8, HALF), F32)
    for h in range(heads):
        grad_f = masked_rows(grad, step, h)
        qs[h] = masked_rows(recv, step, h).astype(BF)
        gs[h] = grad_f.astype(BF)
        deltas[h] = lax.dot_general(
            ones,
            grad_f * masked_rows(out, step, h),
            NT,
            precision=lax.Precision.HIGHEST,
            preferred_element_type=F32,
        )
    acc[...] = jnp.zeros_like(acc)


def back_tile(micro, step, j, heads, groups, lse, tags, ks, vs, dk, dv, qs, gs, deltas, acc):
    keys = pl.ds(pl.multiple_of(j * TILE, TILE), TILE)
    same = lax.broadcasted_iota(jnp.int32, (TILE, TILE), 0) == lax.broadcasted_iota(
        jnp.int32, (TILE, TILE), 1
    )
    key_tag = column(tags[j % groups, 1, j // groups])
    seen = (key_tag <= tags[step, 0, micro]) | (same & (j == groups * micro + step))
    for h in range(heads):
        key, value = ks[h, keys, :], vs[h, keys, :]
        scores = dot(key, qs[h], NT)
        probs = jnp.where(seen, jnp.exp(scores - lse[step, h : h + 1, :]), 0.0)
        dv[h, keys, :] += dot(probs.astype(BF), gs[h])
        slope = (probs * (dot(value, gs[h], NT) - deltas[h, :1])).astype(BF)
        dk[h, keys, :] += dot(slope, qs[h])
        acc[h] += dot(slope, key, TN)


def back_pack(dk, dv, pay, src, base, heads):
    rows = slice((base + src) * TILE, (base + src + 1) * TILE)
    for h in range(heads):
        pay[src, heads + h] = pack_rows(dk[h, rows]).astype(BF)
        pay[src, 2 * heads + h] = pack_rows(dv[h, rows]).astype(BF)


def natural(ref, first_kind, pair, per):
    tiles = []
    for head in (2 * pair, 2 * pair + 1):
        tiles.append(ref[head // per, first_kind * per + head % per].astype(F32))
    return jnp.concatenate(swap_heads(*tiles), 0)


def remote(src, dst, sems, index, target, arrival=None):
    return pltpu.make_async_remote_copy(
        src_ref=src,
        dst_ref=dst,
        send_sem=sems[0].at[index],
        recv_sem=sems[1].at[index if arrival is None else arrival],
        device_id=target,
        device_id_type=pl.DeviceIdType.MESH,
    )


def meet(barrier, targets):
    for target in targets:
        pl.semaphore_signal(barrier, inc=1, device_id=target, device_id_type=pl.DeviceIdType.MESH)
    pl.semaphore_wait(barrier, len(targets))


def project_out(got, tokens, w_ref, gain, att, res, nf, heads):
    for pair in range(tokens.shape[1] // HALF):
        att[:, pair * HALF : (pair + 1) * HALF] = natural(got, 0, pair, heads).astype(BF)
    residual = tokens.astype(F32) + dot(att[...], w_ref[...])
    res[...] = residual
    nf[...] = (residual * rms_scale(residual) * gain).astype(BF)


class Trade:
    def __init__(self, src, dst, sems, local):
        self.src, self.dst, self.sems, self.local = src, dst, sems, local
        self.z = lax.axis_index("context")
        self.groups = src.shape[0]

    def wire(self, other, arrival):
        return remote(self.src.at[other], self.dst.at[arrival], self.sems, other, {"context": other}, arrival)

    def keep(self, index):
        return pltpu.make_async_copy(self.src.at[index], self.dst.at[index], self.local)

    def send(self, dest):
        @pl.when(dest != self.z)
        def _():
            self.wire(dest, self.z).start()

        @pl.when(dest == self.z)
        def _():
            self.keep(dest).start()

    def await_from(self, other):
        @pl.when(other != self.z)
        def _():
            self.wire(other, other).wait_recv()

        @pl.when(other == self.z)
        def _():
            self.keep(other).wait()

    def collect(self):
        for other in range(self.groups):
            self.await_from(other)

    def release(self):
        for other in range(self.groups):

            @pl.when(other != self.z)
            def _(other=other):
                self.wire(other, self.z).wait_send()


def front_kernel(*refs, heads, groups):
    refs = list(refs)
    take = lambda n: [refs.pop(0) for _ in range(n)]
    x_ref, gains_in, blocks, keeps, gates_in = take(5)
    w_qkv, w_out, w_ein, w_eout, w_sin, w_sout, cot = take(7)
    recv_out, mixed_out, lse_out, cot_out = take(2), take(2), take(2), take(2)
    att_out, res_out, rows_out, got_out, gates_out, tags_out = take(6)
    qkv_out, wout_out, ein_out, eout_out, sin_out, sout_out, gains_out, table_out = take(8)
    wq, wo, gains, tags, pay, recv, ks, vs, scores, mixed, got, lse, att, res, nf, table = take(16)
    s_qkv, s_out, s_gain, s_exp, s_tag, s_gate, s_cot, s_pay, s_mix, s_row = [take(2) for _ in range(10)]
    local, self_pay, self_mix, stores = take(4)
    e, z, d = lax.axis_index("expert"), lax.axis_index("context"), lax.axis_index("dp")
    core, y = e % 2, e // 2 % 2
    to_x, to_core, to_y = {"dp": 1 - d}, {"expert": e + 1 - 2 * core}, {"expert": e + 2 - 4 * y}
    others = [{"context": (z + k) % groups} for k in range(1, groups)]
    width = x_ref.shape[2]

    loads = [
        pltpu.make_async_copy(w_qkv, wq.at[d], local.at[0]),
        pltpu.make_async_copy(w_out, wo.at[d], local.at[1]),
        pltpu.make_async_copy(gains_in, gains.at[d], local.at[2]),
    ]
    for copy in loads:
        copy.start()
    meet(pltpu.get_barrier_semaphore(), [to_x, to_core, to_y, *others])

    x_qkv = remote(w_qkv.at[core], wq.at[d, core], s_qkv, 0, to_x)
    x_gain = remote(gains_in, gains.at[d], s_gain, 0, to_x)
    x_out = remote(w_out.at[core], wo.at[d, core], s_out, 0, to_x)
    half = z % 2
    to_mate = {"context": z + 1 - 2 * half}
    x_exp = [
        remote(w_ein.at[half], ein_out.at[half], s_exp, 0, to_x),
        remote(w_eout, eout_out, s_exp, 1, to_x),
        remote(w_sin.at[core, y], sin_out.at[core, y], s_exp, 2, to_x),
        remote(w_sout.at[core, y], sout_out.at[core, y], s_exp, 3, to_x),
    ]
    n_exp = [
        remote(ein_out.at[half], ein_out.at[half], s_exp, 4, to_mate),
        remote(sin_out.at[core, y], sin_out.at[core, y], s_exp, 5, to_y),
        remote(sout_out.at[core, y], sout_out.at[core, y], s_exp, 6, to_y),
        remote(sin_out.at[core], sin_out.at[core], s_exp, 7, to_core),
        remote(sout_out.at[core], sout_out.at[core], s_exp, 8, to_core),
    ]
    for copy in (x_qkv, x_gain, x_out, x_exp[0], x_exp[2], x_exp[3], x_exp[1]):
        copy.start()
    for m in range(MICRO):
        block = blocks[0, m : m + 1, :] + 8 * m
        tags[z, 0, m] = block
        tags[z, 1, m] = jnp.where(keeps[0, m : m + 1, :] == 1, block, HIDDEN)
    tag_trade = [remote(tags.at[z], tags.at[z], s_tag, k, others[k]) for k in range(groups - 1)]
    for copy in tag_trade:
        copy.start()
    own_copies = [
        pltpu.make_async_copy(gates_in, gates_out.at[0], stores.at[0]),
        pltpu.make_async_copy(cot.at[0], cot_out[0].at[0], stores.at[1]),
        pltpu.make_async_copy(cot.at[1], cot_out[1].at[0], stores.at[2]),
    ]
    for copy in own_copies:
        copy.start()
    y_gate = remote(gates_in, gates_out.at[1], s_gate, 0, to_y)
    y_cot = [remote(cot.at[m], cot_out[m].at[1], s_cot, m, to_y) for m in range(MICRO)]
    c_gate = [
        remote(gates_in, gates_out.at[2], s_gate, 1, to_core),
        remote(gates_out.at[1], gates_out.at[3], s_gate, 2, to_core),
    ]
    c_cot = [remote(cot.at[m], cot_out[m].at[2], s_cot, 2 + m, to_core) for m in range(MICRO)] + [
        remote(cot_out[m].at[1], cot_out[m].at[3], s_cot, 4 + m, to_core) for m in range(MICRO)
    ]
    y_gate.start()
    for copy in y_cot:
        copy.start()

    row = lax.broadcasted_iota(jnp.int32, (MICRO * TILE, HALF), 0)
    lane = lax.broadcasted_iota(jnp.int32, (MICRO * TILE, HALF), 1)
    place = row // TILE * (TILE * groups) + z * TILE + row % TILE
    freq = jnp.exp((-math.log(ROPE_BASE) * 2.0 / HEAD) * (lane % (HEAD // 2)).astype(F32))
    angle = place.astype(F32) * freq
    table[0] = jnp.cos(angle)
    table[1] = jnp.where(lane % HEAD < HEAD // 2, -jnp.sin(angle), jnp.sin(angle))

    c_qkv = remote(wq.at[1 - d, core], wq.at[1 - d, core], s_qkv, 1, to_core)
    c_out = remote(wo.at[1 - d, core], wo.at[1 - d, core], s_out, 1, to_core)
    for copy in loads:
        copy.wait()
    x_qkv.wait_recv()
    c_qkv.start()
    x_gain.wait_recv()
    c_qkv.wait_recv()
    both = [gain_row(gains, k) for k in range(2)]
    w_full = wq.reshape(width, 3 * width)
    trades, returns = [], []
    for m in range(MICRO):
        span = slice(m * TILE, (m + 1) * TILE)
        project(x_ref[m].astype(F32), both[0], w_full, table[0, span, :], table[1, span, :], pay.at[m], groups)
        trade = Trade(pay.at[m], recv.at[m], [s.at[m] for s in s_pay], self_pay.at[m])
        for dest in range(groups):
            trade.send(dest)
        trades.append(trade)
    c_gate[0].start()
    for copy in c_cot[:MICRO]:
        copy.start()
    for k in range(groups - 1):
        source = (z + groups - 1 - k) % groups
        remote(tags.at[z], tags.at[source], s_tag, k, others[k]).wait_recv()

    def attend(m, first, last):
        trade = Trade(mixed.at[m], got.at[m], [s.at[m] for s in s_mix], self_mix.at[m])

        def one(step, carry):
            attend_step(step, m, heads, groups, recv.at[m], tags, mixed.at[m], lse.at[m], ks, vs, scores)
            trade.send(step)
            return carry

        lax.fori_loop(first, last, one, 0)
        return trade

    row_y = remote(nf, rows_out.at[1], s_row, 0, to_y)
    row_core = remote(nf, rows_out.at[2], s_row, 1, to_core)
    row_next = remote(rows_out.at[1], rows_out.at[3], s_row, 2, to_core)

    trades[0].collect()
    fill_keys(recv.at[0], 0, ks, vs, heads)
    back0 = attend(0, 0, groups)
    x_exp[0].wait_recv()
    n_exp[0].start()
    x_out.wait_recv()
    c_out.start()
    y_gate.wait_recv()
    c_gate[1].start()
    for m in range(MICRO):
        y_cot[m].wait_recv()
        c_cot[MICRO + m].start()
    trades[1].collect()
    fill_keys(recv.at[1], 1, ks, vs, heads)
    for k in (2, 3):
        x_exp[k].wait_recv()
        n_exp[k - 1].start()
    back1 = attend(1, 0, 2)
    c_out.wait_recv()
    back0.collect()
    project_out(got.at[0], x_ref[0], wo.reshape(width, width), both[1], att, res, nf, heads)
    row_y.start()
    row_core.start()
    back1 = attend(1, 2, groups)
    row_y.wait_recv()
    row_next.start()
    for k in (1, 2):
        n_exp[k].wait_recv()
        n_exp[k + 2].start()
    keep = []
    for m in range(MICRO):
        keep += [(recv.at[m], recv_out[m]), (mixed.at[m], mixed_out[m]), (lse.at[m], lse_out[m])]
    keep += [(att, att_out), (res, res_out), (nf, rows_out.at[0])]
    keep += [(tags, tags_out), (wq, qkv_out), (wo, wout_out), (gains, gains_out), (table, table_out)]
    keep = [pltpu.make_async_copy(a, b, stores.at[3 + i]) for i, (a, b) in enumerate(keep)]
    for copy in keep:
        copy.start()
    back1.collect()
    got_copy = pltpu.make_async_copy(got.at[1], got_out, stores.at[3 + len(keep)])
    got_copy.start()
    for copy in (*keep, got_copy, *own_copies):
        copy.wait()
    for m in range(MICRO):
        trades[m].release()
    row_y.wait_send()
    row_core.wait()
    row_next.wait()
    back0.release()
    back1.release()
    x_exp[1].wait_recv()
    for copy in n_exp:
        copy.wait_send()
    for copy in (n_exp[0], n_exp[3], n_exp[4]):
        copy.wait_recv()
    for copy in (*c_gate, *c_cot):
        copy.wait()
    for copy in (*x_exp, x_qkv, x_gain, x_out, c_qkv, c_out, y_gate, *y_cot, *tag_trade):
        copy.wait_send()


def run_front(x, gains, blocks, keeps, gates, w_qkv, w_out, w_ein, w_eout, w_sin, w_sout, cot, groups):
    _, rows, width = x.shape
    heads = width // HEAD // groups
    k = width // 4
    tags = (groups, 2, MICRO, 1, rows)
    w_qkv = w_qkv.reshape(2, k, 3 * width)
    w_out = w_out.reshape(2, k, width)
    w_ein = w_ein.reshape(2, -1, w_ein.shape[1])
    w_sin, w_sout = [w.reshape(2, 2, -1, w.shape[1]) for w in (w_sin, w_sout)]
    vmem = pl.BlockSpec(memory_space=pltpu.VMEM)
    anywhere = pl.BlockSpec(memory_space=pl.ANY)
    packed = lambda n: (groups, n * heads, HALF, HALF)
    held = MICRO * groups * TILE
    twice = lambda *a: [struct(*a)] * 2
    outs = (
        twice(packed(3), BF)
        + twice(packed(1), BF)
        + twice((groups, 8, TILE), F32)
        + twice((4, rows, width), BF)
        + [
            struct((rows, width), BF),
            struct((rows, width), F32),
            struct((4, rows, width), BF),
            struct(packed(1), BF),
            struct((4, *gates.shape), F32),
            struct(tags, jnp.int32),
            struct((2, 2, k, 3 * width), BF),
            struct((2, 2, k, width), BF),
            struct(w_ein.shape, BF),
            struct(w_eout.shape, BF),
            struct(w_sin.shape, BF),
            struct(w_sout.shape, BF),
            struct((2, *gains.shape), F32),
            struct((2, MICRO * rows, HALF), F32),
        ]
    )
    v = pltpu.VMEM
    dma = lambda *n: pltpu.SemaphoreType.DMA(n)
    scratch = [
        v((2, 2, k, 3 * width), BF),
        v((2, 2, k, width), BF),
        v((2, *gains.shape), F32),
        v(tags, jnp.int32),
        v((MICRO, *packed(3)), BF),
        v((MICRO, *packed(3)), BF),
        v((heads, held, HALF), BF),
        v((heads, held, HALF), BF),
        v((heads, TILE, held), F32),
        v((MICRO, *packed(1)), BF),
        v((MICRO, *packed(1)), BF),
        v((MICRO, groups, 8, TILE), F32),
        v((rows, width), BF),
        v((rows, width), F32),
        v((rows, width), BF),
        v((2, MICRO * rows, HALF), F32),
    ]
    for shape in ((2,), (2,), (1,), (9,), (groups - 1,), (3,), (6,), (MICRO, groups), (MICRO, groups), (3,)):
        scratch += [dma(*shape), dma(*shape)]
    scratch += [dma(3), dma(MICRO), dma(MICRO), dma(3 + 3 * MICRO + 9)]
    return pl.pallas_call(
        functools.partial(front_kernel, heads=heads, groups=groups),
        out_shape=tuple(outs),
        in_specs=[vmem] * 5 + [anywhere] * 7,
        out_specs=(anywhere,) * len(outs),
        scratch_shapes=scratch,
        compiler_params=pltpu.CompilerParams(
            vmem_limit_bytes=VMEM_LIMIT, collective_id=3, has_side_effects=True
        ),
        cost_estimate=price(130),
    )(x, gains, blocks, keeps, gates, w_qkv, w_out, w_ein, w_eout, w_sin, w_sout, cot)


def ffn_kernel(*refs, tr, halves, gated, micro, summed, guest, guest_counts):
    refs = list(refs)
    take = lambda n: [refs.pop(0) for _ in range(n)]
    x_ref, dy_in = take(2)
    gate_in = take(1)[0] if gated else None
    wg_parts, wu_parts, wo_parts = take(2), take(2), take(2)
    g0 = take(3) if summed else None
    guest_in = take(guest_counts[0])
    y_ref, dx_ref, dwg_ref, dwu_ref, dwo_ref = take(5)
    guest_out = take(guest_counts[1])
    xt, yacc, dxacc, hs, djg, dju, wg_ref, wu_ref, wo_ref = take(9)
    dy_ref, gate_ref = take(2) if gated else (dy_in, None)
    f = pl.program_id(0)
    last = pl.num_programs(0) - 1
    rows = x_ref.shape[0]
    span = wg_parts[0].shape[0]
    dp = lax.axis_index("dp")
    visits = guest(guest_in, guest_out, refs) if guest else {}

    @pl.when(f == 0)
    def _():
        if 0 in visits:
            visits[0]()
        xt[...] = x_ref[...].T
        yacc[...] = jnp.zeros_like(yacc)
        dxacc[...] = jnp.zeros_like(dxacc)
        if gated:
            if micro is None:
                gate_ref[...] = gate_in[...]
            else:
                for block in range(gate_in.shape[0]):
                    row = gate_in[block, lax.axis_index("expert"), micro : micro + 1, :]
                    gate_ref[block * TILE : (block + 1) * TILE, :] = column(row)
            dy_ref[...] = (dy_in[...].astype(F32) * gate_ref[...]).astype(BF)

    for step, visit in visits.items():
        if step not in (0, "end"):
            pl.when(f == step)(visit)

    for index, part in enumerate((dp, 1 - dp)):
        place = pl.ds(pl.multiple_of(part * span, HALF // 2), span)
        wg_ref[place, :] = wg_parts[index][...]
        wu_ref[place, :] = wu_parts[index][...]

        @pl.when(f // halves == part)
        def _(index=index):
            wo_ref[...] = wo_parts[index][...]

    wg, wu, wo = wg_ref[...], wu_ref[...], wo_ref[...]

    def tile(i, carry):
        r = pl.ds(pl.multiple_of(i * tr, tr), tr)
        x = x_ref[r, :]
        g = dot(x, wg)
        u = dot(x, wu)
        dh = dot(dy_ref[r, :], wo, NT)
        sig = 1.0 / (1.0 + jnp.exp(-g))
        act = g * sig
        h = (act * u).astype(BF)
        dg = (dh * u * (sig * (1.0 + g * (1.0 - sig)))).astype(BF)
        du = (dh * act).astype(BF)
        hs[r, :] = h
        djg[r, :] = dg
        dju[r, :] = du
        yacc[r, :] += dot(h, wo)
        dxacc[r, :] += dot(dg, wg, NT) + dot(du, wu, NT)
        return carry

    lax.fori_loop(0, rows // tr, tile, 0)
    grads = [dot(xt[...], djg[...]), dot(xt[...], dju[...]), dot(hs[...], dy_ref[...], TN)]
    for k, out in enumerate((dwg_ref, dwu_ref, dwo_ref)):
        value = grads[k]
        if summed:
            value = value + g0[k][...].astype(F32)
        out[...] = value.astype(BF)

    @pl.when(f == last)
    def _():
        made = yacc[...].astype(BF)
        if gated:
            made = (made.astype(F32) * gate_ref[...]).astype(BF)
        y_ref[...] = made
        dx_ref[...] = dxacc[...].astype(BF)
        if "end" in visits:
            visits["end"]()


def run_ffn(x, dy, gate, w_in, w_out, grads=None, tr=512, fb=FB, us=10, guest=None):
    rows, d = x.shape
    ff = sum(w.shape[0] for w in w_out)
    nf = ff // fb
    halves = nf // 2
    gated = gate is not None
    gate, micro = gate if isinstance(gate, tuple) else (gate, None)
    whole = lambda a: pl.BlockSpec(a.shape, lambda f: (0,) * a.ndim, pipeline_mode=pl.Buffered(1))
    args = [x, dy] + ([gate] if gated else [])
    specs = [whole(a) for a in args]
    args += list(w_in) * 2 + list(w_out)
    span = w_in[0].shape[0]
    specs += [pl.BlockSpec((span, fb), lambda f: (0, f))] * 2
    specs += [pl.BlockSpec((span, fb), lambda f: (0, f + nf))] * 2
    specs += [pl.BlockSpec((fb, d), lambda f: (f % halves, 0))] * 2
    wide = pl.BlockSpec((d, fb), lambda f: (0, f))
    tall = pl.BlockSpec((fb, d), lambda f: (f, 0))
    if grads is not None:
        args += list(grads)
        specs += [wide, wide, tall]
    full = pl.BlockSpec((rows, d), lambda f: (0, 0), pipeline_mode=pl.Buffered(1))
    outs = [
        struct((rows, d), BF),
        struct((rows, d), BF),
        struct((d, ff), BF),
        struct((d, ff), BF),
        struct((ff, d), BF),
    ]
    out_specs = [full, full, wide, wide, tall]
    scratch = [
        pltpu.VMEM((d, rows), BF),
        pltpu.VMEM((rows, d), F32),
        pltpu.VMEM((rows, d), F32),
        pltpu.VMEM((rows, fb), BF),
        pltpu.VMEM((rows, fb), BF),
        pltpu.VMEM((rows, fb), BF),
        pltpu.VMEM((d, fb), BF),
        pltpu.VMEM((d, fb), BF),
        pltpu.VMEM((fb, d), BF),
    ] + ([pltpu.VMEM((rows, d), BF), pltpu.VMEM((rows, 1), F32)] if gated else [])
    anywhere = pl.BlockSpec(memory_space=pl.ANY)
    counts, visit, params = (0, 0), None, {}
    if guest is not None:
        visit, guest_args, guest_outs, guest_scratch, collective_id = guest
        args += [a for a, _ in guest_args]
        specs += [whole(a) if near else anywhere for a, near in guest_args]
        outs += guest_outs
        out_specs += [anywhere] * len(guest_outs)
        scratch += guest_scratch
        counts = (len(guest_args), len(guest_outs))
        params = {"collective_id": collective_id, "has_side_effects": True}
    return pl.pallas_call(
        functools.partial(
            ffn_kernel,
            tr=math.gcd(tr, rows),
            halves=halves,
            gated=gated,
            micro=micro,
            summed=grads is not None,
            guest=visit,
            guest_counts=counts,
        ),
        out_shape=tuple(outs),
        grid=(nf,),
        in_specs=specs,
        out_specs=tuple(out_specs),
        scratch_shapes=scratch,
        compiler_params=pltpu.CompilerParams(vmem_limit_bytes=VMEM_LIMIT, **params),
        cost_estimate=price(us),
    )(*args)


def rows_guest(ins, outs, bufs, *, heads):
    got, x_ref, w_ref, gain_ref, first_rows = ins
    att_out, res_out, rows_out, both_out = outs
    att, res, nf, sends, recvs, stores = bufs
    e = lax.axis_index("expert")
    core, y = e % 2, e // 2 % 2
    to_core, to_y = {"expert": e + 1 - 2 * core}, {"expert": e + 2 - 4 * y}
    wires = [
        remote(nf, rows_out.at[1], (sends, recvs), 0, to_y),
        remote(nf, rows_out.at[2], (sends, recvs), 1, to_core),
        remote(rows_out.at[1], rows_out.at[3], (sends, recvs), 2, to_core),
    ]
    keep = [
        (att, att_out),
        (res, res_out),
        (nf, rows_out.at[0]),
        (nf, both_out.at[1]),
        (first_rows.at[0], both_out.at[0]),
    ]
    keep = [pltpu.make_async_copy(a, b, stores.at[i]) for i, (a, b) in enumerate(keep)]

    def begin():
        meet(pltpu.get_barrier_semaphore(), [to_core, to_y])
        project_out(got, x_ref[1], w_ref, gain_row(gain_ref, 1), att, res, nf, heads)
        for copy in (wires[0], wires[1], *keep):
            copy.start()

    def later():
        wires[0].wait_recv()
        wires[2].start()

    def end():
        wires[0].wait_send()
        wires[1].wait()
        wires[2].wait()
        for copy in keep:
            copy.wait()

    return {0: begin, 2: later, "end": end}


def halves_guest(ins, outs, bufs):
    n = len(ins)
    totals, cores, gots = bufs[:n], bufs[n : 2 * n], bufs[2 * n : 3 * n]
    loads, sends, recvs, stores = bufs[3 * n :]
    e, d = lax.axis_index("expert"), lax.axis_index("dp")
    core, y = e % 2, e // 2 % 2
    to_x, to_core, to_y = {"dp": 1 - d}, {"expert": e + 1 - 2 * core}, {"expert": e + 2 - 4 * y}
    both = [(i, h) for i in range(n) for h in range(2)]
    sems = (sends, recvs)
    load = {(i, h): pltpu.make_async_copy(ins[i].at[h, core], totals[i].at[h], loads.at[2 * i + h]) for i, h in both}
    first = {(i, h): remote(ins[i].at[h, 1 - core], cores[i].at[h], sems, 2 * i + h, to_core) for i, h in both}

    def half(i, h):
        if i in FLIPPED:
            return remote(totals[i].at[1 - d, h], gots[i].at[h], sems, 2 * n + 2 * i + h, to_x)
        return remote(totals[i].at[h, 1 - y], gots[i].at[h], sems, 2 * n + 2 * i + h, to_y)

    store = [pltpu.make_async_copy(gots[i], outs[i], stores.at[i]) for i in range(n)]

    def begin():
        meet(pltpu.get_barrier_semaphore(), [to_x, to_core, to_y])
        for key in both:
            first[key].start()
            load[key].start()

    def later():
        for i in range(n):
            for h in range(2):
                load[i, h].wait()
                first[i, h].wait_recv()
            totals[i][...] = totals[i][...] + cores[i][...]
            for h in range(2):
                half(i, h).start()

    def end():
        for i, h in both:
            half(i, h).wait_recv()
            mine = totals[i][d, h] if i in FLIPPED else totals[i][h, y]
            gots[i][h] = mine + gots[i][h]
        for copy in store:
            copy.start()
        for key in both:
            first[key].wait_send()
            half(*key).wait_send()
        for copy in store:
            copy.wait()

    return {0: begin, 1: later, "end": end}


def price(us):
    return pl.CostEstimate(flops=int(us * 1.15e9), bytes_accessed=0, transcendentals=0)


def norm_back(values, scale, gain, grad):
    gain_grad = jnp.sum(grad * values * scale, 0, keepdims=True)
    scaled = gain * grad
    grad_in = scale * scaled - values * (scale * scale * scale) * jnp.mean(
        scaled * values, -1, keepdims=True
    )
    return grad_in, gain_grad


def mid_core(grad, residual, gain, cot, w_ref, pay, gres_ref, gbf_ref, per):
    back, gain_grad = norm_back(residual, rms_scale(residual), gain, grad)
    total = cot.astype(F32) + back
    gres_ref[...] = total
    gbf_ref[...] = total.astype(BF)
    mixed = dot(gbf_ref[...], w_ref[...], NT)
    for pair in range(mixed.shape[1] // HALF):
        tile = mixed[:, pair * HALF : (pair + 1) * HALF]
        for side, packed in enumerate(swap_heads(tile[:HALF], tile[HALF:])):
            head = 2 * pair + side
            pay[head // per, head % per] = packed.astype(BF)
    return gain_grad


def finish(d0, d1, x_ref, gain_ref, w_ref, table, gres, atts, gbfs, gin_ref, gq, gv, go, gj, per):
    width = x_ref.shape[2]
    for micro, ref in enumerate((d0, d1)):
        rows = slice(micro * TILE, (micro + 1) * TILE)
        cosines, sines = table[0, rows, :], table[1, rows, :]
        for kind in range(3):
            for pair in range(width // HALF):
                tile = natural(ref, kind, pair, per)
                if kind == 0:
                    tile = tile * 0.125
                if kind < 2:
                    tile = rotate(tile, cosines, -sines)
                gj[rows, kind * width + pair * HALF : kind * width + (pair + 1) * HALF] = tile.astype(BF)
    tokens = x_ref[...].reshape(MICRO * TILE, width).astype(F32)
    scale = rms_scale(tokens)
    gain = gain_row(gain_ref, 0)
    turned = (tokens * scale * gain).astype(BF).T
    split = gq.shape[-1]
    gq[...] = dot(turned, gj[:, :split]).astype(BF).reshape(gq.shape)
    gv[...] = dot(turned, gj[:, split:]).astype(BF).reshape(gv.shape)
    go[...] = (dot(atts[0][...], gbfs[0], TN) + dot(atts[1][...], gbfs[1], TN)).astype(BF).reshape(go.shape)
    yield
    first = dot(gj[...], w_ref[...], NT)
    back, _ = norm_back(tokens, scale, gain, first)
    for micro in range(MICRO):
        rows = slice(micro * TILE, (micro + 1) * TILE)
        gin_ref[rows, :] = gres[micro] + back[rows]


def exchange(value, axis, mask):
    size = lax.axis_size(axis)
    return lax.ppermute(value, axis, [(i, i ^ mask) for i in range(size)])


def bits_of(size):
    return [1 << b for b in range(size.bit_length() - 1)]


def gather_rest(value):
    for mask in bits_of(lax.axis_size("expert"))[2:]:
        value = jnp.concatenate([value, exchange(value, "expert", mask)], 0)
    return value


def scatter_rest(value):
    for mask in reversed(bits_of(lax.axis_size("expert"))[2:]):
        half = value.shape[0] // 2
        got = exchange(value[half:], "expert", mask)
        value = (value[:half].astype(F32) + got.astype(F32)).astype(value.dtype)
    return value


def ordered(flag, mine, theirs):
    first = jnp.where(flag == 0, mine, theirs)
    second = jnp.where(flag == 0, theirs, mine)
    return jnp.concatenate([first, second], 0)


def pick(value, parts, index):
    size = value.shape[0] // parts
    return lax.dynamic_slice_in_dim(value, index * size, size, 0)


def after(value, token):
    return lax.optimization_barrier((value, token))[0]


PIECES = 4
FLIPPED = (1,)
EARLY = 7
AHEAD = 2
PLAN = {
    -1: ("b0", "b1", "b2", "A0", "rs1", "c1", "A1", "B0", "rs2", "c0", "d1", "c2", "C0", "rs3", "B1", "A2",),
    4: ("e1",),
    6: ("A3",),
    7: ("d0",),
    9: ("A4",),
    12: ("d2",),
    15: ("C1",),
    16: ("A5",),
    18: ("B2",),
    19: ("e0",),
    20: ("B3",),
    21: ("e2",),
    24: ("A6", "f2",),
    25: ("C2",),
    27: ("B4",),
    28: ("f1",),
    29: ("C3",),
    32: ("B5",),
    34: ("C4",),
    37: ("B6",),
    39: ("C5", "f0",),
    42: ("zhome", "A7", "g1", "D5", "A8", "D3", "g2", "D2", "A10", "g0", "h1", "C6", "A9", "h2", "D1", "h0", "A11", "D0", "D4", "D6",),
}
LAST_PLAN = (
    "A0", "A1", "A2", "A3", "B0", "a0", "B1", "C0", "a1", "a2",
    "b0", "B2", "C1", "b2", "D0", "B3", "b1", "C2", "c0", "c2",
    "d0", "c1", "A4", "C3", "f0", "d2", "d1", "e0", "B4", "f1",
    "g0", "e1", "f2", "e2", "D3", "zrest", "C4", "D2", "g1", "g2",
    "D1", "h0", "D4", "h1", "h2",
)


class Engine:
    def __init__(self, own, com, own_buf, com_buf, own_out, com_out, sems, halved=False):
        self.halved = halved
        self.flip = [i in FLIPPED for i in range(len(com))]
        self.own, self.com, self.own_buf, self.com_buf = own, com, own_buf, com_buf
        self.own_out, self.com_out = own_out, com_out
        e, z, d = lax.axis_index("expert"), lax.axis_index("context"), lax.axis_index("dp")
        groups = lax.axis_size("context")
        self.d, self.core, self.y = d, e % 2, e // 2 % 2
        self.outer = (z == 0) | (z == 3)
        self.inner = (z == 1) | (z == 2)
        self.to_x = {"dp": 1 - d}
        self.to_core = {"expert": e + 1 - 2 * self.core}
        self.to_y = {"expert": e + 2 - 4 * self.y}
        self.to_mate = {"context": z + 1 - 2 * (z % 2)}
        self.to_mid = {"context": 3 - z}
        self.others = [{"context": (z + k) % groups} for k in range(1, groups)]
        sems = list(sems)
        take = lambda n: [sems.pop(0) for _ in range(n)]
        self.o_load, self.o_store = take(2)
        self.o = {k: take(2) for k in "x123"}
        self.c_load, self.c_store = take(2)
        self.c = {k: take(2) for k in ("core", "y", "x", "1", "2", "3", "fore", "last")}

    @staticmethod
    def scratch(own_shapes, kinds, com_shapes, halved=False):
        v, dma = pltpu.VMEM, lambda n: pltpu.SemaphoreType.DMA((max(n, 1),))
        tiny = (16, HALF)
        own_buf = []
        for s, kind in zip(own_shapes, kinds):
            own_buf += [v(s, BF), v(s if "x" in kind else tiny, BF)]
            own_buf += [v(s if "z" in kind else tiny, BF)] * 2
        com_buf = []
        for s in com_shapes:
            tiny = (16, HALF)
            if halved:
                com_buf += [v((2, *s), BF), v(tiny, BF), v(tiny, BF)] + [v(s, BF)] * 3
            else:
                com_buf += [v((2, 2, *s), BF)] * 2 + [v((2, *s), BF)] + [v(s, BF)] * 3
        chunks, n = len(own_shapes), len(com_shapes)
        sems = [dma(chunks)] * 10 + [dma(2 * n), dma(n)] + [dma(2 * n)] * 4 + [dma(n)] * 12
        return own_buf, com_buf, sems

    def greet(self):
        meet(
            pltpu.get_barrier_semaphore(), [self.to_x, self.to_core, self.to_y, *self.others]
        )

    def o_wire(self, stage, c):
        total, r_x, r_1, r_2 = self.own_buf[c]
        src, k, _ = self.own[c]
        target = {"x": self.to_x, "1": self.to_mate, "2": self.to_mid, "3": self.to_mate}[stage]
        source = {"x": lambda: src.at[1 - self.d, k], "1": lambda: total, "2": lambda: total, "3": lambda: r_1}
        place = {"x": r_x, "1": r_1, "2": r_2, "3": self.own_out[c]}[stage]
        return remote(source[stage](), place, self.o[stage], c, target)

    def o_loading(self, c):
        src, k, kind = self.own[c]
        src = src.at[k] if kind == "z" else src.at[self.d, k]
        return pltpu.make_async_copy(src, self.own_buf[c][0], self.o_load.at[c])

    def o_storing(self, c):
        buf = self.own_buf[c][0 if self.own[c][2] == "x" else 2]
        return pltpu.make_async_copy(buf, self.own_out[c], self.o_store.at[c])

    def A(self, c):
        total, r_x = self.own_buf[c][:2]
        kind = self.own[c][2]
        self.o_loading(c).wait()
        if kind != "z":
            self.o_wire("x", c).wait_recv()
            if c + self.ahead < len(self.own):
                self.o_wire("x", c + self.ahead).start()
            total[...] = total[...] + r_x[...]
        if kind == "x":
            self.o_storing(c).start()
            return

        @pl.when(self.outer)
        def _():
            self.o_wire("1", c).start()

    def B(self, c):
        total, _, r_1, _ = self.own_buf[c]

        @pl.when(self.inner)
        def _():
            self.o_wire("1", c).wait_recv()
            total[...] = total[...] + r_1[...]
            self.o_wire("2", c).start()

    def C(self, c):
        total, _, r_1, r_2 = self.own_buf[c]

        @pl.when(self.inner)
        def _():
            self.o_wire("2", c).wait_recv()
            r_1[...] = total[...] + r_2[...]
            self.o_wire("3", c).start()
            self.o_storing(c).start()

    def D(self, c):
        @pl.when(self.outer)
        def _():
            self.o_wire("3", c).wait_recv()

    def slot(self, i):
        total = self.com_buf[i][0]
        if self.halved:
            return total.at[self.y if self.flip[i] else self.d]
        return total.at[self.d, self.y]

    def c_loading(self, i, h):
        if self.halved:
            return pltpu.make_async_copy(self.com[i], self.com_buf[i][0], self.c_load.at[2 * i])
        return pltpu.make_async_copy(
            self.com[i].at[h, self.core], self.com_buf[i][0].at[h], self.c_load.at[2 * i + h]
        )

    def c_storing(self, i):
        return pltpu.make_async_copy(
            self.com_buf[i][4], self.com_out[i].at[self.core, self.y], self.c_store.at[i]
        )

    def c_wire(self, stage, i, h=0):
        total, r_core, r_y, r_x, r_1, r_2 = self.com_buf[i]
        core, y, d = self.core, self.y, self.d
        out = self.com_out[i]
        if stage == "core":
            return remote(self.com[i].at[h, 1 - core], r_core.at[h], self.c["core"], 2 * i + h, self.to_core)
        if stage == "y" and self.flip[i]:
            return remote(total.at[1 - d, h], r_y.at[h], self.c["y"], 2 * i + h, self.to_x)
        if stage == "x" and self.halved:
            other, target = (1 - y, self.to_y) if self.flip[i] else (1 - d, self.to_x)
            return remote(total.at[other], r_x, self.c["x"], i, target)
        if stage == "x" and self.flip[i]:
            return remote(total.at[d, 1 - y], r_x, self.c["x"], i, self.to_y)
        if stage == "y":
            return remote(total.at[h, 1 - y], r_y.at[h], self.c["y"], 2 * i + h, self.to_y)
        if stage == "x":
            return remote(total.at[1 - d, y], r_x, self.c["x"], i, self.to_x)
        if stage == "1":
            return remote(self.slot(i), r_1, self.c["1"], i, self.to_mate)
        if stage == "2":
            return remote(self.slot(i), r_2, self.c["2"], i, self.to_mid)
        if stage == "3":
            return remote(r_1, out.at[core, y], self.c["3"], i, self.to_mate)
        if stage == "fore":
            return remote(r_1, out.at[core, y], self.c["fore"], i, self.to_y)
        if stage == "back":
            return remote(out.at[core, y], out.at[core, y], self.c["fore"], i, self.to_y)
        return remote(out.at[core], out.at[core], self.c["last"], i, self.to_core)

    def c_start(self, i):
        if self.halved:
            self.c_loading(i, 0).start()
            return
        for h in range(2):
            self.c_wire("core", i, h).start()
            self.c_loading(i, h).start()

    def a(self, i):
        total, r_core = self.com_buf[i][:2]
        for h in range(2):
            self.c_loading(i, h).wait()
            self.c_wire("core", i, h).wait_recv()
        total[...] = total[...] + r_core[...]
        for h in range(2):
            self.c_wire("y", i, h).start()

    def b(self, i):
        total, r_y, y = self.com_buf[i][0], self.com_buf[i][2], self.y
        if self.halved:
            self.c_loading(i, 0).wait()
            self.c_wire("x", i).start()
            return
        for h in range(2):
            self.c_wire("y", i, h).wait_recv()
            if self.flip[i]:
                total[self.d, h] = total[self.d, h] + r_y[h]
            else:
                total[h, y] = total[h, y] + r_y[h]
        self.c_wire("x", i).start()

    def c_(self, i):
        total, r_x = self.slot(i), self.com_buf[i][3]
        self.c_wire("x", i).wait_recv()
        total[...] = total[...] + r_x[...]

        @pl.when(self.outer)
        def _():
            self.c_wire("1", i).start()

    def d_(self, i):
        total, r_1 = self.slot(i), self.com_buf[i][4]

        @pl.when(self.inner)
        def _():
            self.c_wire("1", i).wait_recv()
            total[...] = total[...] + r_1[...]
            self.c_wire("2", i).start()

    def e(self, i):
        total, r_1, r_2 = self.slot(i), self.com_buf[i][4], self.com_buf[i][5]

        @pl.when(self.inner)
        def _():
            self.c_wire("2", i).wait_recv()
            r_1[...] = total[...] + r_2[...]
            self.c_wire("3", i).start()
            self.c_wire("fore", i).start()
            self.c_storing(i).start()

    def f(self, i):
        @pl.when(self.outer)
        def _():
            self.c_wire("3", i).wait_recv()
            self.c_wire("back", i).start()

    def g(self, i):
        @pl.when(self.inner)
        def _():
            self.c_storing(i).wait()

        self.c_wire("fore", i).wait_recv()
        self.c_wire("last", i).start()

    def h(self, i):
        self.c_wire("last", i).wait_recv()

    def start(self, ahead, com=True):
        self.ahead = ahead
        for c in range(min(ahead, len(self.own))):
            if self.own[c][2] != "z":
                self.o_wire("x", c).start()
        if com:
            for i in range(len(self.com)):
                self.c_start(i)
        for c in range(len(self.own)):
            self.o_loading(c).start()

    def run(self, name):
        kind, index = name[0], int(name[1:])
        {"c": self.c_, "d": self.d_}.get(kind, getattr(self, kind, None))(index)

    def close(self):
        chunks, common = range(len(self.own)), range(len(self.com))
        for c in chunks:
            if self.own[c][2] != "z":
                self.o_wire("x", c).wait_send()
            if self.own[c][2] == "x":
                self.o_storing(c).wait()
        chunks = [c for c in chunks if self.own[c][2] != "x"]
        for i in common:
            for h in range(0 if self.halved else 2):
                self.c_wire("core", i, h).wait_send()
                self.c_wire("y", i, h).wait_send()
            self.c_wire("x", i).wait_send()
            self.c_wire("last", i).wait_send()

        @pl.when(self.outer)
        def _():
            for c in chunks:
                self.o_wire("1", c).wait_send()
            for i in common:
                self.c_wire("1", i).wait_send()
                self.c_wire("back", i).wait_send()

        @pl.when(self.inner)
        def _():
            for c in chunks:
                self.o_wire("2", c).wait_send()
                self.o_wire("3", c).wait_send()
                self.o_storing(c).wait()
            for i in common:
                self.c_wire("2", i).wait_send()
                self.c_wire("3", i).wait_send()
                self.c_wire("fore", i).wait_send()


class Arrays:
    def __init__(self, refs):
        self.refs = list(refs)

    def take(self, n):
        got, self.refs = self.refs[:n], self.refs[n:]
        return got

    def engine(self, own_at, sources, own_out, com, com_out, halved=False):
        own_buf = [self.take(4) for _ in own_at]
        com_buf = [self.take(6) for _ in com]
        own = [(sources[j], k, kind) for j, k, kind in own_at]
        places = [own_out[j].at[k] for j, k, _ in own_at]
        return Engine(own, com, own_buf, com_buf, places, com_out, self.take(10 + 18), halved)


def back_kernel(*refs, own_at, sources, common, heads, groups):
    refs = Arrays(refs)
    own_in, com_in = refs.take(sources), refs.take(common)
    recv0, recv1, out0, out1, lse0, lse1, tags = refs.take(7)
    dxs, res0, res1, gain_ref, cot_ref, w_ref = refs.take(6)
    dx_made = refs.take(MICRO)
    own_out, com_out = refs.take(sources), refs.take(common)
    d0_out, d1_out, gres_out, gbf_out, gg_out = refs.take(5)
    engine = refs.engine(own_at, own_in, own_out, com_in, com_out, True)
    dx, r_core, r_y, gres, gbf, gg, pay_o, back_o, pay0, pay1 = refs.take(10)
    ks, vs, dk, dv, qs, gs, deltas, acc = refs.take(8)
    s_dx, s_o, s_0, s_1 = [refs.take(2) for _ in range(4)]
    local, = refs.take(1)

    engine.greet()
    both = range(MICRO)
    send_core = [remote(dx_made[m].at[2:4], r_core.at[m], s_dx, m, engine.to_core) for m in both]
    own_dx = [pltpu.make_async_copy(dx_made[m].at[0:2], dx.at[m], local.at[m]) for m in both]
    for m in both:
        send_core[m].start()
        own_dx[m].start()
    engine.start(AHEAD)
    send_y = [remote(dx.at[m, 1], r_y.at[m], s_dx, MICRO + m, engine.to_y) for m in both]
    trade_o = [
        Trade(pay_o.at[m], back_o.at[m], [s.at[m] for s in s_o], local.at[2 + m]) for m in both
    ]
    homes = [Trade(pay0, d0_out, s_0, local.at[4]), Trade(pay1, d1_out, s_1, local.at[5])]
    results = [
        pltpu.make_async_copy(a, b, local.at[6 + i])
        for i, (a, b) in enumerate(((gres, gres_out), (gbf, gbf_out), (gg, gg_out)))
    ]

    def rs1():
        for m in both:
            own_dx[m].wait()
            send_core[m].wait_recv()
            dx[m] = dx[m] + r_core[m]
            send_y[m].start()

    def middle(m, res_ref):
        send_y[m].wait_recv()
        grad = dxs[m * TILE : (m + 1) * TILE, :].astype(F32) + dx[m, 0].astype(F32) + r_y[m].astype(F32)
        part = mid_core(
            grad, res_ref[...], gain_row(gain_ref, 1), cot_ref[m], w_ref, pay_o.at[m], gres.at[m], gbf.at[m], heads
        )
        for dest in range(groups):
            trade_o[m].send(dest)
        return part

    def rs2():
        gg[...] = middle(0, res0)

    def rs3():
        gg[...] = gg[...] + middle(1, res1)
        for copy in results:
            copy.start()

    def zhome():
        for base, pay, trade in ((groups, pay1, homes[1]), (0, pay0, homes[0])):
            for dest in range(groups):
                back_pack(dk, dv, pay, dest, base, heads)
                trade.send(dest)

    named = {"rs1": rs1, "rs2": rs2, "rs3": rs3, "zhome": zhome}

    def events(slot):
        for name in PLAN.get(slot, ()):
            named[name]() if name in named else engine.run(name)

    for recv, micro in ((recv0, 0), (recv1, 1)):
        fill_keys(recv, micro, ks, vs, heads)
    dk[...] = jnp.zeros_like(dk)
    dv[...] = jnp.zeros_like(dv)
    first_of = (0, sum(min(s + 2, groups) for s in range(groups)))
    total = 2 * first_of[1] + groups * groups
    for micro, (recv, grad, out, lse, pay) in enumerate(
        ((recv0, back_o.at[0], out0, lse0, pay0), (recv1, back_o.at[1], out1, lse1, pay1))
    ):
        begin, end = first_of[micro], (first_of + (total,))[micro + 1]
        if micro == 0:
            events(-1)
        trade_o[micro].collect()

        def step(s, carry, micro=micro, recv=recv, grad=grad, out=out, lse=lse, pay=pay, begin=begin, end=end):
            back_begin(micro, s, heads, recv, grad, out, qs, gs, deltas, acc)
            before = begin + s * (s + 3) // 2 + groups * micro * s

            def tile(j, carry):
                for slot in range(begin, end):
                    if slot in PLAN:

                        @pl.when(before + j == slot)
                        def _(slot=slot):
                            events(slot)

                back_tile(
                    micro, s, j, heads, groups, lse, tags, ks, vs, dk, dv, qs, gs, deltas, acc
                )
                return carry

            lax.fori_loop(0, groups * micro + jnp.minimum(s + 2, groups), tile, 0)
            for h in range(heads):
                pay[s, h] = pack_rows(acc[h]).astype(BF)
            return carry

        lax.fori_loop(0, groups, step, 0)
    events(total)
    for trade in homes:
        trade.collect()
        trade.release()
    for m in both:
        trade_o[m].release()
        send_core[m].wait_send()
        send_y[m].wait_send()
    for copy in results:
        copy.wait()
    engine.close()


def chunk_views(grads):
    return [g.reshape(2, PIECES, g.shape[0] // (2 * PIECES), g.shape[1]) for g in grads]


def shared_shape(shape):
    return (2, 2, 2, shape[0] // 8, shape[1])


def device_call(kernel, args, vmem_args, outs, scratch, collective_id, us, aliases=None):
    anywhere = pl.BlockSpec(memory_space=pl.ANY)
    return pl.pallas_call(
        kernel,
        out_shape=tuple(outs),
        in_specs=[pl.BlockSpec(memory_space=pltpu.VMEM) if v else anywhere for v in vmem_args],
        out_specs=(anywhere,) * len(outs),
        scratch_shapes=scratch,
        input_output_aliases=aliases or {},
        compiler_params=pltpu.CompilerParams(
            vmem_limit_bytes=VMEM_LIMIT, collective_id=collective_id, has_side_effects=True
        ),
        cost_estimate=price(us),
    )(*args)


def rest_sum(value):
    for mask in bits_of(lax.axis_size("expert"))[2:]:
        value = value + exchange(value, "expert", mask)
    return value


def run_back(expert_grads, own_at, shared_grads, attention, middle, dx_made, groups):
    own = chunk_views(expert_grads)
    com = shared_grads
    heads = attention[0].shape[1] // 3
    rows, width = middle[1].shape
    args = [*own, *com, *attention, *middle, *dx_made]
    own_shapes = [own[j].shape[2:] for j, _, _ in own_at]
    com_shapes = [g.shape[1:] for g in com]
    own_buf, com_buf, sems = Engine.scratch(own_shapes, [kind for *_, kind in own_at], com_shapes, True)
    held = MICRO * groups * TILE
    v, dma = pltpu.VMEM, lambda n: pltpu.SemaphoreType.DMA((n,))
    pay = lambda n: (groups, n * heads, HALF, HALF)
    outs = (
        [struct(g.shape[1:], BF) for g in own]
        + [struct((2, 2, *s), BF) for s in com_shapes]
        + [struct(pay(3), BF)] * 2
        + [struct((MICRO, rows, width), F32), struct((MICRO, rows, width), BF), struct((1, width), F32)]
    )
    scratch = [
        *own_buf,
        *com_buf,
        *sems,
        v((MICRO, 2, rows, width), BF),
        v((MICRO, 2, rows, width), BF),
        v((MICRO, rows, width), BF),
        v((MICRO, rows, width), F32),
        v((MICRO, rows, width), BF),
        v((1, width), F32),
        v((MICRO, *pay(1)), BF),
        v((MICRO, *pay(1)), BF),
        v(pay(3), BF),
        v(pay(3), BF),
        v((heads, held, HALF), BF),
        v((heads, held, HALF), BF),
        v((heads, held, HALF), F32),
        v((heads, held, HALF), F32),
        v((heads, TILE, HALF), BF),
        v((heads, TILE, HALF), BF),
        v((heads, 8, TILE), F32),
        v((heads, TILE, HALF), F32),
        dma(2 * MICRO),
        dma(2 * MICRO),
        *[pltpu.SemaphoreType.DMA((MICRO, groups))] * 2,
        *[dma(groups)] * 4,
        dma(9),
    ]
    flags = [False] * (len(own) + len(com)) + [True] * (len(attention) + len(middle))
    flags += [False] * len(dx_made)
    kernel = functools.partial(
        back_kernel, own_at=own_at, sources=len(own), common=len(com), heads=heads, groups=groups
    )
    got = device_call(kernel, args, flags, outs, scratch, 1, 165)
    n, m = len(own), len(com)
    return got[:n], [rest_sum(g.reshape(-1, g.shape[-1]).astype(F32)) for g in got[n : n + m]], got[n + m :]


def last_kernel(*refs, own_at, sources, per):
    refs = Arrays(refs)
    own_in = refs.take(sources)
    d0, d1, x_ref, gain_ref, w_ref, table = refs.take(6)
    (gres, gbfs, gg_in), atts, made = refs.take(3), refs.take(2), refs.take(MICRO)
    own_out, com_out = refs.take(sources), refs.take(3)
    gin_out, gg_out, routed_out = refs.take(3)
    sources = [refs.refs.pop(len(own_at) * 4 + 3 * 6 + 28) for _ in range(3)]
    engine = refs.engine(own_at, own_in, own_out, sources, com_out)
    gj, gin, gg_sum, gg_got, g_send, g_recv, local, row, row_core, row_y, m_send, m_recv = refs.take(12)
    engine.greet()
    engine.start(0, com=False)
    z = lax.axis_index("context")
    rounds = (engine.to_core, engine.to_y, engine.to_x, engine.to_mate, {"context": z + 2 - 4 * (z // 2)})
    wires = [
        remote(gg_sum.at[k], gg_got.at[k], (g_send, g_recv), k, target) for k, target in enumerate(rounds)
    ]
    gg_sum[0] = jnp.broadcast_to(gg_in[...], gg_sum.shape[1:])
    wires[0].start()
    both = range(MICRO)
    row_wires = [remote(made[m].at[2:4], row_core.at[m], (m_send, m_recv), m, engine.to_core) for m in both]
    row_next = [remote(row.at[m, 1], row_y.at[m], (m_send, m_recv), MICRO + m, engine.to_y) for m in both]
    row_own = [pltpu.make_async_copy(made[m].at[0:2], row.at[m], local.at[2 + m]) for m in both]
    row_out = [pltpu.make_async_copy(row.at[m, 0], routed_out.at[m], local.at[2 + m]) for m in both]
    for m in both:
        row_wires[m].start()
        row_own[m].start()
    work = finish(
        d0, d1, x_ref, gain_ref, w_ref, table, gres, atts, gbfs, gin, *sources, gj, per
    )
    store = pltpu.make_async_copy(gin, gin_out, local.at[0])
    next(work)
    for i in range(3):
        engine.c_start(i)
    turn = 0
    for index, name in enumerate(LAST_PLAN):
        if name == "zrest":
            for _ in work:
                pass
            store.start()
        else:
            engine.run(name)
        if name == "a2":
            for m in both:
                row_own[m].wait()
                row_wires[m].wait_recv()
                row[m] = row[m] + row_core[m]
                row_next[m].start()
        if index == len(LAST_PLAN) - 9:
            for m in both:
                row_next[m].wait_recv()
                row[m, 0] = row[m, 0] + row_y[m]
                row_out[m].start()
        if index % 5 == 4 and turn < len(wires):
            wires[turn].wait_recv()
            gg_sum[turn + 1] = gg_sum[turn] + gg_got[turn]
            turn += 1
            if turn < len(wires):
                wires[turn].start()
    total = pltpu.make_async_copy(gg_sum.at[len(wires)], gg_out, local.at[1])
    total.start()
    store.wait()
    total.wait()
    for wire in (*wires, *row_wires, *row_next):
        wire.wait_send()
    for copy in row_out:
        copy.wait()
    engine.close()


def run_last(sums, own_at, parts, made, groups):
    x, w = parts[2], parts[4]
    _, rows, width = x.shape
    args = [*sums, *parts, *made]
    own_shapes = [sums[j].shape[1:] for j, _, _ in own_at]
    com = [shared_shape((width, 3 * width // 2))] * 2 + [shared_shape((width, width))]
    own_buf, com_buf, sems = Engine.scratch(own_shapes, [k for *_, k in own_at], [s[3:] for s in com])
    v = pltpu.VMEM
    outs = (
        [struct(g.shape, BF) for g in sums]
        + [struct((2, 2, *s[3:]), BF) for s in com]
        + [struct((MICRO * rows, width), F32), struct((8, width), F32), struct((MICRO, rows, width), BF)]
    )
    rounds = 5
    scratch = [
        *own_buf,
        *com_buf,
        *sems,
        *[v(s, BF) for s in com],
        v((MICRO * rows, 3 * width), BF),
        v((MICRO * rows, width), F32),
        v((rounds + 1, 8, width), F32),
        v((rounds, 8, width), F32),
        *[pltpu.SemaphoreType.DMA((rounds,))] * 2,
        pltpu.SemaphoreType.DMA((2 + MICRO,)),
        v((MICRO, 2, rows, width), BF),
        v((MICRO, 2, rows, width), BF),
        v((MICRO, rows, width), BF),
        *[pltpu.SemaphoreType.DMA((2 * MICRO,))] * 2,
    ]
    flags = [False] * len(sums) + [True] * len(parts) + [False] * len(made)
    kernel = functools.partial(
        last_kernel, own_at=own_at, sources=len(sums), per=width // HEAD // groups
    )
    got = device_call(
        kernel, args, flags, outs, scratch, 2, 90, {i: i for i in range(len(sums))}
    )
    n = len(sums)
    return got[:n], [rest_sum(g.reshape(-1, g.shape[-1]).astype(F32)) for g in got[n : n + 3]], *got[n + 3 :]


def body(
    inputs,
    keep_flags,
    block_ids,
    expert_ids,
    gate_weights,
    norm_attn,
    w_qkv,
    w_attn_out,
    norm_ffn,
    w_shared_in,
    w_shared_out,
    w_expert_in,
    w_expert_out,
    cotangent,
):
    width = w_qkv.shape[1] // 3
    rows = inputs.shape[2]
    groups = lax.axis_size("context")
    experts = lax.axis_size("expert")
    z = lax.axis_index("context")
    seq_rows = rows * groups
    x = inputs[0]
    cot = cotangent[0].reshape(MICRO * rows, width)

    per_expert = jnp.sum(
        jnp.where(
            expert_ids[0][None] == jnp.arange(experts, dtype=jnp.int32)[:, None, None, None],
            gate_weights[0][None],
            0.0,
        ),
        -1,
    )
    gains = jnp.stack([norm_attn, norm_ffn]).astype(F32)
    (
        *pairs,
        att0,
        res0,
        rows0,
        got1,
        gates_four,
        all_tags,
        mat_qkv,
        mat_out,
        ein_parts,
        eout_other,
        sin_parts,
        sout_parts,
        gains,
        table,
    ) = run_front(
        x,
        gains,
        block_ids,
        keep_flags,
        per_expert,
        w_qkv,
        w_attn_out,
        w_expert_in[0],
        w_expert_out[0],
        w_shared_in,
        w_shared_out,
        cotangent[0],
        groups,
    )
    recvs, mixed, lses, cot_four = [pairs[2 * i : 2 * i + 2] for i in range(4)]
    mat_qkv = mat_qkv.reshape(width, -1)
    mat_out = mat_out.reshape(width, width)
    core = lax.axis_index("expert") % 2
    dp = lax.axis_index("dp")
    whole = lambda w: w.reshape(-1, w.shape[-1])
    ein_parts = (w_expert_in[0], whole(ein_parts))
    eout_parts = (w_expert_out[0], eout_other)
    sin_parts = (w_shared_in, whole(sin_parts))
    sout_parts = (w_shared_out, whole(sout_parts))

    capacity = 4 * rows // experts

    def expert_pass(m, four, grads, guest=None, token=None):
        hidden = gather_rest(four).reshape(-1, width)
        if token is not None:
            hidden = after(hidden, token)
        grad, weight = gather_rest(cot_four[m]).reshape(-1, width), (gates_four, m)
        if capacity < rows:
            weight = lax.dynamic_index_in_dim(
                gather_rest(gates_four)[:, :, m], lax.axis_index("expert"), 1, False
            )
            chosen = weight > 0
            slots = jnp.cumsum(chosen.astype(jnp.int32), 1) - 1
            select = (
                chosen[:, None] & (slots[:, None] == jnp.arange(capacity, dtype=jnp.int32)[:, None])
            ).astype(BF)
            squeeze = lambda v: jnp.einsum("bcr,brd->bcd", select, v.reshape(-1, rows, width)).reshape(-1, width)
            spread = lambda v: jnp.einsum("bcr,bcd->brd", select, v.reshape(-1, capacity, width)).reshape(-1, width)
            hidden, grad = squeeze(hidden), squeeze(grad)
            weight = jnp.sum(select.astype(F32) * weight.reshape(-1, 1, rows), -1).reshape(-1, 1)
        made, dx, *rest = run_ffn(
            hidden, grad, weight, ein_parts, eout_parts, grads=grads, us=42, guest=guest, fb=FB // (1 + m), tr=512 * (1 + m)
        )
        if capacity < rows:
            made, dx = spread(made), spread(dx)
        return made, dx, rest[:3], rest[3:]

    heads = width // HEAD // groups
    buf, dma = pltpu.VMEM, pltpu.SemaphoreType.DMA
    guest = (
        functools.partial(rows_guest, heads=heads),
        ((got1, True), (x, True), (mat_out, True), (gains, True), (rows0, False)),
        [
            struct((rows, width), BF),
            struct((rows, width), F32),
            struct((4, rows, width), BF),
            struct((MICRO, rows, width), BF),
        ],
        [buf((rows, width), BF), buf((rows, width), F32), buf((rows, width), BF), dma((3,)), dma((3,)), dma((5,))],
        4,
    )
    made0, dx0, g_expert, (att1, res1, rows1, nf_both) = expert_pass(0, rows0, None, guest)
    att, res = (att0, att1), (res0, res1)
    shared, dx_shared, *g_shared = run_ffn(
        nf_both.reshape(-1, width), cot, None, sin_parts, sout_parts, us=23
    )
    g_shared = [g.reshape(shared_shape(g.shape)) for g in g_shared]
    shapes = [g.shape[3:] for g in g_shared]
    guest = (
        halves_guest,
        [(g, False) for g in g_shared],
        [struct((2, *sh), BF) for sh in shapes],
        [buf((2, 2, *sh), BF) for sh in shapes] * 2
        + [buf((2, *sh), BF) for sh in shapes]
        + [dma((6,)), dma((12,)), dma((12,)), dma((3,))],
        5,
    )
    made1, dx1, g_expert, g_shared = expert_pass(1, rows1, g_expert, guest)
    dx0, dx1, made0, made1 = [scatter_rest(v).reshape(4, rows, width) for v in (dx0, dx1, made0, made1)]

    spread = [(j, k) for j in range(3) for k in range(PIECES)]
    early = [(j, k, "xz" if i < EARLY else "x") for i, (j, k) in enumerate(spread)]
    first = spread[EARLY][0]
    late = [(j - first, k, "z") for j, k in spread[EARLY:]]
    attention = (*recvs, *mixed, *lses, all_tags)
    own_sums, (r_gate, r_up, r_sout), (d0, d1, gres, gbf, gg) = run_back(
        g_expert,
        early,
        g_shared,
        attention,
        (dx_shared, *res, gains, cotangent[0], mat_out),
        (dx0, dx1),
        groups,
    )
    own_late, (r_qk, r_v, r_out), grad_input, gain_sum, routed = run_last(
        own_sums[first:],
        late,
        (d0, d1, x, gains, mat_qkv, table, gres, gbf, gg, *att),
        (made0, made1),
        groups,
    )
    output = jnp.stack(
        [
            (res[m] + shared[m * rows : (m + 1) * rows].astype(F32) + routed[m].astype(F32)).astype(BF)
            for m in range(MICRO)
        ]
    )
    r_gain_ffn = pick(rest_sum(gain_sum)[0], 2, dp)
    r_qkv = jnp.concatenate([r_qk, r_v], 1)
    r_sin = jnp.concatenate([r_gate, r_up], 1)
    r_gain_attn = jnp.sum(w_qkv.astype(F32) * r_qkv, 1) / norm_attn.astype(F32)
    e_gate, e_up, r_eout = [
        g.reshape(-1, g.shape[-1]).astype(F32) for g in (*own_sums[:first], *own_late)
    ]
    r_ein = jnp.concatenate([e_gate, e_up], 1)
    return (
        output[None],
        grad_input.reshape(1, MICRO, rows, width),
        r_gain_attn,
        r_qkv,
        r_out,
        r_gain_ffn,
        r_sin,
        r_sout,
        r_ein[None],
        r_eout[None],
    )


def solution(mesh):
    tokens = P(("expert", "dp"), None, "context", None)
    flags = P(("expert", "dp"), None, "context")
    placed = (
        tokens,
        flags,
        flags,
        tokens,
        tokens,
        P("dp"),
        P("dp", None),
        P("dp", None),
        P("dp"),
        P("dp", None),
        P("dp", None),
        P("expert", "dp", None),
        P("expert", "dp", None),
        tokens,
    )
    return jax.shard_map(
        body,
        mesh=mesh,
        in_specs=placed,
        out_specs=(
            tokens,
            tokens,
            P("dp"),
            P("dp", None),
            P("dp", None),
            P("dp"),
            P("dp", None),
            P("dp", None),
            P("expert", "dp", None),
            P("expert", "dp", None),
        ),
        check_vma=False,
    )
```
